32 devices in a mesh: dp: 4 (over z), context: 4 (over y, core), tensor: 2 (over x).
Axes of the slice: x: 2, y: 2, z: 4, core: 2. Of those that a mesh axis runs over, the one named last changes fastest.
Arguments:
- hidden_in: bfloat16 [16, 2048, 768], P('dp', 'context'), may hold values from -6 to 6
- out_grad: bfloat16 [16, 2048, 768], P('dp', 'context'), may hold values from -6 to 6
- segment_ids: int32 [16, 2048], P('dp'), may hold values from 0 to 15, never falling along the last dimension, each value on 1 to 1024 neighbouring positions
- token_valid: int32 [16, 2048], P('dp'), may hold values 0 or 1
- random_blocks: int32 [16, 32, 3], P('dp'), may hold values from 2 to 31, as said below
- query_weight: bfloat16 [768, 768], P('dp', 'tensor'), may hold values from -0.21875 to 0.21875
- query_bias: bfloat16 [768], P('tensor'), may hold values from -3 to 3
- key_weight: bfloat16 [768, 768], P('dp', 'tensor'), may hold values from -0.21875 to 0.21875
- value_weight: bfloat16 [768, 768], P('dp', 'tensor'), may hold values from -0.21875 to 0.21875
- value_bias: bfloat16 [768], P('tensor'), may hold values from -3 to 3
- output_weight: bfloat16 [768, 768], P('tensor', 'dp'), may hold values from -0.625 to 0.625
- output_bias: bfloat16 [768], replicated, may hold values from -3 to 3
- norm1_gain: bfloat16 [768], replicated, may hold values from 0.5 to 1.5
- norm1_shift: bfloat16 [768], replicated, may hold values from -3 to 3
- up_weight: bfloat16 [768, 3072], P('dp', 'tensor'), may hold values from -0.21875 to 0.21875
- up_bias: bfloat16 [3072], P('tensor'), may hold values from -3 to 3
- down_weight: bfloat16 [3072, 768], P('tensor', 'dp'), may hold values from -0.109375 to 0.109375
- down_bias: bfloat16 [768], replicated, may hold values from -3 to 3
- norm2_gain: bfloat16 [768], replicated, may hold values from 0.5 to 1.5
- norm2_shift: bfloat16 [768], replicated, may hold values from -3 to 3
Outputs:
- layer_out: bfloat16 [16, 2048, 768], P('dp', 'context')
- input_grad: float32 [16, 2048, 768], P('dp', 'context')
- query_weight_grad: float32 [768, 768], P('dp', 'tensor')
- query_bias_grad: float32 [768], P('tensor')
- key_weight_grad: float32 [768, 768], P('dp', 'tensor')
- value_weight_grad: float32 [768, 768], P('dp', 'tensor')
- value_bias_grad: float32 [768], P('tensor')
- output_weight_grad: float32 [768, 768], P('tensor', 'dp')
- output_bias_grad: float32 [768], replicated
- norm1_gain_grad: float32 [768], replicated
- norm1_shift_grad: float32 [768], replicated
- up_weight_grad: float32 [768, 3072], P('dp', 'tensor')
- up_bias_grad: float32 [3072], P('tensor')
- down_weight_grad: float32 [3072, 768], P('tensor', 'dp')
- down_bias_grad: float32 [768], replicated
- norm2_gain_grad: float32 [768], replicated
- norm2_shift_grad: float32 [768], replicated
- input_rms: float32 [5], replicated
The draws below stay inside these ranges and needn't reach their ends.
Inputs may be any that keep to these rules, and one draw needn't show every extreme that they name: `random_blocks`: for query block b the 3 numbers are distinct, none is 0, 1, b - 1, b or b + 1. `segment_ids`: numbers never fall along a sequence; a document spans 1 to 1024 tokens.
All inputs are finite; a program needn't handle non-finite values. No bound on the sum of `token_valid` on one device may be relied on, other than what follows from the above.
Results may differ from the reference program's by a relative error of at most 0.019.
Values may be sent and summed in bfloat16 or wider, within the bound.
A program may use at most 384 MiB of HBM per device.

```python
import math
import jax
import jax.numpy as jnp
import numpy as np
from jax import lax

D = 768
H = 12
HD = 64
FF = 3072
BLK = 64
RAND = 3
SEQ = 2048
DOCS = 16
SEQS = 16
NB = 32


def draw_random_blocks(key, part):
    scores = jax.random.randint(key, (SEQS, NB, NB), 0, 1 << 20, dtype=jnp.int32)
    scores = scores * NB + jnp.arange(NB, dtype=jnp.int32)
    query_ids = jnp.arange(NB, dtype=jnp.int32)[:, None]
    key_ids = jnp.arange(NB, dtype=jnp.int32)[None, :]
    banned = (jnp.abs(key_ids - query_ids) <= 1) | (key_ids < 2)
    scores = jnp.where(banned[None], -1, scores)
    return lax.top_k(scores, RAND)[1].astype(jnp.int32)


def plant(values, rng, least, top_value):
    spot = [jax.random.randint(jax.random.fold_in(rng, axis), (), 0, length) for axis, length in enumerate(values.shape)]
    widest = values.shape.index(max(values.shape))
    neighbour = spot[:widest] + [(spot[widest] + 1) % values.shape[widest]] + spot[widest + 1:]
    return values.at[tuple(spot)].set(least).at[tuple(neighbour)].set(top_value)


def level_of(own_key, extent, split, smallest, top_value):
    loudness = 1.0
    for position, blocks in split:
        steps = jax.random.uniform(jax.random.fold_in(jax.random.fold_in(own_key, 6), position), (blocks,), jnp.float32, smallest / len(split), top_value / len(split))
        loudness = loudness * jnp.repeat(jnp.exp(steps), extent[position] // blocks).reshape((-1,) + (1,) * (len(extent) - 1 - position))
    return loudness


def profile(number_of, total, limit, skew):
    loads = [(1 << 20) // math.isqrt(standing ** skew) + 1 for standing in range(2, number_of + 1)]
    spare, holding = total - limit - (number_of - 1), [1] * (number_of - 1)
    while spare > 0:
        free = [i for i in range(number_of - 1) if holding[i] < limit]
        pool, remaining = sum([loads[i] for i in free]), spare
        for i in free:
            addition = min(limit - holding[i], max(1, remaining * loads[i] // pool), spare)
            holding[i] = holding[i] + addition
            spare = spare - addition
    return np.array([limit] + holding)


def ragged_sizes(rng, count, total, reach, skew):
    if count == 2:
        one = jax.random.randint(rng, (), max(1, total - reach), min(reach, total - 1) + 1)
        return jnp.stack([one, total - one])
    tallies = jnp.asarray(profile(count, total, reach, skew), jnp.int32)
    twos = (count - 1) // 2
    giver, sink = tallies[1:1 + 2 * twos:2], tallies[2:2 + 2 * twos:2]
    margin = jnp.minimum(giver - 1, reach - sink)
    passed = jax.random.randint(jax.random.fold_in(rng, 1), (twos,), 0, 1 << 20) % (margin + 1)
    tallies = tallies.at[1:1 + 2 * twos:2].set(giver - passed).at[2:2 + 2 * twos:2].set(sink + passed)
    return tallies[jax.random.permutation(jax.random.fold_in(rng, 2), count)]


def noise(stream_key, shape, width, limit, cuts=(), kind=jnp.bfloat16):
    gain = level_of(stream_key, shape, cuts, -0.22, 0.18) if cuts else 1.0
    entries = jax.random.normal(stream_key, shape, jnp.float32) * width * gain
    return jnp.minimum(jnp.maximum(entries, -limit), limit).astype(kind)


def setup_inputs(seed: int = 0) -> dict:
    arg_keys = jax.random.split(jax.random.key(seed), 21)
    hidden_in = noise(arg_keys[0], (SEQS, SEQ, D), 1.0, 6.0, ((0, 4), (1, 4)))
    out_grad = noise(arg_keys[1], (SEQS, SEQ, D), 1.0, 6.0, ((0, 4), (1, 4)))
    segment_ids = jax.vmap(lambda own: jnp.searchsorted(jnp.cumsum(ragged_sizes(own, DOCS, SEQ, SEQ // 2, 2)), jnp.arange(SEQ), side="right"))(jax.random.split(arg_keys[2], SEQS)).reshape((SEQS, SEQ)).astype(jnp.int32)
    token_valid = plant((jax.random.randint(arg_keys[3], (SEQS, SEQ), 0, 8) < 7).astype(jnp.int32), jax.random.fold_in(arg_keys[3], 1), 0, 1)
    random_blocks = draw_random_blocks(jax.random.fold_in(arg_keys[20], 71), 0)
    query_weight = noise(arg_keys[5], (D, D), D ** -0.5, 0.21875, ((0, 4), (1, 2)))
    query_bias = noise(arg_keys[6], (D,), 0.5, 3.0, ((0, 2),))
    key_weight = noise(arg_keys[7], (D, D), D ** -0.5, 0.21875, ((0, 4), (1, 2)))
    value_weight = noise(arg_keys[8], (D, D), D ** -0.5, 0.21875, ((0, 4), (1, 2)))
    value_bias = noise(arg_keys[9], (D,), 0.5, 3.0, ((0, 2),))
    output_weight = noise(arg_keys[10], (D, D), (D // 8) ** -0.5, 0.625, ((0, 2), (1, 4)))
    output_bias = noise(arg_keys[11], (D,), 0.5, 3.0)
    norm1_gain = jnp.clip(1.0 + 0.1 * jax.random.normal(arg_keys[12], (D,), jnp.float32), 0.5, 1.5).astype(jnp.bfloat16)
    norm1_shift = noise(arg_keys[13], (D,), 0.5, 3.0)
    up_weight = noise(arg_keys[14], (D, FF), D ** -0.5, 0.21875, ((0, 4), (1, 2)))
    up_bias = noise(arg_keys[15], (FF,), 0.5, 3.0, ((0, 2),))
    down_weight = noise(arg_keys[16], (FF, D), FF ** -0.5, 0.109375, ((0, 2), (1, 4)))
    down_bias = noise(arg_keys[17], (D,), 0.5, 3.0)
    norm2_gain = jnp.clip(1.0 + 0.1 * jax.random.normal(arg_keys[18], (D,), jnp.float32), 0.5, 1.5).astype(jnp.bfloat16)
    norm2_shift = noise(arg_keys[19], (D,), 0.5, 3.0)
    return {"hidden_in": hidden_in, "out_grad": out_grad, "segment_ids": segment_ids, "token_valid": token_valid, "random_blocks": random_blocks, "query_weight": query_weight, "query_bias": query_bias, "key_weight": key_weight, "value_weight": value_weight, "value_bias": value_bias, "output_weight": output_weight, "output_bias": output_bias, "norm1_gain": norm1_gain, "norm1_shift": norm1_shift, "up_weight": up_weight, "up_bias": up_bias, "down_weight": down_weight, "down_bias": down_bias, "norm2_gain": norm2_gain, "norm2_shift": norm2_shift}


@jax.custom_vjp
def low(v):
    return lax.optimization_barrier(v.astype(jnp.bfloat16)).astype(jnp.float32)

@jax.custom_vjp
def low_back(v):
    return v

def low_keep(v):
    return (low(v), None)

def low_pass(kept, grad):
    return (grad,)

def back_keep(v):
    return (v, None)

def back_low(kept, grad):
    return (low(grad),)
low.defvjp(low_keep, low_pass)
low_back.defvjp(back_keep, back_low)
EPSILON = 1e-06
NEG_FILL = -1e+30
HIGH_PREC = lax.Precision.HIGHEST

def matmul(left, right):
    return jnp.dot(left, right, precision=HIGH_PREC)

def layer_norm(values, norm_gain, norm_shift):
    row_mean = lax.optimization_barrier(jnp.mean(values, -1, keepdims=True))
    centered = values - row_mean
    row_var = lax.optimization_barrier(jnp.mean(centered * centered, -1, keepdims=True))
    return centered * lax.rsqrt(row_var + EPSILON) * norm_gain + norm_shift

def gelu_tanh(values):
    return jax.nn.gelu(values, approximate=True)

def slot_table(first_block, local_blocks, all_blocks, random_local):
    block_ids = first_block + jnp.arange(local_blocks, dtype=jnp.int32)
    near_ids = jnp.stack([block_ids - 1, block_ids, block_ids + 1], -1)
    global_ids = jnp.broadcast_to(jnp.arange(2, dtype=jnp.int32), (local_blocks, 2))
    fixed_ids = jnp.concatenate([near_ids, global_ids], -1)
    near_ok = jnp.stack([block_ids >= 3, block_ids >= 2, (block_ids >= 1) & (block_ids <= all_blocks - 2)], -1)
    fixed_ok = jnp.concatenate([near_ok, jnp.ones((local_blocks, 2), jnp.bool_)], -1)
    seq_count = random_local.shape[0]
    slot_ids = jnp.concatenate([jnp.broadcast_to(fixed_ids, (seq_count,) + fixed_ids.shape), random_local.astype(jnp.int32)], -1)
    slot_ok = jnp.concatenate([jnp.broadcast_to(fixed_ok, (seq_count,) + fixed_ok.shape), jnp.ones(random_local.shape, jnp.bool_)], -1)
    return (jnp.clip(slot_ids, 0, all_blocks - 1), slot_ok)

def pick_rows(table, index_set):
    return jax.vmap(lambda one_table, one_index: one_table[one_index])(table, index_set)

def sparse_mask(slot_ids, slot_ok, first_block, block_len, segments, valid_keys):
    seq_count, local_blocks, slot_count = slot_ids.shape
    offsets = jnp.arange(block_len, dtype=jnp.int32)
    key_pos = (slot_ids[..., None] * block_len + offsets).reshape(seq_count, local_blocks, slot_count * block_len)
    query_pos = (first_block + jnp.arange(local_blocks, dtype=jnp.int32))[:, None] * block_len + offsets
    key_seg = pick_rows(segments, key_pos)
    key_live = pick_rows(valid_keys, key_pos)
    query_seg = pick_rows(segments, jnp.broadcast_to(query_pos, (seq_count,) + query_pos.shape))
    slot_live = jnp.repeat(slot_ok, block_len, axis=-1)
    same_doc = (query_seg[..., :, None] == key_seg[..., None, :]) & (key_live[..., None, :] == 1)
    self_pair = query_pos[None, :, :, None] == key_pos[:, :, None, :]
    return slot_live[:, :, None, :] & (same_doc | self_pair)

def dense_mask(glob_len, segments, valid_keys):
    full_len = segments.shape[1]
    same_doc = (segments[:, :glob_len, None] == segments[:, None, :]) & (valid_keys[:, None, :] == 1)
    self_pair = jnp.arange(glob_len)[:, None] == jnp.arange(full_len)[None, :]
    return same_doc | self_pair[None]

def softmax_rows(masked):
    row_top = lax.optimization_barrier(jnp.max(masked, -1, keepdims=True))
    shifted_exp = jnp.exp(masked - row_top)
    totals = lax.optimization_barrier(jnp.sum(shifted_exp, -1, keepdims=True))
    return (shifted_exp / totals, row_top + jnp.log(totals))

def attend_one(packed):
    q_seq, k_seq, v_seq, segments, valid_keys, random_local = packed
    all_blocks = SEQ // BLK
    score_scale = HD ** (-0.5)
    slot_ids, slot_ok = slot_table(0, all_blocks, all_blocks, random_local[None])
    allowed = sparse_mask(slot_ids, slot_ok, 0, BLK, segments[None], valid_keys[None])
    query_blocks = q_seq.reshape(1, all_blocks, BLK, H, HD)
    key_sel = pick_rows(k_seq.reshape(1, all_blocks, BLK, H, HD), slot_ids).reshape(1, all_blocks, -1, H, HD)
    value_sel = pick_rows(v_seq.reshape(1, all_blocks, BLK, H, HD), slot_ids).reshape(1, all_blocks, -1, H, HD)
    raw_scores = jnp.einsum('snqhd,snkhd->snhqk', query_blocks, key_sel, precision=HIGH_PREC) * score_scale
    scores = low_back(raw_scores)
    sparse_probs = softmax_rows(jnp.where(allowed[:, :, None], scores, NEG_FILL))[0]
    sparse_out = jnp.einsum('snhqk,snkhd->snqhd', low(sparse_probs), value_sel, precision=HIGH_PREC).reshape(SEQ, H * HD)
    glob_len = 2 * BLK
    query_glob = q_seq.reshape(SEQ, H, HD)[:glob_len]
    raw_glob = jnp.einsum('qhd,khd->hqk', query_glob, k_seq.reshape(SEQ, H, HD), precision=HIGH_PREC) * score_scale
    scores_glob = low_back(raw_glob)
    glob_allowed = dense_mask(glob_len, segments[None], valid_keys[None])[0]
    glob_probs = softmax_rows(jnp.where(glob_allowed[None], scores_glob, NEG_FILL))[0]
    glob_out = jnp.einsum('hqk,khd->qhd', low(glob_probs), v_seq.reshape(SEQ, H, HD), precision=HIGH_PREC).reshape(glob_len, H * HD)
    return jnp.concatenate([glob_out, sparse_out[glob_len:]], 0)

def layer(x_in, params, segment_ids, token_valid, random_blocks):
    w_query, b_query, w_key, w_value, b_value, w_out, b_out, gain_one, shift_one, w_up, b_up, w_down, b_down, gain_two, shift_two = params
    shaped = (SEQS, SEQ, D)
    flat = x_in.reshape(SEQS * SEQ, D)
    x_low = low(flat)
    q_rows = low_back(low(matmul(x_low, w_query) + b_query))
    k_rows = low_back(low(matmul(x_low, w_key)))
    v_rows = low_back(low(matmul(x_low, w_value) + b_value))
    attended = lax.map(jax.checkpoint(attend_one), (q_rows.reshape(shaped), k_rows.reshape(shaped), v_rows.reshape(shaped), segment_ids, token_valid, random_blocks))
    attended = low_back(low(attended.reshape(SEQS * SEQ, D)))
    attn_out = low_back(matmul(attended, w_out) + b_out)
    first_sum = flat + attn_out
    normed = layer_norm(first_sum, gain_one, shift_one)
    pre_act = low_back(matmul(low(normed), w_up) + b_up)
    act_low = low(gelu_tanh(pre_act))
    ffn_out = low_back(matmul(act_low, w_down) + b_down)
    second_sum = normed + ffn_out
    result = layer_norm(second_sum, gain_two, shift_two).reshape(shaped)
    return (result, (flat, first_sum, second_sum, attn_out, ffn_out))

def reference(hidden_in, out_grad, segment_ids, token_valid, random_blocks, query_weight, query_bias, key_weight, value_weight, value_bias, output_weight, output_bias, norm1_gain, norm1_shift, up_weight, up_bias, down_weight, down_bias, norm2_gain, norm2_shift):
    params = tuple((weight_arg.astype(jnp.float32) for weight_arg in (query_weight, query_bias, key_weight, value_weight, value_bias, output_weight, output_bias, norm1_gain, norm1_shift, up_weight, up_bias, down_weight, down_bias, norm2_gain, norm2_shift)))

    def forward(x_in, *weights):
        return layer(x_in, weights, segment_ids, token_valid, random_blocks)
    layer_out, pullback, statistics = jax.vjp(forward, hidden_in.astype(jnp.float32), *params, has_aux=True)
    gradients = pullback(out_grad.astype(jnp.float32))
    valid_rows = token_valid.reshape(-1).astype(jnp.float32)
    valid_count = jnp.maximum(jnp.sum(valid_rows), 1.0)
    input_rms = jnp.stack([jnp.sqrt(jnp.sum(valid_rows * lax.optimization_barrier(jnp.sum(member * member, -1))) / (valid_count * D)) for member in statistics])
    return (layer_out.astype(jnp.bfloat16), gradients[0], gradients[1], gradients[2], gradients[3], gradients[4], gradients[5], gradients[6], gradients[7], gradients[8], gradients[9], gradients[10], gradients[11], gradients[12], gradients[13], gradients[14], gradients[15], input_rms)
```

```python
import jax
import jax.numpy as jnp
from jax import lax
from jax.experimental import pallas as pl
from jax.experimental.pallas import tpu as pltpu
from jax.sharding import PartitionSpec as P

HD = 64
BLK = 64
PAIR = 128
SLOTS = 8
WIDE = 512
SCALE = HD ** (-0.5)
EPSILON = 1e-06


NEG_FILL = -1e30


def pair_rows(block, left, scale=None):
    if scale is not None:
        block = block * jnp.asarray(scale, block.dtype)
    zero = jnp.zeros_like(block)
    return jnp.concatenate([jnp.where(left, block, zero), jnp.where(left, zero, block)], 0)


def lane_left(rows):
    return lax.broadcasted_iota(jnp.int32, (rows, PAIR), 1) < HD


def eye_pair():
    lanes = lax.broadcasted_iota(jnp.int32, (BLK, PAIR), 1)
    rows = lax.broadcasted_iota(jnp.int32, (BLK, PAIR), 0)
    return rows == lanes % BLK


def block_rows(index):
    return pl.ds(pl.multiple_of(index * BLK, BLK), BLK)


def slot_bias(table, row, key_code, query_code, own):
    pieces = []
    for slot in range(SLOTS):
        code = query_code
        if slot == 0:
            code = jnp.where(table[row, 9] == 1, query_code, -2)
        if slot == 2:
            code = jnp.where(table[row, 10] == 1, query_code, -2)
        same = key_code[block_rows(table[row, 1 + slot]), :] == code
        if slot == 1:
            same = same | own
        pieces.append(jnp.where(same, 0.0, NEG_FILL))
    return jnp.concatenate(pieces, 0)


def slot_rows(ref, table, row, lanes):
    return jnp.concatenate(
        [ref[block_rows(table[row, 1 + slot]), lanes] for slot in range(SLOTS)], 0
    )


def wide_bias(key_code, query_code, block, chunk):
    start = pl.multiple_of(chunk * WIDE, WIDE)
    same = key_code[pl.ds(start, WIDE), :] == query_code
    key_pos = start + lax.broadcasted_iota(jnp.int32, (WIDE, PAIR), 0)
    query_pos = block * BLK + lax.broadcasted_iota(jnp.int32, (WIDE, PAIR), 1) % BLK
    return jnp.where(same | (key_pos == query_pos), 0.0, NEG_FILL)


def dot_nt(left, right):
    return lax.dot_general(
        left, right, (((1,), (1,)), ((), ())), preferred_element_type=jnp.float32
    )


def dot_tn(left, right):
    return lax.dot_general(
        left, right, (((0,), (0,)), ((), ())), preferred_element_type=jnp.float32
    )


def dot_nn(left, right):
    return jnp.dot(left, right, preferred_element_type=jnp.float32)


def attend_kernel(table, wide, q_ref, k_ref, v_ref, key_code, query_code, o_ref, lse_ref, acc):
    length, width = q_ref.shape
    pairs = width // PAIR
    left = lane_left(BLK)
    own = eye_pair()

    def narrow(row, carry):
        block = table[row, 0]
        rows = block_rows(block)
        bias = slot_bias(table, row, key_code, query_code[pl.ds(block, 1), :], own)
        for pair in range(pairs):
            lanes = slice(pair * PAIR, (pair + 1) * PAIR)
            query = pair_rows(q_ref[rows, lanes], left, SCALE)
            scores = dot_nt(slot_rows(k_ref, table, row, lanes), query) + bias
            top = jnp.max(scores, 0, keepdims=True)
            weight = jnp.exp(scores - top)
            total = jnp.sum(weight, 0, keepdims=True)
            probs = (weight * (1.0 / total)).astype(jnp.bfloat16)
            lse_ref[block, pl.ds(pair, 1), :] = top + jnp.log(total)
            both = dot_tn(probs, slot_rows(v_ref, table, row, lanes))
            o_ref[rows, lanes] = jnp.where(left, both[:BLK], both[BLK:]).astype(o_ref.dtype)
        return carry

    lax.fori_loop(0, table.shape[0], narrow, 0)

    for which in range(2):
        block = wide[which]
        rows = block_rows(block)
        code = query_code[pl.ds(block, 1), :]

        def first(chunk, carry):
            bias = wide_bias(key_code, code, block, chunk)
            keys = pl.ds(pl.multiple_of(chunk * WIDE, WIDE), WIDE)
            out = []
            for pair in range(pairs):
                lanes = slice(pair * PAIR, (pair + 1) * PAIR)
                query = pair_rows(q_ref[rows, lanes], left, SCALE)
                scores = dot_nt(k_ref[keys, lanes], query) + bias
                top_old, total_old = carry[pair]
                top = jnp.maximum(top_old, jnp.max(scores, 0, keepdims=True))
                total = total_old * jnp.exp(top_old - top) + jnp.sum(
                    jnp.exp(scores - top), 0, keepdims=True
                )
                out.append((top, total))
            return tuple(out)

        start = (jnp.full((1, PAIR), NEG_FILL), jnp.zeros((1, PAIR), jnp.float32))
        ends = lax.fori_loop(0, length // WIDE, first, (start,) * pairs)
        for pair in range(pairs):
            lse_ref[block, pl.ds(pair, 1), :] = ends[pair][0] + jnp.log(ends[pair][1])
        acc[...] = jnp.zeros_like(acc)

        def second(chunk, carry):
            bias = wide_bias(key_code, code, block, chunk)
            keys = pl.ds(pl.multiple_of(chunk * WIDE, WIDE), WIDE)
            for pair in range(pairs):
                lanes = slice(pair * PAIR, (pair + 1) * PAIR)
                query = pair_rows(q_ref[rows, lanes], left, SCALE)
                scores = dot_nt(k_ref[keys, lanes], query) + bias
                probs = jnp.exp(scores - lse_ref[block, pl.ds(pair, 1), :]).astype(jnp.bfloat16)
                acc[pair] += dot_tn(probs, v_ref[keys, lanes])
            return carry

        lax.fori_loop(0, length // WIDE, second, 0)
        for pair in range(pairs):
            lanes = slice(pair * PAIR, (pair + 1) * PAIR)
            both = acc[pair]
            o_ref[rows, lanes] = jnp.where(left, both[:BLK], both[BLK:]).astype(o_ref.dtype)


def attend_back_kernel(
    table, wide, q_ref, k_ref, v_ref, do_ref, key_code, query_code, lse_ref,
    dq_ref, dk_ref, dv_ref, dk_sum, dv_sum, dq_acc,
):
    length, width = q_ref.shape
    pairs = width // PAIR
    left = lane_left(BLK)
    own = eye_pair()
    dk_sum[...] = jnp.zeros_like(dk_sum)
    dv_sum[...] = jnp.zeros_like(dv_sum)

    def narrow(row, carry):
        block = table[row, 0]
        rows = block_rows(block)
        bias = slot_bias(table, row, key_code, query_code[pl.ds(block, 1), :], own)
        for pair in range(pairs):
            lanes = slice(pair * PAIR, (pair + 1) * PAIR)
            query = pair_rows(q_ref[rows, lanes], left, SCALE)
            grad = pair_rows(do_ref[rows, lanes], left)
            keys = slot_rows(k_ref, table, row, lanes)
            values = slot_rows(v_ref, table, row, lanes)
            scores = dot_nt(keys, query) + bias
            probs = jnp.exp(scores - lse_ref[block, pl.ds(pair, 1), :])
            g_probs = dot_nt(values, grad)
            terms = probs * g_probs
            g_scores = (terms - probs * jnp.sum(terms, 0, keepdims=True)).astype(jnp.bfloat16)
            dv = dot_nn(probs.astype(jnp.bfloat16), grad)
            dk = dot_nn(g_scores, query)
            both = dot_tn(g_scores, keys)
            dq_ref[rows, lanes] = (jnp.where(left, both[:BLK], both[BLK:]) * SCALE).astype(
                dq_ref.dtype
            )
            for slot in range(SLOTS):
                spot = block_rows(table[row, 1 + slot])
                part = slice(slot * BLK, (slot + 1) * BLK)
                dk_sum[spot, lanes] += dk[part]
                dv_sum[spot, lanes] += dv[part]
        return carry

    lax.fori_loop(0, table.shape[0], narrow, 0)

    for which in range(2):
        block = wide[which]
        rows = block_rows(block)
        code = query_code[pl.ds(block, 1), :]

        def pieces(chunk, pair, bias):
            keys_at = pl.ds(pl.multiple_of(chunk * WIDE, WIDE), WIDE)
            lanes = slice(pair * PAIR, (pair + 1) * PAIR)
            query = pair_rows(q_ref[rows, lanes], left, SCALE)
            grad = pair_rows(do_ref[rows, lanes], left)
            keys = k_ref[keys_at, lanes]
            scores = dot_nt(keys, query) + bias
            probs = jnp.exp(scores - lse_ref[block, pl.ds(pair, 1), :])
            return keys_at, lanes, query, grad, keys, probs, probs * dot_nt(v_ref[keys_at, lanes], grad)

        def first(chunk, carry):
            bias = wide_bias(key_code, code, block, chunk)
            return tuple(
                carry[pair] + jnp.sum(pieces(chunk, pair, bias)[-1], 0, keepdims=True)
                for pair in range(pairs)
            )

        deltas = lax.fori_loop(
            0, length // WIDE, first, (jnp.zeros((1, PAIR), jnp.float32),) * pairs
        )
        dq_acc[...] = jnp.zeros_like(dq_acc)

        def second(chunk, carry):
            bias = wide_bias(key_code, code, block, chunk)
            for pair in range(pairs):
                keys_at, lanes, query, grad, keys, probs, terms = pieces(chunk, pair, bias)
                g_scores = (terms - probs * carry[pair]).astype(jnp.bfloat16)
                dv_sum[keys_at, lanes] += dot_nn(probs.astype(jnp.bfloat16), grad)
                dk_sum[keys_at, lanes] += dot_nn(g_scores, query)
                dq_acc[pair] += dot_tn(g_scores, keys)
            return carry

        lax.fori_loop(0, length // WIDE, second, deltas)
        for pair in range(pairs):
            lanes = slice(pair * PAIR, (pair + 1) * PAIR)
            both = dq_acc[pair]
            dq_ref[rows, lanes] = (jnp.where(left, both[:BLK], both[BLK:]) * SCALE).astype(
                dq_ref.dtype
            )
    dk_ref[...] = dk_sum[...].astype(dk_ref.dtype)
    dv_ref[...] = dv_sum[...].astype(dv_ref.dtype)


VMEM_SPEC = pl.BlockSpec(memory_space=pltpu.VMEM)
SMEM_SPEC = pl.BlockSpec(memory_space=pltpu.SMEM)
ROOM = pltpu.CompilerParams(vmem_limit_bytes=60 * 1024 * 1024)


def attend(table, wide, q, k, v, key_code, query_code):
    length, width = q.shape
    return pl.pallas_call(
        attend_kernel,
        out_shape=(
            jax.ShapeDtypeStruct((length, width), jnp.bfloat16),
            jax.ShapeDtypeStruct((length // BLK, 8, PAIR), jnp.float32),
        ),
        in_specs=[SMEM_SPEC] * 2 + [VMEM_SPEC] * 5,
        out_specs=(VMEM_SPEC, VMEM_SPEC),
        scratch_shapes=[pltpu.VMEM((width // PAIR, PAIR, PAIR), jnp.float32)],
        compiler_params=ROOM,
        cost_estimate=pl.CostEstimate(
            flops=length * width * 1024 * 6, bytes_accessed=length * width * 8,
            transcendentals=length * width * 8,
        ),
        name="attend",
    )(table, wide, q, k, v, key_code, query_code)


def attend_back(table, wide, q, k, v, do, key_code, query_code, lse):
    length, width = q.shape
    shape = jax.ShapeDtypeStruct((length, width), jnp.bfloat16)
    return pl.pallas_call(
        attend_back_kernel,
        out_shape=(shape, shape, shape),
        in_specs=[SMEM_SPEC] * 2 + [VMEM_SPEC] * 7,
        out_specs=(VMEM_SPEC,) * 3,
        scratch_shapes=[
            pltpu.VMEM((length, width), jnp.float32),
            pltpu.VMEM((length, width), jnp.float32),
            pltpu.VMEM((width // PAIR, PAIR, PAIR), jnp.float32),
        ],
        compiler_params=ROOM,
        cost_estimate=pl.CostEstimate(
            flops=length * width * 1024 * 15, bytes_accessed=length * width * 14,
            transcendentals=length * width * 8,
        ),
        name="attend_back",
    )(table, wide, q, k, v, do, key_code, query_code, lse)


def layer_norm(values, norm_gain, norm_shift):
    row_mean = jnp.mean(values, -1, keepdims=True)
    centered = values - row_mean
    row_var = jnp.mean(centered * centered, -1, keepdims=True)
    return centered * lax.rsqrt(row_var + EPSILON) * norm_gain + norm_shift


def gelu_tanh(values):
    return jax.nn.gelu(values, approximate=True)


def block_tables(random_seq, all_blocks, place):
    block = jnp.arange(2, all_blocks, dtype=jnp.int32)
    last = all_blocks - 1
    zero = jnp.zeros_like(block)
    true_ids = jnp.stack(
        [block, block - 1, block, jnp.minimum(block + 1, last), zero, zero + 1], -1
    )
    true_ids = jnp.concatenate([true_ids, random_seq[2:]], -1)
    flags = jnp.stack([block >= 3, block <= last - 1], -1).astype(jnp.int32)
    return (
        jnp.concatenate([place(true_ids), flags], -1).astype(jnp.int32),
        place(jnp.arange(2, dtype=jnp.int32)),
    )


def local(
    hidden_in, out_grad, segment_ids, token_valid, random_blocks,
    query_weight, query_bias, key_weight, value_weight, value_bias,
    output_weight, output_bias, norm1_gain, norm1_shift,
    up_weight, up_bias, down_weight, down_bias, norm2_gain, norm2_shift,
):
    f32, bf16 = jnp.float32, jnp.bfloat16
    seqs, span, width = hidden_in.shape
    length = segment_ids.shape[1]
    places = length // span
    halves = lax.axis_size("tensor")
    turns = seqs // halves
    shares = places // turns
    my_half = lax.axis_index("tensor")
    my_place = lax.axis_index("context")
    my_turn, my_share = my_place // shares, my_place % shares
    my_seq = my_half * turns + my_turn
    blocks = length // BLK
    rows = turns * span
    everyone = ("dp", "context", "tensor")

    def send_turn(value, step):
        if step % turns == 0:
            return value
        pairs = [
            (t * shares + s, ((t + step) % turns) * shares + s)
            for t in range(turns)
            for s in range(shares)
        ]
        return lax.ppermute(value, "context", pairs)

    def send_share(value, step):
        if step % shares == 0:
            return value
        pairs = [
            (t * shares + s, t * shares + (s + step) % shares)
            for t in range(turns)
            for s in range(shares)
        ]
        return lax.ppermute(value, "context", pairs)

    def bring(value):
        return jnp.concatenate(
            [
                send_turn(
                    lax.dynamic_index_in_dim(
                        value, my_half * turns + (my_turn + k) % turns, 0, keepdims=False
                    ),
                    k,
                )
                for k in range(turns)
            ],
            0,
        )

    def deliver(value):
        value = value.reshape(turns, span, width)
        got = jnp.stack([send_turn(value[k], -k) for k in range(turns)])
        order = (jnp.arange(turns) - my_turn) % turns
        got = jnp.stack(
            [lax.dynamic_index_in_dim(got, order[t], 0, keepdims=False) for t in range(turns)]
        )
        return lax.all_gather(got, "tensor", axis=0, tiled=True)

    def own_slice(value, count, which, axis):
        size = value.shape[axis] // count
        return lax.dynamic_slice_in_dim(value, which * size, size, axis)

    both = lambda w, a, b: lax.all_gather(
        lax.all_gather(w, "dp", axis=a, tiled=True), "tensor", axis=b, tiled=True
    )
    w_q, w_k, w_v = (both(w, 0, 1) for w in (query_weight, key_weight, value_weight))
    w_out = both(output_weight, 1, 0)
    w_up, w_down = both(up_weight, 0, 1), both(down_weight, 1, 0)
    b_q, b_v, b_up = (
        lax.all_gather(b, "tensor", axis=0, tiled=True) for b in (query_bias, value_bias, up_bias)
    )
    part = width // shares
    padded = -(-part // PAIR) * PAIR
    pad_cols = lambda w: jnp.pad(w, [(0, 0)] * (w.ndim - 1) + [(0, padded - part)])
    mine = lambda w: pad_cols(own_slice(w, shares, my_share, w.ndim - 1))
    w_qkv = jnp.concatenate([mine(w_q), mine(w_k), mine(w_v)], 1)
    b_qkv = jnp.concatenate([mine(b_q), jnp.zeros((padded,), bf16), mine(b_v)]).astype(f32)
    w_out_mine = jnp.concatenate(
        [own_slice(w_out, shares, (my_share + k) % shares, 0) for k in range(shares)], 0
    )

    x_own = bring(hidden_in)
    g_out = bring(out_grad).astype(f32)
    x_seq = jnp.concatenate([send_share(x_own, k) for k in range(shares)], 0)
    per = span // BLK

    def place(block_ids):
        chunk = block_ids // per
        turn, share = chunk // shares, chunk % shares
        spot = ((my_share - share) % shares) * turns + (my_turn - turn) % turns
        return spot * per + block_ids % per

    def in_order(row):
        return jnp.concatenate(
            [
                lax.dynamic_slice_in_dim(
                    row,
                    (((my_turn - k) % turns) * shares + (my_share - s) % shares) * span,
                    span,
                )
                for s in range(shares)
                for k in range(turns)
            ]
        )

    seg = in_order(lax.dynamic_index_in_dim(segment_ids, my_seq, 0, keepdims=False))
    live = in_order(lax.dynamic_index_in_dim(token_valid, my_seq, 0, keepdims=False))
    random_seq = lax.dynamic_index_in_dim(random_blocks, my_seq, 0, keepdims=False)
    table, wide = block_tables(random_seq, blocks, place)
    key_code = jnp.broadcast_to(jnp.where(live == 1, seg, -1)[:, None], (length, PAIR))
    query_code = jnp.tile(seg.reshape(blocks, BLK), (1, PAIR // BLK))

    qkv = (jnp.dot(x_seq, w_qkv, preferred_element_type=f32) + b_qkv).astype(bf16)
    q, k, v = (qkv[:, i * padded : (i + 1) * padded] for i in range(3))
    att, lse = attend(table, wide, q, k, v, key_code, query_code)
    att = att[:, :part].reshape(shares, rows, part)
    att_own = jnp.concatenate([send_share(att[s], -s) for s in range(shares)], 1)
    attn_out = jnp.dot(att_own, w_out_mine, preferred_element_type=f32) + output_bias.astype(f32)
    x_full = x_own.astype(f32)
    first_sum = x_full + attn_out
    gain_one, shift_one = norm1_gain.astype(f32), norm1_shift.astype(f32)
    normed = layer_norm(first_sum, gain_one, shift_one)
    normed_low = normed.astype(bf16)
    pre_act = jnp.dot(normed_low, w_up, preferred_element_type=f32) + b_up.astype(f32)
    act_low = gelu_tanh(pre_act).astype(bf16)
    ffn_out = jnp.dot(act_low, w_down, preferred_element_type=f32) + down_bias.astype(f32)
    second_sum = normed + ffn_out
    gain_two, shift_two = norm2_gain.astype(f32), norm2_shift.astype(f32)
    layer_out, norm_back = jax.vjp(layer_norm, second_sum, gain_two, shift_two)
    g_second, gain_two_grad, shift_two_grad = norm_back(g_out)
    layer_out = deliver(layer_out.astype(bf16))
    g_ffn = g_second.astype(bf16)
    g_act = jnp.dot(g_ffn, w_down.T, preferred_element_type=f32)
    g_pre = jax.vjp(gelu_tanh, pre_act)[1](g_act)[0].astype(bf16)
    up_part = jnp.dot(normed_low.T, g_pre, preferred_element_type=f32)
    down_part = jnp.dot(act_low.T, g_ffn, preferred_element_type=f32)
    g_normed = g_second + jnp.dot(g_pre, w_up.T, preferred_element_type=f32)
    g_first, gain_one_grad, shift_one_grad = jax.vjp(layer_norm, first_sum, gain_one, shift_one)[1](
        g_normed
    )
    g_attn = g_first.astype(bf16)
    out_part = jnp.dot(att_own.T, g_attn, preferred_element_type=f32).astype(bf16)
    g_att = jnp.dot(g_attn, w_out_mine.T, preferred_element_type=f32).astype(bf16)
    do = jnp.concatenate(
        [send_share(own_slice(g_att, shares, s, 1), s) for s in range(shares)], 0
    )
    dq, dk, dv = attend_back(table, wide, q, k, v, pad_cols(do), key_code, query_code, lse)
    dqkv = jnp.concatenate([dq, dk, dv], 1)
    qkv_part = jnp.dot(x_seq.T, dqkv, preferred_element_type=f32).astype(bf16)
    back = jnp.dot(dqkv, w_qkv.T, preferred_element_type=f32).reshape(shares, rows, width)
    back_own = back[0]
    for s in range(1, shares):
        back_own = back_own + send_share(back[s].astype(bf16), -s).astype(f32)
    input_grad = deliver((g_first + back_own).astype(bf16)).astype(f32)

    def spread(value, which, axis):
        shape = list(value.shape)
        size = shape[axis]
        shape[axis] = size * shares
        return lax.dynamic_update_slice_in_dim(
            jnp.zeros(shape, value.dtype), value, which * size, axis
        )

    def shard(value, dp_axis, tensor_axis):
        value = lax.psum_scatter(value, "tensor", scatter_dimension=tensor_axis, tiled=True)
        value = lax.psum_scatter(value, "dp", scatter_dimension=dp_axis, tiled=True)
        return lax.psum(value, "context").astype(f32)

    shard_q, shard_k, shard_v = (
        shard(spread(qkv_part[:, i * padded : i * padded + part], my_share, 1), 0, 1)
        for i in range(3)
    )
    out_full = jnp.concatenate(
        [own_slice(out_part, shares, (s - my_share) % shares, 0) for s in range(shares)], 0
    )
    shard_o = shard(out_full, 1, 0)
    shard_up = shard(up_part.astype(bf16), 0, 1)
    shard_down = shard(down_part.astype(bf16), 1, 0)

    sums = lambda value: jnp.sum(value.astype(f32), 0)
    valid = live[:rows].astype(f32)
    squares = lambda member: jnp.sum(valid * jnp.sum(member * member, -1))
    stats = jnp.stack(
        [squares(m) for m in (x_full, first_sum, second_sum, attn_out, ffn_out)] + [jnp.sum(valid)]
    )
    small = [
        spread(sums(dq)[:part], my_share, 0),
        spread(sums(dv)[:part], my_share, 0),
        sums(g_pre),
        sums(g_attn),
        gain_one_grad,
        shift_one_grad,
        sums(g_ffn),
        gain_two_grad,
        shift_two_grad,
        stats,
    ]
    small = lax.psum(tuple(small), everyone)
    s_q, s_v, s_up = (own_slice(value, halves, my_half, 0) for value in small[:3])
    s_o, s_g1, s_s1, s_down, s_g2, s_s2, stats = small[3:]
    input_rms = jnp.sqrt(stats[:5] / (jnp.maximum(stats[5], 1.0) * width))
    return (
        layer_out, input_grad, shard_q, s_q, shard_k, shard_v, s_v, shard_o, s_o,
        s_g1, s_s1, shard_up, s_up, shard_down, s_down, s_g2, s_s2, input_rms,
    )


def solution(mesh):
    rows, plain = P("dp", "context", None), P()
    columns, across, halves = P("dp", "tensor"), P("tensor", "dp"), P("tensor")
    return jax.shard_map(
        local,
        mesh=mesh,
        in_specs=(
            rows, rows, P("dp", None), P("dp", None), P("dp", None, None),
            columns, halves, columns, columns, halves, across, plain, plain, plain,
            columns, halves, across, plain, plain, plain,
        ),
        out_specs=(
            rows, rows, columns, halves, columns, columns, halves, across, plain,
            plain, plain, columns, halves, across, plain, plain, plain, plain,
        ),
        check_vma=False,
    )
```

```python
import jax
import jax.numpy as jnp
from jax import lax
from jax.experimental import pallas as pl
from jax.experimental.pallas import tpu as pltpu
from jax.sharding import PartitionSpec as P

HD = 64
BLK = 64
PAIR = 128
SLOTS = 8
WIDE = 512
SCALE = HD ** (-0.5)
EPSILON = 1e-06


NEG_FILL = -1e30


def pair_rows(block, left, scale=None):
    if scale is not None:
        block = block * jnp.asarray(scale, block.dtype)
    zero = jnp.zeros_like(block)
    return jnp.concatenate([jnp.where(left, block, zero), jnp.where(left, zero, block)], 0)


def lane_left(rows):
    return lax.broadcasted_iota(jnp.int32, (rows, PAIR), 1) < HD


def eye_pair():
    lanes = lax.broadcasted_iota(jnp.int32, (BLK, PAIR), 1)
    rows = lax.broadcasted_iota(jnp.int32, (BLK, PAIR), 0)
    return rows == lanes % BLK


def block_rows(index):
    return pl.ds(pl.multiple_of(index * BLK, BLK), BLK)


def slot_bias(table, row, key_code, query_code, own):
    pieces = []
    for slot in range(SLOTS):
        code = query_code
        if slot == 0:
            code = jnp.where(table[row, 9] == 1, query_code, -2)
        if slot == 2:
            code = jnp.where(table[row, 10] == 1, query_code, -2)
        same = key_code[block_rows(table[row, 1 + slot]), :] == code
        if slot == 1:
            same = same | own
        pieces.append(jnp.where(same, 0.0, NEG_FILL))
    return jnp.concatenate(pieces, 0)


def slot_rows(ref, table, row, lanes):
    return jnp.concatenate(
        [ref[block_rows(table[row, 1 + slot]), lanes] for slot in range(SLOTS)], 0
    )


def wide_bias(key_code, query_code, block, chunk):
    start = pl.multiple_of(chunk * WIDE, WIDE)
    same = key_code[pl.ds(start, WIDE), :] == query_code
    key_pos = start + lax.broadcasted_iota(jnp.int32, (WIDE, PAIR), 0)
    query_pos = block * BLK + lax.broadcasted_iota(jnp.int32, (WIDE, PAIR), 1) % BLK
    return jnp.where(same | (key_pos == query_pos), 0.0, NEG_FILL)


def dot_nt(left, right):
    return lax.dot_general(
        left, right, (((1,), (1,)), ((), ())), preferred_element_type=jnp.float32
    )


def dot_tn(left, right):
    return lax.dot_general(
        left, right, (((0,), (0,)), ((), ())), preferred_element_type=jnp.float32
    )


def dot_nn(left, right):
    return jnp.dot(left, right, preferred_element_type=jnp.float32)


def attend_kernel(table, wide, q_ref, k_ref, v_ref, key_code, query_code, o_ref, lse_ref, acc):
    length, width = q_ref.shape
    pairs = width // PAIR
    left = lane_left(BLK)
    own = eye_pair()

    def narrow(row, carry):
        block = table[row, 0]
        rows = block_rows(block)
        bias = slot_bias(table, row, key_code, query_code[pl.ds(block, 1), :], own)
        for pair in range(pairs):
            lanes = slice(pair * PAIR, (pair + 1) * PAIR)
            query = pair_rows(q_ref[rows, lanes], left, SCALE)
            scores = dot_nt(slot_rows(k_ref, table, row, lanes), query) + bias
            top = jnp.max(scores, 0, keepdims=True)
            weight = jnp.exp(scores - top)
            total = jnp.sum(weight, 0, keepdims=True)
            probs = (weight * (1.0 / total)).astype(jnp.bfloat16)
            lse_ref[block, pl.ds(pair, 1), :] = top + jnp.log(total)
            both = dot_tn(probs, slot_rows(v_ref, table, row, lanes))
            o_ref[rows, lanes] = jnp.where(left, both[:BLK], both[BLK:]).astype(o_ref.dtype)
        return carry

    lax.fori_loop(0, table.shape[0], narrow, 0)

    for which in range(2):
        block = wide[which]
        rows = block_rows(block)
        code = query_code[pl.ds(block, 1), :]

        def first(chunk, carry):
            bias = wide_bias(key_code, code, block, chunk)
            keys = pl.ds(pl.multiple_of(chunk * WIDE, WIDE), WIDE)
            out = []
            for pair in range(pairs):
                lanes = slice(pair * PAIR, (pair + 1) * PAIR)
                query = pair_rows(q_ref[rows, lanes], left, SCALE)
                scores = dot_nt(k_ref[keys, lanes], query) + bias
                top_old, total_old = carry[pair]
                top = jnp.maximum(top_old, jnp.max(scores, 0, keepdims=True))
                total = total_old * jnp.exp(top_old - top) + jnp.sum(
                    jnp.exp(scores - top), 0, keepdims=True
                )
                out.append((top, total))
            return tuple(out)

        start = (jnp.full((1, PAIR), NEG_FILL), jnp.zeros((1, PAIR), jnp.float32))
        ends = lax.fori_loop(0, length // WIDE, first, (start,) * pairs)
        for pair in range(pairs):
            lse_ref[block, pl.ds(pair, 1), :] = ends[pair][0] + jnp.log(ends[pair][1])
        acc[...] = jnp.zeros_like(acc)

        def second(chunk, carry):
            bias = wide_bias(key_code, code, block, chunk)
            keys = pl.ds(pl.multiple_of(chunk * WIDE, WIDE), WIDE)
            for pair in range(pairs):
                lanes = slice(pair * PAIR, (pair + 1) * PAIR)
                query = pair_rows(q_ref[rows, lanes], left, SCALE)
                scores = dot_nt(k_ref[keys, lanes], query) + bias
                probs = jnp.exp(scores - lse_ref[block, pl.ds(pair, 1), :]).astype(jnp.bfloat16)
                acc[pair] += dot_tn(probs, v_ref[keys, lanes])
            return carry

        lax.fori_loop(0, length // WIDE, second, 0)
        for pair in range(pairs):
            lanes = slice(pair * PAIR, (pair + 1) * PAIR)
            both = acc[pair]
            o_ref[rows, lanes] = jnp.where(left, both[:BLK], both[BLK:]).astype(o_ref.dtype)


def attend_back_kernel(
    table, wide, q_ref, k_ref, v_ref, do_ref, key_code, query_code, lse_ref,
    dq_ref, dk_ref, dv_ref, dk_sum, dv_sum, dq_acc,
):
    length, width = q_ref.shape
    pairs = width // PAIR
    left = lane_left(BLK)
    own = eye_pair()
    dk_sum[...] = jnp.zeros_like(dk_sum)
    dv_sum[...] = jnp.zeros_like(dv_sum)

    def narrow(row, carry):
        block = table[row, 0]
        rows = block_rows(block)
        bias = slot_bias(table, row, key_code, query_code[pl.ds(block, 1), :], own)
        for pair in range(pairs):
            lanes = slice(pair * PAIR, (pair + 1) * PAIR)
            query = pair_rows(q_ref[rows, lanes], left, SCALE)
            grad = pair_rows(do_ref[rows, lanes], left)
            keys = slot_rows(k_ref, table, row, lanes)
            values = slot_rows(v_ref, table, row, lanes)
            scores = dot_nt(keys, query) + bias
            probs = jnp.exp(scores - lse_ref[block, pl.ds(pair, 1), :])
            g_probs = dot_nt(values, grad)
            terms = probs * g_probs
            g_scores = (terms - probs * jnp.sum(terms, 0, keepdims=True)).astype(jnp.bfloat16)
            dv = dot_nn(probs.astype(jnp.bfloat16), grad)
            dk = dot_nn(g_scores, query)
            both = dot_tn(g_scores, keys)
            dq_ref[rows, lanes] = (jnp.where(left, both[:BLK], both[BLK:]) * SCALE).astype(
                dq_ref.dtype
            )
            for slot in range(SLOTS):
                spot = block_rows(table[row, 1 + slot])
                part = slice(slot * BLK, (slot + 1) * BLK)
                dk_sum[spot, lanes] += dk[part]
                dv_sum[spot, lanes] += dv[part]
        return carry

    lax.fori_loop(0, table.shape[0], narrow, 0)

    for which in range(2):
        block = wide[which]
        rows = block_rows(block)
        code = query_code[pl.ds(block, 1), :]

        def pieces(chunk, pair, bias):
            keys_at = pl.ds(pl.multiple_of(chunk * WIDE, WIDE), WIDE)
            lanes = slice(pair * PAIR, (pair + 1) * PAIR)
            query = pair_rows(q_ref[rows, lanes], left, SCALE)
            grad = pair_rows(do_ref[rows, lanes], left)
            keys = k_ref[keys_at, lanes]
            scores = dot_nt(keys, query) + bias
            probs = jnp.exp(scores - lse_ref[block, pl.ds(pair, 1), :])
            return keys_at, lanes, query, grad, keys, probs, probs * dot_nt(v_ref[keys_at, lanes], grad)

        def first(chunk, carry):
            bias = wide_bias(key_code, code, block, chunk)
            return tuple(
                carry[pair] + jnp.sum(pieces(chunk, pair, bias)[-1], 0, keepdims=True)
                for pair in range(pairs)
            )

        deltas = lax.fori_loop(
            0, length // WIDE, first, (jnp.zeros((1, PAIR), jnp.float32),) * pairs
        )
        dq_acc[...] = jnp.zeros_like(dq_acc)

        def second(chunk, carry):
            bias = wide_bias(key_code, code, block, chunk)
            for pair in range(pairs):
                keys_at, lanes, query, grad, keys, probs, terms = pieces(chunk, pair, bias)
                g_scores = (terms - probs * carry[pair]).astype(jnp.bfloat16)
                dv_sum[keys_at, lanes] += dot_nn(probs.astype(jnp.bfloat16), grad)
                dk_sum[keys_at, lanes] += dot_nn(g_scores, query)
                dq_acc[pair] += dot_tn(g_scores, keys)
            return carry

        lax.fori_loop(0, length // WIDE, second, deltas)
        for pair in range(pairs):
            lanes = slice(pair * PAIR, (pair + 1) * PAIR)
            both = dq_acc[pair]
            dq_ref[rows, lanes] = (jnp.where(left, both[:BLK], both[BLK:]) * SCALE).astype(
                dq_ref.dtype
            )
    dk_ref[...] = dk_sum[...].astype(dk_ref.dtype)
    dv_ref[...] = dv_sum[...].astype(dv_ref.dtype)


VMEM_SPEC = pl.BlockSpec(memory_space=pltpu.VMEM)
SMEM_SPEC = pl.BlockSpec(memory_space=pltpu.SMEM)
ROOM = pltpu.CompilerParams(vmem_limit_bytes=60 * 1024 * 1024)


def attend(table, wide, q, k, v, key_code, query_code):
    length, width = q.shape
    return pl.pallas_call(
        attend_kernel,
        out_shape=(
            jax.ShapeDtypeStruct((length, width), jnp.bfloat16),
            jax.ShapeDtypeStruct((length // BLK, 8, PAIR), jnp.float32),
        ),
        in_specs=[SMEM_SPEC] * 2 + [VMEM_SPEC] * 5,
        out_specs=(VMEM_SPEC, VMEM_SPEC),
        scratch_shapes=[pltpu.VMEM((width // PAIR, PAIR, PAIR), jnp.float32)],
        compiler_params=ROOM,
        cost_estimate=pl.CostEstimate(
            flops=length * width * 1024 * 60, bytes_accessed=length * width * 8,
            transcendentals=length * width * 8,
        ),
        name="attend",
    )(table, wide, q, k, v, key_code, query_code)


def attend_back(table, wide, q, k, v, do, key_code, query_code, lse):
    length, width = q.shape
    shape = jax.ShapeDtypeStruct((length, width), jnp.bfloat16)
    return pl.pallas_call(
        attend_back_kernel,
        out_shape=(shape, shape, shape),
        in_specs=[SMEM_SPEC] * 2 + [VMEM_SPEC] * 7,
        out_specs=(VMEM_SPEC,) * 3,
        scratch_shapes=[
            pltpu.VMEM((length, width), jnp.float32),
            pltpu.VMEM((length, width), jnp.float32),
            pltpu.VMEM((width // PAIR, PAIR, PAIR), jnp.float32),
        ],
        compiler_params=ROOM,
        cost_estimate=pl.CostEstimate(
            flops=length * width * 1024 * 70, bytes_accessed=length * width * 14,
            transcendentals=length * width * 8,
        ),
        name="attend_back",
    )(table, wide, q, k, v, do, key_code, query_code, lse)


GROUPS = 8
DUOS = GROUPS // 2
TILE = 256
ANY_SPEC = pl.BlockSpec(memory_space=pl.ANY)
DMA = pltpu.SemaphoreType.DMA
WIDE_ROOM = pltpu.CompilerParams(vmem_limit_bytes=63 * 1024 * 1024)


def normalize(values):
    row_mean = jnp.mean(values, -1, keepdims=True)
    centered = values - row_mean
    row_var = jnp.mean(centered * centered, -1, keepdims=True)
    inverse = lax.rsqrt(row_var + EPSILON)
    return centered * inverse, inverse


def normalize_back(grad, unit, inverse):
    return inverse * (
        grad
        - jnp.mean(grad, -1, keepdims=True)
        - unit * jnp.mean(grad * unit, -1, keepdims=True)
    )


def gelu_both(u):
    root = 0.7978845608028654
    square = u * u
    inner = jnp.tanh(u * (root + (root * 0.044715) * square))
    half = 0.5 + 0.5 * inner
    slope = half + u * (0.5 - 0.5 * (inner * inner)) * (root + (3.0 * root * 0.044715) * square)
    return u * half, slope


def start_copies(pairs, sem):
    copies = [pltpu.make_async_copy(src, dst, sem.at[i]) for i, (src, dst) in enumerate(pairs)]
    for copy in copies:
        copy.start()
    return copies


def wait_copies(copies):
    for copy in copies:
        copy.wait()


def my_spot():
    place = lax.axis_index("context")
    return lax.axis_index("tensor"), place // 2, place % 2


def group_homes():
    half, turn, share = my_spot()
    return [
        ((half + h) % 2, ((turn + t) % 2) * 2 + (share + s) % 2)
        for s in range(2)
        for h in range(2)
        for t in range(2)
    ]


def lanes_of(g, cols):
    return pl.ds((g % 2) * cols, cols)


def project_attend_kernel(
    table, wide, x0, x1, x2, x3, n0, n1, n2, n3, f0, f1, b_qkv, key_code, query_code,
    own_ref, other_ref, q_home, k_home, v_home, w_home, lse_ref,
    x_v, q_v, k_v, v_v, o_v, w_v, acc, in_sem, out_sem, w_sem,
):
    span = x0.shape[0]
    length, width = q_v.shape
    half, turn, share = my_spot()
    weights = []
    for t in range(2):
        at = (turn + t) % 2
        homes = [w_v.at[:, at, share], w_v.at[:, at, (share + 1) % 2]]
        same, swap = ((n0, n2), (n1, n3))[t]
        copies = [pltpu.make_async_copy(src, homes[0], w_sem.at[t]) for src in (same, swap)]

        @pl.when(half == share)
        def _():
            copies[0].start()

        @pl.when(half != share)
        def _():
            copies[1].start()

        far = pltpu.make_async_copy((f0, f1)[t], homes[1], w_sem.at[2 + t])
        far.start()
        weights += [copies[0], far]
    loads = start_copies(
        [(x, x_v.at[pl.ds(i * span, span)]) for i, x in enumerate((x0, x1, x2, x3))], in_sem
    )
    wait_copies(weights)
    w_qkv = w_v[...].reshape(x_v.shape[1], 3 * width)
    for i in range(4):
        loads[i].wait()
        at = pl.ds(i * span, span)
        value = (dot_nn(x_v[at, :], w_qkv) + b_qkv[...]).astype(jnp.bfloat16)
        q_v[at, :] = value[:, :width]
        k_v[at, :] = value[:, width : 2 * width]
        v_v[at, :] = value[:, 2 * width :]
    stores = start_copies([(q_v, q_home), (k_v, k_home), (v_v, v_home), (w_v, w_home)], out_sem)
    attend_kernel(table, wide, q_v, k_v, v_v, key_code, query_code, o_v, lse_ref, acc)
    own_ref[...] = o_v[: length // 2, :]
    other_ref[...] = o_v[length // 2 :, :]
    wait_copies(stores)


def project_attend(table, wide, chunks, near, far, b_qkv, key_code, query_code):
    span, features = chunks[0].shape
    length = 4 * span
    depth, slim, cols = near[0].shape
    width = cols // 3
    bf16, shape = jnp.bfloat16, jax.ShapeDtypeStruct
    outs = pl.pallas_call(
        project_attend_kernel,
        out_shape=(shape((length // 2, width), bf16),) * 2
        + (shape((length, width), bf16),) * 3
        + (
            shape((depth, 2, 2, slim, cols), bf16),
            shape((length // BLK, 8, PAIR), jnp.float32),
        ),
        in_specs=[SMEM_SPEC] * 2 + [ANY_SPEC] * 10 + [VMEM_SPEC] * 3,
        out_specs=(VMEM_SPEC,) * 2 + (ANY_SPEC,) * 4 + (VMEM_SPEC,),
        scratch_shapes=[pltpu.VMEM((length, features), bf16)]
        + [pltpu.VMEM((length, width), bf16)] * 4
        + [
            pltpu.VMEM((depth, 2, 2, slim, cols), bf16),
            pltpu.VMEM((width // PAIR, PAIR, PAIR), jnp.float32),
            DMA((4,)), DMA((4,)), DMA((4,)),
        ],
        compiler_params=WIDE_ROOM,
        cost_estimate=pl.CostEstimate(
            flops=length * width * 1024 * 65, bytes_accessed=length * width * 16,
            transcendentals=length * width * 8,
        ),
        name="project_attend",
    )(table, wide, *chunks, *near, *far, b_qkv, key_code, query_code)
    att0, att1, q, k, v, w_qkv, lse = outs
    return att0, att1, q, k, v, lse, w_qkv.reshape(features, cols)


def attend_project_kernel(
    table, wide, x0, x1, x2, x3, do0, do1, q_in, k_in, v_in, w_qkv, key_code, query_code, lse_ref,
    back_own, back_other, keep_home, send_home, sums,
    x_v, q_v, k_v, v_v, do_v, d_v, dk_sum, dv_sum, acc, grad_v, in_sem, x_sem, out_sem,
):
    f32, bf16 = jnp.float32, jnp.bfloat16
    span = x0.shape[0]
    length, width = q_v.shape
    depth, turns, shares, slim, cols = grad_v.shape
    half_length = length // 2
    loads = start_copies(
        [
            (q_in, q_v), (k_in, k_v), (v_in, v_v),
            (do0, do_v.at[pl.ds(0, half_length)]),
            (do1, do_v.at[pl.ds(half_length, half_length)]),
        ],
        in_sem,
    )
    x_loads = start_copies(
        [(x, x_v.at[pl.ds(i * span, span)]) for i, x in enumerate((x0, x1, x2, x3))], x_sem
    )
    wait_copies(loads)
    parts = [d_v.at[:, pl.ds(i * width, width)] for i in range(3)]
    attend_back_kernel(
        table, wide, q_v, k_v, v_v, do_v, key_code, query_code, lse_ref,
        *parts, dk_sum, dv_sum, acc,
    )
    wait_copies(x_loads)
    sums[0:1, :] = jnp.sum(d_v[:, :width].astype(f32), 0, keepdims=True)
    sums[1:2, :] = jnp.sum(d_v[:, 2 * width :].astype(f32), 0, keepdims=True)
    grad_v[...] = dot_tn(x_v[...], d_v[...]).astype(bf16).reshape(grad_v.shape)
    half, turn, share = my_spot()
    stores = start_copies(
        [
            (grad_v.at[:, (turn + t) % 2, who], home.at[t])
            for t in range(turns)
            for who, home in ((share, keep_home), ((share + 1) % 2, send_home))
        ],
        out_sem,
    )
    for i in range(4):
        value = dot_nt(d_v[pl.ds(i * span, span), :], w_qkv[...])
        if i < 2:
            back_own[pl.ds(i * span, span), :] = value
        else:
            back_other[pl.ds((i - 2) * span, span), :] = value.astype(bf16)
    wait_copies(stores)


def attend_project(
    table, wide, chunks, do0, do1, q, k, v, w_qkv, key_code, query_code, lse, depth
):
    span, features = chunks[0].shape
    length, width = q.shape
    f32, bf16, shape = jnp.float32, jnp.bfloat16, jax.ShapeDtypeStruct
    slim = features // depth // 4
    grads = shape((2, depth, slim, 3 * width), bf16)
    return pl.pallas_call(
        attend_project_kernel,
        out_shape=(
            shape((length // 2, features), f32), shape((length // 2, features), bf16),
            grads, grads, shape((8, width), f32),
        ),
        in_specs=[SMEM_SPEC] * 2 + [ANY_SPEC] * 9 + [VMEM_SPEC] * 4,
        out_specs=(VMEM_SPEC,) * 2 + (ANY_SPEC,) * 2 + (VMEM_SPEC,),
        scratch_shapes=[pltpu.VMEM((length, features), bf16)]
        + [pltpu.VMEM((length, width), bf16)] * 4
        + [pltpu.VMEM((length, 3 * width), bf16)]
        + [pltpu.VMEM((length, width), f32)] * 2
        + [
            pltpu.VMEM((width // PAIR, PAIR, PAIR), f32),
            pltpu.VMEM((depth, 2, 2, slim, 3 * width), bf16),
            DMA((5,)), DMA((4,)), DMA((4,)),
        ],
        compiler_params=WIDE_ROOM,
        cost_estimate=pl.CostEstimate(
            flops=length * width * 1024 * 85, bytes_accessed=length * width * 30,
            transcendentals=length * width * 8,
        ),
        name="attend_project",
    )(table, wide, *chunks, do0, do1, q, k, v, w_qkv, key_code, query_code, lse)


def load_weights(groups, w_up, w_dn, w_out, up_sem, dn_sem, wo_sem):
    depth, deep, cols = groups[0].shape
    thin = w_up.shape[2]
    slim = deep - 2 * thin
    homes = group_homes()
    out_loads = []
    for g in range(GROUPS):
        half, at = homes[g]
        for d in range(depth):
            spot = pl.ds(pl.multiple_of(d * thin + at * slim, 16), slim)
            out_loads.append(
                pltpu.make_async_copy(
                    groups[g].at[d, pl.ds(2 * thin, slim)], w_out.at[half, spot], wo_sem.at[g, d]
                )
            )
    up_loads = [
        pltpu.make_async_copy(
            groups[g].at[:, pl.ds(0, thin)], w_up.at[g // 2, :, :, lanes_of(g, cols)], up_sem.at[g]
        )
        for g in range(GROUPS)
    ]
    dn_loads = [
        pltpu.make_async_copy(
            groups[g].at[:, pl.ds(thin, thin)],
            w_dn.at[g // 2, :, :, lanes_of(g, cols)],
            dn_sem.at[g],
        )
        for g in range(GROUPS)
    ]
    return out_loads, up_loads, dn_loads


def whole(ref, g):
    depth, thin, cols = ref.shape[1:]
    return ref[g].reshape(depth * thin, cols)


def ffn_front_kernel(att0, att1, x0, x1, g0, g1, *rest):
    groups = rest[:GROUPS]
    (
        valid, vectors, b_up,
        out0_home, out1_home, slope_home, g_second_home, unit_home, norm_t_home, near_ref, far_ref,
        inverse_ref, sums,
        att_v, x_v, g_v, w_up, w_dn, w_out, act, slope, normed_low,
        out_v, g_second_v, unit_v, norm_t, g_ffn_t, stage,
        in_sem, up_sem, dn_sem, wo_sem, stage_sem, home_sem, end_sem,
    ) = rest[GROUPS:]
    f32, bf16 = jnp.float32, jnp.bfloat16
    rows, width = x_v.shape
    span = x0.shape[0]
    depth, deep, cols = groups[0].shape
    half, turn, share = my_spot()
    other = (share + 1) % 2
    out_loads, up_loads, dn_loads = load_weights(groups, w_up, w_dn, w_out, up_sem, dn_sem, wo_sem)
    loads = start_copies(
        [(a, att_v.at[:, lanes_of(i, cols)]) for i, a in enumerate((att0, att1))]
        + [(x, x_v.at[pl.ds(i * span, span)]) for i, x in enumerate((x0, x1))]
        + [(g, g_v.at[pl.ds(i * span, span)]) for i, g in enumerate((g0, g1))],
        in_sem,
    )
    for copy in out_loads + up_loads + dn_loads:
        copy.start()
    sums[...] = jnp.zeros_like(sums)
    wait_copies(loads + out_loads)
    b_out, gain1, shift1, b_down, gain2, shift2 = (vectors[i : i + 1, :] for i in range(6))

    def add_sum(index, value):
        sums[index : index + 1, :] += jnp.sum(value, 0, keepdims=True)

    def homes(tile):
        at = pl.ds(pl.multiple_of(tile * TILE, TILE), TILE)
        return [
            pltpu.make_async_copy(src, dst, home_sem.at[i, tile])
            for i, (src, dst) in enumerate(
                [
                    (slope.at[:, at], slope_home.at[:, at]),
                    (g_second_v.at[at], g_second_home.at[at]),
                    (unit_v.at[at], unit_home.at[at]),
                ]
            )
        ]

    def tile_step(tile, carry):
        at = pl.ds(pl.multiple_of(tile * TILE, TILE), TILE)
        live = valid[at, :]
        attn = b_out + dot_nt(att_v[at, :], jnp.concatenate([w_out[share], w_out[other]], 1))
        x = x_v[at, :].astype(f32)
        first = x + attn
        add_sum(6, live * (x * x))
        add_sum(7, live * (first * first))
        add_sum(9, live * (attn * attn))
        unit1, inverse1 = normalize(first)
        unit_v[at, :] = unit1
        inverse_ref[at, :] = inverse1
        normed = unit1 * gain1 + shift1
        low = normed.astype(bf16)
        normed_low[...] = low
        norm_t[:, at] = low.T

        @pl.when(tile == 0)
        def _():
            wait_copies(up_loads + dn_loads)

        def up_step(g, ffn):
            pre = dot_nn(normed_low[...], whole(w_up, g)) + b_up[pl.ds(g, 1), :]
            value, rise = gelu_both(pre)
            value = value.astype(bf16)
            act[g, at, :] = value
            slope[g, at, :] = rise.astype(bf16)
            return ffn + dot_nt(value, whole(w_dn, g))

        ffn = lax.fori_loop(0, DUOS, up_step, jnp.broadcast_to(b_down, (TILE, width)))
        second = normed + ffn
        add_sum(8, live * (second * second))
        add_sum(10, live * (ffn * ffn))
        unit2, inverse2 = normalize(second)
        out_v[at, :] = (unit2 * gain2 + shift2).astype(bf16)
        g_out = g_v[at, :].astype(f32)
        add_sum(4, g_out * unit2)
        add_sum(5, g_out)
        g_second = normalize_back(g_out * gain2, unit2, inverse2)
        g_second_v[at, :] = g_second
        g_ffn = g_second.astype(bf16)
        add_sum(3, g_ffn.astype(f32))
        g_ffn_t[:, at] = g_ffn.T
        for copy in homes(tile):
            copy.start()
        return carry

    lax.fori_loop(0, rows // TILE, tile_step, 0)
    last = start_copies(
        [
            (norm_t, norm_t_home),
            (out_v.at[pl.ds(0, span)], out0_home),
            (out_v.at[pl.ds(span, span)], out1_home),
        ],
        end_sem,
    )
    stores = [None] * GROUPS
    for duo in range(DUOS):
        down = dot_nn(g_ffn_t[...], act[duo]).astype(bf16).reshape(depth, -1, 2 * cols)
        for g in (2 * duo, 2 * duo + 1):
            slot = g % 4
            if g >= 4:
                stores[g - 4].wait()
            stage[slot] = down[:, :, (g % 2) * cols : (g % 2 + 1) * cols]
            home = near_ref.at[g] if g < DUOS else far_ref.at[g - DUOS]
            stores[g] = pltpu.make_async_copy(stage.at[slot], home, stage_sem.at[slot])
            stores[g].start()
    for tile in range(rows // TILE):
        wait_copies(homes(tile))
    wait_copies(stores[-4:] + last)


def ffn_front(att0, att1, x_chunks, g_chunks, groups, valid, vectors, b_up):
    rows, part = att0.shape
    width = x_chunks[0].shape[1]
    depth, deep, cols = groups[0].shape
    thin = width // depth
    f32, bf16, shape = jnp.float32, jnp.bfloat16, jax.ShapeDtypeStruct
    grads = shape((DUOS, depth, thin, cols), bf16)
    weights = pltpu.VMEM((DUOS, depth, thin, 2 * cols), bf16)
    flat = pltpu.VMEM((rows, width), bf16)
    tall = pltpu.VMEM((rows, width), f32)
    deep_rows = pltpu.VMEM((DUOS, rows, 2 * cols), bf16)
    turned = pltpu.VMEM((width, rows), bf16)
    return pl.pallas_call(
        ffn_front_kernel,
        out_shape=(
            shape((rows // 2, width), bf16), shape((rows // 2, width), bf16),
            shape((DUOS, rows, 2 * cols), bf16),
            shape((rows, width), f32), shape((rows, width), f32), shape((width, rows), bf16),
            grads, grads, shape((rows, 1), f32), shape((16, width), f32),
        ),
        in_specs=[ANY_SPEC] * (6 + GROUPS) + [VMEM_SPEC] * 3,
        out_specs=(ANY_SPEC,) * 8 + (VMEM_SPEC,) * 2,
        scratch_shapes=[
            flat, flat, flat, weights, weights, pltpu.VMEM((2, width, part), bf16),
            deep_rows, deep_rows, pltpu.VMEM((TILE, width), bf16),
            flat, tall, tall, turned, turned, pltpu.VMEM((4, depth, thin, cols), bf16),
            DMA((6,)), DMA((GROUPS,)), DMA((GROUPS,)), DMA((GROUPS, depth)), DMA((4,)),
            DMA((3, rows // TILE)), DMA((3,)),
        ],
        compiler_params=WIDE_ROOM,
        cost_estimate=pl.CostEstimate(
            flops=38 * 10**9, bytes_accessed=40 * 10**6, transcendentals=rows * GROUPS * cols
        ),
        name="ffn_front",
    )(att0, att1, *x_chunks, *g_chunks, *groups, valid, vectors, b_up)


def ffn_rear_kernel(att0, att1, slope_in, g_second_in, unit_in, norm_t_in, *rest):
    groups = rest[:GROUPS]
    (
        inverse_ref, vectors,
        g_first_home, g_att0_home, g_att1_home, near_ref, far_ref, sums, up_sums,
        att_v, slope, g_second_v, unit_v, norm_t, w_up, w_dn, w_out, g_pre,
        g_first_v, g_att_v, g_attn_t, stage,
        in_sem, up_sem, dn_sem, wo_sem, stage_sem, home_sem,
    ) = rest[GROUPS:]
    f32, bf16 = jnp.float32, jnp.bfloat16
    rows, width = unit_v.shape
    depth, deep, cols = groups[0].shape
    thin = w_up.shape[2]
    slim = deep - 2 * thin
    half, turn, share = my_spot()
    other = (share + 1) % 2
    out_loads, up_loads, dn_loads = load_weights(groups, w_up, w_dn, w_out, up_sem, dn_sem, wo_sem)
    wait_order = [
        pltpu.make_async_copy(src, dst, in_sem.at[i])
        for i, (src, dst) in enumerate(
            [
                (g_second_in, g_second_v), (slope_in, slope), (unit_in, unit_v),
                (norm_t_in, norm_t), (att0, att_v.at[:, lanes_of(0, cols)]),
                (att1, att_v.at[:, lanes_of(1, cols)]),
            ]
        )
    ]
    for copy in wait_order[:1] + dn_loads + wait_order[1:2] + up_loads + wait_order[2:3]:
        copy.start()
    for copy in out_loads + wait_order[3:]:
        copy.start()
    sums[...] = jnp.zeros_like(sums)
    up_sums[...] = jnp.zeros_like(up_sums)
    gain1 = vectors[1:2, :]
    wait_copies(wait_order[:1] + dn_loads + wait_order[1:2])
    out_weight = lambda: jnp.concatenate([w_out[share], w_out[other]], 1)

    def add_sum(index, value):
        sums[index : index + 1, :] += jnp.sum(value, 0, keepdims=True)

    def tile_step(tile, carry):
        at = pl.ds(pl.multiple_of(tile * TILE, TILE), TILE)

        @pl.when(tile == 0)
        def _():
            wait_copies(up_loads + wait_order[2:] + out_loads)

        g_second = g_second_v[at, :]
        g_ffn = g_second.astype(bf16)

        def back_step(g, total):
            grad = (dot_nn(g_ffn, whole(w_dn, g)) * slope[g, at, :].astype(f32)).astype(bf16)
            g_pre[g, at, :] = grad
            up_sums[pl.ds(g, 1), :] += jnp.sum(grad.astype(f32), 0, keepdims=True)
            return total + dot_nt(grad, whole(w_up, g))

        g_normed = lax.fori_loop(0, DUOS, back_step, g_second)
        unit1 = unit_v[at, :]
        add_sum(1, g_normed * unit1)
        add_sum(2, g_normed)
        g_first = normalize_back(g_normed * gain1, unit1, inverse_ref[at, :])
        g_first_v[at, :] = g_first
        g_attn = g_first.astype(bf16)
        add_sum(0, g_attn.astype(f32))
        g_attn_t[:, at] = g_attn.T
        g_att_v[at, :] = dot_nn(g_attn, out_weight()).astype(bf16)
        return carry

    lax.fori_loop(0, rows // TILE, tile_step, 0)
    homes = start_copies(
        [
            (g_att_v.at[:, lanes_of(0, cols)], g_att0_home),
            (g_att_v.at[:, lanes_of(1, cols)], g_att1_home),
            (g_first_v, g_first_home),
        ],
        home_sem,
    )
    both = dot_nn(g_attn_t[...], att_v[...]).astype(bf16)
    w_out[share] = both[:, :cols]
    w_out[other] = both[:, cols:]
    spots = group_homes()
    stores = [None] * GROUPS
    for duo in range(DUOS):
        up = dot_nn(norm_t[...], g_pre[duo]).astype(bf16).reshape(depth, thin, 2 * cols)
        for g in (2 * duo, 2 * duo + 1):
            slot = g % 4
            if g >= 4:
                stores[g - 4].wait()
            stage[slot, :, pl.ds(0, thin), :] = up[:, :, (g % 2) * cols : (g % 2 + 1) * cols]
            where, at = spots[g]
            for d in range(depth):
                spot = pl.ds(pl.multiple_of(d * thin + at * slim, 16), slim)
                stage[slot, d, pl.ds(thin, slim), :] = w_out[where, spot, :]
            home = near_ref.at[g] if g < DUOS else far_ref.at[g - DUOS]
            stores[g] = pltpu.make_async_copy(stage.at[slot], home, stage_sem.at[slot])
            stores[g].start()
    wait_copies(stores[-4:] + homes)


def ffn_rear(att0, att1, slope, g_second, unit, norm_t, groups, inverse, vectors):
    rows, part = att0.shape
    width = unit.shape[1]
    depth, deep, cols = groups[0].shape
    thin = width // depth
    f32, bf16, shape = jnp.float32, jnp.bfloat16, jax.ShapeDtypeStruct
    grads = shape((DUOS, depth, deep - thin, cols), bf16)
    weights = pltpu.VMEM((DUOS, depth, thin, 2 * cols), bf16)
    flat = pltpu.VMEM((rows, width), bf16)
    tall = pltpu.VMEM((rows, width), f32)
    deep_rows = pltpu.VMEM((DUOS, rows, 2 * cols), bf16)
    turned = pltpu.VMEM((width, rows), bf16)
    return pl.pallas_call(
        ffn_rear_kernel,
        out_shape=(
            shape((rows, width), f32), shape((rows, part), bf16), shape((rows, part), bf16),
            grads, grads, shape((16, width), f32), shape((DUOS, 2 * cols), f32),
        ),
        in_specs=[ANY_SPEC] * (6 + GROUPS) + [VMEM_SPEC] * 2,
        out_specs=(ANY_SPEC,) * 5 + (VMEM_SPEC,) * 2,
        scratch_shapes=[
            flat, deep_rows, tall, tall, turned, weights, weights,
            pltpu.VMEM((2, width, part), bf16), deep_rows, tall, flat, turned,
            pltpu.VMEM((4, depth, deep - thin, cols), bf16),
            DMA((6,)), DMA((GROUPS,)), DMA((GROUPS,)), DMA((GROUPS, depth)), DMA((4,)), DMA((3,)),
        ],
        compiler_params=WIDE_ROOM,
        cost_estimate=pl.CostEstimate(
            flops=38 * 10**9, bytes_accessed=40 * 10**6, transcendentals=0
        ),
        name="ffn_rear",
    )(att0, att1, slope, g_second, unit, norm_t, *groups, inverse, vectors)


def gather_chunks_kernel(c0, c1, c2, c3, home, held, ready, in_sem, out_sem):
    half, turn, share = my_spot()
    loads = start_copies([(c, held.at[i]) for i, c in enumerate((c0, c1, c2, c3))], in_sem)
    stores = []
    for i in range(4):
        loads[i].wait()
        ready[i] = held[i].astype(ready.dtype)
        at = ((half + i // 2) % 2) * 2 + (turn + i) % 2
        stores.append(pltpu.make_async_copy(ready.at[i], home.at[at], out_sem.at[i]))
        stores[i].start()
    wait_copies(stores)


def gather_chunks(chunks, dtype):
    span, width = chunks[0].shape
    return pl.pallas_call(
        gather_chunks_kernel,
        out_shape=jax.ShapeDtypeStruct((4, span, width), dtype),
        in_specs=[ANY_SPEC] * 4,
        out_specs=ANY_SPEC,
        scratch_shapes=[
            pltpu.VMEM((4, span, width), chunks[0].dtype), pltpu.VMEM((4, span, width), dtype),
            DMA((4,)), DMA((4,)),
        ],
        compiler_params=WIDE_ROOM,
        name="gather_chunks",
    )(*chunks)


def layer_norm(values, norm_gain, norm_shift):
    row_mean = jnp.mean(values, -1, keepdims=True)
    centered = values - row_mean
    row_var = jnp.mean(centered * centered, -1, keepdims=True)
    return centered * lax.rsqrt(row_var + EPSILON) * norm_gain + norm_shift


def gelu_tanh(values):
    return jax.nn.gelu(values, approximate=True)


def block_tables(random_seq, all_blocks, place):
    block = jnp.arange(2, all_blocks, dtype=jnp.int32)
    last = all_blocks - 1
    zero = jnp.zeros_like(block)
    true_ids = jnp.stack(
        [block, block - 1, block, jnp.minimum(block + 1, last), zero, zero + 1], -1
    )
    true_ids = jnp.concatenate([true_ids, random_seq[2:]], -1)
    flags = jnp.stack([block >= 3, block <= last - 1], -1).astype(jnp.int32)
    return (
        jnp.concatenate([place(true_ids), flags], -1).astype(jnp.int32),
        place(jnp.arange(2, dtype=jnp.int32)),
    )


def local(
    hidden_in, out_grad, segment_ids, token_valid, random_blocks,
    query_weight, query_bias, key_weight, value_weight, value_bias,
    output_weight, output_bias, norm1_gain, norm1_shift,
    up_weight, up_bias, down_weight, down_bias, norm2_gain, norm2_shift,
):
    f32, bf16 = jnp.float32, jnp.bfloat16
    seqs, span, width = hidden_in.shape
    length = segment_ids.shape[1]
    places = length // span
    halves = lax.axis_size("tensor")
    depth = lax.axis_size("dp")
    turns = seqs // halves
    shares = places // turns
    my_half = lax.axis_index("tensor")
    my_place = lax.axis_index("context")
    my_depth = lax.axis_index("dp")
    my_turn, my_share = my_place // shares, my_place % shares
    my_seq = my_half * turns + my_turn
    blocks = length // BLK
    rows = turns * span
    spots = [(h, t) for h in range(halves) for t in range(turns)]

    def send(value, half=0, turn=0, share=0):
        if half % halves == 0 and turn % turns == 0 and share % shares == 0:
            return value
        pairs = []
        for h in range(halves):
            for t in range(turns):
                for s in range(shares):
                    to_place = (t + turn) % turns * shares + (s + share) % shares
                    pairs.append(
                        ((t * shares + s) * halves + h, to_place * halves + (h + half) % halves)
                    )
        return lax.ppermute(value, ("context", "tensor"), pairs)

    def send_deep(value, step):
        return lax.ppermute(value, "dp", [(i, (i + step) % depth) for i in range(depth)])

    def pick(value, index, axis=0):
        return lax.dynamic_index_in_dim(value, index, axis, keepdims=False)

    def own_slice(value, count, which, axis):
        size = value.shape[axis] // count
        return lax.dynamic_slice_in_dim(value, which * size, size, axis)

    def gather_deep(value):
        if depth > 4:
            return lax.all_gather(value, "dp", axis=0)
        got = [value] + [send_deep(value, k) for k in range(1, depth)]
        ring = jnp.stack([got[depth - 1 - i % depth] for i in range(2 * depth - 1)])
        return lax.dynamic_slice_in_dim(ring, depth - 1 - my_depth, depth, 0)

    def reduce_deep(value):
        if depth > 4:
            return lax.psum_scatter(value, "dp", scatter_dimension=0)
        total = pick(value, my_depth).astype(f32)
        for k in range(1, depth):
            total = total + send_deep(pick(value, (my_depth + k) % depth), k).astype(f32)
        return total.astype(bf16)

    def gather_square(value):
        near = {spot: send(value, *spot) for spot in spots}
        near = jnp.stack([near[spot] for spot in spots])
        return [near] + [send(near, 0, 0, s) for s in range(1, shares)]

    def reduce_square(value):
        total = value[0].astype(f32)
        for i, (h, t) in enumerate(spots[1:], 1):
            total = total + send(value[i], -h, -t).astype(f32)
        return total.astype(bf16)

    def gather_places(value):
        near = [send(value, 0, t) for t in range(turns)]
        near = jnp.stack(near)
        far = jnp.stack([near] + [send(near, 0, 0, s) for s in range(1, shares)])
        return jnp.stack(
            [
                pick(pick(far, (my_share - s) % shares), (my_turn - t) % turns)
                for t in range(turns)
                for s in range(shares)
            ]
        )

    def sum_all(value):
        for step in range(halves.bit_length() - 1):
            value = value + send(value, 1 << step)
        size = 1
        while size < places:
            value = value + lax.ppermute(value, "context", [(i, i ^ size) for i in range(places)])
            size *= 2
        size = 1
        while size < depth:
            value = value + lax.ppermute(value, "dp", [(i, i ^ size) for i in range(depth)])
            size *= 2
        return value

    def bring(value):
        return jnp.concatenate(
            [
                send(pick(value, my_half * turns + (my_turn + k) % turns), 0, k)
                for k in range(turns)
            ],
            0,
        )

    def deliver(value):
        value = value.reshape(turns, span, width)
        got = jnp.stack([send(value[t], h, -t) for h, t in spots])
        return jnp.stack(
            [
                pick(got, (my_half - h) % halves * turns + (t - my_turn) % turns)
                for h in range(halves)
                for t in range(turns)
            ]
        )

    def after(value, *earlier):
        return lax.optimization_barrier((value, *earlier))[0]

    per = span // BLK

    def place(block_ids):
        chunk = block_ids // per
        turn, share = chunk // shares, chunk % shares
        spot = ((my_share - share) % shares) * turns + (my_turn - turn) % turns
        return spot * per + block_ids % per

    def in_order(row):
        return jnp.concatenate(
            [
                lax.dynamic_slice_in_dim(
                    row,
                    (((my_turn - k) % turns) * shares + (my_share - s) % shares) * span,
                    span,
                )
                for s in range(shares)
                for k in range(turns)
            ]
        )

    seg = in_order(pick(segment_ids, my_seq))
    live = in_order(pick(token_valid, my_seq))
    random_seq = pick(random_blocks, my_seq)
    table, wide = block_tables(random_seq, blocks, place)
    key_code = jnp.broadcast_to(jnp.where(live == 1, seg, -1)[:, None], (length, PAIR))
    query_code = jnp.tile(seg.reshape(blocks, BLK), (1, PAIR // BLK))
    half_width = query_weight.shape[1]
    thin = query_weight.shape[0]
    slim = thin // places
    hidden = up_weight.shape[1] // places
    biases = jnp.concatenate([query_bias, value_bias, up_bias])
    biases = jnp.stack([send(biases, h) for h in range(halves)])
    biases = jnp.stack([pick(biases, (my_half - h) % halves) for h in range(halves)])
    b_q, b_v, b_up = (
        biases[:, at : at + b.shape[0]].reshape(-1)
        for b, at in ((query_bias, 0), (value_bias, half_width), (up_bias, 2 * half_width))
    )

    def spread(value, which, count):
        return lax.dynamic_update_slice_in_dim(
            jnp.zeros((value.shape[0] * count,), value.dtype), value, which * value.shape[0], 0
        )

    def summed(values):
        flat = sum_all(jnp.concatenate(values))
        out, at = [], 0
        for value in values:
            out.append(flat[at : at + value.shape[0]])
            at += value.shape[0]
        return out

    def finish(
        layer_out, input_grad, qkv_shard, ffn_shard, up_sums, group_at, norm_sums, stats, sum_q, sum_v
    ):
        up_natural = jnp.zeros_like(up_sums)
        for i, at in enumerate(group_at):
            up_natural = lax.dynamic_update_slice_in_dim(
                up_natural, up_sums[i * hidden : (i + 1) * hidden], at * hidden, 0
            )
        values = [up_natural, *norm_sums, stats]
        values += [spread(sum_q, my_share, shares), spread(sum_v, my_share, shares)]
        s_up, s_o, s_g1, s_s1, s_down, s_g2, s_s2, stats, s_q, s_v = summed(values)
        s_q, s_v, s_up = (own_slice(value, halves, my_half, 0) for value in (s_q, s_v, s_up))
        input_rms = jnp.sqrt(stats[:5] / (jnp.maximum(stats[5], 1.0) * width))
        join = lambda w: jnp.moveaxis(w, 0, 1).reshape(thin, -1).astype(f32)
        shard_up = join(ffn_shard[:, :thin])
        shard_down = join(ffn_shard[:, thin : 2 * thin]).T
        shard_o = ffn_shard[:, 2 * thin :].reshape(thin, -1)[:, :half_width].astype(f32).T
        shard_q, shard_k, shard_v = (qkv_shard[:, i].astype(f32) for i in range(3))
        return (
            layer_out, input_grad, shard_q, s_q, shard_k, shard_v, s_v, shard_o, s_o,
            s_g1, s_s1, shard_up, s_up, shard_down, s_down, s_g2, s_s2, input_rms,
        )

    if (turns, shares, halves) == (2, 2, 2) and depth <= 4 and rows % TILE == 0:
        qkv_piece = own_slice(
            jnp.concatenate([query_weight, key_weight, value_weight], 1), places, my_place, 0
        )
        qkv_deep = gather_deep(qkv_piece)
        x_own = [pick(hidden_in, my_seq)]
        x_own.append(send(pick(hidden_in, my_half * turns + (my_turn + 1) % turns), 0, 1))
        near_qkv = [send(qkv_deep, *spot) for spot in spots]
        mine = my_half == my_share
        far_qkv = [
            send(jnp.where(mine, near_qkv[2 + t], near_qkv[t]), 0, 0, 1) for t in range(turns)
        ]
        chunks = x_own + [send(x, 0, 0, 1) for x in x_own]
        own_bias = lambda b: own_slice(b, shares, my_share, 0)
        b_qkv = jnp.concatenate([own_bias(b_q), jnp.zeros((half_width,), bf16), own_bias(b_v)])
        b_qkv = b_qkv.astype(f32)[None]

        ffn_piece = jnp.concatenate(
            [
                own_slice(up_weight, places, my_place, 1),
                own_slice(down_weight, places, my_place, 0).T,
                own_slice(output_weight.T, places, my_place, 0),
            ],
            0,
        )
        ffn_deep = gather_deep(after(ffn_piece, qkv_deep))
        g_own = [pick(out_grad, my_seq)]
        g_next = pick(out_grad, my_half * turns + (my_turn + 1) % turns)
        g_own.append(send(after(g_next, near_qkv[1]), 0, 1))
        ffn_deep = after(ffn_deep, *near_qkv[1:])
        near = [send(ffn_deep, *spot) for spot in spots]
        group_at = [
            (
                (my_half - h) % halves * places
                + (my_turn - t) % turns * shares
                + (my_share - s) % shares
            )
            for s in range(shares)
            for h, t in spots
        ]
        b_up = jnp.concatenate(
            [lax.dynamic_slice_in_dim(b_up, at * hidden, hidden) for at in group_at]
        ).astype(f32)

        att0, att1, q, k, v, lse, w_qkv = project_attend(
            table, wide, chunks, near_qkv, far_qkv, b_qkv, key_code, query_code
        )
        att0, att1, near, g_own = lax.optimization_barrier((att0, att1, near, g_own))
        att1 = send(att1, 0, 0, 1)
        groups = near + [send(g, 0, 0, 1) for g in near]
        vectors = jnp.stack(
            [output_bias, norm1_gain, norm1_shift, down_bias, norm2_gain, norm2_shift]
        ).astype(f32)
        (
            out0, out1, slope, g_second, unit, norm_t, near_dn, far_dn, inverse, front_sums
        ) = ffn_front(
            att0, att1, x_own, g_own, groups, live[:rows, None].astype(f32), vectors,
            b_up.reshape(DUOS, -1),
        )
        out_chunks = [out0, send(out1, 0, 1), send(out0, 1), send(out1, 1, 1)]
        got_dn = send(far_dn, 0, 0, 1)
        g_first, g_att0, g_att1, near_uo, far_uo, rear_sums, up_sums = ffn_rear(
            att0, att1, slope, g_second, unit, norm_t, groups, inverse, vectors
        )
        out_chunks, got_dn, g_first, g_att0, g_att1, near_uo, far_uo = lax.optimization_barrier(
            (out_chunks, got_dn, g_first, g_att0, g_att1, near_uo, far_uo)
        )
        got_uo = send(far_uo, 0, 0, 1)
        g_att1 = send(g_att1, 0, 0, 1)
        total_dn = (near_dn.astype(f32) + got_dn.astype(f32)).astype(bf16)
        total_uo = (near_uo.astype(f32) + got_uo.astype(f32)).astype(bf16)
        parts_dn = [send(total_dn[i], *spots[i]) for i in range(len(spots))]
        parts_uo = [send(total_uo[i], *spots[i]) for i in range(len(spots))]
        g_att1 = after(g_att1, total_dn, total_uo)
        back_own, back_other, keep, swap, head_sums = attend_project(
            table, wide, chunks, g_att0, g_att1, q, k, v, w_qkv, key_code, query_code, lse, depth
        )
        back_own, back_other, keep, swap, parts_dn, parts_uo = lax.optimization_barrier(
            (back_own, back_other, keep, swap, parts_dn, parts_uo)
        )
        back_got = send(back_other, 0, 0, 1)
        swap = send(swap, 0, 0, 1)
        pieces = [jnp.where(mine, keep, swap), jnp.where(mine, swap, keep)]
        square = jnp.stack([pieces[h][t] for h, t in spots])
        qkv_shard = gather_places(reduce_deep(reduce_square(square)))
        qkv_shard = qkv_shard.reshape(thin, 3, half_width)
        total = [
            sum([p.astype(f32) for p in parts[1:]], parts[0].astype(f32)).astype(bf16)
            for parts in (parts_dn, parts_uo)
        ]
        total = jnp.concatenate([total[1][:, :thin], total[0], total[1][:, thin:]], 1)
        ffn_shard = gather_places(reduce_deep(total))
        grads = (g_first + back_own + back_got.astype(f32)).astype(bf16)
        g0, g1 = grads[:span], grads[span:]
        grad_chunks = [g0, send(g1, 0, 1), send(g0, 1), send(g1, 1, 1)]
        norm_sums = [rear_sums[0], rear_sums[1], rear_sums[2]] + [front_sums[i] for i in (3, 4, 5)]
        stats = jnp.concatenate(
            [
                jnp.sum(front_sums[6:11], 1),
                jnp.sum(live[:rows]).astype(f32)[None],
                jnp.zeros((2,), f32),
            ]
        )
        return finish(
            gather_chunks(out_chunks, bf16), gather_chunks(grad_chunks, f32), qkv_shard, ffn_shard,
            up_sums.reshape(-1), group_at, norm_sums, stats, head_sums[0], head_sums[1],
        )

    part = width // shares
    padded = -(-part // PAIR) * PAIR
    x_own = bring(hidden_in)
    qkv_piece = own_slice(
        jnp.concatenate([query_weight, key_weight, value_weight], 1), places, my_place, 0
    )
    qkv_all = jnp.stack(gather_square(gather_deep(qkv_piece)))
    per_half = shares // halves
    target = my_share // per_half
    qkv_all = jnp.stack(
        [
            pick(
                pick(qkv_all, (my_share - s) % shares),
                (my_half - target) % halves * turns + (my_turn - t) % turns,
            )
            for t in range(turns)
            for s in range(shares)
        ],
        1,
    ).reshape(width, 3, half_width)
    pad_cols = lambda w: jnp.pad(w, [(0, 0)] * (w.ndim - 1) + [(0, padded - part)])
    mine = lambda w: pad_cols(own_slice(w, per_half, my_share % per_half, w.ndim - 1))
    w_qkv = mine(qkv_all).reshape(width, 3 * padded)
    mine_b = lambda b: pad_cols(own_slice(b, shares, my_share, 0))
    b_qkv = jnp.concatenate([mine_b(b_q), jnp.zeros((padded,), bf16), mine_b(b_v)]).astype(f32)

    ffn_piece = jnp.concatenate(
        [
            own_slice(up_weight, places, my_place, 1),
            own_slice(down_weight, places, my_place, 0).T,
            jnp.pad(
                own_slice(output_weight.T, places, my_place, 0),
                [(0, 0), (0, max(0, hidden - half_width))],
            ).reshape(-1, hidden),
        ],
        0,
    )
    ffn_all = gather_square(gather_deep(ffn_piece))
    groups = [
        (s, i, ffn_all[s][i]) for s in range(shares) for i in range(len(spots))
    ]
    w_up = jnp.concatenate([g[:, :thin].reshape(width, hidden) for _, _, g in groups], 1)
    w_down_t = jnp.concatenate(
        [g[:, thin : 2 * thin].reshape(width, hidden) for _, _, g in groups], 1
    )
    out_all = jnp.stack(
        [jnp.stack([g[:, 2 * thin :] for g in ffn_all[s]]) for s in range(shares)]
    )
    w_out_t = jnp.stack(
        [
            jnp.stack(
                [
                    pick(
                        pick(out_all, (my_share - s) % shares),
                        (my_half - h) % halves * turns + (my_turn - t) % turns,
                    )
                    for t in range(turns)
                    for s in range(shares)
                ],
                1,
            ).reshape(width, half_width)
            for h in range(halves)
        ],
        1,
    ).reshape(width, width)
    w_out_t = jnp.concatenate(
        [own_slice(w_out_t, shares, (my_share + k) % shares, 1) for k in range(shares)], 1
    )
    group_at = [
        ((my_half - spots[i][0]) % halves * places
         + (my_turn - spots[i][1]) % turns * shares + (my_share - s) % shares)
        for s, i, _ in groups
    ]
    b_up = jnp.concatenate(
        [lax.dynamic_slice_in_dim(b_up, at * hidden, hidden) for at in group_at]
    ).astype(f32)

    g_out = bring(out_grad).astype(f32)
    x_seq = jnp.concatenate([send(x_own, 0, 0, k) for k in range(shares)], 0)
    q, k, v = (
        (
            jnp.dot(x_seq, w_qkv[:, i * padded : (i + 1) * padded], preferred_element_type=f32)
            + b_qkv[i * padded : (i + 1) * padded]
        ).astype(bf16)
        for i in range(3)
    )
    att, lse = attend(table, wide, q, k, v, key_code, query_code)
    att = att[:, :part].reshape(shares, rows, part)
    att_own = jnp.concatenate([send(att[s], 0, 0, -s) for s in range(shares)], 1)
    attn_out = lax.dot_general(
        att_own, w_out_t, (((1,), (1,)), ((), ())), preferred_element_type=f32
    ) + output_bias.astype(f32)
    x_full = x_own.astype(f32)
    first_sum = x_full + attn_out
    gain_one, shift_one = norm1_gain.astype(f32), norm1_shift.astype(f32)
    normed = layer_norm(first_sum, gain_one, shift_one)
    normed_low = normed.astype(bf16)
    pre_act = jnp.dot(normed_low, w_up, preferred_element_type=f32) + b_up
    act_low = gelu_tanh(pre_act).astype(bf16)
    ffn_out = lax.dot_general(
        act_low, w_down_t, (((1,), (1,)), ((), ())), preferred_element_type=f32
    ) + down_bias.astype(f32)
    second_sum = normed + ffn_out
    gain_two, shift_two = norm2_gain.astype(f32), norm2_shift.astype(f32)
    layer_out, norm_back = jax.vjp(layer_norm, second_sum, gain_two, shift_two)
    g_second, gain_two_grad, shift_two_grad = norm_back(g_out)
    layer_out = deliver(layer_out.astype(bf16))
    g_ffn = g_second.astype(bf16)
    g_act = jnp.dot(g_ffn, w_down_t, preferred_element_type=f32)
    g_pre = jax.vjp(gelu_tanh, pre_act)[1](g_act)[0].astype(bf16)
    up_part = jnp.dot(normed_low.T, g_pre, preferred_element_type=f32).astype(bf16)
    down_part_t = jnp.dot(g_ffn.T, act_low, preferred_element_type=f32).astype(bf16)
    g_normed = g_second + jnp.dot(g_pre, w_up.T, preferred_element_type=f32)
    g_first, gain_one_grad, shift_one_grad = jax.vjp(layer_norm, first_sum, gain_one, shift_one)[1](
        g_normed
    )
    g_attn = g_first.astype(bf16)
    out_part_t = jnp.dot(g_attn.T, att_own, preferred_element_type=f32).astype(bf16)
    g_att = jnp.dot(g_attn, w_out_t, preferred_element_type=f32).astype(bf16)
    do = jnp.concatenate(
        [send(own_slice(g_att, shares, s, 1), 0, 0, s) for s in range(shares)], 0
    )
    dq, dk, dv = attend_back(table, wide, q, k, v, pad_cols(do), key_code, query_code, lse)

    out_natural = jnp.concatenate(
        [own_slice(out_part_t, shares, (s - my_share) % shares, 1) for s in range(shares)], 1
    ).reshape(depth, turns, shares, slim, halves, half_width)

    def ffn_group(s, i):
        h, t = spots[i]
        at = (s * len(spots) + i) * hidden
        out = pick(out_natural, (my_half - h) % halves, 4)
        out = pick(pick(out, (my_turn - t) % turns, 1), (my_share - s) % shares, 1)
        out = jnp.pad(out, [(0, 0), (0, 0), (0, max(0, hidden - half_width))])
        cut = lambda w: w[:, at : at + hidden].reshape(depth, thin, hidden)
        return jnp.concatenate(
            [cut(up_part), cut(down_part_t), out.reshape(depth, -1, hidden)], 1
        )

    ffn_grads = [
        jnp.stack([ffn_group(s, i) for i in range(len(spots))]) for s in range(shares)
    ]
    total = ffn_grads[0].astype(f32)
    for s in range(1, shares):
        total = total + send(ffn_grads[s], 0, 0, -s).astype(f32)
    ffn_shard = gather_places(reduce_deep(reduce_square(total.astype(bf16))))
    dqkv = jnp.concatenate([dq, dk, dv], 1)
    qkv_part = (
        jnp.dot(x_seq.T, dqkv, preferred_element_type=f32)
        .astype(bf16)
        .reshape(depth, turns, shares, slim, 3, padded)[..., :part]
    )
    got = jnp.stack(
        [send(pick(qkv_part, (my_share + s) % shares, 2), 0, 0, s) for s in range(shares)]
    )
    got = jnp.stack([pick(got, (my_share - s) % shares) for s in range(shares)], 4)
    got = got.reshape(depth, turns, slim, 3, halves, half_width)
    square = jnp.stack(
        [
            pick(pick(got, (my_half - h) % halves, 4), (my_turn - t) % turns, 1)
            for h, t in spots
        ]
    ).reshape(len(spots), depth, slim, 3 * half_width)
    qkv_shard = gather_places(reduce_deep(reduce_square(square))).reshape(thin, 3, half_width)
    back = jnp.dot(dqkv, w_qkv.T, preferred_element_type=f32).reshape(shares, rows, width)
    back_own = back[0]
    for s in range(1, shares):
        back_own = back_own + send(back[s].astype(bf16), 0, 0, -s).astype(f32)
    input_grad = deliver((g_first + back_own).astype(bf16)).astype(f32)

    sums = lambda value: jnp.sum(value.astype(f32), 0)
    valid = live[:rows].astype(f32)
    squares = lambda member: jnp.sum(valid * jnp.sum(member * member, -1))
    stats = jnp.stack(
        [squares(m) for m in (x_full, first_sum, second_sum, attn_out, ffn_out)]
        + [jnp.sum(valid), 0.0, 0.0]
    )
    up_sums = sums(g_pre)
    norm_sums = [
        sums(g_attn), gain_one_grad, shift_one_grad, sums(g_ffn), gain_two_grad, shift_two_grad
    ]
    return finish(
        layer_out, input_grad, qkv_shard, ffn_shard, up_sums, group_at, norm_sums, stats,
        sums(dq)[:part], sums(dv)[:part],
    )


def solution(mesh):
    rows, plain = P("dp", "context", None), P()
    columns, across, halves = P("dp", "tensor"), P("tensor", "dp"), P("tensor")
    return jax.shard_map(
        local,
        mesh=mesh,
        in_specs=(
            rows, rows, P("dp", None), P("dp", None), P("dp", None, None),
            columns, halves, columns, columns, halves, across, plain, plain, plain,
            columns, halves, across, plain, plain, plain,
        ),
        out_specs=(
            rows, rows, columns, halves, columns, columns, halves, across, plain,
            plain, plain, columns, halves, across, plain, plain, plain, plain,
        ),
        check_vma=False,
    )
```

```python
import jax
import jax.numpy as jnp
from jax import lax
from jax.experimental import pallas as pl
from jax.experimental.pallas import tpu as pltpu
from jax.sharding import PartitionSpec as P

HD = 64
BLK = 64
PAIR = 128
SLOTS = 8
WIDE = 512
SCALE = HD ** (-0.5)
EPSILON = 1e-06


NEG_FILL = -1e30


def pair_rows(block, left, scale=None):
    if scale is not None:
        block = block * jnp.asarray(scale, block.dtype)
    zero = jnp.zeros_like(block)
    return jnp.concatenate([jnp.where(left, block, zero), jnp.where(left, zero, block)], 0)


def lane_left(rows):
    return lax.broadcasted_iota(jnp.int32, (rows, PAIR), 1) < HD


def eye_pair():
    lanes = lax.broadcasted_iota(jnp.int32, (BLK, PAIR), 1)
    rows = lax.broadcasted_iota(jnp.int32, (BLK, PAIR), 0)
    return rows == lanes % BLK


def block_rows(index):
    return pl.ds(pl.multiple_of(index * BLK, BLK), BLK)


def slot_bias(table, row, key_code, query_code, own):
    pieces = []
    for slot in range(SLOTS):
        code = query_code
        if slot == 0:
            code = jnp.where(table[row, 9] == 1, query_code, -2)
        if slot == 2:
            code = jnp.where(table[row, 10] == 1, query_code, -2)
        same = key_code[block_rows(table[row, 1 + slot]), :] == code
        if slot == 1:
            same = same | own
        pieces.append(jnp.where(same, 0.0, NEG_FILL))
    return jnp.concatenate(pieces, 0)


def slot_rows(ref, table, row, lanes):
    return jnp.concatenate(
        [ref[block_rows(table[row, 1 + slot]), lanes] for slot in range(SLOTS)], 0
    )


def wide_bias(key_code, query_code, block, chunk):
    start = pl.multiple_of(chunk * WIDE, WIDE)
    same = key_code[pl.ds(start, WIDE), :] == query_code
    key_pos = start + lax.broadcasted_iota(jnp.int32, (WIDE, PAIR), 0)
    query_pos = block * BLK + lax.broadcasted_iota(jnp.int32, (WIDE, PAIR), 1) % BLK
    return jnp.where(same | (key_pos == query_pos), 0.0, NEG_FILL)


def dot_nt(left, right):
    return lax.dot_general(
        left, right, (((1,), (1,)), ((), ())), preferred_element_type=jnp.float32
    )


def dot_tn(left, right):
    return lax.dot_general(
        left, right, (((0,), (0,)), ((), ())), preferred_element_type=jnp.float32
    )


def dot_nn(left, right):
    return jnp.dot(left, right, preferred_element_type=jnp.float32)


def attend_kernel(table, wide, q_ref, k_ref, v_ref, key_code, query_code, o_ref, lse_ref, acc):
    length, width = q_ref.shape
    pairs = width // PAIR
    left = lane_left(BLK)
    own = eye_pair()

    def narrow(row, carry):
        block = table[row, 0]
        rows = block_rows(block)
        bias = slot_bias(table, row, key_code, query_code[pl.ds(block, 1), :], own)
        for pair in range(pairs):
            lanes = slice(pair * PAIR, (pair + 1) * PAIR)
            query = pair_rows(q_ref[rows, lanes], left, SCALE)
            scores = dot_nt(slot_rows(k_ref, table, row, lanes), query) + bias
            top = jnp.max(scores, 0, keepdims=True)
            weight = jnp.exp(scores - top)
            total = jnp.sum(weight, 0, keepdims=True)
            probs = (weight * (1.0 / total)).astype(jnp.bfloat16)
            lse_ref[block, pl.ds(pair, 1), :] = top + jnp.log(total)
            both = dot_tn(probs, slot_rows(v_ref, table, row, lanes))
            o_ref[rows, lanes] = jnp.where(left, both[:BLK], both[BLK:]).astype(o_ref.dtype)
        return carry

    lax.fori_loop(0, table.shape[0], narrow, 0)

    for which in range(2):
        block = wide[which]
        rows = block_rows(block)
        code = query_code[pl.ds(block, 1), :]

        def first(chunk, carry):
            bias = wide_bias(key_code, code, block, chunk)
            keys = pl.ds(pl.multiple_of(chunk * WIDE, WIDE), WIDE)
            out = []
            for pair in range(pairs):
                lanes = slice(pair * PAIR, (pair + 1) * PAIR)
                query = pair_rows(q_ref[rows, lanes], left, SCALE)
                scores = dot_nt(k_ref[keys, lanes], query) + bias
                top_old, total_old = carry[pair]
                top = jnp.maximum(top_old, jnp.max(scores, 0, keepdims=True))
                total = total_old * jnp.exp(top_old - top) + jnp.sum(
                    jnp.exp(scores - top), 0, keepdims=True
                )
                out.append((top, total))
            return tuple(out)

        start = (jnp.full((1, PAIR), NEG_FILL), jnp.zeros((1, PAIR), jnp.float32))
        ends = lax.fori_loop(0, length // WIDE, first, (start,) * pairs)
        for pair in range(pairs):
            lse_ref[block, pl.ds(pair, 1), :] = ends[pair][0] + jnp.log(ends[pair][1])
        acc[...] = jnp.zeros_like(acc)

        def second(chunk, carry):
            bias = wide_bias(key_code, code, block, chunk)
            keys = pl.ds(pl.multiple_of(chunk * WIDE, WIDE), WIDE)
            for pair in range(pairs):
                lanes = slice(pair * PAIR, (pair + 1) * PAIR)
                query = pair_rows(q_ref[rows, lanes], left, SCALE)
                scores = dot_nt(k_ref[keys, lanes], query) + bias
                probs = jnp.exp(scores - lse_ref[block, pl.ds(pair, 1), :]).astype(jnp.bfloat16)
                acc[pair] += dot_tn(probs, v_ref[keys, lanes])
            return carry

        lax.fori_loop(0, length // WIDE, second, 0)
        for pair in range(pairs):
            lanes = slice(pair * PAIR, (pair + 1) * PAIR)
            both = acc[pair]
            o_ref[rows, lanes] = jnp.where(left, both[:BLK], both[BLK:]).astype(o_ref.dtype)


def attend_back_kernel(
    table, wide, q_ref, k_ref, v_ref, do_ref, key_code, query_code, lse_ref,
    dq_ref, dk_ref, dv_ref, dk_sum, dv_sum, dq_acc,
):
    length, width = q_ref.shape
    pairs = width // PAIR
    left = lane_left(BLK)
    own = eye_pair()
    dk_sum[...] = jnp.zeros_like(dk_sum)
    dv_sum[...] = jnp.zeros_like(dv_sum)

    def narrow(row, carry):
        block = table[row, 0]
        rows = block_rows(block)
        bias = slot_bias(table, row, key_code, query_code[pl.ds(block, 1), :], own)
        for pair in range(pairs):
            lanes = slice(pair * PAIR, (pair + 1) * PAIR)
            query = pair_rows(q_ref[rows, lanes], left, SCALE)
            grad = pair_rows(do_ref[rows, lanes], left)
            keys = slot_rows(k_ref, table, row, lanes)
            values = slot_rows(v_ref, table, row, lanes)
            scores = dot_nt(keys, query) + bias
            probs = jnp.exp(scores - lse_ref[block, pl.ds(pair, 1), :])
            g_probs = dot_nt(values, grad)
            terms = probs * g_probs
            g_scores = (terms - probs * jnp.sum(terms, 0, keepdims=True)).astype(jnp.bfloat16)
            dv = dot_nn(probs.astype(jnp.bfloat16), grad)
            dk = dot_nn(g_scores, query)
            both = dot_tn(g_scores, keys)
            dq_ref[rows, lanes] = (jnp.where(left, both[:BLK], both[BLK:]) * SCALE).astype(
                dq_ref.dtype
            )
            for slot in range(SLOTS):
                spot = block_rows(table[row, 1 + slot])
                part = slice(slot * BLK, (slot + 1) * BLK)
                dk_sum[spot, lanes] += dk[part]
                dv_sum[spot, lanes] += dv[part]
        return carry

    lax.fori_loop(0, table.shape[0], narrow, 0)

    for which in range(2):
        block = wide[which]
        rows = block_rows(block)
        code = query_code[pl.ds(block, 1), :]

        def pieces(chunk, pair, bias):
            keys_at = pl.ds(pl.multiple_of(chunk * WIDE, WIDE), WIDE)
            lanes = slice(pair * PAIR, (pair + 1) * PAIR)
            query = pair_rows(q_ref[rows, lanes], left, SCALE)
            grad = pair_rows(do_ref[rows, lanes], left)
            keys = k_ref[keys_at, lanes]
            scores = dot_nt(keys, query) + bias
            probs = jnp.exp(scores - lse_ref[block, pl.ds(pair, 1), :])
            return keys_at, lanes, query, grad, keys, probs, probs * dot_nt(v_ref[keys_at, lanes], grad)

        def first(chunk, carry):
            bias = wide_bias(key_code, code, block, chunk)
            return tuple(
                carry[pair] + jnp.sum(pieces(chunk, pair, bias)[-1], 0, keepdims=True)
                for pair in range(pairs)
            )

        deltas = lax.fori_loop(
            0, length // WIDE, first, (jnp.zeros((1, PAIR), jnp.float32),) * pairs
        )
        dq_acc[...] = jnp.zeros_like(dq_acc)

        def second(chunk, carry):
            bias = wide_bias(key_code, code, block, chunk)
            for pair in range(pairs):
                keys_at, lanes, query, grad, keys, probs, terms = pieces(chunk, pair, bias)
                g_scores = (terms - probs * carry[pair]).astype(jnp.bfloat16)
                dv_sum[keys_at, lanes] += dot_nn(probs.astype(jnp.bfloat16), grad)
                dk_sum[keys_at, lanes] += dot_nn(g_scores, query)
                dq_acc[pair] += dot_tn(g_scores, keys)
            return carry

        lax.fori_loop(0, length // WIDE, second, deltas)
        for pair in range(pairs):
            lanes = slice(pair * PAIR, (pair + 1) * PAIR)
            both = dq_acc[pair]
            dq_ref[rows, lanes] = (jnp.where(left, both[:BLK], both[BLK:]) * SCALE).astype(
                dq_ref.dtype
            )
    dk_ref[...] = dk_sum[...].astype(dk_ref.dtype)
    dv_ref[...] = dv_sum[...].astype(dv_ref.dtype)


VMEM_SPEC = pl.BlockSpec(memory_space=pltpu.VMEM)
SMEM_SPEC = pl.BlockSpec(memory_space=pltpu.SMEM)
ROOM = pltpu.CompilerParams(vmem_limit_bytes=60 * 1024 * 1024)


def attend(table, wide, q, k, v, key_code, query_code):
    length, width = q.shape
    return pl.pallas_call(
        attend_kernel,
        out_shape=(
            jax.ShapeDtypeStruct((length, width), jnp.bfloat16),
            jax.ShapeDtypeStruct((length // BLK, 8, PAIR), jnp.float32),
        ),
        in_specs=[SMEM_SPEC] * 2 + [VMEM_SPEC] * 5,
        out_specs=(VMEM_SPEC, VMEM_SPEC),
        scratch_shapes=[pltpu.VMEM((width // PAIR, PAIR, PAIR), jnp.float32)],
        compiler_params=ROOM,
        cost_estimate=pl.CostEstimate(
            flops=length * width * 1024 * 60, bytes_accessed=length * width * 8,
            transcendentals=length * width * 8,
        ),
        name="attend",
    )(table, wide, q, k, v, key_code, query_code)


def attend_back(table, wide, q, k, v, do, key_code, query_code, lse):
    length, width = q.shape
    shape = jax.ShapeDtypeStruct((length, width), jnp.bfloat16)
    return pl.pallas_call(
        attend_back_kernel,
        out_shape=(shape, shape, shape),
        in_specs=[SMEM_SPEC] * 2 + [VMEM_SPEC] * 7,
        out_specs=(VMEM_SPEC,) * 3,
        scratch_shapes=[
            pltpu.VMEM((length, width), jnp.float32),
            pltpu.VMEM((length, width), jnp.float32),
            pltpu.VMEM((width // PAIR, PAIR, PAIR), jnp.float32),
        ],
        compiler_params=ROOM,
        cost_estimate=pl.CostEstimate(
            flops=length * width * 1024 * 70, bytes_accessed=length * width * 14,
            transcendentals=length * width * 8,
        ),
        name="attend_back",
    )(table, wide, q, k, v, do, key_code, query_code, lse)


GROUPS = 8
DUOS = GROUPS // 2
TILE = 256
ANY_SPEC = pl.BlockSpec(memory_space=pl.ANY)
DMA = pltpu.SemaphoreType.DMA
WIDE_ROOM = pltpu.CompilerParams(vmem_limit_bytes=63 * 1024 * 1024)


def normalize(values):
    row_mean = jnp.mean(values, -1, keepdims=True)
    centered = values - row_mean
    row_var = jnp.mean(centered * centered, -1, keepdims=True)
    inverse = lax.rsqrt(row_var + EPSILON)
    return centered * inverse, inverse


def normalize_back(grad, unit, inverse):
    return inverse * (
        grad
        - jnp.mean(grad, -1, keepdims=True)
        - unit * jnp.mean(grad * unit, -1, keepdims=True)
    )


def gelu_both(u):
    root = 0.7978845608028654
    square = u * u
    inner = jnp.tanh(u * (root + (root * 0.044715) * square))
    half = 0.5 + 0.5 * inner
    slope = half + u * (0.5 - 0.5 * (inner * inner)) * (root + (3.0 * root * 0.044715) * square)
    return u * half, slope


def start_copies(pairs, sem):
    copies = [pltpu.make_async_copy(src, dst, sem.at[i]) for i, (src, dst) in enumerate(pairs)]
    for copy in copies:
        copy.start()
    return copies


def wait_copies(copies):
    for copy in copies:
        copy.wait()


def my_spot():
    place = lax.axis_index("context")
    return lax.axis_index("tensor"), place // 2, place % 2


def group_homes():
    half, turn, share = my_spot()
    return [
        ((half + h) % 2, ((turn + t) % 2) * 2 + (share + s) % 2)
        for s in range(2)
        for h in range(2)
        for t in range(2)
    ]


def lanes_of(g, cols):
    return pl.ds((g % 2) * cols, cols)


def project_attend_kernel(
    table, wide, hidden, x_in, q_all, b_qkv, key_code, query_code,
    own_ref, other_ref, q_home, k_home, v_home, w_home, lse_ref,
    x_v, q_v, k_v, v_v, o_v, w_v, acc, in_sem, out_sem, w_sem,
):
    span = hidden.shape[1]
    length, width = q_v.shape
    half, turn, share = my_spot()
    weights = start_copies(
        [(q_all.at[share, t, s], w_v.at[:, t, s]) for t in range(2) for s in range(2)], w_sem
    )
    chunks = [hidden.at[half * 2 + turn]] + [x_in.at[i] for i in range(3)]
    loads = start_copies(
        [(x, x_v.at[pl.ds(i * span, span)]) for i, x in enumerate(chunks)], in_sem
    )
    wait_copies(weights)
    w_qkv = w_v[...].reshape(x_v.shape[1], 3 * width)
    for i in range(4):
        loads[i].wait()
        at = pl.ds(i * span, span)
        value = (dot_nn(x_v[at, :], w_qkv) + b_qkv[...]).astype(jnp.bfloat16)
        q_v[at, :] = value[:, :width]
        k_v[at, :] = value[:, width : 2 * width]
        v_v[at, :] = value[:, 2 * width :]
    stores = start_copies([(q_v, q_home), (k_v, k_home), (v_v, v_home), (w_v, w_home)], out_sem)
    attend_kernel(table, wide, q_v, k_v, v_v, key_code, query_code, o_v, lse_ref, acc)
    own_ref[...] = o_v[: length // 2, :]
    other_ref[...] = o_v[length // 2 :, :]
    wait_copies(stores)


def project_attend(table, wide, hidden, x_in, q_all, b_qkv, key_code, query_code):
    span, features = hidden.shape[1:]
    length = 4 * span
    depth, slim, cols = q_all.shape[3:]
    width = cols // 3
    bf16, shape = jnp.bfloat16, jax.ShapeDtypeStruct
    outs = pl.pallas_call(
        project_attend_kernel,
        out_shape=(shape((length // 2, width), bf16),) * 2
        + (shape((length, width), bf16),) * 3
        + (
            shape((depth, 2, 2, slim, cols), bf16),
            shape((length // BLK, 8, PAIR), jnp.float32),
        ),
        in_specs=[SMEM_SPEC] * 2 + [ANY_SPEC] * 3 + [VMEM_SPEC] * 3,
        out_specs=(VMEM_SPEC,) * 2 + (ANY_SPEC,) * 4 + (VMEM_SPEC,),
        scratch_shapes=[pltpu.VMEM((length, features), bf16)]
        + [pltpu.VMEM((length, width), bf16)] * 4
        + [
            pltpu.VMEM((depth, 2, 2, slim, cols), bf16),
            pltpu.VMEM((width // PAIR, PAIR, PAIR), jnp.float32),
            DMA((4,)), DMA((4,)), DMA((4,)),
        ],
        compiler_params=WIDE_ROOM,
        cost_estimate=pl.CostEstimate(
            flops=length * width * 1024 * 65, bytes_accessed=length * width * 16,
            transcendentals=length * width * 8,
        ),
        name="project_attend",
    )(table, wide, hidden, x_in, q_all, b_qkv, key_code, query_code)
    att0, att1, q, k, v, w_qkv, lse = outs
    return att0, att1, q, k, v, lse, w_qkv.reshape(features, cols)


def attend_grad_kernel(
    table, wide, do0, do1, q_in, k_in, v_in, key_code, query_code, lse_ref,
    d_ref, sums,
    q_v, k_v, v_v, do_v, dk_sum, dv_sum, acc, in_sem,
):
    f32 = jnp.float32
    length, width = q_v.shape
    half_length = length // 2
    loads = start_copies(
        [
            (q_in, q_v), (k_in, k_v), (v_in, v_v),
            (do0, do_v.at[pl.ds(0, half_length)]),
            (do1, do_v.at[pl.ds(half_length, half_length)]),
        ],
        in_sem,
    )
    wait_copies(loads)
    parts = [d_ref.at[:, pl.ds(i * width, width)] for i in range(3)]
    attend_back_kernel(
        table, wide, q_v, k_v, v_v, do_v, key_code, query_code, lse_ref,
        *parts, dk_sum, dv_sum, acc,
    )
    share = my_spot()[2]
    sums[...] = jnp.zeros_like(sums)
    for s in range(2):

        @pl.when(share == s)
        def _():
            lanes = slice(s * width, (s + 1) * width)
            sums[0:1, lanes] = jnp.sum(d_ref[:, :width].astype(f32), 0, keepdims=True)
            sums[1:2, lanes] = jnp.sum(d_ref[:, 2 * width :].astype(f32), 0, keepdims=True)


def attend_grad(table, wide, do0, do1, q, k, v, key_code, query_code, lse):
    length, width = q.shape
    f32, bf16, shape = jnp.float32, jnp.bfloat16, jax.ShapeDtypeStruct
    return pl.pallas_call(
        attend_grad_kernel,
        out_shape=(shape((length, 3 * width), bf16), shape((8, 2 * width), f32)),
        in_specs=[SMEM_SPEC] * 2 + [ANY_SPEC] * 5 + [VMEM_SPEC] * 3,
        out_specs=(VMEM_SPEC,) * 2,
        scratch_shapes=[pltpu.VMEM((length, width), bf16)] * 4
        + [pltpu.VMEM((length, width), f32)] * 2
        + [pltpu.VMEM((width // PAIR, PAIR, PAIR), f32), DMA((5,))],
        compiler_params=WIDE_ROOM,
        cost_estimate=pl.CostEstimate(
            flops=length * width * 1024 * 75, bytes_accessed=length * width * 30,
            transcendentals=length * width * 8,
        ),
        name="attend_grad",
    )(table, wide, do0, do1, q, k, v, key_code, query_code, lse)


def load_weights(groups, w_up, w_dn, w_out, up_sem, dn_sem, wo_sem):
    depth, deep, cols = groups[0].shape
    thin = w_up.shape[2]
    slim = deep - 2 * thin
    homes = group_homes()
    out_loads = []
    for g in range(GROUPS):
        half, at = homes[g]
        for d in range(depth):
            spot = pl.ds(pl.multiple_of(d * thin + at * slim, 16), slim)
            out_loads.append(
                pltpu.make_async_copy(
                    groups[g].at[d, pl.ds(2 * thin, slim)], w_out.at[half, spot], wo_sem.at[g, d]
                )
            )
    up_loads = [
        pltpu.make_async_copy(
            groups[g].at[:, pl.ds(0, thin)], w_up.at[g // 2, :, :, lanes_of(g, cols)], up_sem.at[g]
        )
        for g in range(GROUPS)
    ]
    dn_loads = [
        pltpu.make_async_copy(
            groups[g].at[:, pl.ds(thin, thin)],
            w_dn.at[g // 2, :, :, lanes_of(g, cols)],
            dn_sem.at[g],
        )
        for g in range(GROUPS)
    ]
    return out_loads, up_loads, dn_loads


def whole(ref, g):
    depth, thin, cols = ref.shape[1:]
    return ref[g].reshape(depth * thin, cols)


def ffn_front_kernel(att0, att1, hidden, x_in, g_all, g_in, *rest):
    groups = rest[:GROUPS]
    (
        valid, vectors, b_up,
        out0_home, out1_home, slope_home, g_second_home, unit_home, norm_t_home, near_ref, far_ref,
        inverse_ref, sums,
        att_v, x_v, g_v, w_up, w_dn, w_out, act, slope, normed_low,
        out_v, g_second_v, unit_v, norm_t, g_ffn_t, stage,
        in_sem, up_sem, dn_sem, wo_sem, stage_sem, home_sem, end_sem,
    ) = rest[GROUPS:]
    f32, bf16 = jnp.float32, jnp.bfloat16
    rows, width = x_v.shape
    span = hidden.shape[1]
    depth, deep, cols = groups[0].shape
    half, turn, share = my_spot()
    x_chunks = (hidden.at[half * 2 + turn], x_in.at[0])
    g_chunks = (g_all.at[half * 2 + turn], g_in)
    other = (share + 1) % 2
    out_loads, up_loads, dn_loads = load_weights(groups, w_up, w_dn, w_out, up_sem, dn_sem, wo_sem)
    loads = start_copies(
        [(a, att_v.at[:, lanes_of(i, cols)]) for i, a in enumerate((att0, att1))]
        + [(x, x_v.at[pl.ds(i * span, span)]) for i, x in enumerate(x_chunks)]
        + [(g, g_v.at[pl.ds(i * span, span)]) for i, g in enumerate(g_chunks)],
        in_sem,
    )
    for copy in out_loads + up_loads + dn_loads:
        copy.start()
    sums[...] = jnp.zeros_like(sums)
    wait_copies(loads + out_loads)
    b_out, gain1, shift1, b_down, gain2, shift2 = (vectors[i : i + 1, :] for i in range(6))

    def add_sum(index, value):
        sums[index : index + 1, :] += jnp.sum(value, 0, keepdims=True)

    def homes(tile):
        at = pl.ds(pl.multiple_of(tile * TILE, TILE), TILE)
        return [
            pltpu.make_async_copy(src, dst, home_sem.at[i, tile])
            for i, (src, dst) in enumerate(
                [
                    (slope.at[:, at], slope_home.at[:, at]),
                    (g_second_v.at[at], g_second_home.at[at]),
                    (unit_v.at[at], unit_home.at[at]),
                ]
            )
        ]

    def tile_step(tile, carry):
        at = pl.ds(pl.multiple_of(tile * TILE, TILE), TILE)
        live = valid[at, :]
        attn = b_out + dot_nt(att_v[at, :], jnp.concatenate([w_out[share], w_out[other]], 1))
        x = x_v[at, :].astype(f32)
        first = x + attn
        add_sum(6, live * (x * x))
        add_sum(7, live * (first * first))
        add_sum(9, live * (attn * attn))
        unit1, inverse1 = normalize(first)
        unit_v[at, :] = unit1
        inverse_ref[at, :] = inverse1
        normed = unit1 * gain1 + shift1
        low = normed.astype(bf16)
        normed_low[...] = low
        norm_t[:, at] = low.T

        @pl.when(tile == 0)
        def _():
            wait_copies(up_loads + dn_loads)

        def up_step(g, ffn):
            pre = dot_nn(normed_low[...], whole(w_up, g)) + b_up[pl.ds(g, 1), :]
            value, rise = gelu_both(pre)
            value = value.astype(bf16)
            act[g, at, :] = value
            slope[g, at, :] = rise.astype(bf16)
            return ffn + dot_nt(value, whole(w_dn, g))

        ffn = lax.fori_loop(0, DUOS, up_step, jnp.broadcast_to(b_down, (TILE, width)))
        second = normed + ffn
        add_sum(8, live * (second * second))
        add_sum(10, live * (ffn * ffn))
        unit2, inverse2 = normalize(second)
        out_v[at, :] = (unit2 * gain2 + shift2).astype(bf16)
        g_out = g_v[at, :].astype(f32)
        add_sum(4, g_out * unit2)
        add_sum(5, g_out)
        g_second = normalize_back(g_out * gain2, unit2, inverse2)
        g_second_v[at, :] = g_second
        g_ffn = g_second.astype(bf16)
        add_sum(3, g_ffn.astype(f32))
        g_ffn_t[:, at] = g_ffn.T
        for copy in homes(tile):
            copy.start()
        return carry

    lax.fori_loop(0, rows // TILE, tile_step, 0)
    last = start_copies(
        [
            (norm_t, norm_t_home),
            (out_v.at[pl.ds(0, span)], out0_home),
            (out_v.at[pl.ds(span, span)], out1_home),
        ],
        end_sem,
    )
    stores = [None] * GROUPS
    for duo in range(DUOS):
        down = dot_nn(g_ffn_t[...], act[duo]).astype(bf16).reshape(depth, -1, 2 * cols)
        for g in (2 * duo, 2 * duo + 1):
            slot = g % 4
            if g >= 4:
                stores[g - 4].wait()
            stage[slot] = down[:, :, (g % 2) * cols : (g % 2 + 1) * cols]
            home = near_ref.at[g] if g < DUOS else far_ref.at[g - DUOS]
            stores[g] = pltpu.make_async_copy(stage.at[slot], home, stage_sem.at[slot])
            stores[g].start()
    for tile in range(rows // TILE):
        wait_copies(homes(tile))
    wait_copies(stores[-4:] + last)


def ffn_front(att0, att1, hidden, x_in, g_all, g_in, groups, valid, vectors, b_up):
    rows, part = att0.shape
    width = hidden.shape[2]
    depth, deep, cols = groups[0].shape
    thin = width // depth
    f32, bf16, shape = jnp.float32, jnp.bfloat16, jax.ShapeDtypeStruct
    grads = shape((DUOS, depth, thin, cols), bf16)
    weights = pltpu.VMEM((DUOS, depth, thin, 2 * cols), bf16)
    flat = pltpu.VMEM((rows, width), bf16)
    tall = pltpu.VMEM((rows, width), f32)
    deep_rows = pltpu.VMEM((DUOS, rows, 2 * cols), bf16)
    turned = pltpu.VMEM((width, rows), bf16)
    return pl.pallas_call(
        ffn_front_kernel,
        out_shape=(
            shape((rows // 2, width), bf16), shape((rows // 2, width), bf16),
            shape((DUOS, rows, 2 * cols), bf16),
            shape((rows, width), f32), shape((rows, width), f32), shape((width, rows), bf16),
            grads, grads, shape((rows, 1), f32), shape((16, width), f32),
        ),
        in_specs=[ANY_SPEC] * (6 + GROUPS) + [VMEM_SPEC] * 3,
        out_specs=(ANY_SPEC,) * 8 + (VMEM_SPEC,) * 2,
        scratch_shapes=[
            flat, flat, flat, weights, weights, pltpu.VMEM((2, width, part), bf16),
            deep_rows, deep_rows, pltpu.VMEM((TILE, width), bf16),
            flat, tall, tall, turned, turned, pltpu.VMEM((4, depth, thin, cols), bf16),
            DMA((6,)), DMA((GROUPS,)), DMA((GROUPS,)), DMA((GROUPS, depth)), DMA((4,)),
            DMA((3, rows // TILE)), DMA((3,)),
        ],
        compiler_params=WIDE_ROOM,
        cost_estimate=pl.CostEstimate(
            flops=38 * 10**9, bytes_accessed=40 * 10**6, transcendentals=rows * GROUPS * cols
        ),
        name="ffn_front",
    )(att0, att1, hidden, x_in, g_all, g_in, *groups, valid, vectors, b_up)


def ffn_rear_kernel(att0, att1, slope_in, g_second_in, unit_in, norm_t_in, *rest):
    groups = rest[:GROUPS]
    (
        inverse_ref, vectors,
        g_first_home, g_att0_home, g_att1_home, near_ref, far_ref, sums, up_sums,
        att_v, slope, g_second_v, unit_v, norm_t, w_up, w_dn, w_out, g_pre,
        g_first_v, g_att_v, g_attn_t, stage,
        in_sem, up_sem, dn_sem, wo_sem, stage_sem, home_sem,
    ) = rest[GROUPS:]
    f32, bf16 = jnp.float32, jnp.bfloat16
    rows, width = unit_v.shape
    depth, deep, cols = groups[0].shape
    thin = w_up.shape[2]
    slim = deep - 2 * thin
    half, turn, share = my_spot()
    other = (share + 1) % 2
    out_loads, up_loads, dn_loads = load_weights(groups, w_up, w_dn, w_out, up_sem, dn_sem, wo_sem)
    wait_order = [
        pltpu.make_async_copy(src, dst, in_sem.at[i])
        for i, (src, dst) in enumerate(
            [
                (g_second_in, g_second_v), (slope_in, slope), (unit_in, unit_v),
                (norm_t_in, norm_t), (att0, att_v.at[:, lanes_of(0, cols)]),
                (att1, att_v.at[:, lanes_of(1, cols)]),
            ]
        )
    ]
    for copy in wait_order[:1] + dn_loads + wait_order[1:2] + up_loads + wait_order[2:3]:
        copy.start()
    for copy in out_loads + wait_order[3:]:
        copy.start()
    sums[...] = jnp.zeros_like(sums)
    up_sums[...] = jnp.zeros_like(up_sums)
    gain1 = vectors[1:2, :]
    wait_copies(wait_order[:1] + dn_loads + wait_order[1:2])
    out_weight = lambda: jnp.concatenate([w_out[share], w_out[other]], 1)

    def add_sum(index, value):
        sums[index : index + 1, :] += jnp.sum(value, 0, keepdims=True)

    def tile_step(tile, carry):
        at = pl.ds(pl.multiple_of(tile * TILE, TILE), TILE)

        @pl.when(tile == 0)
        def _():
            wait_copies(up_loads + wait_order[2:] + out_loads)

        g_second = g_second_v[at, :]
        g_ffn = g_second.astype(bf16)

        def back_step(g, total):
            grad = (dot_nn(g_ffn, whole(w_dn, g)) * slope[g, at, :].astype(f32)).astype(bf16)
            g_pre[g, at, :] = grad
            up_sums[pl.ds(g, 1), :] += jnp.sum(grad.astype(f32), 0, keepdims=True)
            return total + dot_nt(grad, whole(w_up, g))

        g_normed = lax.fori_loop(0, DUOS, back_step, g_second)
        unit1 = unit_v[at, :]
        add_sum(1, g_normed * unit1)
        add_sum(2, g_normed)
        g_first = normalize_back(g_normed * gain1, unit1, inverse_ref[at, :])
        g_first_v[at, :] = g_first
        g_attn = g_first.astype(bf16)
        add_sum(0, g_attn.astype(f32))
        g_attn_t[:, at] = g_attn.T
        g_att_v[at, :] = dot_nn(g_attn, out_weight()).astype(bf16)
        return carry

    lax.fori_loop(0, rows // TILE, tile_step, 0)
    homes = start_copies(
        [
            (g_att_v.at[:, lanes_of(0, cols)], g_att0_home),
            (g_att_v.at[:, lanes_of(1, cols)], g_att1_home),
            (g_first_v, g_first_home),
        ],
        home_sem,
    )
    both = dot_nn(g_attn_t[...], att_v[...]).astype(bf16)
    w_out[share] = both[:, :cols]
    w_out[other] = both[:, cols:]
    spots = group_homes()
    stores = [None] * GROUPS
    for duo in range(DUOS):
        up = dot_nn(norm_t[...], g_pre[duo]).astype(bf16).reshape(depth, thin, 2 * cols)
        for g in (2 * duo, 2 * duo + 1):
            slot = g % 4
            if g >= 4:
                stores[g - 4].wait()
            stage[slot, :, pl.ds(0, thin), :] = up[:, :, (g % 2) * cols : (g % 2 + 1) * cols]
            where, at = spots[g]
            for d in range(depth):
                spot = pl.ds(pl.multiple_of(d * thin + at * slim, 16), slim)
                stage[slot, d, pl.ds(thin, slim), :] = w_out[where, spot, :]
            home = near_ref.at[g] if g < DUOS else far_ref.at[g - DUOS]
            stores[g] = pltpu.make_async_copy(stage.at[slot], home, stage_sem.at[slot])
            stores[g].start()
    wait_copies(stores[-4:] + homes)


def ffn_rear(att0, att1, slope, g_second, unit, norm_t, groups, inverse, vectors):
    rows, part = att0.shape
    width = unit.shape[1]
    depth, deep, cols = groups[0].shape
    thin = width // depth
    f32, bf16, shape = jnp.float32, jnp.bfloat16, jax.ShapeDtypeStruct
    grads = shape((DUOS, depth, deep - thin, cols), bf16)
    weights = pltpu.VMEM((DUOS, depth, thin, 2 * cols), bf16)
    flat = pltpu.VMEM((rows, width), bf16)
    tall = pltpu.VMEM((rows, width), f32)
    deep_rows = pltpu.VMEM((DUOS, rows, 2 * cols), bf16)
    turned = pltpu.VMEM((width, rows), bf16)
    return pl.pallas_call(
        ffn_rear_kernel,
        out_shape=(
            shape((rows, width), f32), shape((rows, part), bf16), shape((rows, part), bf16),
            grads, grads, shape((16, width), f32), shape((DUOS, 2 * cols), f32),
        ),
        in_specs=[ANY_SPEC] * (6 + GROUPS) + [VMEM_SPEC] * 2,
        out_specs=(ANY_SPEC,) * 5 + (VMEM_SPEC,) * 2,
        scratch_shapes=[
            flat, deep_rows, tall, tall, turned, weights, weights,
            pltpu.VMEM((2, width, part), bf16), deep_rows, tall, flat, turned,
            pltpu.VMEM((4, depth, deep - thin, cols), bf16),
            DMA((6,)), DMA((GROUPS,)), DMA((GROUPS,)), DMA((GROUPS, depth)), DMA((4,)), DMA((3,)),
        ],
        compiler_params=WIDE_ROOM,
        cost_estimate=pl.CostEstimate(
            flops=38 * 10**9, bytes_accessed=40 * 10**6, transcendentals=0
        ),
        name="ffn_rear",
    )(att0, att1, slope, g_second, unit, norm_t, *groups, inverse, vectors)


def gather_chunks_kernel(c0, c1, c2, c3, home, held, ready, in_sem, out_sem):
    half, turn, share = my_spot()
    loads = start_copies([(c, held.at[i]) for i, c in enumerate((c0, c1, c2, c3))], in_sem)
    stores = []
    for i in range(4):
        loads[i].wait()
        ready[i] = held[i].astype(ready.dtype)
        at = ((half + i // 2) % 2) * 2 + (turn + i) % 2
        stores.append(pltpu.make_async_copy(ready.at[i], home.at[at], out_sem.at[i]))
        stores[i].start()
    wait_copies(stores)


def gather_chunks(chunks, dtype):
    span, width = chunks[0].shape
    return pl.pallas_call(
        gather_chunks_kernel,
        out_shape=jax.ShapeDtypeStruct((4, span, width), dtype),
        in_specs=[ANY_SPEC] * 4,
        out_specs=ANY_SPEC,
        scratch_shapes=[
            pltpu.VMEM((4, span, width), chunks[0].dtype), pltpu.VMEM((4, span, width), dtype),
            DMA((4,)), DMA((4,)),
        ],
        compiler_params=WIDE_ROOM,
        name="gather_chunks",
    )(*chunks)


MESH = pl.DeviceIdType.MESH
CUTS = 8
THIRDS = 3


def signal_all(devices):
    barrier = pltpu.get_barrier_semaphore()
    for device in devices:
        pl.semaphore_signal(barrier, inc=1, device_id=device, device_id_type=MESH)
    pl.semaphore_wait(barrier, len(devices))


def neighbours():
    half, turn, share = my_spot()
    return (
        {"tensor": (half + 1) % 2},
        {"context": ((turn + 1) % 2) * 2 + share},
        {"context": turn * 2 + (share + 1) % 2},
    )


def remote(src, dst, send_sem, recv_sem, device):
    return pltpu.make_async_remote_copy(
        src_ref=src, dst_ref=dst, send_sem=send_sem, recv_sem=recv_sem,
        device_id=device, device_id_type=MESH,
    )


def fetch_kernel(
    hidden, qkv, ffn, bias, x_out, q_all, f_deep, bias_out,
    own_sem, x_send, x_recv, z_send, z_recv, f_send, f_recv,
    h_send, h_recv, t_send, t_recv, c_send, c_recv, b_sem,
):
    half, turn, share = my_spot()
    deep = lax.axis_index("dp")
    depth = f_deep.shape[0]
    across, beside, partner = neighbours()
    up, down = {"dp": (deep + 1) % depth}, {"dp": (deep + depth - 1) % depth}
    signal_all([across, beside, partner, up, down])

    slot = lambda h, t, d: q_all.at[h, t, share, d]
    own = start_copies([(qkv, slot(half, turn, deep)), (ffn, f_deep.at[deep])], own_sem)

    def to_up(d):
        return remote(slot(half, turn, d), slot(half, turn, d), z_send.at[0, d], z_recv.at[d], up)

    def to_down(d):
        return remote(slot(half, turn, d), slot(half, turn, d), z_send.at[1, d], z_recv.at[d], down)

    third = f_deep.shape[1] // THIRDS

    def f_copies(d, side, device):
        return [
            remote(
                f_deep.at[d, pl.ds(i * third, third)], f_deep.at[d, pl.ds(i * third, third)],
                f_send.at[side, d, i], f_recv.at[d, i], device,
            )
            for i in range(THIRDS)
        ]

    f_up = lambda d: f_copies(d, 0, up)
    f_down = lambda d: f_copies(d, 1, down)

    def to_across(t, d):
        return remote(slot(half, t, d), slot(half, t, d), h_send.at[t, d], h_recv.at[t, d], across)

    def from_across(t, d):
        other = slot((half + 1) % 2, t, d)
        return remote(other, other, h_send.at[t, d], h_recv.at[t, d], across)

    def to_beside(d):
        return remote(slot(half, turn, d), slot(half, turn, d), t_send.at[d], t_recv.at[d], beside)

    def from_beside(d):
        other = slot(half, (turn + 1) % 2, d)
        return remote(other, other, t_send.at[d], t_recv.at[d], beside)

    def to_partner(t, d):
        piece = slot((share + 1) % 2, t, d)
        return remote(piece, piece, c_send.at[t, d], c_recv.at[t, d], partner)

    def from_partner(t, d):
        piece = q_all.at[share, t, (share + 1) % 2, d]
        return remote(piece, piece, c_send.at[t, d], c_recv.at[t, d], partner)

    cut = x_out.shape[1] // CUTS
    piece_rows = lambda i: pl.ds(i * cut, cut)
    x_next = [
        remote(
            hidden.at[half * 2 + (turn + 1) % 2, piece_rows(i)], x_out.at[0, piece_rows(i)],
            x_send.at[0, i], x_recv.at[0, i], beside,
        )
        for i in range(CUTS)
    ]
    x_mine = remote(
        hidden.at[half * 2 + turn], x_out.at[1], x_send.at[1, 0], x_recv.at[1, 0], partner
    )
    x_relay = [
        remote(
            x_out.at[0, piece_rows(i)], x_out.at[2, piece_rows(i)],
            x_send.at[2, i], x_recv.at[2, i], partner,
        )
        for i in range(CUTS)
    ]
    bias_copy = remote(bias, bias_out, b_sem.at[0], b_sem.at[1], across)
    wait_copies(own)
    own_turn = (share + 1) % 2 == half

    def spread_own(d):
        to_across(turn, d).start()
        to_beside(d).start()

        @pl.when(own_turn)
        def _():
            to_partner(turn, d).start()

    def when(condition, *copies):
        @pl.when(condition)
        def _():
            for copy in copies:
                copy.start()

    when(deep < depth - 1, to_up(deep))
    when(deep > 0, to_down(deep))
    when(deep < depth - 1, f_up(deep)[0])
    when(deep > 0, f_down(deep)[0])
    spread_own(deep)
    x_next[0].start()
    bias_copy.start()
    x_mine.start()
    for k in range(1, depth):
        low, high = (deep + depth - k) % depth, (deep + k) % depth

        @pl.when(deep >= k)
        def _():
            to_up(low).wait_recv()
            when(deep < depth - 1, to_up(low))
            spread_own(low)

        @pl.when(deep + k < depth)
        def _():
            to_down(high).wait_recv()
            when(deep > 0, to_down(high))
            spread_own(high)

        if k < THIRDS:
            when(deep < depth - 1, f_up(deep)[k])
            when(deep > 0, f_down(deep)[k])
        x_next[k].start()

    for i in range(depth, THIRDS):
        when(deep < depth - 1, f_up(deep)[i])
        when(deep > 0, f_down(deep)[i])
    for copy in x_next[depth:]:
        copy.start()
    for k in range(depth):
        d = (deep + k) % depth
        from_beside(d).wait_recv()
        to_across((turn + 1) % 2, d).start()

        @pl.when(own_turn)
        def _():
            to_partner((turn + 1) % 2, d).start()

    def f_step(k):
        low, high = (deep + depth - k) % depth, (deep + k) % depth

        @pl.when(deep >= k)
        def _():
            for copy in f_up(low):
                copy.wait_recv()
                when(deep < depth - 1, copy)

        @pl.when(deep + k < depth)
        def _():
            for copy in f_down(high):
                copy.wait_recv()
                when(deep > 0, copy)

    def x_step(step):
        for i in range(step * CUTS // (depth + 1), (step + 1) * CUTS // (depth + 1)):
            x_next[i].wait_recv()
            x_relay[i].start()

    f_step(1)
    for step, t in enumerate((turn, (turn + 1) % 2)):
        for k in range(depth):
            d = (deep + k) % depth
            from_across(t, d).wait_recv()

            @pl.when(jnp.logical_not(own_turn))
            def _():
                to_partner(t, d).start()

        x_step(step)
        if step == 0 and depth > 2:
            f_step(2)
    for k in range(3, depth):
        x_step(k - 1)
        f_step(k)
    for step in range(max(2, depth - 1), depth + 1):
        x_step(step)

    for t in range(2):
        for d in range(depth):
            from_partner(t, d).wait_recv()
    x_mine.wait_recv()
    bias_copy.wait_recv()
    for copy in x_relay:
        copy.wait_recv()
    for d in range(depth):
        for copy in (to_across(0, d), to_across(1, d), to_beside(d), to_partner(0, d), to_partner(1, d)):
            copy.wait_send()

        @pl.when(jnp.logical_and(deep < depth - 1, deep >= d))
        def _():
            for copy in [to_up(d)] + f_up(d):
                copy.wait_send()

        @pl.when(jnp.logical_and(deep > 0, deep <= d))
        def _():
            for copy in [to_down(d)] + f_down(d):
                copy.wait_send()

    for copy in x_next + x_relay + [x_mine, bias_copy]:
        copy.wait_send()


def fetch(hidden_in, qkv_piece, ffn_piece, bias, depth):
    span, width = hidden_in.shape[1:]
    bf16, shape = jnp.bfloat16, jax.ShapeDtypeStruct
    pair = DMA((2, depth))
    return pl.pallas_call(
        fetch_kernel,
        out_shape=(
            shape((3, span, width), bf16),
            shape((2, 2, 2, depth) + qkv_piece.shape, bf16),
            shape((depth,) + ffn_piece.shape, bf16),
            shape(bias.shape, bf16),
        ),
        in_specs=[ANY_SPEC] + [VMEM_SPEC] * 3,
        out_specs=(ANY_SPEC,) * 3 + (VMEM_SPEC,),
        scratch_shapes=[
            DMA((2,)), DMA((3, CUTS)), DMA((3, CUTS)), pair, DMA((depth,)),
            DMA((2, depth, THIRDS)), DMA((depth, THIRDS)),
            pair, pair, DMA((depth,)), DMA((depth,)), pair, pair, DMA((2,)),
        ],
        compiler_params=pltpu.CompilerParams(collective_id=0, has_side_effects=True),
        cost_estimate=pl.CostEstimate(
            flops=30 * 10**9, bytes_accessed=10 * 10**6, transcendentals=0
        ),
        name="fetch",
    )(hidden_in, qkv_piece, ffn_piece, bias)


SUBS = 4


def settle_kernel(hidden, x_in, dqkv, w_qkv, g_first, small, *rest):
    f32, bf16 = jnp.float32, jnp.bfloat16
    parts_dn, parts_uo = rest[:4], rest[4:8]
    (
        out, qkv_out, dn_out, uo_out, small_out,
        x_v, d_v, w_v, first_v, dn_v, uo_v, small_v, small_got,
        back_v, got_v, fin_v, land_v, tot_dn, tot_uo, zdn_v, zuo_v, fdn_v, fuo_v,
        grad_v, swap_v, pq_v, yl_v, xs_v, xl_v, rs_v, zq_v, qf_v,
        in_sem, out_sem, send_sem, recv_sem,
    ) = rest[8:]
    half, turn, share = my_spot()
    deep = lax.axis_index("dp")
    depth = tot_dn.shape[0]
    span = hidden.shape[1]
    sub = span // SUBS
    other = (share + 1) % 2
    far_half, far_turn = (half + 1) % 2, (turn + 1) % 2
    across, beside, partner = neighbours()
    deeps = [{"dp": (deep + k) % depth} for k in range(1, depth)]
    ids = iter(range(send_sem.shape[0]))
    started = []

    def link(src, dst, device):
        i = next(ids)
        copy = remote(src, dst, send_sem.at[i], recv_sem.at[i], device)
        started.append(copy)
        return copy

    def go(src, dst, device):
        copy = link(src, dst, device)
        copy.start()
        return copy

    chunk = lambda i: pl.ds(i * span, span)
    chunks = [hidden.at[half * 2 + turn]] + [x_in.at[i] for i in range(3)]
    loads = [
        pltpu.make_async_copy(src, dst, in_sem.at[i])
        for i, (src, dst) in enumerate(
            [(w_qkv, w_v)]
            + [(dqkv.at[chunk(i)], d_v.at[chunk(i)]) for i in (2, 3, 0, 1)]
            + [(p, dn_v.at[i]) for i, p in enumerate(parts_dn)]
            + [(p, uo_v.at[i]) for i, p in enumerate(parts_uo)]
            + [(g_first, first_v)]
            + [(c, x_v.at[chunk(i)]) for i, c in enumerate(chunks)]
        )
    ]
    for copy in loads:
        copy.start()
    signal_all([across, beside, partner] + deeps)
    small_v[...] = small[...]
    s0 = go(small, small_got.at[0], partner)

    wait_copies(loads[:3])
    back = []
    for i in range(2):
        back_v[i] = dot_nt(d_v[chunk(2 + i), :], w_v[...]).astype(bf16)
        back.append(go(back_v.at[i], got_v.at[i], partner))
    wait_copies(loads[3:13])
    total = lambda ref: (
        (ref[0].astype(f32) + ref[1].astype(f32)) + (ref[2].astype(f32) + ref[3].astype(f32))
    ).astype(bf16)
    tot_dn[...] = total(dn_v)
    tot_uo[...] = total(uo_v)
    wait_copies(loads[13:14])
    z_dn, z_uo, outs = [], [], []
    for k, device in enumerate(deeps):
        to = (deep + k + 1) % depth
        z_dn.append(go(tot_dn.at[to], zdn_v.at[k], device))
        z_uo.append(go(tot_uo.at[to], zuo_v.at[k], device))

    def own_back(i):
        value = dot_nt(d_v[chunk(i), :], w_v[...]) + first_v[chunk(i), :]
        back[i].wait_recv()
        fin_v[i] = (value + got_v[i].astype(f32)).astype(bf16)

    rows = lambda j: pl.ds(j * sub, sub)

    def put(ref, h, t):
        copy = pltpu.make_async_copy(ref, out.at[h * 2 + t], out_sem.at[len(outs)])
        copy.start()
        outs.append(copy)

    own_back(0)
    x_subs = [go(fin_v.at[0, rows(j)], land_v.at[1, rows(j)], across) for j in range(SUBS)]
    put(fin_v.at[0], half, turn)
    own_back(1)
    y_subs = [go(fin_v.at[1, rows(j)], land_v.at[0, rows(j)], beside) for j in range(SUBS // 2)]

    s0.wait_recv()
    s0.wait_send()
    small_v[...] += small_got[0]
    s1 = go(small_v, small_got.at[1], beside)
    wait_copies(loads[14:])
    grad_v[...] = dot_tn(x_v[...], d_v[...]).astype(bf16).reshape(grad_v.shape)
    swap_v[...] = grad_v[:, :, other]
    swap = go(swap_v, pq_v.at[share], partner)
    pq_v[share] = grad_v[:, :, share]
    s1.wait_recv()
    s1.wait_send()
    small_v[...] += small_got[1]
    s2 = go(small_v, small_got.at[2], across)
    swap.wait_recv()
    keep_v = lambda h, t: pq_v[h, :, t]
    q1 = go(pq_v.at[far_half, :, far_turn], yl_v.at[0], beside)
    q2 = go(pq_v.at[half, :, far_turn], yl_v.at[1], beside)
    y_subs += [
        go(fin_v.at[1, rows(j)], land_v.at[0, rows(j)], beside) for j in range(SUBS // 2, SUBS)
    ]
    s2.wait_recv()
    s2.wait_send()
    small_v[...] += small_got[2]
    s3 = [go(small_v, small_got.at[3 + k], device) for k, device in enumerate(deeps)]
    relays = []

    def relay(j):
        y_subs[j].wait_recv()
        relays.append(go(land_v.at[0, rows(j)], land_v.at[2, rows(j)], across))

    for j in range(SUBS // 2):
        relay(j)
    q1.wait_recv()
    xs_v[...] = (keep_v(far_half, turn).astype(f32) + yl_v[0].astype(f32)).astype(bf16)
    qx = go(xs_v, xl_v, across)

    for copy in z_dn + z_uo:
        copy.wait_recv()
    ranks = range(depth - 1)
    spread = lambda ref, got: sum([got[k].astype(f32) for k in ranks], ref[deep].astype(f32))
    fdn_v[turn, share] = spread(tot_dn, zdn_v).astype(bf16)
    fuo_v[turn, share] = spread(tot_uo, zuo_v).astype(bf16)

    def gather_first(ref):
        piece = ref.at[turn, share]
        return go(piece, piece, beside), go(piece, piece, partner)

    def gather_next(ref, first):
        first.wait_recv()
        piece = ref.at[far_turn, share]
        return go(piece, piece, partner)

    f_first = [gather_first(ref) for ref in (fdn_v, fuo_v)]
    q2.wait_recv()
    for j in range(SUBS // 2, SUBS):
        relay(j)
    qx.wait_recv()
    rs_v[...] = (
        keep_v(half, turn).astype(f32) + yl_v[1].astype(f32) + xl_v[...].astype(f32)
    ).astype(bf16)
    z_q = [
        go(rs_v.at[(deep + k + 1) % depth], zq_v.at[k], device) for k, device in enumerate(deeps)
    ]
    for copy in s3:
        copy.wait_recv()
    small_out[...] = small_v[...] + sum([small_got[4 + k] for k in range(depth - 2)], small_got[3])
    f_next = [gather_next(ref, first[0]) for ref, first in zip((fdn_v, fuo_v), f_first)]
    for copy in z_q:
        copy.wait_recv()
    qf_v[turn, share] = spread(rs_v, zq_v).astype(bf16)
    q_first = gather_first(qf_v)
    put(land_v.at[0], half, far_turn)
    for copy in x_subs:
        copy.wait_recv()
    put(land_v.at[1], far_half, turn)
    for first, copy in zip(f_first, f_next):
        first[1].wait_recv()
        copy.wait_recv()
    ends = start_copies([(fdn_v, dn_out), (fuo_v, uo_out)], in_sem)
    q_next = gather_next(qf_v, q_first[0])
    for copy in relays:
        copy.wait_recv()
    put(land_v.at[2], far_half, far_turn)
    q_first[1].wait_recv()
    q_next.wait_recv()
    last = pltpu.make_async_copy(qf_v, qkv_out, in_sem.at[2])
    last.start()
    wait_copies(ends + [last] + outs)
    waited = [s0, s1, s2]
    for copy in started:
        if not any(copy is w for w in waited):
            copy.wait_send()


def settle(hidden_in, x_in, dqkv, w_qkv, g_first, small, parts_dn, parts_uo):
    rows, width = g_first.shape
    span = hidden_in.shape[1]
    depth, thin, cols = parts_dn[0].shape
    mixed = parts_uo[0].shape[1]
    wide = dqkv.shape[1]
    slim = width // depth // 4
    f32, bf16, shape = jnp.float32, jnp.bfloat16, jax.ShapeDtypeStruct
    v = pltpu.VMEM
    count = 80
    return pl.pallas_call(
        settle_kernel,
        out_shape=(
            shape((4, span, width), bf16), shape((2, 2, slim, wide), bf16),
            shape((2, 2, thin, cols), bf16), shape((2, 2, mixed, cols), bf16),
            shape(small.shape, f32),
        ),
        in_specs=[ANY_SPEC] * 5 + [VMEM_SPEC] + [ANY_SPEC] * 8,
        out_specs=(ANY_SPEC,) * 4 + (VMEM_SPEC,),
        scratch_shapes=[
            v((2 * rows, width), bf16), v((2 * rows, wide), bf16), v((width, wide), bf16),
            v((rows, width), f32), v((4, depth, thin, cols), bf16),
            v((4, depth, mixed, cols), bf16), v(small.shape, f32),
            v((2 + depth,) + small.shape, f32),
            v((2, span, width), bf16), v((2, span, width), bf16), v((2, span, width), bf16),
            v((3, span, width), bf16),
            v((depth, thin, cols), bf16), v((depth, mixed, cols), bf16),
            v((depth - 1, thin, cols), bf16), v((depth - 1, mixed, cols), bf16),
            v((2, 2, thin, cols), bf16), v((2, 2, mixed, cols), bf16),
            v((depth, 2, 2, slim, wide), bf16), v((depth, 2, slim, wide), bf16),
            v((2, depth, 2, slim, wide), bf16), v((2, depth, slim, wide), bf16),
            v((depth, slim, wide), bf16), v((depth, slim, wide), bf16),
            v((depth, slim, wide), bf16), v((depth - 1, slim, wide), bf16),
            v((2, 2, slim, wide), bf16),
            DMA((20,)), DMA((4,)), DMA((count,)), DMA((count,)),
        ],
        compiler_params=pltpu.CompilerParams(
            vmem_limit_bytes=63 * 1024 * 1024, collective_id=1, has_side_effects=True
        ),
        cost_estimate=pl.CostEstimate(
            flops=60 * 10**9, bytes_accessed=30 * 10**6, transcendentals=0
        ),
        name="settle",
    )(hidden_in, x_in, dqkv, w_qkv, g_first, small, *parts_dn, *parts_uo)


def layer_norm(values, norm_gain, norm_shift):
    row_mean = jnp.mean(values, -1, keepdims=True)
    centered = values - row_mean
    row_var = jnp.mean(centered * centered, -1, keepdims=True)
    return centered * lax.rsqrt(row_var + EPSILON) * norm_gain + norm_shift


def gelu_tanh(values):
    return jax.nn.gelu(values, approximate=True)


def block_tables(random_seq, all_blocks, place):
    block = jnp.arange(2, all_blocks, dtype=jnp.int32)
    last = all_blocks - 1
    zero = jnp.zeros_like(block)
    true_ids = jnp.stack(
        [block, block - 1, block, jnp.minimum(block + 1, last), zero, zero + 1], -1
    )
    true_ids = jnp.concatenate([true_ids, random_seq[2:]], -1)
    flags = jnp.stack([block >= 3, block <= last - 1], -1).astype(jnp.int32)
    return (
        jnp.concatenate([place(true_ids), flags], -1).astype(jnp.int32),
        place(jnp.arange(2, dtype=jnp.int32)),
    )


def local(
    hidden_in, out_grad, segment_ids, token_valid, random_blocks,
    query_weight, query_bias, key_weight, value_weight, value_bias,
    output_weight, output_bias, norm1_gain, norm1_shift,
    up_weight, up_bias, down_weight, down_bias, norm2_gain, norm2_shift,
):
    f32, bf16 = jnp.float32, jnp.bfloat16
    seqs, span, width = hidden_in.shape
    length = segment_ids.shape[1]
    places = length // span
    halves = lax.axis_size("tensor")
    depth = lax.axis_size("dp")
    turns = seqs // halves
    shares = places // turns
    my_half = lax.axis_index("tensor")
    my_place = lax.axis_index("context")
    my_depth = lax.axis_index("dp")
    my_turn, my_share = my_place // shares, my_place % shares
    my_seq = my_half * turns + my_turn
    blocks = length // BLK
    rows = turns * span
    spots = [(h, t) for h in range(halves) for t in range(turns)]

    def send(value, half=0, turn=0, share=0):
        if half % halves == 0 and turn % turns == 0 and share % shares == 0:
            return value
        pairs = []
        for h in range(halves):
            for t in range(turns):
                for s in range(shares):
                    to_place = (t + turn) % turns * shares + (s + share) % shares
                    pairs.append(
                        ((t * shares + s) * halves + h, to_place * halves + (h + half) % halves)
                    )
        return lax.ppermute(value, ("context", "tensor"), pairs)

    def send_deep(value, step):
        return lax.ppermute(value, "dp", [(i, (i + step) % depth) for i in range(depth)])

    def pick(value, index, axis=0):
        return lax.dynamic_index_in_dim(value, index, axis, keepdims=False)

    def own_slice(value, count, which, axis):
        size = value.shape[axis] // count
        return lax.dynamic_slice_in_dim(value, which * size, size, axis)

    def gather_deep(value):
        if depth > 4:
            return lax.all_gather(value, "dp", axis=0)
        got = [value] + [send_deep(value, k) for k in range(1, depth)]
        ring = jnp.stack([got[depth - 1 - i % depth] for i in range(2 * depth - 1)])
        return lax.dynamic_slice_in_dim(ring, depth - 1 - my_depth, depth, 0)

    def reduce_deep(value):
        if depth > 4:
            return lax.psum_scatter(value, "dp", scatter_dimension=0)
        total = pick(value, my_depth).astype(f32)
        for k in range(1, depth):
            total = total + send_deep(pick(value, (my_depth + k) % depth), k).astype(f32)
        return total.astype(bf16)

    def gather_square(value):
        near = {spot: send(value, *spot) for spot in spots}
        near = jnp.stack([near[spot] for spot in spots])
        return [near] + [send(near, 0, 0, s) for s in range(1, shares)]

    def reduce_square(value):
        total = value[0].astype(f32)
        for i, (h, t) in enumerate(spots[1:], 1):
            total = total + send(value[i], -h, -t).astype(f32)
        return total.astype(bf16)

    def gather_places(value):
        near = [send(value, 0, t) for t in range(turns)]
        near = jnp.stack(near)
        far = jnp.stack([near] + [send(near, 0, 0, s) for s in range(1, shares)])
        return jnp.stack(
            [
                pick(pick(far, (my_share - s) % shares), (my_turn - t) % turns)
                for t in range(turns)
                for s in range(shares)
            ]
        )

    def sum_all(value):
        for step in range(halves.bit_length() - 1):
            value = value + send(value, 1 << step)
        size = 1
        while size < places:
            value = value + lax.ppermute(value, "context", [(i, i ^ size) for i in range(places)])
            size *= 2
        size = 1
        while size < depth:
            value = value + lax.ppermute(value, "dp", [(i, i ^ size) for i in range(depth)])
            size *= 2
        return value

    def bring(value):
        return jnp.concatenate(
            [
                send(pick(value, my_half * turns + (my_turn + k) % turns), 0, k)
                for k in range(turns)
            ],
            0,
        )

    def deliver(value):
        value = value.reshape(turns, span, width)
        got = jnp.stack([send(value[t], h, -t) for h, t in spots])
        return jnp.stack(
            [
                pick(got, (my_half - h) % halves * turns + (t - my_turn) % turns)
                for h in range(halves)
                for t in range(turns)
            ]
        )

    def after(value, *earlier):
        return lax.optimization_barrier((value, *earlier))[0]

    per = span // BLK

    def place(block_ids):
        chunk = block_ids // per
        turn, share = chunk // shares, chunk % shares
        spot = ((my_share - share) % shares) * turns + (my_turn - turn) % turns
        return spot * per + block_ids % per

    def in_order(row):
        return jnp.concatenate(
            [
                lax.dynamic_slice_in_dim(
                    row,
                    (((my_turn - k) % turns) * shares + (my_share - s) % shares) * span,
                    span,
                )
                for s in range(shares)
                for k in range(turns)
            ]
        )

    seg = in_order(pick(segment_ids, my_seq))
    live = in_order(pick(token_valid, my_seq))
    random_seq = pick(random_blocks, my_seq)
    table, wide = block_tables(random_seq, blocks, place)
    key_code = jnp.broadcast_to(jnp.where(live == 1, seg, -1)[:, None], (length, PAIR))
    query_code = jnp.tile(seg.reshape(blocks, BLK), (1, PAIR // BLK))
    half_width = query_weight.shape[1]
    thin = query_weight.shape[0]
    slim = thin // places
    hidden = up_weight.shape[1] // places
    biases = jnp.concatenate([query_bias, value_bias, up_bias])

    def split_biases(by_half):
        by_half = jnp.stack([pick(by_half, (my_half - h) % halves) for h in range(halves)])
        return (
            by_half[:, at : at + b.shape[0]].reshape(-1)
            for b, at in ((query_bias, 0), (value_bias, half_width), (up_bias, 2 * half_width))
        )

    def spread(value, which, count):
        return lax.dynamic_update_slice_in_dim(
            jnp.zeros((value.shape[0] * count,), value.dtype), value, which * value.shape[0], 0
        )

    def small_rows(up_sums, group_at, norm_sums, stats):
        up_natural = jnp.zeros_like(up_sums)
        for i, at in enumerate(group_at):
            up_natural = lax.dynamic_update_slice_in_dim(
                up_natural, up_sums[i * hidden : (i + 1) * hidden], at * hidden, 0
            )
        stats = jnp.pad(stats, (0, width - stats.shape[0]))
        return jnp.concatenate(
            [up_natural.reshape(-1, width), *(row[None] for row in norm_sums), stats[None]], 0
        )

    def finish(layer_out, input_grad, qkv_shard, up_part, down_part, out_part, small):
        deep = up_weight.shape[1] * halves // width
        s_up, (s_o, s_g1, s_s1, s_down, s_g2, s_s2, stats, s_q, s_v) = (
            small[:deep].reshape(-1), small[deep : deep + 9]
        )
        s_q, s_v, s_up = (own_slice(value, halves, my_half, 0) for value in (s_q, s_v, s_up))
        input_rms = jnp.sqrt(stats[:5] / (jnp.maximum(stats[5], 1.0) * width))
        join = lambda w: jnp.moveaxis(w, 0, 1).reshape(thin, -1).astype(f32)
        shard_o = out_part.reshape(thin, -1)[:, :half_width].astype(f32).T
        shard_q, shard_k, shard_v = (qkv_shard[:, i].astype(f32) for i in range(3))
        return (
            layer_out, input_grad, shard_q, s_q, shard_k, shard_v, s_v, shard_o, s_o,
            s_g1, s_s1, join(up_part), s_up, join(down_part).T, s_down, s_g2, s_s2, input_rms,
        )

    if (turns, shares, halves) == (2, 2, 2) and depth <= 4 and rows % TILE == 0:
        qkv_piece = own_slice(
            jnp.concatenate([query_weight, key_weight, value_weight], 1), places, my_place, 0
        )
        ffn_piece = jnp.concatenate(
            [
                own_slice(up_weight, places, my_place, 1),
                own_slice(down_weight, places, my_place, 0).T,
                own_slice(output_weight.T, places, my_place, 0),
            ],
            0,
        )
        x_in, q_all, ffn_deep, far_biases = fetch(
            hidden_in, qkv_piece, ffn_piece, jnp.broadcast_to(biases, (8,) + biases.shape), depth
        )
        b_q, b_v, b_up = split_biases(jnp.stack([biases, far_biases[0]]))
        own_bias = lambda b: own_slice(b, shares, my_share, 0)
        b_qkv = jnp.concatenate([own_bias(b_q), jnp.zeros((half_width,), bf16), own_bias(b_v)])
        b_qkv = b_qkv.astype(f32)[None]
        g_next = pick(out_grad, my_half * turns + (my_turn + 1) % turns)
        g_own = send(after(g_next, ffn_deep), 0, 1)
        near = [send(ffn_deep, *spot) for spot in spots]
        group_at = [
            (
                (my_half - h) % halves * places
                + (my_turn - t) % turns * shares
                + (my_share - s) % shares
            )
            for s in range(shares)
            for h, t in spots
        ]
        b_up = jnp.concatenate(
            [lax.dynamic_slice_in_dim(b_up, at * hidden, hidden) for at in group_at]
        ).astype(f32)

        att0, att1, q, k, v, lse, w_qkv = project_attend(
            table, wide, hidden_in, x_in, q_all, b_qkv, key_code, query_code
        )
        att0, att1, near, g_own = lax.optimization_barrier((att0, att1, near, g_own))
        att1 = send(att1, 0, 0, 1)
        groups = near + [send(g, 0, 0, 1) for g in near]
        vectors = jnp.stack(
            [output_bias, norm1_gain, norm1_shift, down_bias, norm2_gain, norm2_shift]
        ).astype(f32)
        (
            out0, out1, slope, g_second, unit, norm_t, near_dn, far_dn, inverse, front_sums
        ) = ffn_front(
            att0, att1, hidden_in, x_in, out_grad, g_own, groups,
            live[:rows, None].astype(f32), vectors,
            b_up.reshape(DUOS, -1),
        )
        out_chunks = [out0, send(out1, 0, 1), send(out0, 1), send(out1, 1, 1)]
        got_dn = send(far_dn, 0, 0, 1)
        g_first, g_att0, g_att1, near_uo, far_uo, rear_sums, up_sums = ffn_rear(
            att0, att1, slope, g_second, unit, norm_t, groups, inverse, vectors
        )
        out_chunks, got_dn, g_first, g_att0, g_att1, near_uo, far_uo = lax.optimization_barrier(
            (out_chunks, got_dn, g_first, g_att0, g_att1, near_uo, far_uo)
        )
        got_uo = send(far_uo, 0, 0, 1)
        g_att1 = send(g_att1, 0, 0, 1)
        total_dn = (near_dn.astype(f32) + got_dn.astype(f32)).astype(bf16)
        total_uo = (near_uo.astype(f32) + got_uo.astype(f32)).astype(bf16)
        parts_dn = [send(total_dn[i], *spots[i]) for i in range(len(spots))]
        parts_uo = [send(total_uo[i], *spots[i]) for i in range(len(spots))]
        g_att1 = after(g_att1, total_dn, total_uo)
        dqkv, head_sums = attend_grad(
            table, wide, g_att0, g_att1, q, k, v, key_code, query_code, lse
        )
        dqkv, head_sums, parts_dn, parts_uo = lax.optimization_barrier(
            (dqkv, head_sums, parts_dn, parts_uo)
        )
        norm_sums = [rear_sums[0], rear_sums[1], rear_sums[2]] + [front_sums[i] for i in (3, 4, 5)]
        stats = jnp.concatenate(
            [jnp.sum(front_sums[6:11], 1), jnp.sum(live[:rows]).astype(f32)[None]]
        )
        small = small_rows(up_sums.reshape(-1), group_at, norm_sums, stats)
        small = jnp.concatenate([small, head_sums], 0)
        small = jnp.pad(small, ((0, -small.shape[0] % 8), (0, 0)))
        input_grad, qkv_shard, down_part, mixed_part, small = settle(
            hidden_in, x_in, dqkv, w_qkv, g_first, small, parts_dn, parts_uo
        )
        ranked = lambda w: w.reshape((places,) + w.shape[2:])
        down_part, mixed_part = ranked(down_part), ranked(mixed_part)
        return finish(
            gather_chunks(out_chunks, bf16), input_grad.astype(f32),
            qkv_shard.reshape(thin, 3, half_width), mixed_part[:, :thin], down_part,
            mixed_part[:, thin:], small,
        )

    part = width // shares
    padded = -(-part // PAIR) * PAIR
    x_own = bring(hidden_in)
    qkv_piece = own_slice(
        jnp.concatenate([query_weight, key_weight, value_weight], 1), places, my_place, 0
    )
    qkv_all = jnp.stack(gather_square(gather_deep(qkv_piece)))
    per_half = shares // halves
    target = my_share // per_half
    qkv_all = jnp.stack(
        [
            pick(
                pick(qkv_all, (my_share - s) % shares),
                (my_half - target) % halves * turns + (my_turn - t) % turns,
            )
            for t in range(turns)
            for s in range(shares)
        ],
        1,
    ).reshape(width, 3, half_width)
    pad_cols = lambda w: jnp.pad(w, [(0, 0)] * (w.ndim - 1) + [(0, padded - part)])
    mine = lambda w: pad_cols(own_slice(w, per_half, my_share % per_half, w.ndim - 1))
    w_qkv = mine(qkv_all).reshape(width, 3 * padded)
    b_q, b_v, b_up = split_biases(jnp.stack([send(biases, h) for h in range(halves)]))
    mine_b = lambda b: pad_cols(own_slice(b, shares, my_share, 0))
    b_qkv = jnp.concatenate([mine_b(b_q), jnp.zeros((padded,), bf16), mine_b(b_v)]).astype(f32)

    ffn_piece = jnp.concatenate(
        [
            own_slice(up_weight, places, my_place, 1),
            own_slice(down_weight, places, my_place, 0).T,
            jnp.pad(
                own_slice(output_weight.T, places, my_place, 0),
                [(0, 0), (0, max(0, hidden - half_width))],
            ).reshape(-1, hidden),
        ],
        0,
    )
    ffn_all = gather_square(gather_deep(ffn_piece))
    groups = [
        (s, i, ffn_all[s][i]) for s in range(shares) for i in range(len(spots))
    ]
    w_up = jnp.concatenate([g[:, :thin].reshape(width, hidden) for _, _, g in groups], 1)
    w_down_t = jnp.concatenate(
        [g[:, thin : 2 * thin].reshape(width, hidden) for _, _, g in groups], 1
    )
    out_all = jnp.stack(
        [jnp.stack([g[:, 2 * thin :] for g in ffn_all[s]]) for s in range(shares)]
    )
    w_out_t = jnp.stack(
        [
            jnp.stack(
                [
                    pick(
                        pick(out_all, (my_share - s) % shares),
                        (my_half - h) % halves * turns + (my_turn - t) % turns,
                    )
                    for t in range(turns)
                    for s in range(shares)
                ],
                1,
            ).reshape(width, half_width)
            for h in range(halves)
        ],
        1,
    ).reshape(width, width)
    w_out_t = jnp.concatenate(
        [own_slice(w_out_t, shares, (my_share + k) % shares, 1) for k in range(shares)], 1
    )
    group_at = [
        ((my_half - spots[i][0]) % halves * places
         + (my_turn - spots[i][1]) % turns * shares + (my_share - s) % shares)
        for s, i, _ in groups
    ]
    b_up = jnp.concatenate(
        [lax.dynamic_slice_in_dim(b_up, at * hidden, hidden) for at in group_at]
    ).astype(f32)

    g_out = bring(out_grad).astype(f32)
    x_seq = jnp.concatenate([send(x_own, 0, 0, k) for k in range(shares)], 0)
    q, k, v = (
        (
            jnp.dot(x_seq, w_qkv[:, i * padded : (i + 1) * padded], preferred_element_type=f32)
            + b_qkv[i * padded : (i + 1) * padded]
        ).astype(bf16)
        for i in range(3)
    )
    att, lse = attend(table, wide, q, k, v, key_code, query_code)
    att = att[:, :part].reshape(shares, rows, part)
    att_own = jnp.concatenate([send(att[s], 0, 0, -s) for s in range(shares)], 1)
    attn_out = lax.dot_general(
        att_own, w_out_t, (((1,), (1,)), ((), ())), preferred_element_type=f32
    ) + output_bias.astype(f32)
    x_full = x_own.astype(f32)
    first_sum = x_full + attn_out
    gain_one, shift_one = norm1_gain.astype(f32), norm1_shift.astype(f32)
    normed = layer_norm(first_sum, gain_one, shift_one)
    normed_low = normed.astype(bf16)
    pre_act = jnp.dot(normed_low, w_up, preferred_element_type=f32) + b_up
    act_low = gelu_tanh(pre_act).astype(bf16)
    ffn_out = lax.dot_general(
        act_low, w_down_t, (((1,), (1,)), ((), ())), preferred_element_type=f32
    ) + down_bias.astype(f32)
    second_sum = normed + ffn_out
    gain_two, shift_two = norm2_gain.astype(f32), norm2_shift.astype(f32)
    layer_out, norm_back = jax.vjp(layer_norm, second_sum, gain_two, shift_two)
    g_second, gain_two_grad, shift_two_grad = norm_back(g_out)
    layer_out = deliver(layer_out.astype(bf16))
    g_ffn = g_second.astype(bf16)
    g_act = jnp.dot(g_ffn, w_down_t, preferred_element_type=f32)
    g_pre = jax.vjp(gelu_tanh, pre_act)[1](g_act)[0].astype(bf16)
    up_part = jnp.dot(normed_low.T, g_pre, preferred_element_type=f32).astype(bf16)
    down_part_t = jnp.dot(g_ffn.T, act_low, preferred_element_type=f32).astype(bf16)
    g_normed = g_second + jnp.dot(g_pre, w_up.T, preferred_element_type=f32)
    g_first, gain_one_grad, shift_one_grad = jax.vjp(layer_norm, first_sum, gain_one, shift_one)[1](
        g_normed
    )
    g_attn = g_first.astype(bf16)
    out_part_t = jnp.dot(g_attn.T, att_own, preferred_element_type=f32).astype(bf16)
    g_att = jnp.dot(g_attn, w_out_t, preferred_element_type=f32).astype(bf16)
    do = jnp.concatenate(
        [send(own_slice(g_att, shares, s, 1), 0, 0, s) for s in range(shares)], 0
    )
    dq, dk, dv = attend_back(table, wide, q, k, v, pad_cols(do), key_code, query_code, lse)

    out_natural = jnp.concatenate(
        [own_slice(out_part_t, shares, (s - my_share) % shares, 1) for s in range(shares)], 1
    ).reshape(depth, turns, shares, slim, halves, half_width)

    def ffn_group(s, i):
        h, t = spots[i]
        at = (s * len(spots) + i) * hidden
        out = pick(out_natural, (my_half - h) % halves, 4)
        out = pick(pick(out, (my_turn - t) % turns, 1), (my_share - s) % shares, 1)
        out = jnp.pad(out, [(0, 0), (0, 0), (0, max(0, hidden - half_width))])
        cut = lambda w: w[:, at : at + hidden].reshape(depth, thin, hidden)
        return jnp.concatenate(
            [cut(up_part), cut(down_part_t), out.reshape(depth, -1, hidden)], 1
        )

    ffn_grads = [
        jnp.stack([ffn_group(s, i) for i in range(len(spots))]) for s in range(shares)
    ]
    total = ffn_grads[0].astype(f32)
    for s in range(1, shares):
        total = total + send(ffn_grads[s], 0, 0, -s).astype(f32)
    ffn_shard = gather_places(reduce_deep(reduce_square(total.astype(bf16))))
    dqkv = jnp.concatenate([dq, dk, dv], 1)
    qkv_part = (
        jnp.dot(x_seq.T, dqkv, preferred_element_type=f32)
        .astype(bf16)
        .reshape(depth, turns, shares, slim, 3, padded)[..., :part]
    )
    got = jnp.stack(
        [send(pick(qkv_part, (my_share + s) % shares, 2), 0, 0, s) for s in range(shares)]
    )
    got = jnp.stack([pick(got, (my_share - s) % shares) for s in range(shares)], 4)
    got = got.reshape(depth, turns, slim, 3, halves, half_width)
    square = jnp.stack(
        [
            pick(pick(got, (my_half - h) % halves, 4), (my_turn - t) % turns, 1)
            for h, t in spots
        ]
    ).reshape(len(spots), depth, slim, 3 * half_width)
    qkv_shard = gather_places(reduce_deep(reduce_square(square))).reshape(thin, 3, half_width)
    back = jnp.dot(dqkv, w_qkv.T, preferred_element_type=f32).reshape(shares, rows, width)
    back_own = back[0]
    for s in range(1, shares):
        back_own = back_own + send(back[s].astype(bf16), 0, 0, -s).astype(f32)
    input_grad = deliver((g_first + back_own).astype(bf16)).astype(f32)

    sums = lambda value: jnp.sum(value.astype(f32), 0)
    valid = live[:rows].astype(f32)
    squares = lambda member: jnp.sum(valid * jnp.sum(member * member, -1))
    stats = jnp.stack(
        [squares(m) for m in (x_full, first_sum, second_sum, attn_out, ffn_out)]
        + [jnp.sum(valid), 0.0, 0.0]
    )
    up_sums = sums(g_pre)
    norm_sums = [
        sums(g_attn), gain_one_grad, shift_one_grad, sums(g_ffn), gain_two_grad, shift_two_grad
    ]
    small = small_rows(up_sums, group_at, norm_sums, stats)
    heads = [spread(sums(d)[:part], my_share, shares)[None] for d in (dq, dv)]
    small = sum_all(jnp.concatenate([small, *heads], 0))
    return finish(
        layer_out, input_grad, qkv_shard, ffn_shard[:, :thin], ffn_shard[:, thin : 2 * thin],
        ffn_shard[:, 2 * thin :], small,
    )


def solution(mesh):
    rows, plain = P("dp", "context", None), P()
    columns, across, halves = P("dp", "tensor"), P("tensor", "dp"), P("tensor")
    return jax.shard_map(
        local,
        mesh=mesh,
        in_specs=(
            rows, rows, P("dp", None), P("dp", None), P("dp", None, None),
            columns, halves, columns, columns, halves, across, plain, plain, plain,
            columns, halves, across, plain, plain, plain,
        ),
        out_specs=(
            rows, rows, columns, halves, columns, columns, halves, across, plain,
            plain, plain, columns, halves, across, plain, plain, plain, plain,
        ),
        check_vma=False,
    )
```

```python
import jax
import jax.numpy as jnp
from jax import lax
from jax.experimental import pallas as pl
from jax.experimental.pallas import tpu as pltpu
from jax.sharding import PartitionSpec as P

HD = 64
BLK = 64
PAIR = 128
SLOTS = 8
WIDE = 512
SCALE = HD ** (-0.5)
EPSILON = 1e-06


NEG_FILL = -1e30


def pair_rows(block, left, scale=None):
    if scale is not None:
        block = block * jnp.asarray(scale, block.dtype)
    zero = jnp.zeros_like(block)
    return jnp.concatenate([jnp.where(left, block, zero), jnp.where(left, zero, block)], 0)


def lane_left(rows):
    return lax.broadcasted_iota(jnp.int32, (rows, PAIR), 1) < HD


def eye_pair():
    lanes = lax.broadcasted_iota(jnp.int32, (BLK, PAIR), 1)
    rows = lax.broadcasted_iota(jnp.int32, (BLK, PAIR), 0)
    return rows == lanes % BLK


def block_rows(index):
    return pl.ds(pl.multiple_of(index * BLK, BLK), BLK)


def slot_bias(slots, first_ok, third_ok, key_code, query_code, own):
    pieces = []
    for slot in range(SLOTS):
        code = query_code
        if slot == 0:
            code = jnp.where(first_ok, query_code, -2)
        if slot == 2:
            code = jnp.where(third_ok, query_code, -2)
        same = key_code[slots[slot]] == code
        if slot == 1:
            same = same | own
        pieces.append(jnp.where(same, 0.0, NEG_FILL))
    return jnp.concatenate(pieces, 0)


def slot_rows(ref, slots, lanes):
    return jnp.concatenate([ref[slot, :, lanes] for slot in slots], 0)


def wide_rows(ref, chunk, lanes):
    count = WIDE // BLK
    return ref[pl.ds(chunk * count, count), :, lanes].reshape(WIDE, PAIR)


def listed(table):
    def find(row):
        slots = [table[row, 1 + slot] for slot in range(SLOTS)]
        return table[row, 0], slots, table[row, 9] == 1, table[row, 10] == 1

    return find


def wide_bias(key_code, query_code, block, chunk):
    same = wide_rows(key_code, chunk, slice(0, PAIR)) == query_code
    key_pos = chunk * WIDE + lax.broadcasted_iota(jnp.int32, (WIDE, PAIR), 0)
    query_pos = block * BLK + lax.broadcasted_iota(jnp.int32, (WIDE, PAIR), 1) % BLK
    return jnp.where(same | (key_pos == query_pos), 0.0, NEG_FILL)


def dot_nt(left, right):
    return lax.dot_general(
        left, right, (((1,), (1,)), ((), ())), preferred_element_type=jnp.float32
    )


def dot_tn(left, right):
    return lax.dot_general(
        left, right, (((0,), (0,)), ((), ())), preferred_element_type=jnp.float32
    )


def dot_nn(left, right):
    return jnp.dot(left, right, preferred_element_type=jnp.float32)


def attend_kernel(table, wide, *refs):
    attend_blocks(listed(table), [wide[0], wide[1]], [(0, table.shape[0], None)], *refs)


def attend_blocks(
    find, wide, legs, q_ref, k_ref, v_ref, key_code, query_code, o_ref, lse_ref, acc, pause=None
):
    length, width = q_ref.shape
    pairs = width // PAIR
    left = lane_left(BLK)
    own = eye_pair()

    def narrow(row, carry):
        block, slots, first_ok, third_ok = find(row)
        rows = block_rows(block)
        code = query_code[pl.ds(block, 1), :]
        bias = slot_bias(slots, first_ok, third_ok, key_code, code, own)
        for pair in range(pairs):
            lanes = slice(pair * PAIR, (pair + 1) * PAIR)
            query = pair_rows(q_ref[rows, lanes], left, SCALE)
            scores = dot_nt(slot_rows(k_ref, slots, lanes), query) + bias
            top = jnp.max(scores, 0, keepdims=True)
            weight = jnp.exp(scores - top)
            total = jnp.sum(weight, 0, keepdims=True)
            probs = (weight * (1.0 / total)).astype(jnp.bfloat16)
            lse_ref[block, pl.ds(pair, 1), :] = top + jnp.log(total)
            both = dot_tn(probs, slot_rows(v_ref, slots, lanes))
            o_ref[rows, lanes] = jnp.where(left, both[:BLK], both[BLK:]).astype(o_ref.dtype)
        return carry

    for start, stop, after in legs:
        lax.fori_loop(start, stop, narrow, 0)
        if after is not None:
            after()

    for which in range(2):
        block = wide[which]
        rows = block_rows(block)
        code = query_code[pl.ds(block, 1), :]

        def first(chunk, carry):
            bias = wide_bias(key_code, code, block, chunk)
            out = []
            for pair in range(pairs):
                lanes = slice(pair * PAIR, (pair + 1) * PAIR)
                query = pair_rows(q_ref[rows, lanes], left, SCALE)
                scores = dot_nt(wide_rows(k_ref, chunk, lanes), query) + bias
                top_old, total_old = carry[pair]
                top = jnp.maximum(top_old, jnp.max(scores, 0, keepdims=True))
                total = total_old * jnp.exp(top_old - top) + jnp.sum(
                    jnp.exp(scores - top), 0, keepdims=True
                )
                out.append((top, total))
            return tuple(out)

        start = (jnp.full((1, PAIR), NEG_FILL), jnp.zeros((1, PAIR), jnp.float32))
        ends = lax.fori_loop(0, length // WIDE, first, (start,) * pairs)
        for pair in range(pairs):
            lse_ref[block, pl.ds(pair, 1), :] = ends[pair][0] + jnp.log(ends[pair][1])
        if pause is not None:
            pause(2 * which)
        acc[...] = jnp.zeros_like(acc)

        def second(chunk, carry):
            bias = wide_bias(key_code, code, block, chunk)
            for pair in range(pairs):
                lanes = slice(pair * PAIR, (pair + 1) * PAIR)
                query = pair_rows(q_ref[rows, lanes], left, SCALE)
                scores = dot_nt(wide_rows(k_ref, chunk, lanes), query) + bias
                probs = jnp.exp(scores - lse_ref[block, pl.ds(pair, 1), :]).astype(jnp.bfloat16)
                acc[pair] += dot_tn(probs, wide_rows(v_ref, chunk, lanes))
            return carry

        lax.fori_loop(0, length // WIDE, second, 0)
        for pair in range(pairs):
            lanes = slice(pair * PAIR, (pair + 1) * PAIR)
            both = acc[pair]
            o_ref[rows, lanes] = jnp.where(left, both[:BLK], both[BLK:]).astype(o_ref.dtype)
        if pause is not None:
            pause(2 * which + 1)


def attend_back_kernel(table, wide, *refs):
    attend_back_blocks(listed(table), [wide[0], wide[1]], table.shape[0], *refs)


def attend_back_blocks(
    find, wide, count, q_ref, k_ref, v_ref, do_ref, key_code, query_code, lse_ref,
    dq_ref, dk_ref, dv_ref, dk_sum, dv_sum, dq_acc,
):
    length, width = q_ref.shape
    pairs = width // PAIR
    left = lane_left(BLK)
    own = eye_pair()
    dk_sum[...] = jnp.zeros_like(dk_sum)
    dv_sum[...] = jnp.zeros_like(dv_sum)

    def narrow(row, carry):
        block, slots, first_ok, third_ok = find(row)
        rows = block_rows(block)
        code = query_code[pl.ds(block, 1), :]
        bias = slot_bias(slots, first_ok, third_ok, key_code, code, own)
        for pair in range(pairs):
            lanes = slice(pair * PAIR, (pair + 1) * PAIR)
            query = pair_rows(q_ref[rows, lanes], left, SCALE)
            grad = pair_rows(do_ref[rows, lanes], left)
            keys = slot_rows(k_ref, slots, lanes)
            values = slot_rows(v_ref, slots, lanes)
            scores = dot_nt(keys, query) + bias
            probs = jnp.exp(scores - lse_ref[block, pl.ds(pair, 1), :])
            g_probs = dot_nt(values, grad)
            terms = probs * g_probs
            g_scores = (terms - probs * jnp.sum(terms, 0, keepdims=True)).astype(jnp.bfloat16)
            dv = dot_nn(probs.astype(jnp.bfloat16), grad)
            dk = dot_nn(g_scores, query)
            both = dot_tn(g_scores, keys)
            dq_ref[rows, lanes] = (jnp.where(left, both[:BLK], both[BLK:]) * SCALE).astype(
                dq_ref.dtype
            )
            for slot in range(SLOTS):
                spot = block_rows(slots[slot])
                part = slice(slot * BLK, (slot + 1) * BLK)
                dk_sum[spot, lanes] += dk[part]
                dv_sum[spot, lanes] += dv[part]
        return carry

    lax.fori_loop(0, count, narrow, 0)

    for which in range(2):
        block = wide[which]
        rows = block_rows(block)
        code = query_code[pl.ds(block, 1), :]

        def pieces(chunk, pair, bias):
            keys_at = pl.ds(pl.multiple_of(chunk * WIDE, WIDE), WIDE)
            lanes = slice(pair * PAIR, (pair + 1) * PAIR)
            query = pair_rows(q_ref[rows, lanes], left, SCALE)
            grad = pair_rows(do_ref[rows, lanes], left)
            keys = wide_rows(k_ref, chunk, lanes)
            scores = dot_nt(keys, query) + bias
            probs = jnp.exp(scores - lse_ref[block, pl.ds(pair, 1), :])
            return keys_at, lanes, query, grad, keys, probs, probs * dot_nt(wide_rows(v_ref, chunk, lanes), grad)

        def first(chunk, carry):
            bias = wide_bias(key_code, code, block, chunk)
            return tuple(
                carry[pair] + jnp.sum(pieces(chunk, pair, bias)[-1], 0, keepdims=True)
                for pair in range(pairs)
            )

        deltas = lax.fori_loop(
            0, length // WIDE, first, (jnp.zeros((1, PAIR), jnp.float32),) * pairs
        )
        dq_acc[...] = jnp.zeros_like(dq_acc)

        def second(chunk, carry):
            bias = wide_bias(key_code, code, block, chunk)
            for pair in range(pairs):
                keys_at, lanes, query, grad, keys, probs, terms = pieces(chunk, pair, bias)
                g_scores = (terms - probs * carry[pair]).astype(jnp.bfloat16)
                dv_sum[keys_at, lanes] += dot_nn(probs.astype(jnp.bfloat16), grad)
                dk_sum[keys_at, lanes] += dot_nn(g_scores, query)
                dq_acc[pair] += dot_tn(g_scores, keys)
            return carry

        lax.fori_loop(0, length // WIDE, second, deltas)
        for pair in range(pairs):
            lanes = slice(pair * PAIR, (pair + 1) * PAIR)
            both = dq_acc[pair]
            dq_ref[rows, lanes] = (jnp.where(left, both[:BLK], both[BLK:]) * SCALE).astype(
                dq_ref.dtype
            )
    dk_ref[...] = dk_sum[...].astype(dk_ref.dtype)
    dv_ref[...] = dv_sum[...].astype(dv_ref.dtype)


def in_blocks(rows):
    return rows.reshape(-1, BLK, rows.shape[-1])


VMEM_SPEC = pl.BlockSpec(memory_space=pltpu.VMEM)
SMEM_SPEC = pl.BlockSpec(memory_space=pltpu.SMEM)
ROOM = pltpu.CompilerParams(vmem_limit_bytes=60 * 1024 * 1024)


def attend(table, wide, q, k, v, key_code, query_code):
    length, width = q.shape
    return pl.pallas_call(
        attend_kernel,
        out_shape=(
            jax.ShapeDtypeStruct((length, width), jnp.bfloat16),
            jax.ShapeDtypeStruct((length // BLK, 8, PAIR), jnp.float32),
        ),
        in_specs=[SMEM_SPEC] * 2 + [VMEM_SPEC] * 5,
        out_specs=(VMEM_SPEC, VMEM_SPEC),
        scratch_shapes=[pltpu.VMEM((width // PAIR, PAIR, PAIR), jnp.float32)],
        compiler_params=ROOM,
        cost_estimate=pl.CostEstimate(
            flops=length * width * 1024 * 60, bytes_accessed=length * width * 8,
            transcendentals=length * width * 8,
        ),
        name="attend",
    )(table, wide, q, in_blocks(k), in_blocks(v), in_blocks(key_code), query_code)


def attend_back(table, wide, q, k, v, do, key_code, query_code, lse):
    length, width = q.shape
    shape = jax.ShapeDtypeStruct((length, width), jnp.bfloat16)
    return pl.pallas_call(
        attend_back_kernel,
        out_shape=(shape, shape, shape),
        in_specs=[SMEM_SPEC] * 2 + [VMEM_SPEC] * 7,
        out_specs=(VMEM_SPEC,) * 3,
        scratch_shapes=[
            pltpu.VMEM((length, width), jnp.float32),
            pltpu.VMEM((length, width), jnp.float32),
            pltpu.VMEM((width // PAIR, PAIR, PAIR), jnp.float32),
        ],
        compiler_params=ROOM,
        cost_estimate=pl.CostEstimate(
            flops=length * width * 1024 * 70, bytes_accessed=length * width * 14,
            transcendentals=length * width * 8,
        ),
        name="attend_back",
    )(table, wide, q, in_blocks(k), in_blocks(v), do, in_blocks(key_code), query_code, lse)


GROUPS = 8
DUOS = GROUPS // 2
TILE = 256
ANY_SPEC = pl.BlockSpec(memory_space=pl.ANY)
DMA = pltpu.SemaphoreType.DMA
WIDE_ROOM = pltpu.CompilerParams(vmem_limit_bytes=63 * 1024 * 1024)


def normalize(values):
    row_mean = jnp.mean(values, -1, keepdims=True)
    centered = values - row_mean
    row_var = jnp.mean(centered * centered, -1, keepdims=True)
    inverse = lax.rsqrt(row_var + EPSILON)
    return centered * inverse, inverse


def normalize_back(grad, unit, inverse):
    return inverse * (
        grad
        - jnp.mean(grad, -1, keepdims=True)
        - unit * jnp.mean(grad * unit, -1, keepdims=True)
    )


def gelu_both(u):
    root = 0.7978845608028654
    square = u * u
    inner = jnp.tanh(u * (root + (root * 0.044715) * square))
    half = 0.5 + 0.5 * inner
    slope = half + u * (0.5 - 0.5 * (inner * inner)) * (root + (3.0 * root * 0.044715) * square)
    return u * half, slope


def start_copies(pairs, sem):
    copies = [pltpu.make_async_copy(src, dst, sem.at[i]) for i, (src, dst) in enumerate(pairs)]
    for copy in copies:
        copy.start()
    return copies


def wait_copies(copies):
    for copy in copies:
        copy.wait()


def my_spot():
    place = lax.axis_index("context")
    return lax.axis_index("tensor"), place // 2, place % 2


def group_homes():
    half, turn, share = my_spot()
    return [
        ((half + h) % 2, ((turn + t) % 2) * 2 + (share + s) % 2)
        for s in range(2)
        for h in range(2)
        for t in range(2)
    ]


def lanes_of(g, cols):
    return pl.ds((g % 2) * cols, cols)


def place_block(block, per):
    half, turn, share = my_spot()
    chunk = block // per
    spot = ((share + chunk) % 2) * 2 + (turn + chunk // 2) % 2
    return spot * per + block % per


def computed(random, per, blocks):
    def find(row):
        block = row + 2
        ids = [block - 1, block, (block + 1) % blocks]
        slots = [place_block(i, per) for i in ids]
        slots += [place_block(jnp.int32(i), per) for i in range(2)]
        slots += [random[block * 3 + i] for i in range(3)]
        return slots[1], slots, block >= 3, block <= blocks - 2

    return find, [place_block(jnp.int32(i), per) for i in range(2)]


def write_codes(segments, live, key_code, query_code, span):
    half, turn, share = my_spot()
    row = pl.ds(half * 2 + turn, 1)
    left = lax.broadcasted_iota(jnp.int32, (1, PAIR), 1) < HD
    per = span // BLK
    for spot in range(4):
        chunk = ((turn + spot) % 2) * 2 + (share + spot // 2) % 2
        lanes = pl.ds(pl.multiple_of(chunk * span, span), span)
        seg = segments[row, lanes]
        code = jnp.where(live[row, lanes] == 1, seg, -1)
        key_code[pl.ds(spot * per, per)] = jnp.broadcast_to(code, (PAIR, span)).T.reshape(
            per, BLK, PAIR
        )
        for two in range(per // 2):
            both = seg[:, two * PAIR : (two + 1) * PAIR]
            turned = pltpu.roll(both, HD, 1)
            at = spot * per + 2 * two
            query_code[at : at + 1, :] = jnp.where(left, both, turned)
            query_code[at + 1 : at + 2, :] = jnp.where(left, turned, both)


def project_attend_kernel(
    random, hidden, x_in, q_all, g_all, f_deep, segments, live, b_q, b_v, far_q, far_v,
    own_ref, other_home, q_home, k_home, v_home, w_home, g_home,
    n1, n2, n3, f0, f1, f2, f3, lse_ref, key_code, query_code,
    x_v, q_v, k_v, v_v, o_v, w_v, acc, in_sem, out_sem, w_sem, send_sem, recv_sem,
):
    span = hidden.shape[1]
    length, width = q_v.shape
    depth = f_deep.shape[0]
    half, turn, share = my_spot()
    across, beside, partner = neighbours()
    weights = start_copies(
        [(q_all.at[share, t, s], w_v.at[:, t, s]) for t in range(2) for s in range(2)], w_sem
    )
    chunks = [hidden.at[half * 2 + turn]] + [x_in.at[i] for i in range(3)]
    loads = start_copies(
        [(x, x_v.at[pl.ds(i * span, span)]) for i, x in enumerate(chunks)], in_sem
    )
    signal_all([across, beside, partner])
    ids = iter(range(send_sem.shape[0]))
    started = []

    def go(src, dst, device):
        i = next(ids)
        copy = remote(src, dst, send_sem.at[i], recv_sem.at[i], device)
        copy.start()
        started.append(copy)
        return copy

    to_beside, to_across, to_partner, relays, ends = [], [], [], [], []
    for d in range(depth):
        to_beside.append(go(f_deep.at[d], n1.at[d], beside))
        to_across.append(go(f_deep.at[d], n2.at[d], across))
        ends.append(go(f_deep.at[d], f0.at[d], partner))
    g_copy = go(g_all.at[half * 2 + (turn + 1) % 2], g_home, beside)

    def arrived(d):
        to_beside[d].wait_recv()
        ends.append(go(n1.at[d], f1.at[d], partner))
        if d < depth - 1 or depth == 1:
            relays.append((d, go(n1.at[d], n3.at[d], across)))
        to_across[d].wait_recv()
        ends.append(go(n2.at[d], f2.at[d], partner))
        if d == depth - 1 and depth > 1:
            relays.append((d, go(n2.at[d], n3.at[d], beside)))

    def relayed():
        if relays:
            d, copy = relays.pop(0)
            copy.wait_recv()
            ends.append(go(n3.at[d], f3.at[d], partner))

    write_codes(segments, live, key_code, query_code, span)
    same = half == share
    bias = jnp.concatenate(
        [
            jnp.where(same, b_q[...], far_q[...]).astype(jnp.float32),
            jnp.zeros((1, width), jnp.float32),
            jnp.where(same, b_v[...], far_v[...]).astype(jnp.float32),
        ],
        1,
    )
    wait_copies(weights)
    w_qkv = w_v[...].reshape(x_v.shape[1], 3 * width)
    for i in range(4):
        loads[i].wait()
        at = pl.ds(i * span, span)
        value = (dot_nn(x_v[at, :], w_qkv) + bias).astype(jnp.bfloat16)
        q_v[at, :] = value[:, :width]
        per = span // BLK
        k_v[pl.ds(i * per, per)] = value[:, width : 2 * width].reshape(per, BLK, width)
        v_v[pl.ds(i * per, per)] = value[:, 2 * width :].reshape(per, BLK, width)
    stores = start_copies([(q_v, q_home), (k_v, k_home), (v_v, v_home), (w_v, w_home)], out_sem)
    blocks = length // BLK
    find, wide = computed(random, span // BLK, blocks)
    count = blocks - 2
    marks = [3 + d * 6 for d in range(depth)]
    marks = [min(mark, count - 1) for mark in marks] + [count]
    legs, start = [], 0
    for d, mark in enumerate(marks):
        legs.append((start, mark, (lambda d=d: arrived(d)) if d < depth else relayed))
        start = mark
    attend_blocks(
        find, wide, legs, q_v, k_v, v_v, key_code, query_code, o_v, lse_ref, acc,
        pause=lambda step: relayed() if step in (1, 2) else None,
    )
    own_ref[...] = o_v[: length // 2, :]
    swap = go(o_v.at[pl.ds(length // 2, length // 2)], other_home, partner)
    while relays:
        relayed()
    for copy in ends + [g_copy, swap]:
        copy.wait_recv()
    for copy in started:
        copy.wait_send()
    wait_copies(stores)


def project_attend(
    random, hidden, x_in, q_all, out_grad, f_deep, segments, live, b_q, b_v, far_q, far_v
):
    span, features = hidden.shape[1:]
    length = 4 * span
    depth, slim, cols = q_all.shape[3:]
    width = cols // 3
    bf16, shape = jnp.bfloat16, jax.ShapeDtypeStruct
    piece = shape(f_deep.shape, bf16)
    outs = pl.pallas_call(
        project_attend_kernel,
        out_shape=(shape((length // 2, width), bf16),) * 2
        + (shape((length, width), bf16),)
        + (shape((length // BLK, BLK, width), bf16),) * 2
        + (shape((depth, 2, 2, slim, cols), bf16), shape((span, features), bf16))
        + (piece,) * 7
        + (
            shape((length // BLK, 8, PAIR), jnp.float32),
            shape((length // BLK, BLK, PAIR), jnp.int32),
            shape((length // BLK, PAIR), jnp.int32),
        ),
        in_specs=[SMEM_SPEC] + [ANY_SPEC] * 5 + [VMEM_SPEC] * 6,
        out_specs=(VMEM_SPEC,) + (ANY_SPEC,) * 13 + (VMEM_SPEC,) * 3,
        scratch_shapes=[pltpu.VMEM((length, features), bf16)]
        + [pltpu.VMEM((length, width), bf16)]
        + [pltpu.VMEM((length // BLK, BLK, width), bf16)] * 2
        + [pltpu.VMEM((length, width), bf16)]
        + [
            pltpu.VMEM((depth, 2, 2, slim, cols), bf16),
            pltpu.VMEM((width // PAIR, PAIR, PAIR), jnp.float32),
            DMA((4,)), DMA((4,)), DMA((4,)), DMA((8 * depth + 2,)), DMA((8 * depth + 2,)),
        ],
        compiler_params=pltpu.CompilerParams(
            vmem_limit_bytes=63 * 1024 * 1024, collective_id=3, has_side_effects=True
        ),
        cost_estimate=pl.CostEstimate(
            flops=length * width * 1024 * 65, bytes_accessed=length * width * 16,
            transcendentals=length * width * 8,
        ),
        name="project_attend",
    )(
        random, hidden, x_in, q_all, out_grad, f_deep, segments, live, b_q, b_v, far_q, far_v
    )
    att0, att1, q, k, v, w_qkv, g_in, *pieces, lse, key_code, query_code = outs
    w_qkv = w_qkv.reshape(features, cols)
    return att0, att1, q, k, v, lse, w_qkv, g_in, [f_deep] + pieces, key_code, query_code


def attend_grad_kernel(
    random, do0, do1, q_in, k_in, v_in, key_code, query_code, lse_ref,
    d_ref, sums,
    q_v, k_v, v_v, do_v, dk_sum, dv_sum, acc, in_sem,
):
    f32 = jnp.float32
    length, width = q_v.shape
    half_length = length // 2
    loads = start_copies(
        [
            (q_in, q_v), (k_in, k_v), (v_in, v_v),
            (do0, do_v.at[pl.ds(0, half_length)]),
            (do1, do_v.at[pl.ds(half_length, half_length)]),
        ],
        in_sem,
    )
    wait_copies(loads)
    parts = [d_ref.at[:, pl.ds(i * width, width)] for i in range(3)]
    blocks = length // BLK
    find, wide = computed(random, blocks // 4, blocks)
    attend_back_blocks(
        find, wide, blocks - 2, q_v, k_v, v_v, do_v, key_code, query_code, lse_ref,
        *parts, dk_sum, dv_sum, acc,
    )
    share = my_spot()[2]
    sums[...] = jnp.zeros_like(sums)
    for s in range(2):

        @pl.when(share == s)
        def _():
            lanes = slice(s * width, (s + 1) * width)
            sums[0:1, lanes] = jnp.sum(d_ref[:, :width].astype(f32), 0, keepdims=True)
            sums[1:2, lanes] = jnp.sum(d_ref[:, 2 * width :].astype(f32), 0, keepdims=True)


def attend_grad(random, do0, do1, q, k, v, key_code, query_code, lse):
    length, width = q.shape
    f32, bf16, shape = jnp.float32, jnp.bfloat16, jax.ShapeDtypeStruct
    return pl.pallas_call(
        attend_grad_kernel,
        out_shape=(shape((length, 3 * width), bf16), shape((8, 2 * width), f32)),
        in_specs=[SMEM_SPEC] + [ANY_SPEC] * 5 + [VMEM_SPEC] * 3,
        out_specs=(VMEM_SPEC,) * 2,
        scratch_shapes=[pltpu.VMEM((length, width), bf16)]
        + [pltpu.VMEM((length // BLK, BLK, width), bf16)] * 2
        + [pltpu.VMEM((length, width), bf16)]
        + [pltpu.VMEM((length, width), f32)] * 2
        + [pltpu.VMEM((width // PAIR, PAIR, PAIR), f32), DMA((5,))],
        compiler_params=WIDE_ROOM,
        cost_estimate=pl.CostEstimate(
            flops=length * width * 1024 * 75, bytes_accessed=length * width * 30,
            transcendentals=length * width * 8,
        ),
        name="attend_grad",
    )(random, do0, do1, q, k, v, key_code, query_code, lse)


def load_weights(groups, w_up, w_dn, w_out, up_sem, dn_sem, wo_sem):
    depth, deep, cols = groups[0].shape
    thin = w_up.shape[2]
    slim = deep - 2 * thin
    homes = group_homes()
    out_loads = []
    for g in range(GROUPS):
        half, at = homes[g]
        for d in range(depth):
            spot = pl.ds(pl.multiple_of(d * thin + at * slim, 16), slim)
            out_loads.append(
                pltpu.make_async_copy(
                    groups[g].at[d, pl.ds(2 * thin, slim)], w_out.at[half, spot], wo_sem.at[g, d]
                )
            )
    up_loads = [
        pltpu.make_async_copy(
            groups[g].at[:, pl.ds(0, thin)], w_up.at[g // 2, :, :, lanes_of(g, cols)], up_sem.at[g]
        )
        for g in range(GROUPS)
    ]
    dn_loads = [
        pltpu.make_async_copy(
            groups[g].at[:, pl.ds(thin, thin)],
            w_dn.at[g // 2, :, :, lanes_of(g, cols)],
            dn_sem.at[g],
        )
        for g in range(GROUPS)
    ]
    return out_loads, up_loads, dn_loads


def whole(ref, g):
    depth, thin, cols = ref.shape[1:]
    return ref[g].reshape(depth * thin, cols)


def ffn_front_kernel(att0, att1, hidden, x_in, g_all, g_in, *rest):
    groups = rest[:GROUPS]
    (
        key_code, vectors, b_near, b_far,
        out0_home, out1_home, slope_home, g_second_home, unit_home, norm_t_home, near_ref, far_ref,
        inverse_ref, sums,
        att_v, x_v, g_v, w_up, w_dn, w_out, act, slope, normed_low,
        out_v, g_second_v, unit_v, norm_t, g_ffn_t, stage, b_up,
        in_sem, up_sem, dn_sem, wo_sem, stage_sem, home_sem, end_sem,
    ) = rest[GROUPS:]
    f32, bf16 = jnp.float32, jnp.bfloat16
    rows, width = x_v.shape
    span = hidden.shape[1]
    depth, deep, cols = groups[0].shape
    half, turn, share = my_spot()
    x_chunks = (hidden.at[half * 2 + turn], x_in.at[0])
    g_chunks = (g_all.at[half * 2 + turn], g_in)
    other = (share + 1) % 2
    out_loads, up_loads, dn_loads = load_weights(groups, w_up, w_dn, w_out, up_sem, dn_sem, wo_sem)
    loads = start_copies(
        [(a, att_v.at[:, lanes_of(i, cols)]) for i, a in enumerate((att0, att1))]
        + [(x, x_v.at[pl.ds(i * span, span)]) for i, x in enumerate(x_chunks)]
        + [(g, g_v.at[pl.ds(i * span, span)]) for i, g in enumerate(g_chunks)],
        in_sem,
    )
    for copy in out_loads + up_loads + dn_loads:
        copy.start()
    sums[...] = jnp.zeros_like(sums)
    for g in range(GROUPS):
        at = group_homes()[g][1]
        lanes = pl.ds(pl.multiple_of(at * cols, PAIR), cols)
        source = b_near if g % 4 < 2 else b_far
        b_up[g // 2 : g // 2 + 1, (g % 2) * cols : (g % 2 + 1) * cols] = source[:, lanes].astype(f32)
    wait_copies(loads + out_loads)
    b_out, gain1, shift1, b_down, gain2, shift2 = (vectors[i : i + 1, :] for i in range(6))

    def add_sum(index, value):
        sums[index : index + 1, :] += jnp.sum(value, 0, keepdims=True)

    def homes(tile):
        at = pl.ds(pl.multiple_of(tile * TILE, TILE), TILE)
        return [
            pltpu.make_async_copy(src, dst, home_sem.at[i, tile])
            for i, (src, dst) in enumerate(
                [
                    (slope.at[:, at], slope_home.at[:, at]),
                    (g_second_v.at[at], g_second_home.at[at]),
                    (unit_v.at[at], unit_home.at[at]),
                ]
            )
        ]

    def tile_step(tile, carry):
        at = pl.ds(pl.multiple_of(tile * TILE, TILE), TILE)
        live = (key_code[at, :1] >= 0).astype(f32)
        add_sum(11, jnp.broadcast_to(live, (TILE, width)))
        attn = b_out + dot_nt(att_v[at, :], jnp.concatenate([w_out[share], w_out[other]], 1))
        x = x_v[at, :].astype(f32)
        first = x + attn
        add_sum(6, live * (x * x))
        add_sum(7, live * (first * first))
        add_sum(9, live * (attn * attn))
        unit1, inverse1 = normalize(first)
        unit_v[at, :] = unit1
        inverse_ref[at, :] = inverse1
        normed = unit1 * gain1 + shift1
        low = normed.astype(bf16)
        normed_low[...] = low
        norm_t[:, at] = low.T

        @pl.when(tile == 0)
        def _():
            wait_copies(up_loads + dn_loads)

        def up_step(g, ffn):
            pre = dot_nn(normed_low[...], whole(w_up, g)) + b_up[pl.ds(g, 1), :]
            value, rise = gelu_both(pre)
            value = value.astype(bf16)
            act[g, at, :] = value
            slope[g, at, :] = rise.astype(bf16)
            return ffn + dot_nt(value, whole(w_dn, g))

        ffn = lax.fori_loop(0, DUOS, up_step, jnp.broadcast_to(b_down, (TILE, width)))
        second = normed + ffn
        add_sum(8, live * (second * second))
        add_sum(10, live * (ffn * ffn))
        unit2, inverse2 = normalize(second)
        out_v[at, :] = (unit2 * gain2 + shift2).astype(bf16)
        g_out = g_v[at, :].astype(f32)
        add_sum(4, g_out * unit2)
        add_sum(5, g_out)
        g_second = normalize_back(g_out * gain2, unit2, inverse2)
        g_second_v[at, :] = g_second
        g_ffn = g_second.astype(bf16)
        add_sum(3, g_ffn.astype(f32))
        g_ffn_t[:, at] = g_ffn.T
        for copy in homes(tile):
            copy.start()
        return carry

    lax.fori_loop(0, rows // TILE, tile_step, 0)
    last = start_copies(
        [
            (norm_t, norm_t_home),
            (out_v.at[pl.ds(0, span)], out0_home),
            (out_v.at[pl.ds(span, span)], out1_home),
        ],
        end_sem,
    )
    stores = [None] * GROUPS
    for duo in range(DUOS):
        down = dot_nn(g_ffn_t[...], act[duo]).astype(bf16).reshape(depth, -1, 2 * cols)
        for g in (2 * duo, 2 * duo + 1):
            slot = g % 4
            if g >= 4:
                stores[g - 4].wait()
            stage[slot] = down[:, :, (g % 2) * cols : (g % 2 + 1) * cols]
            home = near_ref.at[g] if g < DUOS else far_ref.at[g - DUOS]
            stores[g] = pltpu.make_async_copy(stage.at[slot], home, stage_sem.at[slot])
            stores[g].start()
    for tile in range(rows // TILE):
        wait_copies(homes(tile))
    wait_copies(stores[-4:] + last)


def ffn_front(att0, att1, hidden, x_in, g_all, g_in, groups, key_code, vectors, b_near, b_far):
    rows, part = att0.shape
    width = hidden.shape[2]
    depth, deep, cols = groups[0].shape
    thin = width // depth
    f32, bf16, shape = jnp.float32, jnp.bfloat16, jax.ShapeDtypeStruct
    grads = shape((DUOS, depth, thin, cols), bf16)
    weights = pltpu.VMEM((DUOS, depth, thin, 2 * cols), bf16)
    flat = pltpu.VMEM((rows, width), bf16)
    tall = pltpu.VMEM((rows, width), f32)
    deep_rows = pltpu.VMEM((DUOS, rows, 2 * cols), bf16)
    turned = pltpu.VMEM((width, rows), bf16)
    return pl.pallas_call(
        ffn_front_kernel,
        out_shape=(
            shape((rows // 2, width), bf16), shape((rows // 2, width), bf16),
            shape((DUOS, rows, 2 * cols), bf16),
            shape((rows, width), f32), shape((rows, width), f32), shape((width, rows), bf16),
            grads, grads, shape((rows, 1), f32), shape((16, width), f32),
        ),
        in_specs=[ANY_SPEC] * (6 + GROUPS) + [VMEM_SPEC] * 4,
        out_specs=(ANY_SPEC,) * 8 + (VMEM_SPEC,) * 2,
        scratch_shapes=[
            flat, flat, flat, weights, weights, pltpu.VMEM((2, width, part), bf16),
            deep_rows, deep_rows, pltpu.VMEM((TILE, width), bf16),
            flat, tall, tall, turned, turned, pltpu.VMEM((4, depth, thin, cols), bf16),
            pltpu.VMEM((DUOS, 2 * cols), f32),
            DMA((6,)), DMA((GROUPS,)), DMA((GROUPS,)), DMA((GROUPS, depth)), DMA((4,)),
            DMA((3, rows // TILE)), DMA((3,)),
        ],
        compiler_params=WIDE_ROOM,
        cost_estimate=pl.CostEstimate(
            flops=38 * 10**9, bytes_accessed=40 * 10**6, transcendentals=rows * GROUPS * cols
        ),
        name="ffn_front",
    )(att0, att1, hidden, x_in, g_all, g_in, *groups, key_code, vectors, b_near, b_far)


def ffn_rear_kernel(
    att0, att1, slope_in, g_second_in, unit_in, norm_t_in, out0, out1, near_dn, far_dn, *rest
):
    groups = rest[:GROUPS]
    (
        inverse_ref, vectors,
        g_first_home, do_own, do_far, layer_home, *totals
    ) = rest[GROUPS : GROUPS + 6 + DUOS]
    (
        sums, up_sums,
        att_v, slope, g_second_v, unit_v, norm_t, w_up, w_dn, w_out, g_pre,
        g_first_v, g_att_v, g_attn_t, out_v, far_v, got_v, got_dn, near_v, stage,
        in_sem, up_sem, dn_sem, wo_sem, stage_sem, home_sem, out_sem,
        l_send, l_recv, a_send, a_recv, u_send, u_recv,
    ) = rest[GROUPS + 6 + DUOS :]
    f32, bf16 = jnp.float32, jnp.bfloat16
    rows, width = unit_v.shape
    span = out0.shape[0]
    depth, deep, cols = groups[0].shape
    thin = w_up.shape[2]
    slim = deep - 2 * thin
    half, turn, share = my_spot()
    other = (share + 1) % 2
    across, beside, partner = neighbours()
    out_loads, up_loads, dn_loads = load_weights(groups, w_up, w_dn, w_out, up_sem, dn_sem, wo_sem)
    wait_order = [
        pltpu.make_async_copy(src, dst, in_sem.at[i])
        for i, (src, dst) in enumerate(
            [
                (g_second_in, g_second_v), (slope_in, slope), (unit_in, unit_v),
                (norm_t_in, norm_t), (att0, att_v.at[:, lanes_of(0, cols)]),
                (att1, att_v.at[:, lanes_of(1, cols)]),
            ]
        )
    ]
    for copy in wait_order[:1] + dn_loads + wait_order[1:2] + up_loads + wait_order[2:3]:
        copy.start()
    for copy in out_loads + wait_order[3:]:
        copy.start()
    late = start_copies([(out0, out_v), (near_dn, near_v)], out_sem)
    signal_all([across, beside, partner])
    mine = layer_home.at[half * 2 + turn]
    theirs = layer_home.at[half * 2 + (turn + 1) % 2]
    layer = [
        remote(out1, mine, l_send.at[0], l_recv.at[0], beside),
        remote(out0, mine, l_send.at[1], l_recv.at[1], across),
        remote(theirs, theirs, l_send.at[2], l_recv.at[2], across),
        remote(far_dn, got_dn, l_send.at[3], l_recv.at[3], partner),
    ]
    layer[0].start()
    layer[1].start()
    layer[3].start()
    sums[...] = jnp.zeros_like(sums)
    up_sums[...] = jnp.zeros_like(up_sums)
    gain1 = vectors[1:2, :]
    wait_copies(wait_order[:1] + dn_loads + wait_order[1:2])
    out_weight = lambda: jnp.concatenate([w_out[share], w_out[other]], 1)

    def add_sum(index, value):
        sums[index : index + 1, :] += jnp.sum(value, 0, keepdims=True)

    def tile_rows(tile):
        return pl.ds(pl.multiple_of(tile * TILE, TILE), TILE)

    def give(tile):
        at = tile_rows(tile)
        return remote(g_att_v.at[1, at], do_far.at[at], a_send.at[tile], a_recv.at[tile], partner)

    tiles = rows // TILE

    def tile_step(tile, carry):
        at = tile_rows(tile)

        @pl.when(tile == 0)
        def _():
            wait_copies(up_loads + wait_order[2:] + out_loads)

        @pl.when(tile == tiles - 1)
        def _():
            layer[0].wait_recv()
            layer[2].start()

        g_second = g_second_v[at, :]
        g_ffn = g_second.astype(bf16)

        def back_step(g, total):
            grad = (dot_nn(g_ffn, whole(w_dn, g)) * slope[g, at, :].astype(f32)).astype(bf16)
            g_pre[g, at, :] = grad
            up_sums[pl.ds(g, 1), :] += jnp.sum(grad.astype(f32), 0, keepdims=True)
            return total + dot_nt(grad, whole(w_up, g))

        g_normed = lax.fori_loop(0, DUOS, back_step, g_second)
        unit1 = unit_v[at, :]
        add_sum(1, g_normed * unit1)
        add_sum(2, g_normed)
        g_first = normalize_back(g_normed * gain1, unit1, inverse_ref[at, :])
        g_first_v[at, :] = g_first
        g_attn = g_first.astype(bf16)
        add_sum(0, g_attn.astype(f32))
        g_attn_t[:, at] = g_attn.T
        both = dot_nn(g_attn, out_weight()).astype(bf16)
        g_att_v[0, at, :] = both[:, :cols]
        g_att_v[1, at, :] = both[:, cols:]
        give(tile).start()
        return carry

    lax.fori_loop(0, tiles, tile_step, 0)
    homes = start_copies([(g_att_v.at[0], do_own), (g_first_v, g_first_home)], home_sem)
    wait_copies(late)
    own_out = pltpu.make_async_copy(out_v, mine, out_sem.at[0])
    own_out.start()
    both = dot_nn(g_attn_t[...], att_v[...]).astype(bf16)
    w_out[share] = both[:, :cols]
    w_out[other] = both[:, cols:]
    spots = group_homes()

    def out_rows(g, d):
        where, at = spots[g]
        return w_out[where, pl.ds(pl.multiple_of(d * thin + at * slim, 16), slim), :]

    def up_of(duo):
        up = dot_nn(norm_t[...], g_pre[duo]).astype(bf16).reshape(depth, thin, 2 * cols)
        return [(2 * duo + i, up[:, :, i * cols : (i + 1) * cols]) for i in range(2)]

    sends = []
    for duo in range(DUOS // 2, DUOS):
        for g, up in up_of(duo):
            i = g - DUOS
            far_v[i, :, pl.ds(0, thin), :] = up
            for d in range(depth):
                far_v[i, d, pl.ds(thin, slim), :] = out_rows(g, d)
            sends.append(remote(far_v.at[i], got_v.at[i], u_send.at[i], u_recv.at[i], partner))
            sends[i].start()
    layer[3].wait_recv()
    add = lambda a, b: (a.astype(f32) + b.astype(f32)).astype(bf16)
    stores = [None] * DUOS
    for duo in range(DUOS // 2):
        for g, up in up_of(duo):
            slot = g % 2
            if g >= 2:
                stores[g - 2].wait()
            sends[g].wait_recv()
            stage[slot, :, pl.ds(0, thin), :] = add(up, got_v[g, :, pl.ds(0, thin), :])
            stage[slot, :, pl.ds(thin, thin), :] = add(near_v[g], got_dn[g])
            for d in range(depth):
                stage[slot, d, pl.ds(2 * thin, slim), :] = add(
                    out_rows(g, d), got_v[g, d, pl.ds(thin, slim), :]
                )
            stores[g] = pltpu.make_async_copy(stage.at[slot], totals[g], stage_sem.at[slot])
            stores[g].start()
    for tile in range(tiles):
        give(tile).wait()
    layer[1].wait_recv()
    layer[2].wait_recv()
    for copy in layer + sends:
        copy.wait_send()
    wait_copies(stores[-2:] + homes + [own_out])


def ffn_rear(
    att0, att1, slope, g_second, unit, norm_t, out0, out1, near_dn, far_dn, groups, inverse, vectors
):
    rows, part = att0.shape
    span, width = out0.shape
    depth, deep, cols = groups[0].shape
    thin = width // depth
    f32, bf16, shape, v = jnp.float32, jnp.bfloat16, jax.ShapeDtypeStruct, pltpu.VMEM
    weights = v((DUOS, depth, thin, 2 * cols), bf16)
    flat = v((rows, width), bf16)
    tall = v((rows, width), f32)
    deep_rows = v((DUOS, rows, 2 * cols), bf16)
    turned = v((width, rows), bf16)
    mixed = v((DUOS, depth, deep - thin, cols), bf16)
    downs = v((DUOS, depth, thin, cols), bf16)
    tiles = rows // TILE
    return pl.pallas_call(
        ffn_rear_kernel,
        out_shape=(
            shape((rows, width), f32), shape((rows, part), bf16), shape((rows, part), bf16),
            shape((4, span, width), bf16),
        )
        + (shape((depth, deep, cols), bf16),) * DUOS
        + (shape((16, width), f32), shape((DUOS, 2 * cols), f32)),
        in_specs=[ANY_SPEC] * (10 + GROUPS) + [VMEM_SPEC] * 2,
        out_specs=(ANY_SPEC,) * (4 + DUOS) + (VMEM_SPEC,) * 2,
        scratch_shapes=[
            flat, deep_rows, tall, tall, turned, weights, weights,
            v((2, width, part), bf16), deep_rows, tall, v((2, rows, part), bf16), turned,
            v((span, width), bf16), mixed, mixed, downs, downs, v((2, depth, deep, cols), bf16),
            DMA((6,)), DMA((GROUPS,)), DMA((GROUPS,)), DMA((GROUPS, depth)), DMA((2,)), DMA((2,)),
            DMA((2,)), DMA((4,)), DMA((4,)), DMA((tiles,)), DMA((tiles,)), DMA((DUOS,)),
            DMA((DUOS,)),
        ],
        compiler_params=pltpu.CompilerParams(
            vmem_limit_bytes=63 * 1024 * 1024, collective_id=2, has_side_effects=True
        ),
        cost_estimate=pl.CostEstimate(
            flops=45 * 10**9, bytes_accessed=40 * 10**6, transcendentals=0
        ),
        name="ffn_rear",
    )(
        att0, att1, slope, g_second, unit, norm_t, out0, out1, near_dn, far_dn, *groups, inverse,
        vectors,
    )


MESH = pl.DeviceIdType.MESH
CUTS = 8
THIRDS = 3


def signal_all(devices):
    barrier = pltpu.get_barrier_semaphore()
    for device in devices:
        pl.semaphore_signal(barrier, inc=1, device_id=device, device_id_type=MESH)
    pl.semaphore_wait(barrier, len(devices))


def neighbours():
    half, turn, share = my_spot()
    return (
        {"tensor": (half + 1) % 2},
        {"context": ((turn + 1) % 2) * 2 + share},
        {"context": turn * 2 + (share + 1) % 2},
    )


def remote(src, dst, send_sem, recv_sem, device):
    return pltpu.make_async_remote_copy(
        src_ref=src, dst_ref=dst, send_sem=send_sem, recv_sem=recv_sem,
        device_id=device, device_id_type=MESH,
    )


def fetch_kernel(
    hidden, qkv, ffn, bias_q, bias_v, bias_u, x_out, q_all, f_deep, far_q, far_v, far_u,
    own_sem, x_send, x_recv, z_send, z_recv, f_send, f_recv,
    h_send, h_recv, t_send, t_recv, c_send, c_recv, b_sem,
):
    half, turn, share = my_spot()
    deep = lax.axis_index("dp")
    depth = f_deep.shape[0]
    across, beside, partner = neighbours()
    up, down = {"dp": (deep + 1) % depth}, {"dp": (deep + depth - 1) % depth}
    signal_all([across, beside, partner, up, down])

    slot = lambda h, t, d: q_all.at[h, t, share, d]
    own = start_copies([(qkv, slot(half, turn, deep)), (ffn, f_deep.at[deep])], own_sem)

    def to_up(d):
        return remote(slot(half, turn, d), slot(half, turn, d), z_send.at[0, d], z_recv.at[d], up)

    def to_down(d):
        return remote(slot(half, turn, d), slot(half, turn, d), z_send.at[1, d], z_recv.at[d], down)

    third = f_deep.shape[1] // THIRDS

    def f_copies(d, side, device):
        return [
            remote(
                f_deep.at[d, pl.ds(i * third, third)], f_deep.at[d, pl.ds(i * third, third)],
                f_send.at[side, d, i], f_recv.at[d, i], device,
            )
            for i in range(THIRDS)
        ]

    f_up = lambda d: f_copies(d, 0, up)
    f_down = lambda d: f_copies(d, 1, down)

    def to_across(t, d):
        return remote(slot(half, t, d), slot(half, t, d), h_send.at[t, d], h_recv.at[t, d], across)

    def from_across(t, d):
        other = slot((half + 1) % 2, t, d)
        return remote(other, other, h_send.at[t, d], h_recv.at[t, d], across)

    def to_beside(d):
        return remote(slot(half, turn, d), slot(half, turn, d), t_send.at[d], t_recv.at[d], beside)

    def from_beside(d):
        other = slot(half, (turn + 1) % 2, d)
        return remote(other, other, t_send.at[d], t_recv.at[d], beside)

    def to_partner(t, d):
        piece = slot((share + 1) % 2, t, d)
        return remote(piece, piece, c_send.at[t, d], c_recv.at[t, d], partner)

    def from_partner(t, d):
        piece = q_all.at[share, t, (share + 1) % 2, d]
        return remote(piece, piece, c_send.at[t, d], c_recv.at[t, d], partner)

    cut = x_out.shape[1] // CUTS
    piece_rows = lambda i: pl.ds(i * cut, cut)
    x_next = [
        remote(
            hidden.at[half * 2 + (turn + 1) % 2, piece_rows(i)], x_out.at[0, piece_rows(i)],
            x_send.at[0, i], x_recv.at[0, i], beside,
        )
        for i in range(CUTS)
    ]
    x_mine = remote(
        hidden.at[half * 2 + turn], x_out.at[1], x_send.at[1, 0], x_recv.at[1, 0], partner
    )
    x_relay = [
        remote(
            x_out.at[0, piece_rows(i)], x_out.at[2, piece_rows(i)],
            x_send.at[2, i], x_recv.at[2, i], partner,
        )
        for i in range(CUTS)
    ]
    biases = [
        remote(src, dst, b_sem.at[0, i], b_sem.at[1, i], across)
        for i, (src, dst) in enumerate(((bias_q, far_q), (bias_v, far_v), (bias_u, far_u)))
    ]
    wait_copies(own)
    own_turn = (share + 1) % 2 == half

    def spread_own(d):
        to_across(turn, d).start()
        to_beside(d).start()

        @pl.when(own_turn)
        def _():
            to_partner(turn, d).start()

    def when(condition, *copies):
        @pl.when(condition)
        def _():
            for copy in copies:
                copy.start()

    when(deep < depth - 1, to_up(deep))
    when(deep > 0, to_down(deep))
    when(deep < depth - 1, f_up(deep)[0])
    when(deep > 0, f_down(deep)[0])
    spread_own(deep)
    x_next[0].start()
    for copy in biases:
        copy.start()
    x_mine.start()
    for k in range(1, depth):
        low, high = (deep + depth - k) % depth, (deep + k) % depth

        @pl.when(deep >= k)
        def _():
            to_up(low).wait_recv()
            when(deep < depth - 1, to_up(low))
            spread_own(low)

        @pl.when(deep + k < depth)
        def _():
            to_down(high).wait_recv()
            when(deep > 0, to_down(high))
            spread_own(high)

        if k < THIRDS:
            when(deep < depth - 1, f_up(deep)[k])
            when(deep > 0, f_down(deep)[k])
        x_next[k].start()

    for i in range(depth, THIRDS):
        when(deep < depth - 1, f_up(deep)[i])
        when(deep > 0, f_down(deep)[i])
    for copy in x_next[depth:]:
        copy.start()
    for k in range(depth):
        d = (deep + k) % depth
        from_beside(d).wait_recv()
        to_across((turn + 1) % 2, d).start()

        @pl.when(own_turn)
        def _():
            to_partner((turn + 1) % 2, d).start()

    def f_step(k):
        low, high = (deep + depth - k) % depth, (deep + k) % depth

        @pl.when(deep >= k)
        def _():
            for copy in f_up(low):
                copy.wait_recv()
                when(deep < depth - 1, copy)

        @pl.when(deep + k < depth)
        def _():
            for copy in f_down(high):
                copy.wait_recv()
                when(deep > 0, copy)

    def x_step(step):
        for i in range(step * CUTS // (depth + 1), (step + 1) * CUTS // (depth + 1)):
            x_next[i].wait_recv()
            x_relay[i].start()

    f_step(1)
    for step, t in enumerate((turn, (turn + 1) % 2)):
        for k in range(depth):
            d = (deep + k) % depth
            from_across(t, d).wait_recv()

            @pl.when(jnp.logical_not(own_turn))
            def _():
                to_partner(t, d).start()

        x_step(step)
        if step == 0 and depth > 2:
            f_step(2)
    for k in range(3, depth):
        x_step(k - 1)
        f_step(k)
    for step in range(max(2, depth - 1), depth + 1):
        x_step(step)

    for t in range(2):
        for d in range(depth):
            from_partner(t, d).wait_recv()
    x_mine.wait_recv()
    for copy in x_relay + biases:
        copy.wait_recv()
    for d in range(depth):
        for copy in (to_across(0, d), to_across(1, d), to_beside(d), to_partner(0, d), to_partner(1, d)):
            copy.wait_send()

        @pl.when(jnp.logical_and(deep < depth - 1, deep >= d))
        def _():
            for copy in [to_up(d)] + f_up(d):
                copy.wait_send()

        @pl.when(jnp.logical_and(deep > 0, deep <= d))
        def _():
            for copy in [to_down(d)] + f_down(d):
                copy.wait_send()

    for copy in x_next + x_relay + [x_mine] + biases:
        copy.wait_send()


def fetch(hidden_in, qkv_piece, ffn_piece, biases, depth):
    span, width = hidden_in.shape[1:]
    bf16, shape = jnp.bfloat16, jax.ShapeDtypeStruct
    pair = DMA((2, depth))
    return pl.pallas_call(
        fetch_kernel,
        out_shape=(
            shape((3, span, width), bf16),
            shape((2, 2, 2, depth) + qkv_piece.shape, bf16),
            shape((depth,) + ffn_piece.shape, bf16),
            *(shape(b.shape, bf16) for b in biases),
        ),
        in_specs=[ANY_SPEC] + [VMEM_SPEC] * 5,
        out_specs=(ANY_SPEC,) * 3 + (VMEM_SPEC,) * 3,
        scratch_shapes=[
            DMA((2,)), DMA((3, CUTS)), DMA((3, CUTS)), pair, DMA((depth,)),
            DMA((2, depth, THIRDS)), DMA((depth, THIRDS)),
            pair, pair, DMA((depth,)), DMA((depth,)), pair, pair, DMA((2, 3)),
        ],
        compiler_params=pltpu.CompilerParams(collective_id=0, has_side_effects=True),
        cost_estimate=pl.CostEstimate(
            flops=30 * 10**9, bytes_accessed=10 * 10**6, transcendentals=0
        ),
        name="fetch",
    )(hidden_in, qkv_piece, ffn_piece, *biases)


SUBS = 4


def settle_kernel(hidden, x_in, dqkv, w_qkv, g_first, small, *rest):
    f32, bf16 = jnp.float32, jnp.bfloat16
    parts = rest[:4]
    (
        out, qkv_out, f_out, small_out,
        x_v, d_v, w_v, first_v, part_v, small_v, small_got,
        back_v, got_v, fin_v, land_v, tot_v, zf_v, ff_v,
        grad_v, swap_v, pq_v, yl_v, xs_v, xl_v, rs_v, zq_v, qf_v,
        in_sem, out_sem, send_sem, recv_sem,
    ) = rest[4:]
    half, turn, share = my_spot()
    deep = lax.axis_index("dp")
    depth = tot_v.shape[0]
    span = hidden.shape[1]
    sub = span // SUBS
    other = (share + 1) % 2
    far_half, far_turn = (half + 1) % 2, (turn + 1) % 2
    across, beside, partner = neighbours()
    deeps = [{"dp": (deep + k) % depth} for k in range(1, depth)]
    ids = iter(range(send_sem.shape[0]))
    started = []

    def link(src, dst, device):
        i = next(ids)
        copy = remote(src, dst, send_sem.at[i], recv_sem.at[i], device)
        started.append(copy)
        return copy

    def go(src, dst, device):
        copy = link(src, dst, device)
        copy.start()
        return copy

    chunk = lambda i: pl.ds(i * span, span)
    chunks = [hidden.at[half * 2 + turn]] + [x_in.at[i] for i in range(3)]
    loads = [
        pltpu.make_async_copy(src, dst, in_sem.at[i])
        for i, (src, dst) in enumerate(
            [(w_qkv, w_v)]
            + [(dqkv.at[chunk(i)], d_v.at[chunk(i)]) for i in (2, 3, 0, 1)]
            + [(p, part_v.at[i]) for i, p in enumerate(parts)]
            + [(g_first, first_v)]
            + [(c, x_v.at[chunk(i)]) for i, c in enumerate(chunks)]
        )
    ]
    for copy in loads:
        copy.start()
    signal_all([across, beside, partner] + deeps)
    small_v[...] = small[...]
    s0 = go(small, small_got.at[0], partner)

    wait_copies(loads[:3])
    back = []
    for i in range(2):
        back_v[i] = dot_nt(d_v[chunk(2 + i), :], w_v[...]).astype(bf16)
        back.append(go(back_v.at[i], got_v.at[i], partner))
    wait_copies(loads[3:10])
    tot_v[...] = (
        (part_v[0].astype(f32) + part_v[1].astype(f32))
        + (part_v[2].astype(f32) + part_v[3].astype(f32))
    ).astype(bf16)
    outs = []
    z_f = [
        go(tot_v.at[(deep + k + 1) % depth], zf_v.at[k], device) for k, device in enumerate(deeps)
    ]

    def own_back(i):
        value = dot_nt(d_v[chunk(i), :], w_v[...]) + first_v[chunk(i), :]
        back[i].wait_recv()
        fin_v[i] = (value + got_v[i].astype(f32)).astype(bf16)

    rows = lambda j: pl.ds(j * sub, sub)

    def put(ref, h, t):
        copy = pltpu.make_async_copy(ref, out.at[h * 2 + t], out_sem.at[len(outs)])
        copy.start()
        outs.append(copy)

    own_back(0)
    x_subs = [go(fin_v.at[0, rows(j)], land_v.at[1, rows(j)], across) for j in range(SUBS)]
    put(fin_v.at[0], half, turn)
    own_back(1)
    y_subs = [go(fin_v.at[1, rows(j)], land_v.at[0, rows(j)], beside) for j in range(SUBS // 2)]

    s0.wait_recv()
    s0.wait_send()
    small_v[...] += small_got[0]
    s1 = go(small_v, small_got.at[1], beside)
    wait_copies(loads[10:])
    grad_v[...] = dot_tn(x_v[...], d_v[...]).astype(bf16).reshape(grad_v.shape)
    swap_v[...] = grad_v[:, :, other]
    swap = go(swap_v, pq_v.at[share], partner)
    pq_v[share] = grad_v[:, :, share]
    s1.wait_recv()
    s1.wait_send()
    small_v[...] += small_got[1]
    s2 = go(small_v, small_got.at[2], across)
    swap.wait_recv()
    keep_v = lambda h, t: pq_v[h, :, t]
    q1 = go(pq_v.at[far_half, :, far_turn], yl_v.at[0], beside)
    q2 = go(pq_v.at[half, :, far_turn], yl_v.at[1], beside)
    y_subs += [
        go(fin_v.at[1, rows(j)], land_v.at[0, rows(j)], beside) for j in range(SUBS // 2, SUBS)
    ]
    s2.wait_recv()
    s2.wait_send()
    small_v[...] += small_got[2]
    s3 = [go(small_v, small_got.at[3 + k], device) for k, device in enumerate(deeps)]
    relays = []

    def relay(j):
        y_subs[j].wait_recv()
        relays.append(go(land_v.at[0, rows(j)], land_v.at[2, rows(j)], across))

    for j in range(SUBS // 2):
        relay(j)
    q1.wait_recv()
    xs_v[...] = (keep_v(far_half, turn).astype(f32) + yl_v[0].astype(f32)).astype(bf16)
    qx = go(xs_v, xl_v, across)

    for copy in z_f:
        copy.wait_recv()
    ranks = range(depth - 1)
    spread = lambda ref, got: sum([got[k].astype(f32) for k in ranks], ref[deep].astype(f32))
    ff_v[turn, share] = spread(tot_v, zf_v).astype(bf16)

    def gather_first(ref):
        piece = ref.at[turn, share]
        return go(piece, piece, beside), go(piece, piece, partner)

    def gather_next(ref, first):
        first.wait_recv()
        piece = ref.at[far_turn, share]
        return go(piece, piece, partner)

    f_first = gather_first(ff_v)
    q2.wait_recv()
    for j in range(SUBS // 2, SUBS):
        relay(j)
    qx.wait_recv()
    rs_v[...] = (
        keep_v(half, turn).astype(f32) + yl_v[1].astype(f32) + xl_v[...].astype(f32)
    ).astype(bf16)
    z_q = [
        go(rs_v.at[(deep + k + 1) % depth], zq_v.at[k], device) for k, device in enumerate(deeps)
    ]
    for copy in s3:
        copy.wait_recv()
    small_out[...] = small_v[...] + sum([small_got[4 + k] for k in range(depth - 2)], small_got[3])
    f_next = gather_next(ff_v, f_first[0])
    for copy in z_q:
        copy.wait_recv()
    qf_v[turn, share] = spread(rs_v, zq_v).astype(bf16)
    q_first = gather_first(qf_v)
    put(land_v.at[0], half, far_turn)
    for copy in x_subs:
        copy.wait_recv()
    put(land_v.at[1], far_half, turn)
    f_first[1].wait_recv()
    f_next.wait_recv()
    ends = start_copies([(ff_v, f_out)], in_sem)
    q_next = gather_next(qf_v, q_first[0])
    for copy in relays:
        copy.wait_recv()
    put(land_v.at[2], far_half, far_turn)
    q_first[1].wait_recv()
    q_next.wait_recv()
    last = pltpu.make_async_copy(qf_v, qkv_out, in_sem.at[2])
    last.start()
    wait_copies(ends + [last] + outs)
    waited = [s0, s1, s2]
    for copy in started:
        if not any(copy is w for w in waited):
            copy.wait_send()


def settle(hidden_in, x_in, dqkv, w_qkv, g_first, small, parts):
    rows, width = g_first.shape
    span = hidden_in.shape[1]
    depth, tall, cols = parts[0].shape
    wide = dqkv.shape[1]
    slim = width // depth // 4
    f32, bf16, shape = jnp.float32, jnp.bfloat16, jax.ShapeDtypeStruct
    v = pltpu.VMEM
    count = 80
    return pl.pallas_call(
        settle_kernel,
        out_shape=(
            shape((4, span, width), bf16), shape((2, 2, slim, wide), bf16),
            shape((2, 2, tall, cols), bf16), shape(small.shape, f32),
        ),
        in_specs=[ANY_SPEC] * 5 + [VMEM_SPEC] + [ANY_SPEC] * 4,
        out_specs=(ANY_SPEC,) * 3 + (VMEM_SPEC,),
        scratch_shapes=[
            v((2 * rows, width), bf16), v((2 * rows, wide), bf16), v((width, wide), bf16),
            v((rows, width), f32), v((4, depth, tall, cols), bf16), v(small.shape, f32),
            v((2 + depth,) + small.shape, f32),
            v((2, span, width), bf16), v((2, span, width), bf16), v((2, span, width), bf16),
            v((3, span, width), bf16),
            v((depth, tall, cols), bf16), v((depth - 1, tall, cols), bf16),
            v((2, 2, tall, cols), bf16),
            v((depth, 2, 2, slim, wide), bf16), v((depth, 2, slim, wide), bf16),
            v((2, depth, 2, slim, wide), bf16), v((2, depth, slim, wide), bf16),
            v((depth, slim, wide), bf16), v((depth, slim, wide), bf16),
            v((depth, slim, wide), bf16), v((depth - 1, slim, wide), bf16),
            v((2, 2, slim, wide), bf16),
            DMA((20,)), DMA((4,)), DMA((count,)), DMA((count,)),
        ],
        compiler_params=pltpu.CompilerParams(
            vmem_limit_bytes=63 * 1024 * 1024, collective_id=1, has_side_effects=True
        ),
        cost_estimate=pl.CostEstimate(
            flops=60 * 10**9, bytes_accessed=30 * 10**6, transcendentals=0
        ),
        name="settle",
    )(hidden_in, x_in, dqkv, w_qkv, g_first, small, *parts)


def layer_norm(values, norm_gain, norm_shift):
    row_mean = jnp.mean(values, -1, keepdims=True)
    centered = values - row_mean
    row_var = jnp.mean(centered * centered, -1, keepdims=True)
    return centered * lax.rsqrt(row_var + EPSILON) * norm_gain + norm_shift


def gelu_tanh(values):
    return jax.nn.gelu(values, approximate=True)


def block_tables(random_seq, all_blocks, place):
    block = jnp.arange(2, all_blocks, dtype=jnp.int32)
    last = all_blocks - 1
    zero = jnp.zeros_like(block)
    true_ids = jnp.stack(
        [block, block - 1, block, jnp.minimum(block + 1, last), zero, zero + 1], -1
    )
    true_ids = jnp.concatenate([true_ids, random_seq[2:]], -1)
    flags = jnp.stack([block >= 3, block <= last - 1], -1).astype(jnp.int32)
    return (
        jnp.concatenate([place(true_ids), flags], -1).astype(jnp.int32),
        place(jnp.arange(2, dtype=jnp.int32)),
    )


def local(
    hidden_in, out_grad, segment_ids, token_valid, random_blocks,
    query_weight, query_bias, key_weight, value_weight, value_bias,
    output_weight, output_bias, norm1_gain, norm1_shift,
    up_weight, up_bias, down_weight, down_bias, norm2_gain, norm2_shift,
):
    f32, bf16 = jnp.float32, jnp.bfloat16
    seqs, span, width = hidden_in.shape
    length = segment_ids.shape[1]
    places = length // span
    halves = lax.axis_size("tensor")
    depth = lax.axis_size("dp")
    turns = seqs // halves
    shares = places // turns
    my_half = lax.axis_index("tensor")
    my_place = lax.axis_index("context")
    my_depth = lax.axis_index("dp")
    my_turn, my_share = my_place // shares, my_place % shares
    my_seq = my_half * turns + my_turn
    blocks = length // BLK
    rows = turns * span
    spots = [(h, t) for h in range(halves) for t in range(turns)]

    def send(value, half=0, turn=0, share=0):
        if half % halves == 0 and turn % turns == 0 and share % shares == 0:
            return value
        pairs = []
        for h in range(halves):
            for t in range(turns):
                for s in range(shares):
                    to_place = (t + turn) % turns * shares + (s + share) % shares
                    pairs.append(
                        ((t * shares + s) * halves + h, to_place * halves + (h + half) % halves)
                    )
        return lax.ppermute(value, ("context", "tensor"), pairs)

    def send_deep(value, step):
        return lax.ppermute(value, "dp", [(i, (i + step) % depth) for i in range(depth)])

    def pick(value, index, axis=0):
        return lax.dynamic_index_in_dim(value, index, axis, keepdims=False)

    def own_slice(value, count, which, axis):
        size = value.shape[axis] // count
        return lax.dynamic_slice_in_dim(value, which * size, size, axis)

    def gather_deep(value):
        if depth > 4:
            return lax.all_gather(value, "dp", axis=0)
        got = [value] + [send_deep(value, k) for k in range(1, depth)]
        ring = jnp.stack([got[depth - 1 - i % depth] for i in range(2 * depth - 1)])
        return lax.dynamic_slice_in_dim(ring, depth - 1 - my_depth, depth, 0)

    def reduce_deep(value):
        if depth > 4:
            return lax.psum_scatter(value, "dp", scatter_dimension=0)
        total = pick(value, my_depth).astype(f32)
        for k in range(1, depth):
            total = total + send_deep(pick(value, (my_depth + k) % depth), k).astype(f32)
        return total.astype(bf16)

    def gather_square(value):
        near = {spot: send(value, *spot) for spot in spots}
        near = jnp.stack([near[spot] for spot in spots])
        return [near] + [send(near, 0, 0, s) for s in range(1, shares)]

    def reduce_square(value):
        total = value[0].astype(f32)
        for i, (h, t) in enumerate(spots[1:], 1):
            total = total + send(value[i], -h, -t).astype(f32)
        return total.astype(bf16)

    def gather_places(value):
        near = [send(value, 0, t) for t in range(turns)]
        near = jnp.stack(near)
        far = jnp.stack([near] + [send(near, 0, 0, s) for s in range(1, shares)])
        return jnp.stack(
            [
                pick(pick(far, (my_share - s) % shares), (my_turn - t) % turns)
                for t in range(turns)
                for s in range(shares)
            ]
        )

    def sum_all(value):
        for step in range(halves.bit_length() - 1):
            value = value + send(value, 1 << step)
        size = 1
        while size < places:
            value = value + lax.ppermute(value, "context", [(i, i ^ size) for i in range(places)])
            size *= 2
        size = 1
        while size < depth:
            value = value + lax.ppermute(value, "dp", [(i, i ^ size) for i in range(depth)])
            size *= 2
        return value

    def bring(value):
        return jnp.concatenate(
            [
                send(pick(value, my_half * turns + (my_turn + k) % turns), 0, k)
                for k in range(turns)
            ],
            0,
        )

    def deliver(value):
        value = value.reshape(turns, span, width)
        got = jnp.stack([send(value[t], h, -t) for h, t in spots])
        return jnp.stack(
            [
                pick(got, (my_half - h) % halves * turns + (t - my_turn) % turns)
                for h in range(halves)
                for t in range(turns)
            ]
        )

    def after(value, *earlier):
        return lax.optimization_barrier((value, *earlier))[0]

    per = span // BLK

    def place(block_ids):
        chunk = block_ids // per
        turn, share = chunk // shares, chunk % shares
        spot = ((my_share - share) % shares) * turns + (my_turn - turn) % turns
        return spot * per + block_ids % per

    def in_order(row):
        return jnp.concatenate(
            [
                lax.dynamic_slice_in_dim(
                    row,
                    (((my_turn - k) % turns) * shares + (my_share - s) % shares) * span,
                    span,
                )
                for s in range(shares)
                for k in range(turns)
            ]
        )

    half_width = query_weight.shape[1]
    thin = query_weight.shape[0]
    slim = thin // places
    hidden = up_weight.shape[1] // places
    biases = jnp.concatenate([query_bias, value_bias, up_bias])

    def split_biases(by_half):
        by_half = jnp.stack([pick(by_half, (my_half - h) % halves) for h in range(halves)])
        return (
            by_half[:, at : at + b.shape[0]].reshape(-1)
            for b, at in ((query_bias, 0), (value_bias, half_width), (up_bias, 2 * half_width))
        )

    def spread(value, which, count):
        return lax.dynamic_update_slice_in_dim(
            jnp.zeros((value.shape[0] * count,), value.dtype), value, which * value.shape[0], 0
        )

    def small_rows(up_sums, group_at, norm_sums, stats):
        up_natural = jnp.zeros_like(up_sums)
        for i, at in enumerate(group_at):
            up_natural = lax.dynamic_update_slice_in_dim(
                up_natural, up_sums[i * hidden : (i + 1) * hidden], at * hidden, 0
            )
        stats = jnp.pad(stats, (0, width - stats.shape[0]))
        return jnp.concatenate(
            [up_natural.reshape(-1, width), *(row[None] for row in norm_sums), stats[None]], 0
        )

    def finish(layer_out, input_grad, qkv_shard, up_part, down_part, out_part, small):
        deep = up_weight.shape[1] * halves // width
        s_up, (s_o, s_g1, s_s1, s_down, s_g2, s_s2, stats, s_q, s_v) = (
            small[:deep].reshape(-1), small[deep : deep + 9]
        )
        s_q, s_v, s_up = (own_slice(value, halves, my_half, 0) for value in (s_q, s_v, s_up))
        input_rms = jnp.sqrt(stats[:5] / (jnp.maximum(stats[5], 1.0) * width))
        join = lambda w: jnp.moveaxis(w, 0, 1).reshape(thin, -1).astype(f32)
        shard_o = out_part.reshape(thin, -1)[:, :half_width].astype(f32).T
        shard_q, shard_k, shard_v = (qkv_shard[:, i].astype(f32) for i in range(3))
        return (
            layer_out, input_grad, shard_q, s_q, shard_k, shard_v, s_v, shard_o, s_o,
            s_g1, s_s1, join(up_part), s_up, join(down_part).T, s_down, s_g2, s_s2, input_rms,
        )

    if (turns, shares, halves) == (2, 2, 2) and depth <= 4 and rows % TILE == 0:
        qkv_piece = own_slice(
            jnp.concatenate([query_weight, key_weight, value_weight], 1), places, my_place, 0
        )
        ffn_piece = jnp.concatenate(
            [
                own_slice(up_weight, places, my_place, 1),
                own_slice(down_weight, places, my_place, 0).T,
                own_slice(output_weight.T, places, my_place, 0),
            ],
            0,
        )
        near_b = [b[None] for b in (query_bias, value_bias, up_bias)]
        x_in, q_all, f_deep, *far_b = fetch(hidden_in, qkv_piece, ffn_piece, near_b, depth)
        random = place(pick(random_blocks, my_seq)).reshape(-1)
        (
            att0, att1, q, k, v, lse, w_qkv, g_own, groups, key_code, query_code
        ) = project_attend(
            random, hidden_in, x_in, q_all, out_grad, f_deep, segment_ids, token_valid,
            near_b[0], near_b[1], far_b[0], far_b[1],
        )
        group_at = [
            (
                (my_half - h) % halves * places
                + (my_turn - t) % turns * shares
                + (my_share - s) % shares
            )
            for s in range(shares)
            for h, t in spots
        ]
        vectors = jnp.stack(
            [output_bias, norm1_gain, norm1_shift, down_bias, norm2_gain, norm2_shift]
        ).astype(f32)
        (
            out0, out1, slope, g_second, unit, norm_t, near_dn, far_dn, inverse, front_sums
        ) = ffn_front(
            att0, att1, hidden_in, x_in, out_grad, g_own, groups,
            key_code.reshape(length, PAIR), vectors, near_b[2], far_b[2],
        )
        g_first, do_own, do_far, layer_out, *totals, rear_sums, up_sums = ffn_rear(
            att0, att1, slope, g_second, unit, norm_t, out0, out1, near_dn, far_dn, groups,
            inverse, vectors,
        )
        parts = [send(piece, *spot) for piece, spot in zip(totals, spots)]
        dqkv, head_sums = attend_grad(
            random, do_own, do_far, q, k, v, key_code, query_code, lse
        )
        dqkv, head_sums, parts = lax.optimization_barrier((dqkv, head_sums, parts))
        norm_sums = [rear_sums[0], rear_sums[1], rear_sums[2]] + [front_sums[i] for i in (3, 4, 5)]
        stats = jnp.concatenate(
            [jnp.sum(front_sums[6:11], 1), front_sums[11, :1]]
        )
        small = small_rows(up_sums.reshape(-1), group_at, norm_sums, stats)
        small = jnp.concatenate([small, head_sums], 0)
        small = jnp.pad(small, ((0, -small.shape[0] % 8), (0, 0)))
        input_grad, qkv_shard, ffn_shard, small = settle(
            hidden_in, x_in, dqkv, w_qkv, g_first, small, parts
        )
        ffn_shard = ffn_shard.reshape((places,) + ffn_shard.shape[2:])
        return finish(
            layer_out, input_grad.astype(f32), qkv_shard.reshape(thin, 3, half_width),
            ffn_shard[:, :thin], ffn_shard[:, thin : 2 * thin], ffn_shard[:, 2 * thin :], small,
        )

    seg = in_order(pick(segment_ids, my_seq))
    live = in_order(pick(token_valid, my_seq))
    random_seq = pick(random_blocks, my_seq)
    table, wide = block_tables(random_seq, blocks, place)
    key_code = jnp.broadcast_to(jnp.where(live == 1, seg, -1)[:, None], (length, PAIR))
    query_code = jnp.tile(seg.reshape(blocks, BLK), (1, PAIR // BLK))
    part = width // shares
    padded = -(-part // PAIR) * PAIR
    x_own = bring(hidden_in)
    qkv_piece = own_slice(
        jnp.concatenate([query_weight, key_weight, value_weight], 1), places, my_place, 0
    )
    qkv_all = jnp.stack(gather_square(gather_deep(qkv_piece)))
    per_half = shares // halves
    target = my_share // per_half
    qkv_all = jnp.stack(
        [
            pick(
                pick(qkv_all, (my_share - s) % shares),
                (my_half - target) % halves * turns + (my_turn - t) % turns,
            )
            for t in range(turns)
            for s in range(shares)
        ],
        1,
    ).reshape(width, 3, half_width)
    pad_cols = lambda w: jnp.pad(w, [(0, 0)] * (w.ndim - 1) + [(0, padded - part)])
    mine = lambda w: pad_cols(own_slice(w, per_half, my_share % per_half, w.ndim - 1))
    w_qkv = mine(qkv_all).reshape(width, 3 * padded)
    b_q, b_v, b_up = split_biases(jnp.stack([send(biases, h) for h in range(halves)]))
    mine_b = lambda b: pad_cols(own_slice(b, shares, my_share, 0))
    b_qkv = jnp.concatenate([mine_b(b_q), jnp.zeros((padded,), bf16), mine_b(b_v)]).astype(f32)

    ffn_piece = jnp.concatenate(
        [
            own_slice(up_weight, places, my_place, 1),
            own_slice(down_weight, places, my_place, 0).T,
            jnp.pad(
                own_slice(output_weight.T, places, my_place, 0),
                [(0, 0), (0, max(0, hidden - half_width))],
            ).reshape(-1, hidden),
        ],
        0,
    )
    ffn_all = gather_square(gather_deep(ffn_piece))
    groups = [
        (s, i, ffn_all[s][i]) for s in range(shares) for i in range(len(spots))
    ]
    w_up = jnp.concatenate([g[:, :thin].reshape(width, hidden) for _, _, g in groups], 1)
    w_down_t = jnp.concatenate(
        [g[:, thin : 2 * thin].reshape(width, hidden) for _, _, g in groups], 1
    )
    out_all = jnp.stack(
        [jnp.stack([g[:, 2 * thin :] for g in ffn_all[s]]) for s in range(shares)]
    )
    w_out_t = jnp.stack(
        [
            jnp.stack(
                [
                    pick(
                        pick(out_all, (my_share - s) % shares),
                        (my_half - h) % halves * turns + (my_turn - t) % turns,
                    )
                    for t in range(turns)
                    for s in range(shares)
                ],
                1,
            ).reshape(width, half_width)
            for h in range(halves)
        ],
        1,
    ).reshape(width, width)
    w_out_t = jnp.concatenate(
        [own_slice(w_out_t, shares, (my_share + k) % shares, 1) for k in range(shares)], 1
    )
    group_at = [
        ((my_half - spots[i][0]) % halves * places
         + (my_turn - spots[i][1]) % turns * shares + (my_share - s) % shares)
        for s, i, _ in groups
    ]
    b_up = jnp.concatenate(
        [lax.dynamic_slice_in_dim(b_up, at * hidden, hidden) for at in group_at]
    ).astype(f32)

    g_out = bring(out_grad).astype(f32)
    x_seq = jnp.concatenate([send(x_own, 0, 0, k) for k in range(shares)], 0)
    q, k, v = (
        (
            jnp.dot(x_seq, w_qkv[:, i * padded : (i + 1) * padded], preferred_element_type=f32)
            + b_qkv[i * padded : (i + 1) * padded]
        ).astype(bf16)
        for i in range(3)
    )
    att, lse = attend(table, wide, q, k, v, key_code, query_code)
    att = att[:, :part].reshape(shares, rows, part)
    att_own = jnp.concatenate([send(att[s], 0, 0, -s) for s in range(shares)], 1)
    attn_out = lax.dot_general(
        att_own, w_out_t, (((1,), (1,)), ((), ())), preferred_element_type=f32
    ) + output_bias.astype(f32)
    x_full = x_own.astype(f32)
    first_sum = x_full + attn_out
    gain_one, shift_one = norm1_gain.astype(f32), norm1_shift.astype(f32)
    normed = layer_norm(first_sum, gain_one, shift_one)
    normed_low = normed.astype(bf16)
    pre_act = jnp.dot(normed_low, w_up, preferred_element_type=f32) + b_up
    act_low = gelu_tanh(pre_act).astype(bf16)
    ffn_out = lax.dot_general(
        act_low, w_down_t, (((1,), (1,)), ((), ())), preferred_element_type=f32
    ) + down_bias.astype(f32)
    second_sum = normed + ffn_out
    gain_two, shift_two = norm2_gain.astype(f32), norm2_shift.astype(f32)
    layer_out, norm_back = jax.vjp(layer_norm, second_sum, gain_two, shift_two)
    g_second, gain_two_grad, shift_two_grad = norm_back(g_out)
    layer_out = deliver(layer_out.astype(bf16))
    g_ffn = g_second.astype(bf16)
    g_act = jnp.dot(g_ffn, w_down_t, preferred_element_type=f32)
    g_pre = jax.vjp(gelu_tanh, pre_act)[1](g_act)[0].astype(bf16)
    up_part = jnp.dot(normed_low.T, g_pre, preferred_element_type=f32).astype(bf16)
    down_part_t = jnp.dot(g_ffn.T, act_low, preferred_element_type=f32).astype(bf16)
    g_normed = g_second + jnp.dot(g_pre, w_up.T, preferred_element_type=f32)
    g_first, gain_one_grad, shift_one_grad = jax.vjp(layer_norm, first_sum, gain_one, shift_one)[1](
        g_normed
    )
    g_attn = g_first.astype(bf16)
    out_part_t = jnp.dot(g_attn.T, att_own, preferred_element_type=f32).astype(bf16)
    g_att = jnp.dot(g_attn, w_out_t, preferred_element_type=f32).astype(bf16)
    do = jnp.concatenate(
        [send(own_slice(g_att, shares, s, 1), 0, 0, s) for s in range(shares)], 0
    )
    dq, dk, dv = attend_back(table, wide, q, k, v, pad_cols(do), key_code, query_code, lse)

    out_natural = jnp.concatenate(
        [own_slice(out_part_t, shares, (s - my_share) % shares, 1) for s in range(shares)], 1
    ).reshape(depth, turns, shares, slim, halves, half_width)

    def ffn_group(s, i):
        h, t = spots[i]
        at = (s * len(spots) + i) * hidden
        out = pick(out_natural, (my_half - h) % halves, 4)
        out = pick(pick(out, (my_turn - t) % turns, 1), (my_share - s) % shares, 1)
        out = jnp.pad(out, [(0, 0), (0, 0), (0, max(0, hidden - half_width))])
        cut = lambda w: w[:, at : at + hidden].reshape(depth, thin, hidden)
        return jnp.concatenate(
            [cut(up_part), cut(down_part_t), out.reshape(depth, -1, hidden)], 1
        )

    ffn_grads = [
        jnp.stack([ffn_group(s, i) for i in range(len(spots))]) for s in range(shares)
    ]
    total = ffn_grads[0].astype(f32)
    for s in range(1, shares):
        total = total + send(ffn_grads[s], 0, 0, -s).astype(f32)
    ffn_shard = gather_places(reduce_deep(reduce_square(total.astype(bf16))))
    dqkv = jnp.concatenate([dq, dk, dv], 1)
    qkv_part = (
        jnp.dot(x_seq.T, dqkv, preferred_element_type=f32)
        .astype(bf16)
        .reshape(depth, turns, shares, slim, 3, padded)[..., :part]
    )
    got = jnp.stack(
        [send(pick(qkv_part, (my_share + s) % shares, 2), 0, 0, s) for s in range(shares)]
    )
    got = jnp.stack([pick(got, (my_share - s) % shares) for s in range(shares)], 4)
    got = got.reshape(depth, turns, slim, 3, halves, half_width)
    square = jnp.stack(
        [
            pick(pick(got, (my_half - h) % halves, 4), (my_turn - t) % turns, 1)
            for h, t in spots
        ]
    ).reshape(len(spots), depth, slim, 3 * half_width)
    qkv_shard = gather_places(reduce_deep(reduce_square(square))).reshape(thin, 3, half_width)
    back = jnp.dot(dqkv, w_qkv.T, preferred_element_type=f32).reshape(shares, rows, width)
    back_own = back[0]
    for s in range(1, shares):
        back_own = back_own + send(back[s].astype(bf16), 0, 0, -s).astype(f32)
    input_grad = deliver((g_first + back_own).astype(bf16)).astype(f32)

    sums = lambda value: jnp.sum(value.astype(f32), 0)
    valid = live[:rows].astype(f32)
    squares = lambda member: jnp.sum(valid * jnp.sum(member * member, -1))
    stats = jnp.stack(
        [squares(m) for m in (x_full, first_sum, second_sum, attn_out, ffn_out)]
        + [jnp.sum(valid), 0.0, 0.0]
    )
    up_sums = sums(g_pre)
    norm_sums = [
        sums(g_attn), gain_one_grad, shift_one_grad, sums(g_ffn), gain_two_grad, shift_two_grad
    ]
    small = small_rows(up_sums, group_at, norm_sums, stats)
    heads = [spread(sums(d)[:part], my_share, shares)[None] for d in (dq, dv)]
    small = sum_all(jnp.concatenate([small, *heads], 0))
    return finish(
        layer_out, input_grad, qkv_shard, ffn_shard[:, :thin], ffn_shard[:, thin : 2 * thin],
        ffn_shard[:, 2 * thin :], small,
    )


def solution(mesh):
    rows, plain = P("dp", "context", None), P()
    columns, across, halves = P("dp", "tensor"), P("tensor", "dp"), P("tensor")
    return jax.shard_map(
        local,
        mesh=mesh,
        in_specs=(
            rows, rows, P("dp", None), P("dp", None), P("dp", None, None),
            columns, halves, columns, columns, halves, across, plain, plain, plain,
            columns, halves, across, plain, plain, plain,
        ),
        out_specs=(
            rows, rows, columns, halves, columns, columns, halves, across, plain,
            plain, plain, columns, halves, across, plain, plain, plain, plain,
        ),
        check_vma=False,
    )
```

```python
import jax
import jax.numpy as jnp
from jax import lax
from jax.experimental import pallas as pl
from jax.experimental.pallas import tpu as pltpu
from jax.sharding import PartitionSpec as P

HD = 64
BLK = 64
PAIR = 128
SLOTS = 8
WIDE = 512
SCALE = HD ** (-0.5)
EPSILON = 1e-06


NEG_FILL = -1e30


def pair_rows(block, left, scale=None):
    if scale is not None:
        block = block * jnp.asarray(scale, block.dtype)
    zero = jnp.zeros_like(block)
    return jnp.concatenate([jnp.where(left, block, zero), jnp.where(left, zero, block)], 0)


def lane_left(rows):
    return lax.broadcasted_iota(jnp.int32, (rows, PAIR), 1) < HD


def eye_pair():
    lanes = lax.broadcasted_iota(jnp.int32, (BLK, PAIR), 1)
    rows = lax.broadcasted_iota(jnp.int32, (BLK, PAIR), 0)
    return rows == lanes % BLK


def block_rows(index):
    return pl.ds(pl.multiple_of(index * BLK, BLK), BLK)


def slot_bias(slots, first_ok, third_ok, key_code, query_code, own):
    pieces = []
    for slot in range(SLOTS):
        code = query_code
        if slot == 0:
            code = jnp.where(first_ok, query_code, -2)
        if slot == 2:
            code = jnp.where(third_ok, query_code, -2)
        same = key_code[slots[slot]] == code
        if slot == 1:
            same = same | own
        pieces.append(jnp.where(same, 0.0, NEG_FILL))
    return jnp.concatenate(pieces, 0)


def slot_rows(ref, slots, lanes):
    return jnp.concatenate([ref[slot, :, lanes] for slot in slots], 0)


def wide_rows(ref, chunk, lanes):
    count = WIDE // BLK
    return ref[pl.ds(chunk * count, count), :, lanes].reshape(WIDE, PAIR)


def listed(table):
    def find(row):
        slots = [table[row, 1 + slot] for slot in range(SLOTS)]
        return table[row, 0], slots, table[row, 9] == 1, table[row, 10] == 1

    return find


def wide_bias(key_code, query_code, block, chunk):
    same = wide_rows(key_code, chunk, slice(0, PAIR)) == query_code
    key_pos = chunk * WIDE + lax.broadcasted_iota(jnp.int32, (WIDE, PAIR), 0)
    query_pos = block * BLK + lax.broadcasted_iota(jnp.int32, (WIDE, PAIR), 1) % BLK
    return jnp.where(same | (key_pos == query_pos), 0.0, NEG_FILL)


def dot_nt(left, right):
    return lax.dot_general(
        left, right, (((1,), (1,)), ((), ())), preferred_element_type=jnp.float32
    )


def dot_tn(left, right):
    return lax.dot_general(
        left, right, (((0,), (0,)), ((), ())), preferred_element_type=jnp.float32
    )


def dot_nn(left, right):
    return jnp.dot(left, right, preferred_element_type=jnp.float32)


def attend_kernel(table, wide, *refs):
    attend_blocks(listed(table), [wide[0], wide[1]], [(0, table.shape[0], None)], *refs)


def attend_blocks(
    find, wide, legs, q_ref, k_ref, v_ref, key_code, query_code, o_ref, lse_ref, acc, pause=None
):
    length, width = q_ref.shape
    pairs = width // PAIR
    left = lane_left(BLK)
    own = eye_pair()

    def narrow(row, carry):
        block, slots, first_ok, third_ok = find(row)
        rows = block_rows(block)
        code = query_code[pl.ds(block, 1), :]
        bias = slot_bias(slots, first_ok, third_ok, key_code, code, own)
        for pair in range(pairs):
            lanes = slice(pair * PAIR, (pair + 1) * PAIR)
            query = pair_rows(q_ref[rows, lanes], left, SCALE)
            scores = dot_nt(slot_rows(k_ref, slots, lanes), query) + bias
            top = jnp.max(scores, 0, keepdims=True)
            weight = jnp.exp(scores - top)
            total = jnp.sum(weight, 0, keepdims=True)
            probs = (weight * (1.0 / total)).astype(jnp.bfloat16)
            lse_ref[block, pl.ds(pair, 1), :] = top + jnp.log(total)
            both = dot_tn(probs, slot_rows(v_ref, slots, lanes))
            o_ref[rows, lanes] = jnp.where(left, both[:BLK], both[BLK:]).astype(o_ref.dtype)
        return carry

    for start, stop, after in legs:
        lax.fori_loop(start, stop, narrow, 0)
        if after is not None:
            after()

    for which in range(2):
        block = wide[which]
        rows = block_rows(block)
        code = query_code[pl.ds(block, 1), :]

        def first(chunk, carry):
            bias = wide_bias(key_code, code, block, chunk)
            out = []
            for pair in range(pairs):
                lanes = slice(pair * PAIR, (pair + 1) * PAIR)
                query = pair_rows(q_ref[rows, lanes], left, SCALE)
                scores = dot_nt(wide_rows(k_ref, chunk, lanes), query) + bias
                top_old, total_old = carry[pair]
                top = jnp.maximum(top_old, jnp.max(scores, 0, keepdims=True))
                total = total_old * jnp.exp(top_old - top) + jnp.sum(
                    jnp.exp(scores - top), 0, keepdims=True
                )
                out.append((top, total))
            return tuple(out)

        start = (jnp.full((1, PAIR), NEG_FILL), jnp.zeros((1, PAIR), jnp.float32))
        ends = lax.fori_loop(0, length // WIDE, first, (start,) * pairs)
        for pair in range(pairs):
            lse_ref[block, pl.ds(pair, 1), :] = ends[pair][0] + jnp.log(ends[pair][1])
        if pause is not None:
            pause(2 * which)
        acc[...] = jnp.zeros_like(acc)

        def second(chunk, carry):
            bias = wide_bias(key_code, code, block, chunk)
            for pair in range(pairs):
                lanes = slice(pair * PAIR, (pair + 1) * PAIR)
                query = pair_rows(q_ref[rows, lanes], left, SCALE)
                scores = dot_nt(wide_rows(k_ref, chunk, lanes), query) + bias
                probs = jnp.exp(scores - lse_ref[block, pl.ds(pair, 1), :]).astype(jnp.bfloat16)
                acc[pair] += dot_tn(probs, wide_rows(v_ref, chunk, lanes))
            return carry

        lax.fori_loop(0, length // WIDE, second, 0)
        for pair in range(pairs):
            lanes = slice(pair * PAIR, (pair + 1) * PAIR)
            both = acc[pair]
            o_ref[rows, lanes] = jnp.where(left, both[:BLK], both[BLK:]).astype(o_ref.dtype)
        if pause is not None:
            pause(2 * which + 1)


def attend_back_kernel(table, wide, *refs):
    attend_back_blocks(listed(table), [wide[0], wide[1]], table.shape[0], *refs)


def attend_back_blocks(
    find, wide, count, q_ref, k_ref, v_ref, do_ref, key_code, query_code, lse_ref,
    dq_ref, dk_ref, dv_ref, dk_sum, dv_sum, dq_acc,
):
    length, width = q_ref.shape
    pairs = width // PAIR
    left = lane_left(BLK)
    own = eye_pair()
    dk_sum[...] = jnp.zeros_like(dk_sum)
    dv_sum[...] = jnp.zeros_like(dv_sum)

    def narrow(row, carry):
        block, slots, first_ok, third_ok = find(row)
        rows = block_rows(block)
        code = query_code[pl.ds(block, 1), :]
        bias = slot_bias(slots, first_ok, third_ok, key_code, code, own)
        for pair in range(pairs):
            lanes = slice(pair * PAIR, (pair + 1) * PAIR)
            query = pair_rows(q_ref[rows, lanes], left, SCALE)
            grad = pair_rows(do_ref[rows, lanes], left)
            keys = slot_rows(k_ref, slots, lanes)
            values = slot_rows(v_ref, slots, lanes)
            scores = dot_nt(keys, query) + bias
            probs = jnp.exp(scores - lse_ref[block, pl.ds(pair, 1), :])
            g_probs = dot_nt(values, grad)
            terms = probs * g_probs
            g_scores = (terms - probs * jnp.sum(terms, 0, keepdims=True)).astype(jnp.bfloat16)
            dv = dot_nn(probs.astype(jnp.bfloat16), grad)
            dk = dot_nn(g_scores, query)
            both = dot_tn(g_scores, keys)
            dq_ref[rows, lanes] = (jnp.where(left, both[:BLK], both[BLK:]) * SCALE).astype(
                dq_ref.dtype
            )
            for slot in range(SLOTS):
                spot = block_rows(slots[slot])
                part = slice(slot * BLK, (slot + 1) * BLK)
                dk_sum[spot, lanes] += dk[part]
                dv_sum[spot, lanes] += dv[part]
        return carry

    lax.fori_loop(0, count, narrow, 0)

    for which in range(2):
        block = wide[which]
        rows = block_rows(block)
        code = query_code[pl.ds(block, 1), :]

        def pieces(chunk, pair, bias):
            keys_at = pl.ds(pl.multiple_of(chunk * WIDE, WIDE), WIDE)
            lanes = slice(pair * PAIR, (pair + 1) * PAIR)
            query = pair_rows(q_ref[rows, lanes], left, SCALE)
            grad = pair_rows(do_ref[rows, lanes], left)
            keys = wide_rows(k_ref, chunk, lanes)
            scores = dot_nt(keys, query) + bias
            probs = jnp.exp(scores - lse_ref[block, pl.ds(pair, 1), :])
            return keys_at, lanes, query, grad, keys, probs, probs * dot_nt(wide_rows(v_ref, chunk, lanes), grad)

        def first(chunk, carry):
            bias = wide_bias(key_code, code, block, chunk)
            return tuple(
                carry[pair] + jnp.sum(pieces(chunk, pair, bias)[-1], 0, keepdims=True)
                for pair in range(pairs)
            )

        deltas = lax.fori_loop(
            0, length // WIDE, first, (jnp.zeros((1, PAIR), jnp.float32),) * pairs
        )
        dq_acc[...] = jnp.zeros_like(dq_acc)

        def second(chunk, carry):
            bias = wide_bias(key_code, code, block, chunk)
            for pair in range(pairs):
                keys_at, lanes, query, grad, keys, probs, terms = pieces(chunk, pair, bias)
                g_scores = (terms - probs * carry[pair]).astype(jnp.bfloat16)
                dv_sum[keys_at, lanes] += dot_nn(probs.astype(jnp.bfloat16), grad)
                dk_sum[keys_at, lanes] += dot_nn(g_scores, query)
                dq_acc[pair] += dot_tn(g_scores, keys)
            return carry

        lax.fori_loop(0, length // WIDE, second, deltas)
        for pair in range(pairs):
            lanes = slice(pair * PAIR, (pair + 1) * PAIR)
            both = dq_acc[pair]
            dq_ref[rows, lanes] = (jnp.where(left, both[:BLK], both[BLK:]) * SCALE).astype(
                dq_ref.dtype
            )
    dk_ref[...] = dk_sum[...].astype(dk_ref.dtype)
    dv_ref[...] = dv_sum[...].astype(dv_ref.dtype)


def in_blocks(rows):
    return rows.reshape(-1, BLK, rows.shape[-1])


VMEM_SPEC = pl.BlockSpec(memory_space=pltpu.VMEM)
SMEM_SPEC = pl.BlockSpec(memory_space=pltpu.SMEM)
ROOM = pltpu.CompilerParams(vmem_limit_bytes=60 * 1024 * 1024)


def attend(table, wide, q, k, v, key_code, query_code):
    length, width = q.shape
    return pl.pallas_call(
        attend_kernel,
        out_shape=(
            jax.ShapeDtypeStruct((length, width), jnp.bfloat16),
            jax.ShapeDtypeStruct((length // BLK, 8, PAIR), jnp.float32),
        ),
        in_specs=[SMEM_SPEC] * 2 + [VMEM_SPEC] * 5,
        out_specs=(VMEM_SPEC, VMEM_SPEC),
        scratch_shapes=[pltpu.VMEM((width // PAIR, PAIR, PAIR), jnp.float32)],
        compiler_params=ROOM,
        cost_estimate=pl.CostEstimate(
            flops=length * width * 1024 * 60, bytes_accessed=length * width * 8,
            transcendentals=length * width * 8,
        ),
        name="attend",
    )(table, wide, q, in_blocks(k), in_blocks(v), in_blocks(key_code), query_code)


def attend_back(table, wide, q, k, v, do, key_code, query_code, lse):
    length, width = q.shape
    shape = jax.ShapeDtypeStruct((length, width), jnp.bfloat16)
    return pl.pallas_call(
        attend_back_kernel,
        out_shape=(shape, shape, shape),
        in_specs=[SMEM_SPEC] * 2 + [VMEM_SPEC] * 7,
        out_specs=(VMEM_SPEC,) * 3,
        scratch_shapes=[
            pltpu.VMEM((length, width), jnp.float32),
            pltpu.VMEM((length, width), jnp.float32),
            pltpu.VMEM((width // PAIR, PAIR, PAIR), jnp.float32),
        ],
        compiler_params=ROOM,
        cost_estimate=pl.CostEstimate(
            flops=length * width * 1024 * 70, bytes_accessed=length * width * 14,
            transcendentals=length * width * 8,
        ),
        name="attend_back",
    )(table, wide, q, in_blocks(k), in_blocks(v), do, in_blocks(key_code), query_code, lse)


GROUPS = 8
DUOS = GROUPS // 2
TILE = 256
FRONT = 512
ANY_SPEC = pl.BlockSpec(memory_space=pl.ANY)
DMA = pltpu.SemaphoreType.DMA
WIDE_ROOM = pltpu.CompilerParams(vmem_limit_bytes=63 * 1024 * 1024)


def normalize(values):
    row_mean = jnp.mean(values, -1, keepdims=True)
    centered = values - row_mean
    row_var = jnp.mean(centered * centered, -1, keepdims=True)
    inverse = lax.rsqrt(row_var + EPSILON)
    return centered * inverse, inverse


def normalize_back(grad, unit, inverse):
    return inverse * (
        grad
        - jnp.mean(grad, -1, keepdims=True)
        - unit * jnp.mean(grad * unit, -1, keepdims=True)
    )


def gelu_both(u):
    root = 0.7978845608028654
    square = u * u
    inner = jnp.tanh(u * (root + (root * 0.044715) * square))
    half = 0.5 + 0.5 * inner
    slope = half + u * (0.5 - 0.5 * (inner * inner)) * (root + (3.0 * root * 0.044715) * square)
    return u * half, slope


def start_copies(pairs, sem):
    copies = [pltpu.make_async_copy(src, dst, sem.at[i]) for i, (src, dst) in enumerate(pairs)]
    for copy in copies:
        copy.start()
    return copies


def wait_copies(copies):
    for copy in copies:
        copy.wait()


def row_of(ref):
    return ref[...].astype(jnp.float32).reshape(1, ref.shape[0])


def my_spot():
    place = lax.axis_index("context")
    return lax.axis_index("tensor"), place // 2, place % 2


def group_homes():
    half, turn, share = my_spot()
    return [
        ((half + h) % 2, ((turn + t) % 2) * 2 + (share + s) % 2)
        for s in range(2)
        for h in range(2)
        for t in range(2)
    ]


def lanes_of(g, cols):
    return pl.ds((g % 2) * cols, cols)


def place_block(block, per):
    half, turn, share = my_spot()
    chunk = block // per
    spot = ((share + chunk) % 2) * 2 + (turn + chunk // 2) % 2
    return spot * per + block % per


def computed(random, per, blocks):
    def find(row):
        block = row + 2
        ids = [block - 1, block, (block + 1) % blocks]
        slots = [place_block(i, per) for i in ids]
        slots += [place_block(jnp.int32(i), per) for i in range(2)]
        slots += [random[block * 3 + i] for i in range(3)]
        return slots[1], slots, block >= 3, block <= blocks - 2

    return find, [place_block(jnp.int32(i), per) for i in range(2)]


def write_codes(segments, live, key_code, query_code, span):
    half, turn, share = my_spot()
    row = pl.ds(half * 2 + turn, 1)
    left = lax.broadcasted_iota(jnp.int32, (1, PAIR), 1) < HD
    per = span // BLK
    for spot in range(4):
        chunk = ((turn + spot) % 2) * 2 + (share + spot // 2) % 2
        lanes = pl.ds(pl.multiple_of(chunk * span, span), span)
        seg = segments[row, lanes]
        code = jnp.where(live[row, lanes] == 1, seg, -1)
        key_code[pl.ds(spot * per, per)] = jnp.broadcast_to(code, (PAIR, span)).T.reshape(
            per, BLK, PAIR
        )
        for two in range(per // 2):
            both = seg[:, two * PAIR : (two + 1) * PAIR]
            turned = pltpu.roll(both, HD, 1)
            at = spot * per + 2 * two
            query_code[at : at + 1, :] = jnp.where(left, both, turned)
            query_code[at + 1 : at + 2, :] = jnp.where(left, turned, both)


def project_attend_kernel(
    random, hidden, x_in, q_all, g_all, f_deep, segments, live, b_q, b_v, far_q, far_v,
    own_ref, other_home, q_home, k_home, v_home, w_home, g_home,
    n1, n2, n3, f0, f1, f2, f3, lse_ref, key_code, query_code,
    x_v, q_v, k_v, v_v, o_v, w_v, acc, in_sem, out_sem, w_sem, send_sem, recv_sem,
):
    span = hidden.shape[1]
    length, width = q_v.shape
    depth = f_deep.shape[0]
    half, turn, share = my_spot()
    across, beside, partner = neighbours()
    weights = start_copies(
        [(q_all.at[share, t, s], w_v.at[:, t, s]) for t in range(2) for s in range(2)], w_sem
    )
    chunks = [hidden.at[half * 2 + turn]] + [x_in.at[i] for i in range(3)]
    loads = start_copies(
        [(x, x_v.at[pl.ds(i * span, span)]) for i, x in enumerate(chunks)], in_sem
    )
    signal_all([across, beside, partner])
    ids = iter(range(send_sem.shape[0]))
    started = []

    def go(src, dst, device):
        i = next(ids)
        copy = remote(src, dst, send_sem.at[i], recv_sem.at[i], device)
        copy.start()
        started.append(copy)
        return copy

    to_beside, to_across, to_partner, relays, ends = [], [], [], [], []
    for d in range(depth):
        to_beside.append(go(f_deep.at[d], n1.at[d], beside))
        to_across.append(go(f_deep.at[d], n2.at[d], across))
        ends.append(go(f_deep.at[d], f0.at[d], partner))
    g_copy = go(g_all.at[half * 2 + (turn + 1) % 2], g_home, beside)

    def arrived(d):
        to_beside[d].wait_recv()
        ends.append(go(n1.at[d], f1.at[d], partner))
        if d < depth - 1 or depth == 1:
            relays.append((d, go(n1.at[d], n3.at[d], across)))
        to_across[d].wait_recv()
        ends.append(go(n2.at[d], f2.at[d], partner))
        if d == depth - 1 and depth > 1:
            relays.append((d, go(n2.at[d], n3.at[d], beside)))

    def relayed():
        if relays:
            d, copy = relays.pop(0)
            copy.wait_recv()
            ends.append(go(n3.at[d], f3.at[d], partner))

    write_codes(segments, live, key_code, query_code, span)
    same = half == share
    bias = jnp.concatenate(
        [
            jnp.where(same, row_of(b_q), row_of(far_q)),
            jnp.zeros((1, width), jnp.float32),
            jnp.where(same, row_of(b_v), row_of(far_v)),
        ],
        1,
    )
    wait_copies(weights)
    wait_copies(loads)
    per = span // BLK

    def project(i, carry):
        at = pl.ds(pl.multiple_of(i * span, span), span)
        w_qkv = w_v[...].reshape(x_v.shape[1], 3 * width)
        value = (dot_nn(x_v[at, :], w_qkv) + bias).astype(jnp.bfloat16)
        q_v[at, :] = value[:, :width]
        k_v[pl.ds(i * per, per)] = value[:, width : 2 * width].reshape(per, BLK, width)
        v_v[pl.ds(i * per, per)] = value[:, 2 * width :].reshape(per, BLK, width)
        return carry

    lax.fori_loop(0, 4, project, 0)
    stores = start_copies([(q_v, q_home), (k_v, k_home), (v_v, v_home), (w_v, w_home)], out_sem)
    blocks = length // BLK
    find, wide = computed(random, span // BLK, blocks)
    count = blocks - 2
    marks = [3 + d * 6 for d in range(depth)]
    marks = [min(mark, count - 1) for mark in marks] + [count]
    legs, start = [], 0
    for d, mark in enumerate(marks):
        legs.append((start, mark, (lambda d=d: arrived(d)) if d < depth else relayed))
        start = mark
    attend_blocks(
        find, wide, legs, q_v, k_v, v_v, key_code, query_code, o_v, lse_ref, acc,
        pause=lambda step: relayed() if step in (1, 2) else None,
    )
    own_ref[...] = o_v[: length // 2, :]
    swap = go(o_v.at[pl.ds(length // 2, length // 2)], other_home, partner)
    while relays:
        relayed()
    for copy in ends + [g_copy, swap]:
        copy.wait_recv()
    for copy in started:
        copy.wait_send()
    wait_copies(stores)


def project_attend(
    random, hidden, x_in, q_all, out_grad, f_deep, segments, live, b_q, b_v, far_q, far_v
):
    span, features = hidden.shape[1:]
    length = 4 * span
    depth, slim, cols = q_all.shape[3:]
    width = cols // 3
    bf16, shape = jnp.bfloat16, jax.ShapeDtypeStruct
    piece = shape(f_deep.shape, bf16)
    outs = pl.pallas_call(
        project_attend_kernel,
        out_shape=(shape((length // 2, width), bf16),) * 2
        + (shape((length, width), bf16),)
        + (shape((length // BLK, BLK, width), bf16),) * 2
        + (shape((depth, 2, 2, slim, cols), bf16), shape((span, features), bf16))
        + (piece,) * 7
        + (
            shape((length // BLK, 8, PAIR), jnp.float32),
            shape((length // BLK, BLK, PAIR), jnp.int32),
            shape((length // BLK, PAIR), jnp.int32),
        ),
        in_specs=[SMEM_SPEC] + [ANY_SPEC] * 5 + [VMEM_SPEC] * 6,
        out_specs=(VMEM_SPEC,) + (ANY_SPEC,) * 13 + (VMEM_SPEC,) * 3,
        scratch_shapes=[pltpu.VMEM((length, features), bf16)]
        + [pltpu.VMEM((length, width), bf16)]
        + [pltpu.VMEM((length // BLK, BLK, width), bf16)] * 2
        + [pltpu.VMEM((length, width), bf16)]
        + [
            pltpu.VMEM((depth, 2, 2, slim, cols), bf16),
            pltpu.VMEM((width // PAIR, PAIR, PAIR), jnp.float32),
            DMA((4,)), DMA((4,)), DMA((4,)), DMA((8 * depth + 2,)), DMA((8 * depth + 2,)),
        ],
        compiler_params=pltpu.CompilerParams(
            vmem_limit_bytes=63 * 1024 * 1024, collective_id=3, has_side_effects=True
        ),
        cost_estimate=pl.CostEstimate(
            flops=length * width * 1024 * 65, bytes_accessed=length * width * 16,
            transcendentals=length * width * 8,
        ),
        name="project_attend",
    )(
        random, hidden, x_in, q_all, out_grad, f_deep, segments, live, b_q, b_v, far_q, far_v
    )
    att0, att1, q, k, v, w_qkv, g_in, *pieces, lse, key_code, query_code = outs
    w_qkv = w_qkv.reshape(features, cols)
    return att0, att1, q, k, v, lse, w_qkv, g_in, [f_deep] + pieces, key_code, query_code


def attend_grad_kernel(
    random, do0, do1, q_in, k_in, v_in, key_code, query_code, lse_ref,
    d_ref, sums,
    q_v, k_v, v_v, do_v, dk_sum, dv_sum, acc, in_sem,
):
    f32 = jnp.float32
    length, width = q_v.shape
    half_length = length // 2
    loads = start_copies(
        [
            (q_in, q_v), (k_in, k_v), (v_in, v_v),
            (do0, do_v.at[pl.ds(0, half_length)]),
            (do1, do_v.at[pl.ds(half_length, half_length)]),
        ],
        in_sem,
    )
    wait_copies(loads)
    parts = [d_ref.at[:, pl.ds(i * width, width)] for i in range(3)]
    blocks = length // BLK
    find, wide = computed(random, blocks // 4, blocks)
    attend_back_blocks(
        find, wide, blocks - 2, q_v, k_v, v_v, do_v, key_code, query_code, lse_ref,
        *parts, dk_sum, dv_sum, acc,
    )
    share = my_spot()[2]
    sums[...] = jnp.zeros_like(sums)
    for s in range(2):

        @pl.when(share == s)
        def _():
            lanes = slice(s * width, (s + 1) * width)
            sums[0:1, lanes] = jnp.sum(d_ref[:, :width].astype(f32), 0, keepdims=True)
            sums[1:2, lanes] = jnp.sum(d_ref[:, 2 * width :].astype(f32), 0, keepdims=True)


def attend_grad(random, do0, do1, q, k, v, key_code, query_code, lse):
    length, width = q.shape
    f32, bf16, shape = jnp.float32, jnp.bfloat16, jax.ShapeDtypeStruct
    return pl.pallas_call(
        attend_grad_kernel,
        out_shape=(shape((length, 3 * width), bf16), shape((8, 2 * width), f32)),
        in_specs=[SMEM_SPEC] + [ANY_SPEC] * 5 + [VMEM_SPEC] * 3,
        out_specs=(VMEM_SPEC,) * 2,
        scratch_shapes=[pltpu.VMEM((length, width), bf16)]
        + [pltpu.VMEM((length // BLK, BLK, width), bf16)] * 2
        + [pltpu.VMEM((length, width), bf16)]
        + [pltpu.VMEM((length, width), f32)] * 2
        + [pltpu.VMEM((width // PAIR, PAIR, PAIR), f32), DMA((5,))],
        compiler_params=WIDE_ROOM,
        cost_estimate=pl.CostEstimate(
            flops=length * width * 1024 * 75, bytes_accessed=length * width * 30,
            transcendentals=length * width * 8,
        ),
        name="attend_grad",
    )(random, do0, do1, q, k, v, key_code, query_code, lse)


def load_weights(groups, w_up, w_dn, w_out, up_sem, dn_sem, wo_sem):
    depth, deep, cols = groups[0].shape
    thin = w_up.shape[2]
    slim = deep - 2 * thin
    homes = group_homes()
    out_loads = []
    for g in range(GROUPS):
        half, at = homes[g]
        for d in range(depth):
            spot = pl.ds(pl.multiple_of(d * thin + at * slim, 16), slim)
            out_loads.append(
                pltpu.make_async_copy(
                    groups[g].at[d, pl.ds(2 * thin, slim)], w_out.at[half, spot], wo_sem.at[g, d]
                )
            )
    up_loads = [
        pltpu.make_async_copy(
            groups[g].at[:, pl.ds(0, thin)], w_up.at[g // 2, :, :, lanes_of(g, cols)], up_sem.at[g]
        )
        for g in range(GROUPS)
    ]
    dn_loads = [
        pltpu.make_async_copy(
            groups[g].at[:, pl.ds(thin, thin)],
            w_dn.at[g // 2, :, :, lanes_of(g, cols)],
            dn_sem.at[g],
        )
        for g in range(GROUPS)
    ]
    return out_loads, up_loads, dn_loads


def whole(ref, g):
    depth, thin, cols = ref.shape[1:]
    return ref[g].reshape(depth * thin, cols)


def ffn_front_kernel(att0, att1, hidden, x_in, g_all, g_in, *rest):
    groups = rest[:GROUPS]
    (
        key_code, v_out, v_gain1, v_shift1, v_down, v_gain2, v_shift2, b_near, b_far,
        out0_home, out1_home, slope_home, g_second_home, unit_home, norm_t_home, down_home,
        inverse_ref, sums,
        att_v, x_v, g_v, w_up, w_dn, w_out, act, slope, normed_low,
        out_v, g_second_v, unit_v, norm_t, g_ffn_t, stage, b_up, b_all,
        in_sem, up_sem, dn_sem, wo_sem, stage_sem, home_sem, end_sem,
    ) = rest[GROUPS:]
    f32, bf16 = jnp.float32, jnp.bfloat16
    rows, width = x_v.shape
    span = hidden.shape[1]
    depth, deep, cols = groups[0].shape
    half, turn, share = my_spot()
    x_chunks = (hidden.at[half * 2 + turn], x_in.at[0])
    g_chunks = (g_all.at[half * 2 + turn], g_in)
    other = (share + 1) % 2
    out_loads, up_loads, dn_loads = load_weights(groups, w_up, w_dn, w_out, up_sem, dn_sem, wo_sem)
    loads = start_copies(
        [(a, att_v.at[:, lanes_of(i, cols)]) for i, a in enumerate((att0, att1))]
        + [(x, x_v.at[pl.ds(i * span, span)]) for i, x in enumerate(x_chunks)]
        + [(g, g_v.at[pl.ds(i * span, span)]) for i, g in enumerate(g_chunks)],
        in_sem,
    )
    for copy in out_loads + up_loads + dn_loads:
        copy.start()
    sums[...] = jnp.zeros_like(sums)
    b_all[0:1, :] = row_of(b_near)
    b_all[1:2, :] = row_of(b_far)
    for g in range(GROUPS):
        at = group_homes()[g][1]
        lanes = pl.ds(pl.multiple_of(at * cols, PAIR), cols)
        value = b_all[g // 2 % 2 : g // 2 % 2 + 1, lanes]
        b_up[g // 2 : g // 2 + 1, (g % 2) * cols : (g % 2 + 1) * cols] = value
    wait_copies(loads + out_loads)
    b_out, gain1, shift1, b_down, gain2, shift2 = (
        row_of(ref) for ref in (v_out, v_gain1, v_shift1, v_down, v_gain2, v_shift2)
    )

    def add_sum(index, value):
        sums[index : index + 1, :] += jnp.sum(value, 0, keepdims=True)

    def homes(tile):
        at = pl.ds(pl.multiple_of(tile * FRONT, FRONT), FRONT)
        return [
            pltpu.make_async_copy(src, dst, home_sem.at[i, tile])
            for i, (src, dst) in enumerate(
                [
                    (slope.at[:, at], slope_home.at[:, at]),
                    (g_second_v.at[at], g_second_home.at[at]),
                    (unit_v.at[at], unit_home.at[at]),
                ]
            )
        ]

    def tile_step(tile, carry):
        at = pl.ds(pl.multiple_of(tile * FRONT, FRONT), FRONT)
        live = (key_code[at, :1] >= 0).astype(f32)
        add_sum(11, jnp.broadcast_to(live, (FRONT, width)))
        attn = b_out + dot_nt(att_v[at, :], jnp.concatenate([w_out[share], w_out[other]], 1))
        x = x_v[at, :].astype(f32)
        first = x + attn
        add_sum(6, live * (x * x))
        add_sum(7, live * (first * first))
        add_sum(9, live * (attn * attn))
        unit1, inverse1 = normalize(first)
        unit_v[at, :] = unit1
        inverse_ref[at, :] = inverse1
        normed = unit1 * gain1 + shift1
        low = normed.astype(bf16)
        normed_low[...] = low
        norm_t[:, at] = low.T

        @pl.when(tile == 0)
        def _():
            wait_copies(up_loads + dn_loads)

        def up_step(g, ffn):
            pre = dot_nn(normed_low[...], whole(w_up, g)) + b_up[pl.ds(g, 1), :]
            value, rise = gelu_both(pre)
            value = value.astype(bf16)
            act[g, at, :] = value
            slope[g, at, :] = rise.astype(bf16)
            return ffn + dot_nt(value, whole(w_dn, g))

        ffn = lax.fori_loop(0, DUOS, up_step, jnp.broadcast_to(b_down, (FRONT, width)))
        second = normed + ffn
        add_sum(8, live * (second * second))
        add_sum(10, live * (ffn * ffn))
        unit2, inverse2 = normalize(second)
        out_v[at, :] = (unit2 * gain2 + shift2).astype(bf16)
        g_out = g_v[at, :].astype(f32)
        add_sum(4, g_out * unit2)
        add_sum(5, g_out)
        g_second = normalize_back(g_out * gain2, unit2, inverse2)
        g_second_v[at, :] = g_second
        g_ffn = g_second.astype(bf16)
        add_sum(3, g_ffn.astype(f32))
        g_ffn_t[:, at] = g_ffn.T
        for copy in homes(tile):
            copy.start()
        return carry

    lax.fori_loop(0, rows // FRONT, tile_step, 0)
    last = start_copies(
        [
            (norm_t, norm_t_home),
            (out_v.at[pl.ds(0, span)], out0_home),
            (out_v.at[pl.ds(span, span)], out1_home),
        ],
        end_sem,
    )

    def leave(g):
        return pltpu.make_async_copy(stage.at[g], down_home.at[g], stage_sem.at[g])

    def down_step(duo, carry):
        down = dot_nn(g_ffn_t[...], act[duo]).astype(bf16).reshape(depth, -1, 2 * cols)
        for i in range(2):
            stage[2 * duo + i] = down[:, :, i * cols : (i + 1) * cols]
            leave(2 * duo + i).start()
        return carry

    lax.fori_loop(0, DUOS, down_step, 0)
    for tile in range(rows // FRONT):
        wait_copies(homes(tile))
    wait_copies([leave(g) for g in range(GROUPS)] + last)


def ffn_front(att0, att1, hidden, x_in, g_all, g_in, groups, key_code, vectors, b_near, b_far):
    rows, part = att0.shape
    width = hidden.shape[2]
    depth, deep, cols = groups[0].shape
    thin = width // depth
    f32, bf16, shape = jnp.float32, jnp.bfloat16, jax.ShapeDtypeStruct
    weights = pltpu.VMEM((DUOS, depth, thin, 2 * cols), bf16)
    flat = pltpu.VMEM((rows, width), bf16)
    tall = pltpu.VMEM((rows, width), f32)
    deep_rows = pltpu.VMEM((DUOS, rows, 2 * cols), bf16)
    turned = pltpu.VMEM((width, rows), bf16)
    return pl.pallas_call(
        ffn_front_kernel,
        out_shape=(
            shape((rows // 2, width), bf16), shape((rows // 2, width), bf16),
            shape((DUOS, rows, 2 * cols), bf16),
            shape((rows, width), f32), shape((rows, width), f32), shape((width, rows), bf16),
            shape((GROUPS, depth, thin, cols), bf16), shape((rows, 1), f32), shape((16, width), f32),
        ),
        in_specs=[ANY_SPEC] * (6 + GROUPS) + [VMEM_SPEC] * 9,
        out_specs=(ANY_SPEC,) * 7 + (VMEM_SPEC,) * 2,
        scratch_shapes=[
            flat, flat, flat, weights, weights, pltpu.VMEM((2, width, part), bf16),
            deep_rows, deep_rows, pltpu.VMEM((FRONT, width), bf16),
            flat, tall, tall, turned, turned, pltpu.VMEM((GROUPS, depth, thin, cols), bf16),
            pltpu.VMEM((DUOS, 2 * cols), f32), pltpu.VMEM((2, 4 * cols), f32),
            DMA((6,)), DMA((GROUPS,)), DMA((GROUPS,)), DMA((GROUPS, depth)), DMA((GROUPS,)),
            DMA((3, rows // FRONT)), DMA((3,)),
        ],
        compiler_params=WIDE_ROOM,
        cost_estimate=pl.CostEstimate(
            flops=38 * 10**9, bytes_accessed=40 * 10**6, transcendentals=rows * GROUPS * cols
        ),
        name="ffn_front",
    )(att0, att1, hidden, x_in, g_all, g_in, *groups, key_code, *vectors, b_near, b_far)


def ffn_rear_kernel(
    att0, att1, slope_in, g_second_in, unit_in, norm_t_in, out0, out1, downs, *rest
):
    groups = rest[:GROUPS]
    (
        inverse_ref, v_gain1,
        g_first_home, do_own, do_far, layer_home, *totals
    ) = rest[GROUPS : GROUPS + 6 + DUOS]
    (
        sums, up_sums,
        att_v, slope, g_second_v, unit_v, norm_t, w_up, w_dn, w_out, g_pre,
        g_first_v, g_att_v, g_attn_t, out_v, far_v, got_v, got_dn, near_v, stage,
        in_sem, up_sem, dn_sem, wo_sem, stage_sem, home_sem, out_sem,
        l_send, l_recv, a_send, a_recv, u_send, u_recv,
    ) = rest[GROUPS + 6 + DUOS :]
    f32, bf16 = jnp.float32, jnp.bfloat16
    rows, width = unit_v.shape
    span = out0.shape[0]
    depth, deep, cols = groups[0].shape
    thin = w_up.shape[2]
    slim = deep - 2 * thin
    half, turn, share = my_spot()
    other = (share + 1) % 2
    across, beside, partner = neighbours()
    out_loads, up_loads, dn_loads = load_weights(groups, w_up, w_dn, w_out, up_sem, dn_sem, wo_sem)
    wait_order = [
        pltpu.make_async_copy(src, dst, in_sem.at[i])
        for i, (src, dst) in enumerate(
            [
                (g_second_in, g_second_v), (slope_in, slope), (unit_in, unit_v),
                (norm_t_in, norm_t), (att0, att_v.at[:, lanes_of(0, cols)]),
                (att1, att_v.at[:, lanes_of(1, cols)]),
            ]
        )
    ]
    for copy in wait_order[:1] + dn_loads + wait_order[1:2] + up_loads + wait_order[2:3]:
        copy.start()
    for copy in out_loads + wait_order[3:]:
        copy.start()
    late = start_copies([(out0, out_v), (downs.at[pl.ds(0, DUOS)], near_v)], out_sem)
    signal_all([across, beside, partner])
    mine = layer_home.at[half * 2 + turn]
    theirs = layer_home.at[half * 2 + (turn + 1) % 2]
    layer = [
        remote(out1, mine, l_send.at[0], l_recv.at[0], beside),
        remote(out0, mine, l_send.at[1], l_recv.at[1], across),
        remote(theirs, theirs, l_send.at[2], l_recv.at[2], across),
        remote(downs.at[pl.ds(DUOS, DUOS)], got_dn, l_send.at[3], l_recv.at[3], partner),
    ]
    layer[0].start()
    layer[1].start()
    layer[3].start()
    sums[...] = jnp.zeros_like(sums)
    up_sums[...] = jnp.zeros_like(up_sums)
    gain1 = row_of(v_gain1)
    wait_copies(wait_order[:1] + dn_loads + wait_order[1:2])
    out_weight = lambda: jnp.concatenate([w_out[share], w_out[other]], 1)

    def add_sum(index, value):
        sums[index : index + 1, :] += jnp.sum(value, 0, keepdims=True)

    def tile_rows(tile):
        return pl.ds(pl.multiple_of(tile * TILE, TILE), TILE)

    def give(tile):
        at = tile_rows(tile)
        return remote(g_att_v.at[1, at], do_far.at[at], a_send.at[tile], a_recv.at[tile], partner)

    tiles = rows // TILE

    def tile_step(tile, carry):
        at = tile_rows(tile)

        @pl.when(tile == 0)
        def _():
            wait_copies(up_loads + wait_order[2:] + out_loads)

        @pl.when(tile == tiles - 1)
        def _():
            layer[0].wait_recv()
            layer[2].start()

        g_second = g_second_v[at, :]
        g_ffn = g_second.astype(bf16)

        def back_step(g, total):
            grad = (dot_nn(g_ffn, whole(w_dn, g)) * slope[g, at, :].astype(f32)).astype(bf16)
            g_pre[g, at, :] = grad
            up_sums[pl.ds(g, 1), :] += jnp.sum(grad.astype(f32), 0, keepdims=True)
            return total + dot_nt(grad, whole(w_up, g))

        g_normed = lax.fori_loop(0, DUOS, back_step, g_second)
        unit1 = unit_v[at, :]
        add_sum(1, g_normed * unit1)
        add_sum(2, g_normed)
        g_first = normalize_back(g_normed * gain1, unit1, inverse_ref[at, :])
        g_first_v[at, :] = g_first
        g_attn = g_first.astype(bf16)
        add_sum(0, g_attn.astype(f32))
        g_attn_t[:, at] = g_attn.T
        both = dot_nn(g_attn, out_weight()).astype(bf16)
        g_att_v[0, at, :] = both[:, :cols]
        g_att_v[1, at, :] = both[:, cols:]
        give(tile).start()
        return carry

    lax.fori_loop(0, tiles, tile_step, 0)
    homes = start_copies([(g_att_v.at[0], do_own), (g_first_v, g_first_home)], home_sem)
    wait_copies(late)
    own_out = pltpu.make_async_copy(out_v, mine, out_sem.at[0])
    own_out.start()
    both = dot_nn(g_attn_t[...], att_v[...]).astype(bf16)
    w_out[share] = both[:, :cols]
    w_out[other] = both[:, cols:]

    def out_rows(g, d):
        where = (half + g // 2) % 2
        at = ((turn + g) % 2) * 2 + (share + g // 4) % 2
        return w_out[where, pl.ds(pl.multiple_of(d * thin + at * slim, 16), slim), :]

    def up_of(duo):
        up = dot_nn(norm_t[...], g_pre[duo]).astype(bf16).reshape(depth, thin, 2 * cols)
        return [(2 * duo + i, up[:, :, i * cols : (i + 1) * cols]) for i in range(2)]

    def pass_on(i):
        return remote(far_v.at[i], got_v.at[i], u_send.at[i], u_recv.at[i], partner)

    def far_step(duo, carry):
        for g, up in up_of(duo):
            i = g - DUOS
            far_v[i, :, pl.ds(0, thin), :] = up
            for d in range(depth):
                far_v[i, d, pl.ds(thin, slim), :] = out_rows(g, d)
            pass_on(i).start()
        return carry

    lax.fori_loop(DUOS // 2, DUOS, far_step, 0)
    sends = [pass_on(i) for i in range(DUOS)]
    layer[3].wait_recv()
    add = lambda a, b: (a.astype(f32) + b.astype(f32)).astype(bf16)
    stores = [None] * DUOS
    for duo in range(DUOS // 2):
        for g, up in up_of(duo):
            slot = g % 2
            if g >= 2:
                stores[g - 2].wait()
            sends[g].wait_recv()
            stage[slot, :, pl.ds(0, thin), :] = add(up, got_v[g, :, pl.ds(0, thin), :])
            stage[slot, :, pl.ds(thin, thin), :] = add(near_v[g], got_dn[g])
            for d in range(depth):
                stage[slot, d, pl.ds(2 * thin, slim), :] = add(
                    out_rows(g, d), got_v[g, d, pl.ds(thin, slim), :]
                )
            stores[g] = pltpu.make_async_copy(stage.at[slot], totals[g], stage_sem.at[slot])
            stores[g].start()
    for tile in range(tiles):
        give(tile).wait()
    layer[1].wait_recv()
    layer[2].wait_recv()
    for copy in layer + sends:
        copy.wait_send()
    wait_copies(stores[-2:] + homes + [own_out])


def ffn_rear(
    att0, att1, slope, g_second, unit, norm_t, out0, out1, downs_in, groups, inverse, gain1
):
    rows, part = att0.shape
    span, width = out0.shape
    depth, deep, cols = groups[0].shape
    thin = width // depth
    f32, bf16, shape, v = jnp.float32, jnp.bfloat16, jax.ShapeDtypeStruct, pltpu.VMEM
    weights = v((DUOS, depth, thin, 2 * cols), bf16)
    flat = v((rows, width), bf16)
    tall = v((rows, width), f32)
    deep_rows = v((DUOS, rows, 2 * cols), bf16)
    turned = v((width, rows), bf16)
    mixed = v((DUOS, depth, deep - thin, cols), bf16)
    downs = v((DUOS, depth, thin, cols), bf16)
    tiles = rows // TILE
    return pl.pallas_call(
        ffn_rear_kernel,
        out_shape=(
            shape((rows, width), f32), shape((rows, part), bf16), shape((rows, part), bf16),
            shape((4, span, width), bf16),
        )
        + (shape((depth, deep, cols), bf16),) * DUOS
        + (shape((16, width), f32), shape((DUOS, 2 * cols), f32)),
        in_specs=[ANY_SPEC] * (9 + GROUPS) + [VMEM_SPEC] * 2,
        out_specs=(ANY_SPEC,) * (4 + DUOS) + (VMEM_SPEC,) * 2,
        scratch_shapes=[
            flat, deep_rows, tall, tall, turned, weights, weights,
            v((2, width, part), bf16), deep_rows, tall, v((2, rows, part), bf16), turned,
            v((span, width), bf16), mixed, mixed, downs, downs, v((2, depth, deep, cols), bf16),
            DMA((6,)), DMA((GROUPS,)), DMA((GROUPS,)), DMA((GROUPS, depth)), DMA((2,)), DMA((2,)),
            DMA((2,)), DMA((4,)), DMA((4,)), DMA((tiles,)), DMA((tiles,)), DMA((DUOS,)),
            DMA((DUOS,)),
        ],
        compiler_params=pltpu.CompilerParams(
            vmem_limit_bytes=63 * 1024 * 1024, collective_id=2, has_side_effects=True
        ),
        cost_estimate=pl.CostEstimate(
            flops=45 * 10**9, bytes_accessed=40 * 10**6, transcendentals=0
        ),
        name="ffn_rear",
    )(
        att0, att1, slope, g_second, unit, norm_t, out0, out1, downs_in, *groups, inverse, gain1
    )


MESH = pl.DeviceIdType.MESH
CUTS = 8
THIRDS = 3


def signal_all(devices):
    barrier = pltpu.get_barrier_semaphore()
    for device in devices:
        pl.semaphore_signal(barrier, inc=1, device_id=device, device_id_type=MESH)
    pl.semaphore_wait(barrier, len(devices))


def neighbours():
    half, turn, share = my_spot()
    return (
        {"tensor": (half + 1) % 2},
        {"context": ((turn + 1) % 2) * 2 + share},
        {"context": turn * 2 + (share + 1) % 2},
    )


def remote(src, dst, send_sem, recv_sem, device):
    return pltpu.make_async_remote_copy(
        src_ref=src, dst_ref=dst, send_sem=send_sem, recv_sem=recv_sem,
        device_id=device, device_id_type=MESH,
    )


def fetch_kernel(
    hidden, w_q, w_k, w_v, w_up, w_down, w_out, bias_q, bias_v, bias_u,
    x_out, q_all, f_deep, far_q, far_v, far_u,
    qkv, ffn, cut_sem, own_sem, x_send, x_recv, z_send, z_recv, f_send, f_recv,
    h_send, h_recv, t_send, t_recv, c_send, c_recv, b_sem,
):
    half, turn, share = my_spot()
    deep = lax.axis_index("dp")
    depth = f_deep.shape[0]
    across, beside, partner = neighbours()
    up, down = {"dp": (deep + 1) % depth}, {"dp": (deep + depth - 1) % depth}
    slim, thin, cols = qkv.shape[0], w_q.shape[0], w_q.shape[1]
    place = turn * 2 + share
    my_rows = pl.ds(pl.multiple_of(place * slim, 16), slim)
    my_lanes = pl.ds(pl.multiple_of(place * cols, PAIR), cols)
    cuts = start_copies(
        [(w.at[my_rows], qkv.at[:, pl.ds(i * cols, cols)]) for i, w in enumerate((w_q, w_k, w_v))]
        + [(w.at[:, my_lanes], ffn.at[pl.ds(i * thin, thin)]) for i, w in enumerate((w_up, w_down))]
        + [(w_out.at[my_rows], ffn.at[pl.ds(2 * thin, slim)])],
        cut_sem,
    )
    signal_all([across, beside, partner, up, down])
    wait_copies(cuts)

    slot = lambda h, t, d: q_all.at[h, t, share, d]
    own = start_copies([(qkv, slot(half, turn, deep)), (ffn, f_deep.at[deep])], own_sem)

    def to_up(d):
        return remote(slot(half, turn, d), slot(half, turn, d), z_send.at[0, d], z_recv.at[d], up)

    def to_down(d):
        return remote(slot(half, turn, d), slot(half, turn, d), z_send.at[1, d], z_recv.at[d], down)

    third = f_deep.shape[1] // THIRDS

    def f_copies(d, side, device):
        return [
            remote(
                f_deep.at[d, pl.ds(i * third, third)], f_deep.at[d, pl.ds(i * third, third)],
                f_send.at[side, d, i], f_recv.at[d, i], device,
            )
            for i in range(THIRDS)
        ]

    f_up = lambda d: f_copies(d, 0, up)
    f_down = lambda d: f_copies(d, 1, down)

    def to_across(t, d):
        return remote(slot(half, t, d), slot(half, t, d), h_send.at[t, d], h_recv.at[t, d], across)

    def from_across(t, d):
        other = slot((half + 1) % 2, t, d)
        return remote(other, other, h_send.at[t, d], h_recv.at[t, d], across)

    def to_beside(d):
        return remote(slot(half, turn, d), slot(half, turn, d), t_send.at[d], t_recv.at[d], beside)

    def from_beside(d):
        other = slot(half, (turn + 1) % 2, d)
        return remote(other, other, t_send.at[d], t_recv.at[d], beside)

    def to_partner(t, d):
        piece = slot((share + 1) % 2, t, d)
        return remote(piece, piece, c_send.at[t, d], c_recv.at[t, d], partner)

    def from_partner(t, d):
        piece = q_all.at[share, t, (share + 1) % 2, d]
        return remote(piece, piece, c_send.at[t, d], c_recv.at[t, d], partner)

    cut = x_out.shape[1] // CUTS
    piece_rows = lambda i: pl.ds(i * cut, cut)
    x_next = [
        remote(
            hidden.at[half * 2 + (turn + 1) % 2, piece_rows(i)], x_out.at[0, piece_rows(i)],
            x_send.at[0, i], x_recv.at[0, i], beside,
        )
        for i in range(CUTS)
    ]
    x_mine = remote(
        hidden.at[half * 2 + turn], x_out.at[1], x_send.at[1, 0], x_recv.at[1, 0], partner
    )
    x_relay = [
        remote(
            x_out.at[0, piece_rows(i)], x_out.at[2, piece_rows(i)],
            x_send.at[2, i], x_recv.at[2, i], partner,
        )
        for i in range(CUTS)
    ]
    biases = [
        remote(src, dst, b_sem.at[0, i], b_sem.at[1, i], across)
        for i, (src, dst) in enumerate(((bias_q, far_q), (bias_v, far_v), (bias_u, far_u)))
    ]
    wait_copies(own)
    own_turn = (share + 1) % 2 == half

    def spread_own(d):
        to_across(turn, d).start()
        to_beside(d).start()

        @pl.when(own_turn)
        def _():
            to_partner(turn, d).start()

    def when(condition, *copies):
        @pl.when(condition)
        def _():
            for copy in copies:
                copy.start()

    when(deep < depth - 1, to_up(deep))
    when(deep > 0, to_down(deep))
    when(deep < depth - 1, f_up(deep)[0])
    when(deep > 0, f_down(deep)[0])
    spread_own(deep)
    x_next[0].start()
    for copy in biases:
        copy.start()
    x_mine.start()
    for k in range(1, depth):
        low, high = (deep + depth - k) % depth, (deep + k) % depth

        @pl.when(deep >= k)
        def _():
            to_up(low).wait_recv()
            when(deep < depth - 1, to_up(low))
            spread_own(low)

        @pl.when(deep + k < depth)
        def _():
            to_down(high).wait_recv()
            when(deep > 0, to_down(high))
            spread_own(high)

        if k < THIRDS:
            when(deep < depth - 1, f_up(deep)[k])
            when(deep > 0, f_down(deep)[k])
        x_next[k].start()

    for i in range(depth, THIRDS):
        when(deep < depth - 1, f_up(deep)[i])
        when(deep > 0, f_down(deep)[i])
    for copy in x_next[depth:]:
        copy.start()
    for k in range(depth):
        d = (deep + k) % depth
        from_beside(d).wait_recv()
        to_across((turn + 1) % 2, d).start()

        @pl.when(own_turn)
        def _():
            to_partner((turn + 1) % 2, d).start()

    def f_step(k):
        low, high = (deep + depth - k) % depth, (deep + k) % depth

        @pl.when(deep >= k)
        def _():
            for copy in f_up(low):
                copy.wait_recv()
                when(deep < depth - 1, copy)

        @pl.when(deep + k < depth)
        def _():
            for copy in f_down(high):
                copy.wait_recv()
                when(deep > 0, copy)

    def x_step(step):
        for i in range(step * CUTS // (depth + 1), (step + 1) * CUTS // (depth + 1)):
            x_next[i].wait_recv()
            x_relay[i].start()

    f_step(1)
    for step, t in enumerate((turn, (turn + 1) % 2)):
        for k in range(depth):
            d = (deep + k) % depth
            from_across(t, d).wait_recv()

            @pl.when(jnp.logical_not(own_turn))
            def _():
                to_partner(t, d).start()

        x_step(step)
        if step == 0 and depth > 2:
            f_step(2)
    for k in range(3, depth):
        x_step(k - 1)
        f_step(k)
    for step in range(max(2, depth - 1), depth + 1):
        x_step(step)

    for t in range(2):
        for d in range(depth):
            from_partner(t, d).wait_recv()
    x_mine.wait_recv()
    for copy in x_relay + biases:
        copy.wait_recv()
    for d in range(depth):
        for copy in (to_across(0, d), to_across(1, d), to_beside(d), to_partner(0, d), to_partner(1, d)):
            copy.wait_send()

        @pl.when(jnp.logical_and(deep < depth - 1, deep >= d))
        def _():
            for copy in [to_up(d)] + f_up(d):
                copy.wait_send()

        @pl.when(jnp.logical_and(deep > 0, deep <= d))
        def _():
            for copy in [to_down(d)] + f_down(d):
                copy.wait_send()

    for copy in x_next + x_relay + [x_mine] + biases:
        copy.wait_send()


def fetch(hidden_in, weights, biases, depth):
    span, width = hidden_in.shape[1:]
    thin, cols = weights[0].shape
    slim = thin // 4
    bf16, shape = jnp.bfloat16, jax.ShapeDtypeStruct
    pair = DMA((2, depth))
    return pl.pallas_call(
        fetch_kernel,
        out_shape=(
            shape((3, span, width), bf16),
            shape((2, 2, 2, depth, slim, 3 * cols), bf16),
            shape((depth, 2 * thin + slim, cols), bf16),
            *(shape(b.shape, bf16) for b in biases),
        ),
        in_specs=[ANY_SPEC] * 7 + [VMEM_SPEC] * 3,
        out_specs=(ANY_SPEC, VMEM_SPEC, ANY_SPEC) + (VMEM_SPEC,) * 3,
        scratch_shapes=[
            pltpu.VMEM((slim, 3 * cols), bf16), pltpu.VMEM((2 * thin + slim, cols), bf16),
            DMA((6,)), DMA((2,)), DMA((3, CUTS)), DMA((3, CUTS)), pair, DMA((depth,)),
            DMA((2, depth, THIRDS)), DMA((depth, THIRDS)),
            pair, pair, DMA((depth,)), DMA((depth,)), pair, pair, DMA((2, 3)),
        ],
        compiler_params=pltpu.CompilerParams(
            vmem_limit_bytes=63 * 1024 * 1024, collective_id=0, has_side_effects=True
        ),
        cost_estimate=pl.CostEstimate(
            flops=30 * 10**9, bytes_accessed=10 * 10**6, transcendentals=0
        ),
        name="fetch",
    )(hidden_in, *weights, *biases)


SUBS = 4


def settle_kernel(
    hidden, x_in, dqkv, w_qkv, g_first, front_sums, rear_sums, up_sums, head_sums, *rest
):
    f32, bf16 = jnp.float32, jnp.bfloat16
    parts = rest[:4]
    (
        out, qkv_out, f_out, small_out,
        x_v, d_v, w_v, first_v, part_v, small_v, small_got,
        back_v, got_v, fin_v, land_v, tot_v, zf_v, ff_v,
        grad_v, swap_v, pq_v, yl_v, xs_v, xl_v, rs_v, zq_v, qf_v,
        in_sem, out_sem, send_sem, recv_sem,
    ) = rest[4:]
    half, turn, share = my_spot()
    deep = lax.axis_index("dp")
    depth = tot_v.shape[0]
    span = hidden.shape[1]
    sub = span // SUBS
    other = (share + 1) % 2
    far_half, far_turn = (half + 1) % 2, (turn + 1) % 2
    across, beside, partner = neighbours()
    deeps = [{"dp": (deep + k) % depth} for k in range(1, depth)]
    ids = iter(range(send_sem.shape[0]))
    started = []

    def link(src, dst, device):
        i = next(ids)
        copy = remote(src, dst, send_sem.at[i], recv_sem.at[i], device)
        started.append(copy)
        return copy

    def go(src, dst, device):
        copy = link(src, dst, device)
        copy.start()
        return copy

    chunk = lambda i: pl.ds(i * span, span)
    chunks = [hidden.at[half * 2 + turn]] + [x_in.at[i] for i in range(3)]
    loads = [
        pltpu.make_async_copy(src, dst, in_sem.at[i])
        for i, (src, dst) in enumerate(
            [(w_qkv, w_v)]
            + [(dqkv.at[chunk(i)], d_v.at[chunk(i)]) for i in (2, 3, 0, 1)]
            + [(p, part_v.at[i]) for i, p in enumerate(parts)]
            + [(g_first, first_v)]
            + [(c, x_v.at[chunk(i)]) for i, c in enumerate(chunks)]
        )
    ]
    for copy in loads:
        copy.start()
    signal_all([across, beside, partner] + deeps)
    small_v[...] = jnp.zeros_like(small_v)
    cols = up_sums.shape[1] // 2
    for g, (where, at) in enumerate(group_homes()):
        row = pl.ds(where * 2 + at // 2, 1)
        lanes = pl.ds(pl.multiple_of((at % 2) * cols, PAIR), cols)
        small_v[row, lanes] = up_sums[g // 2 : g // 2 + 1, (g % 2) * cols : (g % 2 + 1) * cols]
    small_v[4:7, :] = rear_sums[0:3, :]
    small_v[7:10, :] = front_sums[3:6, :]
    lane = lax.broadcasted_iota(jnp.int32, (1, small_v.shape[1]), 1)
    stats = jnp.where(lane == 5, front_sums[11:12, :], 0.0)
    for i in range(5):
        stats = jnp.where(lane == i, jnp.sum(front_sums[6 + i : 7 + i, :], 1, keepdims=True), stats)
    small_v[10:11, :] = stats
    small_v[11:13, :] = head_sums[0:2, :]

    s0 = go(small_v, small_got.at[0], partner)
    wait_copies(loads[:3])
    back = []
    for i in range(2):
        back_v[i] = dot_nt(d_v[chunk(2 + i), :], w_v[...]).astype(bf16)
        back.append(go(back_v.at[i], got_v.at[i], partner))
    wait_copies(loads[3:10])
    tot_v[...] = (
        (part_v[0].astype(f32) + part_v[1].astype(f32))
        + (part_v[2].astype(f32) + part_v[3].astype(f32))
    ).astype(bf16)
    outs = []
    z_f = [
        go(tot_v.at[(deep + k + 1) % depth], zf_v.at[k], device) for k, device in enumerate(deeps)
    ]

    def own_back(i):
        value = dot_nt(d_v[chunk(i), :], w_v[...]) + first_v[chunk(i), :]
        back[i].wait_recv()
        fin_v[i] = (value + got_v[i].astype(f32)).astype(bf16)

    rows = lambda j: pl.ds(j * sub, sub)

    def put(ref, h, t):
        copy = pltpu.make_async_copy(ref, out.at[h * 2 + t], out_sem.at[len(outs)])
        copy.start()
        outs.append(copy)

    own_back(0)
    x_subs = [go(fin_v.at[0, rows(j)], land_v.at[1, rows(j)], across) for j in range(SUBS)]
    put(fin_v.at[0], half, turn)
    own_back(1)
    y_subs = [go(fin_v.at[1, rows(j)], land_v.at[0, rows(j)], beside) for j in range(SUBS // 2)]

    s0.wait_recv()
    s0.wait_send()
    small_v[...] += small_got[0]
    s1 = go(small_v, small_got.at[1], beside)
    wait_copies(loads[10:])
    third = grad_v.shape[0] // 3

    def grad_step(i, carry):
        at = pl.ds(pl.multiple_of(i * third, PAIR), third)
        grad_v[at, :] = dot_tn(x_v[:, at], d_v[...]).astype(bf16)
        return carry

    lax.fori_loop(0, 3, grad_step, 0)
    slim = swap_v.shape[2]

    def grad_rows(d, t, s):
        return grad_v[pl.ds(pl.multiple_of((d * 4 + t * 2 + s) * slim, 16), slim), :]

    for d in range(depth):
        for t in range(2):
            swap_v[d, t] = grad_rows(d, t, other)
    swap = go(swap_v, pq_v.at[share], partner)
    for d in range(depth):
        for t in range(2):
            pq_v[share, d, t] = grad_rows(d, t, share)
    s1.wait_recv()
    s1.wait_send()
    small_v[...] += small_got[1]
    s2 = go(small_v, small_got.at[2], across)
    swap.wait_recv()
    keep_v = lambda h, t: pq_v[h, :, t]
    q1 = go(pq_v.at[far_half, :, far_turn], yl_v.at[0], beside)
    q2 = go(pq_v.at[half, :, far_turn], yl_v.at[1], beside)
    y_subs += [
        go(fin_v.at[1, rows(j)], land_v.at[0, rows(j)], beside) for j in range(SUBS // 2, SUBS)
    ]
    s2.wait_recv()
    s2.wait_send()
    small_v[...] += small_got[2]
    s3 = [go(small_v, small_got.at[3 + k], device) for k, device in enumerate(deeps)]
    relays = []

    def relay(j):
        y_subs[j].wait_recv()
        relays.append(go(land_v.at[0, rows(j)], land_v.at[2, rows(j)], across))

    for j in range(SUBS // 2):
        relay(j)
    q1.wait_recv()
    xs_v[...] = (keep_v(far_half, turn).astype(f32) + yl_v[0].astype(f32)).astype(bf16)
    qx = go(xs_v, xl_v, across)

    for copy in z_f:
        copy.wait_recv()
    ranks = range(depth - 1)
    spread = lambda ref, got: sum([got[k].astype(f32) for k in ranks], ref[deep].astype(f32))
    ff_v[turn, share] = spread(tot_v, zf_v).astype(bf16)

    def gather_first(ref):
        piece = ref.at[turn, share]
        return go(piece, piece, beside), go(piece, piece, partner)

    def gather_next(ref, first):
        first.wait_recv()
        piece = ref.at[far_turn, share]
        return go(piece, piece, partner)

    f_first = gather_first(ff_v)
    q2.wait_recv()
    for j in range(SUBS // 2, SUBS):
        relay(j)
    qx.wait_recv()
    rs_v[...] = (
        keep_v(half, turn).astype(f32) + yl_v[1].astype(f32) + xl_v[...].astype(f32)
    ).astype(bf16)
    z_q = [
        go(rs_v.at[(deep + k + 1) % depth], zq_v.at[k], device) for k, device in enumerate(deeps)
    ]
    for copy in s3:
        copy.wait_recv()
    small_out[...] = small_v[...] + sum([small_got[4 + k] for k in range(depth - 2)], small_got[3])
    f_next = gather_next(ff_v, f_first[0])
    for copy in z_q:
        copy.wait_recv()
    qf_v[turn, share] = spread(rs_v, zq_v).astype(bf16)
    q_first = gather_first(qf_v)
    put(land_v.at[0], half, far_turn)
    for copy in x_subs:
        copy.wait_recv()
    put(land_v.at[1], far_half, turn)
    f_first[1].wait_recv()
    f_next.wait_recv()
    ends = start_copies([(ff_v, f_out)], in_sem)
    q_next = gather_next(qf_v, q_first[0])
    for copy in relays:
        copy.wait_recv()
    put(land_v.at[2], far_half, far_turn)
    q_first[1].wait_recv()
    q_next.wait_recv()
    last = pltpu.make_async_copy(qf_v, qkv_out, in_sem.at[2])
    last.start()
    wait_copies(ends + [last] + outs)
    waited = [s0, s1, s2]
    for copy in started:
        if not any(copy is w for w in waited):
            copy.wait_send()


def settle(hidden_in, x_in, dqkv, w_qkv, g_first, sums, parts):
    rows, width = g_first.shape
    span = hidden_in.shape[1]
    depth, tall, cols = parts[0].shape
    wide = dqkv.shape[1]
    slim = width // depth // 4
    f32, bf16, shape = jnp.float32, jnp.bfloat16, jax.ShapeDtypeStruct
    v = pltpu.VMEM
    count = 80
    return pl.pallas_call(
        settle_kernel,
        out_shape=(
            shape((4, span, width), bf16), shape((2, 2, slim, wide), bf16),
            shape((2, 2, tall, cols), bf16), shape((16, width), f32),
        ),
        in_specs=[ANY_SPEC] * 5 + [VMEM_SPEC] * 4 + [ANY_SPEC] * 4,
        out_specs=(ANY_SPEC,) * 3 + (VMEM_SPEC,),
        scratch_shapes=[
            v((2 * rows, width), bf16), v((2 * rows, wide), bf16), v((width, wide), bf16),
            v((rows, width), f32), v((4, depth, tall, cols), bf16), v((16, width), f32),
            v((2 + depth, 16, width), f32),
            v((2, span, width), bf16), v((2, span, width), bf16), v((2, span, width), bf16),
            v((3, span, width), bf16),
            v((depth, tall, cols), bf16), v((depth - 1, tall, cols), bf16),
            v((2, 2, tall, cols), bf16),
            v((width, wide), bf16), v((depth, 2, slim, wide), bf16),
            v((2, depth, 2, slim, wide), bf16), v((2, depth, slim, wide), bf16),
            v((depth, slim, wide), bf16), v((depth, slim, wide), bf16),
            v((depth, slim, wide), bf16), v((depth - 1, slim, wide), bf16),
            v((2, 2, slim, wide), bf16),
            DMA((20,)), DMA((4,)), DMA((count,)), DMA((count,)),
        ],
        compiler_params=pltpu.CompilerParams(
            vmem_limit_bytes=63 * 1024 * 1024, collective_id=1, has_side_effects=True
        ),
        cost_estimate=pl.CostEstimate(
            flops=60 * 10**9, bytes_accessed=30 * 10**6, transcendentals=0
        ),
        name="settle",
    )(hidden_in, x_in, dqkv, w_qkv, g_first, *sums, *parts)


def finish_kernel(
    grad, layer, qkv, ffn, small,
    grad_home, layer_home, o_q, o_bq, o_k, o_v, o_bv, o_o, o_bo, o_g1, o_s1, o_up, o_bup, o_down, o_bdown,
    o_g2, o_s2, o_rms,
    grad_in, grad_out, layer_v, in_sem, out_sem,
):
    f32 = jnp.float32
    seqs, span, width = grad.shape
    half = my_spot()[0]
    thin = o_q.shape[0]
    cols = o_q.shape[1]
    loads = start_copies(
        [(grad.at[i], grad_in.at[i]) for i in range(seqs)]
        + [(layer.at[i], layer_v.at[i]) for i in range(seqs)],
        in_sem,
    )
    stores = []
    for i in range(seqs):
        loads[i].wait()
        grad_out[i] = grad_in[i].astype(f32)
        stores.append(pltpu.make_async_copy(grad_out.at[i], grad_home.at[i], out_sem.at[i]))
        stores[i].start()
    for i in range(seqs):
        loads[seqs + i].wait()
        copy = pltpu.make_async_copy(layer_v.at[i], layer_home.at[i], out_sem.at[seqs + i])
        copy.start()
        stores.append(copy)
    for i, ref in enumerate((o_q, o_k, o_v)):
        ref[...] = qkv[:, i * cols : (i + 1) * cols].astype(f32)
    slim = ffn.shape[1] - 2 * thin
    for p in range(4):
        at = slice(p * cols, (p + 1) * cols)
        o_up[:, at] = ffn[p, :thin, :].astype(f32)
        o_down[:, at] = ffn[p, thin : 2 * thin, :].astype(f32)
        o_o[p * slim : (p + 1) * slim, :] = ffn[p, 2 * thin :, :].astype(f32)
    flat = lambda row: row.reshape(row.shape[1])
    up = [small[pl.ds(half * 2 + i, 1), :] for i in range(2)]
    o_bup[...] = flat(jnp.concatenate(up, 1))
    for i, ref in enumerate((o_bo, o_g1, o_s1, o_bdown, o_g2, o_s2)):
        ref[...] = flat(small[4 + i : 5 + i, :])
    own = pl.ds(pl.multiple_of(half * cols, PAIR), cols)
    o_bq[...] = flat(small[11:12, own])
    o_bv[...] = flat(small[12:13, own])
    stats = small[10:11, :]
    o_rms[...] = jnp.sqrt(stats / (jnp.maximum(stats[:, 5:6], 1.0) * width))[:, :PAIR]
    wait_copies(stores)


def finish_all(grad, layer, qkv, ffn, small):
    seqs, span, width = grad.shape
    thin, cols = qkv.shape[0], qkv.shape[1] // 3
    f32 = jnp.float32
    shape = lambda *s: jax.ShapeDtypeStruct(s, f32)
    outs = pl.pallas_call(
        finish_kernel,
        out_shape=(
            shape(seqs, span, width), jax.ShapeDtypeStruct(layer.shape, layer.dtype),
            shape(thin, cols), shape(cols), shape(thin, cols),
            shape(thin, cols), shape(cols), shape(thin, cols), shape(width), shape(width),
            shape(width), shape(thin, 4 * cols), shape(4 * cols), shape(thin, 4 * cols),
            shape(width), shape(width), shape(width), shape(1, PAIR),
        ),
        in_specs=[ANY_SPEC] * 2 + [VMEM_SPEC] * 3,
        out_specs=(ANY_SPEC,) * 2 + (VMEM_SPEC,) * 16,
        scratch_shapes=[
            pltpu.VMEM((seqs, span, width), grad.dtype), pltpu.VMEM((seqs, span, width), f32),
            pltpu.VMEM((seqs, span, width), layer.dtype), DMA((2 * seqs,)), DMA((2 * seqs,)),
        ],
        compiler_params=WIDE_ROOM,
        name="finish_all",
    )(grad, layer, qkv, ffn, small)
    outs = list(outs)
    outs[7], outs[13] = outs[7].T, outs[13].T
    return (outs[1], outs[0], *outs[2:-1], outs[-1][0, :5])


def layer_norm(values, norm_gain, norm_shift):
    row_mean = jnp.mean(values, -1, keepdims=True)
    centered = values - row_mean
    row_var = jnp.mean(centered * centered, -1, keepdims=True)
    return centered * lax.rsqrt(row_var + EPSILON) * norm_gain + norm_shift


def gelu_tanh(values):
    return jax.nn.gelu(values, approximate=True)


def block_tables(random_seq, all_blocks, place):
    block = jnp.arange(2, all_blocks, dtype=jnp.int32)
    last = all_blocks - 1
    zero = jnp.zeros_like(block)
    true_ids = jnp.stack(
        [block, block - 1, block, jnp.minimum(block + 1, last), zero, zero + 1], -1
    )
    true_ids = jnp.concatenate([true_ids, random_seq[2:]], -1)
    flags = jnp.stack([block >= 3, block <= last - 1], -1).astype(jnp.int32)
    return (
        jnp.concatenate([place(true_ids), flags], -1).astype(jnp.int32),
        place(jnp.arange(2, dtype=jnp.int32)),
    )


def local(
    hidden_in, out_grad, segment_ids, token_valid, random_blocks,
    query_weight, query_bias, key_weight, value_weight, value_bias,
    output_weight, output_bias, norm1_gain, norm1_shift,
    up_weight, up_bias, down_weight, down_bias, norm2_gain, norm2_shift,
):
    f32, bf16 = jnp.float32, jnp.bfloat16
    seqs, span, width = hidden_in.shape
    length = segment_ids.shape[1]
    places = length // span
    halves = lax.axis_size("tensor")
    depth = lax.axis_size("dp")
    turns = seqs // halves
    shares = places // turns
    my_half = lax.axis_index("tensor")
    my_place = lax.axis_index("context")
    my_depth = lax.axis_index("dp")
    my_turn, my_share = my_place // shares, my_place % shares
    my_seq = my_half * turns + my_turn
    blocks = length // BLK
    rows = turns * span
    spots = [(h, t) for h in range(halves) for t in range(turns)]

    def send(value, half=0, turn=0, share=0):
        if half % halves == 0 and turn % turns == 0 and share % shares == 0:
            return value
        pairs = []
        for h in range(halves):
            for t in range(turns):
                for s in range(shares):
                    to_place = (t + turn) % turns * shares + (s + share) % shares
                    pairs.append(
                        ((t * shares + s) * halves + h, to_place * halves + (h + half) % halves)
                    )
        return lax.ppermute(value, ("context", "tensor"), pairs)

    def send_deep(value, step):
        return lax.ppermute(value, "dp", [(i, (i + step) % depth) for i in range(depth)])

    def pick(value, index, axis=0):
        return lax.dynamic_index_in_dim(value, index, axis, keepdims=False)

    def own_slice(value, count, which, axis):
        size = value.shape[axis] // count
        return lax.dynamic_slice_in_dim(value, which * size, size, axis)

    def gather_deep(value):
        if depth > 4:
            return lax.all_gather(value, "dp", axis=0)
        got = [value] + [send_deep(value, k) for k in range(1, depth)]
        ring = jnp.stack([got[depth - 1 - i % depth] for i in range(2 * depth - 1)])
        return lax.dynamic_slice_in_dim(ring, depth - 1 - my_depth, depth, 0)

    def reduce_deep(value):
        if depth > 4:
            return lax.psum_scatter(value, "dp", scatter_dimension=0)
        total = pick(value, my_depth).astype(f32)
        for k in range(1, depth):
            total = total + send_deep(pick(value, (my_depth + k) % depth), k).astype(f32)
        return total.astype(bf16)

    def gather_square(value):
        near = {spot: send(value, *spot) for spot in spots}
        near = jnp.stack([near[spot] for spot in spots])
        return [near] + [send(near, 0, 0, s) for s in range(1, shares)]

    def reduce_square(value):
        total = value[0].astype(f32)
        for i, (h, t) in enumerate(spots[1:], 1):
            total = total + send(value[i], -h, -t).astype(f32)
        return total.astype(bf16)

    def gather_places(value):
        near = [send(value, 0, t) for t in range(turns)]
        near = jnp.stack(near)
        far = jnp.stack([near] + [send(near, 0, 0, s) for s in range(1, shares)])
        return jnp.stack(
            [
                pick(pick(far, (my_share - s) % shares), (my_turn - t) % turns)
                for t in range(turns)
                for s in range(shares)
            ]
        )

    def sum_all(value):
        for step in range(halves.bit_length() - 1):
            value = value + send(value, 1 << step)
        size = 1
        while size < places:
            value = value + lax.ppermute(value, "context", [(i, i ^ size) for i in range(places)])
            size *= 2
        size = 1
        while size < depth:
            value = value + lax.ppermute(value, "dp", [(i, i ^ size) for i in range(depth)])
            size *= 2
        return value

    def bring(value):
        return jnp.concatenate(
            [
                send(pick(value, my_half * turns + (my_turn + k) % turns), 0, k)
                for k in range(turns)
            ],
            0,
        )

    def deliver(value):
        value = value.reshape(turns, span, width)
        got = jnp.stack([send(value[t], h, -t) for h, t in spots])
        return jnp.stack(
            [
                pick(got, (my_half - h) % halves * turns + (t - my_turn) % turns)
                for h in range(halves)
                for t in range(turns)
            ]
        )

    def after(value, *earlier):
        return lax.optimization_barrier((value, *earlier))[0]

    per = span // BLK

    def place(block_ids):
        chunk = block_ids // per
        turn, share = chunk // shares, chunk % shares
        spot = ((my_share - share) % shares) * turns + (my_turn - turn) % turns
        return spot * per + block_ids % per

    def in_order(row):
        return jnp.concatenate(
            [
                lax.dynamic_slice_in_dim(
                    row,
                    (((my_turn - k) % turns) * shares + (my_share - s) % shares) * span,
                    span,
                )
                for s in range(shares)
                for k in range(turns)
            ]
        )

    half_width = query_weight.shape[1]
    thin = query_weight.shape[0]
    slim = thin // places
    hidden = up_weight.shape[1] // places
    biases = jnp.concatenate([query_bias, value_bias, up_bias])

    def split_biases(by_half):
        by_half = jnp.stack([pick(by_half, (my_half - h) % halves) for h in range(halves)])
        return (
            by_half[:, at : at + b.shape[0]].reshape(-1)
            for b, at in ((query_bias, 0), (value_bias, half_width), (up_bias, 2 * half_width))
        )

    def spread(value, which, count):
        return lax.dynamic_update_slice_in_dim(
            jnp.zeros((value.shape[0] * count,), value.dtype), value, which * value.shape[0], 0
        )

    def small_rows(up_sums, group_at, norm_sums, stats):
        up_natural = jnp.zeros_like(up_sums)
        for i, at in enumerate(group_at):
            up_natural = lax.dynamic_update_slice_in_dim(
                up_natural, up_sums[i * hidden : (i + 1) * hidden], at * hidden, 0
            )
        stats = jnp.pad(stats, (0, width - stats.shape[0]))
        return jnp.concatenate(
            [up_natural.reshape(-1, width), *(row[None] for row in norm_sums), stats[None]], 0
        )

    def finish(layer_out, input_grad, qkv_shard, up_part, down_part, out_part, small):
        deep = up_weight.shape[1] * halves // width
        s_up, (s_o, s_g1, s_s1, s_down, s_g2, s_s2, stats, s_q, s_v) = (
            small[:deep].reshape(-1), small[deep : deep + 9]
        )
        s_q, s_v, s_up = (own_slice(value, halves, my_half, 0) for value in (s_q, s_v, s_up))
        input_rms = jnp.sqrt(stats[:5] / (jnp.maximum(stats[5], 1.0) * width))
        join = lambda w: jnp.moveaxis(w, 0, 1).reshape(thin, -1).astype(f32)
        shard_o = out_part.reshape(thin, -1)[:, :half_width].astype(f32).T
        shard_q, shard_k, shard_v = (qkv_shard[:, i].astype(f32) for i in range(3))
        return (
            layer_out, input_grad, shard_q, s_q, shard_k, shard_v, s_v, shard_o, s_o,
            s_g1, s_s1, join(up_part), s_up, join(down_part).T, s_down, s_g2, s_s2, input_rms,
        )

    if (turns, shares, halves) == (2, 2, 2) and depth <= 4 and rows % TILE == 0:
        near_b = [query_bias, value_bias, up_bias]
        x_in, q_all, f_deep, *far_b = fetch(
            hidden_in,
            [query_weight, key_weight, value_weight, up_weight, down_weight.T, output_weight.T],
            near_b, depth,
        )
        random = place(pick(random_blocks, my_seq)).reshape(-1)
        (
            att0, att1, q, k, v, lse, w_qkv, g_own, groups, key_code, query_code
        ) = project_attend(
            random, hidden_in, x_in, q_all, out_grad, f_deep, segment_ids, token_valid,
            near_b[0], near_b[1], far_b[0], far_b[1],
        )
        vectors = [output_bias, norm1_gain, norm1_shift, down_bias, norm2_gain, norm2_shift]
        out0, out1, slope, g_second, unit, norm_t, downs, inverse, front_sums = ffn_front(
            att0, att1, hidden_in, x_in, out_grad, g_own, groups,
            key_code.reshape(length, PAIR), vectors, near_b[2], far_b[2],
        )
        g_first, do_own, do_far, layer_out, *totals, rear_sums, up_sums = ffn_rear(
            att0, att1, slope, g_second, unit, norm_t, out0, out1, downs, groups, inverse,
            norm1_gain,
        )
        parts = [send(piece, *spot) for piece, spot in zip(totals, spots)]
        dqkv, head_sums = attend_grad(
            random, do_own, do_far, q, k, v, key_code, query_code, lse
        )
        dqkv, head_sums, parts = lax.optimization_barrier((dqkv, head_sums, parts))
        input_grad, qkv_shard, ffn_shard, small = settle(
            hidden_in, x_in, dqkv, w_qkv, g_first, (front_sums, rear_sums, up_sums, head_sums), parts
        )
        return finish_all(
            input_grad, layer_out, qkv_shard.reshape(thin, -1),
            ffn_shard.reshape((places,) + ffn_shard.shape[2:]), small,
        )

    seg = in_order(pick(segment_ids, my_seq))
    live = in_order(pick(token_valid, my_seq))
    random_seq = pick(random_blocks, my_seq)
    table, wide = block_tables(random_seq, blocks, place)
    key_code = jnp.broadcast_to(jnp.where(live == 1, seg, -1)[:, None], (length, PAIR))
    query_code = jnp.tile(seg.reshape(blocks, BLK), (1, PAIR // BLK))
    part = width // shares
    padded = -(-part // PAIR) * PAIR
    x_own = bring(hidden_in)
    qkv_piece = own_slice(
        jnp.concatenate([query_weight, key_weight, value_weight], 1), places, my_place, 0
    )
    qkv_all = jnp.stack(gather_square(gather_deep(qkv_piece)))
    per_half = shares // halves
    target = my_share // per_half
    qkv_all = jnp.stack(
        [
            pick(
                pick(qkv_all, (my_share - s) % shares),
                (my_half - target) % halves * turns + (my_turn - t) % turns,
            )
            for t in range(turns)
            for s in range(shares)
        ],
        1,
    ).reshape(width, 3, half_width)
    pad_cols = lambda w: jnp.pad(w, [(0, 0)] * (w.ndim - 1) + [(0, padded - part)])
    mine = lambda w: pad_cols(own_slice(w, per_half, my_share % per_half, w.ndim - 1))
    w_qkv = mine(qkv_all).reshape(width, 3 * padded)
    b_q, b_v, b_up = split_biases(jnp.stack([send(biases, h) for h in range(halves)]))
    mine_b = lambda b: pad_cols(own_slice(b, shares, my_share, 0))
    b_qkv = jnp.concatenate([mine_b(b_q), jnp.zeros((padded,), bf16), mine_b(b_v)]).astype(f32)

    ffn_piece = jnp.concatenate(
        [
            own_slice(up_weight, places, my_place, 1),
            own_slice(down_weight, places, my_place, 0).T,
            jnp.pad(
                own_slice(output_weight.T, places, my_place, 0),
                [(0, 0), (0, max(0, hidden - half_width))],
            ).reshape(-1, hidden),
        ],
        0,
    )
    ffn_all = gather_square(gather_deep(ffn_piece))
    groups = [
        (s, i, ffn_all[s][i]) for s in range(shares) for i in range(len(spots))
    ]
    w_up = jnp.concatenate([g[:, :thin].reshape(width, hidden) for _, _, g in groups], 1)
    w_down_t = jnp.concatenate(
        [g[:, thin : 2 * thin].reshape(width, hidden) for _, _, g in groups], 1
    )
    out_all = jnp.stack(
        [jnp.stack([g[:, 2 * thin :] for g in ffn_all[s]]) for s in range(shares)]
    )
    w_out_t = jnp.stack(
        [
            jnp.stack(
                [
                    pick(
                        pick(out_all, (my_share - s) % shares),
                        (my_half - h) % halves * turns + (my_turn - t) % turns,
                    )
                    for t in range(turns)
                    for s in range(shares)
                ],
                1,
            ).reshape(width, half_width)
            for h in range(halves)
        ],
        1,
    ).reshape(width, width)
    w_out_t = jnp.concatenate(
        [own_slice(w_out_t, shares, (my_share + k) % shares, 1) for k in range(shares)], 1
    )
    group_at = [
        ((my_half - spots[i][0]) % halves * places
         + (my_turn - spots[i][1]) % turns * shares + (my_share - s) % shares)
        for s, i, _ in groups
    ]
    b_up = jnp.concatenate(
        [lax.dynamic_slice_in_dim(b_up, at * hidden, hidden) for at in group_at]
    ).astype(f32)

    g_out = bring(out_grad).astype(f32)
    x_seq = jnp.concatenate([send(x_own, 0, 0, k) for k in range(shares)], 0)
    q, k, v = (
        (
            jnp.dot(x_seq, w_qkv[:, i * padded : (i + 1) * padded], preferred_element_type=f32)
            + b_qkv[i * padded : (i + 1) * padded]
        ).astype(bf16)
        for i in range(3)
    )
    att, lse = attend(table, wide, q, k, v, key_code, query_code)
    att = att[:, :part].reshape(shares, rows, part)
    att_own = jnp.concatenate([send(att[s], 0, 0, -s) for s in range(shares)], 1)
    attn_out = lax.dot_general(
        att_own, w_out_t, (((1,), (1,)), ((), ())), preferred_element_type=f32
    ) + output_bias.astype(f32)
    x_full = x_own.astype(f32)
    first_sum = x_full + attn_out
    gain_one, shift_one = norm1_gain.astype(f32), norm1_shift.astype(f32)
    normed = layer_norm(first_sum, gain_one, shift_one)
    normed_low = normed.astype(bf16)
    pre_act = jnp.dot(normed_low, w_up, preferred_element_type=f32) + b_up
    act_low = gelu_tanh(pre_act).astype(bf16)
    ffn_out = lax.dot_general(
        act_low, w_down_t, (((1,), (1,)), ((), ())), preferred_element_type=f32
    ) + down_bias.astype(f32)
    second_sum = normed + ffn_out
    gain_two, shift_two = norm2_gain.astype(f32), norm2_shift.astype(f32)
    layer_out, norm_back = jax.vjp(layer_norm, second_sum, gain_two, shift_two)
    g_second, gain_two_grad, shift_two_grad = norm_back(g_out)
    layer_out = deliver(layer_out.astype(bf16))
    g_ffn = g_second.astype(bf16)
    g_act = jnp.dot(g_ffn, w_down_t, preferred_element_type=f32)
    g_pre = jax.vjp(gelu_tanh, pre_act)[1](g_act)[0].astype(bf16)
    up_part = jnp.dot(normed_low.T, g_pre, preferred_element_type=f32).astype(bf16)
    down_part_t = jnp.dot(g_ffn.T, act_low, preferred_element_type=f32).astype(bf16)
    g_normed = g_second + jnp.dot(g_pre, w_up.T, preferred_element_type=f32)
    g_first, gain_one_grad, shift_one_grad = jax.vjp(layer_norm, first_sum, gain_one, shift_one)[1](
        g_normed
    )
    g_attn = g_first.astype(bf16)
    out_part_t = jnp.dot(g_attn.T, att_own, preferred_element_type=f32).astype(bf16)
    g_att = jnp.dot(g_attn, w_out_t, preferred_element_type=f32).astype(bf16)
    do = jnp.concatenate(
        [send(own_slice(g_att, shares, s, 1), 0, 0, s) for s in range(shares)], 0
    )
    dq, dk, dv = attend_back(table, wide, q, k, v, pad_cols(do), key_code, query_code, lse)

    out_natural = jnp.concatenate(
        [own_slice(out_part_t, shares, (s - my_share) % shares, 1) for s in range(shares)], 1
    ).reshape(depth, turns, shares, slim, halves, half_width)

    def ffn_group(s, i):
        h, t = spots[i]
        at = (s * len(spots) + i) * hidden
        out = pick(out_natural, (my_half - h) % halves, 4)
        out = pick(pick(out, (my_turn - t) % turns, 1), (my_share - s) % shares, 1)
        out = jnp.pad(out, [(0, 0), (0, 0), (0, max(0, hidden - half_width))])
        cut = lambda w: w[:, at : at + hidden].reshape(depth, thin, hidden)
        return jnp.concatenate(
            [cut(up_part), cut(down_part_t), out.reshape(depth, -1, hidden)], 1
        )

    ffn_grads = [
        jnp.stack([ffn_group(s, i) for i in range(len(spots))]) for s in range(shares)
    ]
    total = ffn_grads[0].astype(f32)
    for s in range(1, shares):
        total = total + send(ffn_grads[s], 0, 0, -s).astype(f32)
    ffn_shard = gather_places(reduce_deep(reduce_square(total.astype(bf16))))
    dqkv = jnp.concatenate([dq, dk, dv], 1)
    qkv_part = (
        jnp.dot(x_seq.T, dqkv, preferred_element_type=f32)
        .astype(bf16)
        .reshape(depth, turns, shares, slim, 3, padded)[..., :part]
    )
    got = jnp.stack(
        [send(pick(qkv_part, (my_share + s) % shares, 2), 0, 0, s) for s in range(shares)]
    )
    got = jnp.stack([pick(got, (my_share - s) % shares) for s in range(shares)], 4)
    got = got.reshape(depth, turns, slim, 3, halves, half_width)
    square = jnp.stack(
        [
            pick(pick(got, (my_half - h) % halves, 4), (my_turn - t) % turns, 1)
            for h, t in spots
        ]
    ).reshape(len(spots), depth, slim, 3 * half_width)
    qkv_shard = gather_places(reduce_deep(reduce_square(square))).reshape(thin, 3, half_width)
    back = jnp.dot(dqkv, w_qkv.T, preferred_element_type=f32).reshape(shares, rows, width)
    back_own = back[0]
    for s in range(1, shares):
        back_own = back_own + send(back[s].astype(bf16), 0, 0, -s).astype(f32)
    input_grad = deliver((g_first + back_own).astype(bf16)).astype(f32)

    sums = lambda value: jnp.sum(value.astype(f32), 0)
    valid = live[:rows].astype(f32)
    squares = lambda member: jnp.sum(valid * jnp.sum(member * member, -1))
    stats = jnp.stack(
        [squares(m) for m in (x_full, first_sum, second_sum, attn_out, ffn_out)]
        + [jnp.sum(valid), 0.0, 0.0]
    )
    up_sums = sums(g_pre)
    norm_sums = [
        sums(g_attn), gain_one_grad, shift_one_grad, sums(g_ffn), gain_two_grad, shift_two_grad
    ]
    small = small_rows(up_sums, group_at, norm_sums, stats)
    heads = [spread(sums(d)[:part], my_share, shares)[None] for d in (dq, dv)]
    small = sum_all(jnp.concatenate([small, *heads], 0))
    return finish(
        layer_out, input_grad, qkv_shard, ffn_shard[:, :thin], ffn_shard[:, thin : 2 * thin],
        ffn_shard[:, 2 * thin :], small,
    )


def solution(mesh):
    rows, plain = P("dp", "context", None), P()
    columns, across, halves = P("dp", "tensor"), P("tensor", "dp"), P("tensor")
    return jax.shard_map(
        local,
        mesh=mesh,
        in_specs=(
            rows, rows, P("dp", None), P("dp", None), P("dp", None, None),
            columns, halves, columns, columns, halves, across, plain, plain, plain,
            columns, halves, across, plain, plain, plain,
        ),
        out_specs=(
            rows, rows, columns, halves, columns, columns, halves, across, plain,
            plain, plain, columns, halves, across, plain, plain, plain, plain,
        ),
        check_vma=False,
    )
```

```python
import functools

import jax
import jax.numpy as jnp
from jax import lax
from jax.experimental import pallas as pl
from jax.experimental.pallas import tpu as pltpu
from jax.sharding import PartitionSpec as P

HD = 64
BLK = 64
PAIR = 128
SLOTS = 8
WIDE = 512
SCALE = HD ** (-0.5)
EPSILON = 1e-06


NEG_FILL = -1e30
LEAP = 3
BACK_LEAP = 3


def pair_rows(block, left, scale=None):
    if scale is not None:
        block = block * jnp.asarray(scale, block.dtype)
    zero = jnp.zeros_like(block)
    return jnp.concatenate([jnp.where(left, block, zero), jnp.where(left, zero, block)], 0)


def lane_left(rows):
    return lax.broadcasted_iota(jnp.int32, (rows, PAIR), 1) < HD


def eye_pair():
    lanes = lax.broadcasted_iota(jnp.int32, (BLK, PAIR), 1)
    rows = lax.broadcasted_iota(jnp.int32, (BLK, PAIR), 0)
    return rows == lanes % BLK


def block_rows(index):
    return pl.ds(pl.multiple_of(index * BLK, BLK), BLK)


def slot_bias(slots, first_ok, third_ok, key_code, query_code, own):
    pieces = []
    for slot in range(SLOTS):
        code = query_code
        if slot == 0:
            code = jnp.where(first_ok, query_code, -2)
        if slot == 2:
            code = jnp.where(third_ok, query_code, -2)
        same = key_code[slots[slot]] == code
        if slot == 1:
            same = same | own
        pieces.append(jnp.where(same, 0.0, NEG_FILL))
    return jnp.concatenate(pieces, 0)


def slot_rows(ref, slots, lanes):
    return jnp.concatenate([ref[slot, :, lanes] for slot in slots], 0)


def wide_rows(ref, chunk, lanes):
    count = WIDE // BLK
    return ref[pl.ds(chunk * count, count), :, lanes].reshape(WIDE, PAIR)


def listed(table):
    def find(row):
        slots = [table[row, 1 + slot] for slot in range(SLOTS)]
        return table[row, 0], slots, table[row, 9] == 1, table[row, 10] == 1

    return find


def wide_bias(key_code, query_code, block, chunk):
    same = wide_rows(key_code, chunk, slice(0, PAIR)) == query_code
    key_pos = chunk * WIDE + lax.broadcasted_iota(jnp.int32, (WIDE, PAIR), 0)
    query_pos = block * BLK + lax.broadcasted_iota(jnp.int32, (WIDE, PAIR), 1) % BLK
    return jnp.where(same | (key_pos == query_pos), 0.0, NEG_FILL)


def dot_nt(left, right):
    return lax.dot_general(
        left, right, (((1,), (1,)), ((), ())), preferred_element_type=jnp.float32
    )


def dot_tn(left, right):
    return lax.dot_general(
        left, right, (((0,), (0,)), ((), ())), preferred_element_type=jnp.float32
    )


def dot_nn(left, right):
    return jnp.dot(left, right, preferred_element_type=jnp.float32)


def attend_kernel(table, wide, *refs):
    attend_blocks(listed(table), [wide[0], wide[1]], [(0, table.shape[0], None)], *refs)


def attend_blocks(
    find, wide, legs, q_ref, k_ref, v_ref, key_code, query_code, o_ref, lse_ref, acc, pause=None
):
    length, width = q_ref.shape
    pairs = width // PAIR
    left = lane_left(BLK)
    own = eye_pair()

    def narrow(row, carry):
        block, slots, first_ok, third_ok = find(row)
        rows = block_rows(block)
        code = query_code[pl.ds(block, 1), :]
        bias = slot_bias(slots, first_ok, third_ok, key_code, code, own)
        for pair in range(pairs):
            lanes = slice(pair * PAIR, (pair + 1) * PAIR)
            query = pair_rows(q_ref[rows, lanes], left, SCALE)
            scores = dot_nt(slot_rows(k_ref, slots, lanes), query) + bias
            top = jnp.max(scores, 0, keepdims=True)
            weight = jnp.exp(scores - top)
            total = jnp.sum(weight, 0, keepdims=True)
            probs = (weight * (1.0 / total)).astype(jnp.bfloat16)
            lse_ref[block, pl.ds(pair, 1), :] = top + jnp.log(total)
            both = dot_tn(probs, slot_rows(v_ref, slots, lanes))
            o_ref[rows, lanes] = jnp.where(left, both[:BLK], both[BLK:]).astype(o_ref.dtype)
        return carry

    for start, stop, after in legs:
        lax.fori_loop(start, stop, narrow, 0, unroll=LEAP if (stop - start) % LEAP == 0 else 1)
        if after is not None:
            after()

    for which in range(2):
        block = wide[which]
        rows = block_rows(block)
        code = query_code[pl.ds(block, 1), :]

        def first(chunk, carry):
            bias = wide_bias(key_code, code, block, chunk)
            out = []
            for pair in range(pairs):
                lanes = slice(pair * PAIR, (pair + 1) * PAIR)
                query = pair_rows(q_ref[rows, lanes], left, SCALE)
                scores = dot_nt(wide_rows(k_ref, chunk, lanes), query) + bias
                top_old, total_old = carry[pair]
                top = jnp.maximum(top_old, jnp.max(scores, 0, keepdims=True))
                total = total_old * jnp.exp(top_old - top) + jnp.sum(
                    jnp.exp(scores - top), 0, keepdims=True
                )
                out.append((top, total))
            return tuple(out)

        start = (jnp.full((1, PAIR), NEG_FILL), jnp.zeros((1, PAIR), jnp.float32))
        ends = lax.fori_loop(0, length // WIDE, first, (start,) * pairs, unroll=2)
        for pair in range(pairs):
            lse_ref[block, pl.ds(pair, 1), :] = ends[pair][0] + jnp.log(ends[pair][1])
        if pause is not None:
            pause(2 * which)
        acc[...] = jnp.zeros_like(acc)

        def second(chunk, carry):
            bias = wide_bias(key_code, code, block, chunk)
            for pair in range(pairs):
                lanes = slice(pair * PAIR, (pair + 1) * PAIR)
                query = pair_rows(q_ref[rows, lanes], left, SCALE)
                scores = dot_nt(wide_rows(k_ref, chunk, lanes), query) + bias
                probs = jnp.exp(scores - lse_ref[block, pl.ds(pair, 1), :]).astype(jnp.bfloat16)
                acc[pair] += dot_tn(probs, wide_rows(v_ref, chunk, lanes))
            return carry

        lax.fori_loop(0, length // WIDE, second, 0, unroll=2)
        for pair in range(pairs):
            lanes = slice(pair * PAIR, (pair + 1) * PAIR)
            both = acc[pair]
            o_ref[rows, lanes] = jnp.where(left, both[:BLK], both[BLK:]).astype(o_ref.dtype)
        if pause is not None:
            pause(2 * which + 1)


def attend_back_kernel(table, wide, *refs):
    attend_back_blocks(listed(table), [wide[0], wide[1]], table.shape[0], *refs)


def attend_back_blocks(
    find, wide, count, q_ref, k_ref, v_ref, do_ref, key_code, query_code, lse_ref,
    dq_ref, dk_ref, dv_ref, dk_sum, dv_sum, dq_acc,
):
    length, width = q_ref.shape
    pairs = width // PAIR
    left = lane_left(BLK)
    own = eye_pair()
    dk_sum[...] = jnp.zeros_like(dk_sum)
    dv_sum[...] = jnp.zeros_like(dv_sum)

    def narrow(row, carry):
        block, slots, first_ok, third_ok = find(row)
        rows = block_rows(block)
        code = query_code[pl.ds(block, 1), :]
        bias = slot_bias(slots, first_ok, third_ok, key_code, code, own)
        for pair in range(pairs):
            lanes = slice(pair * PAIR, (pair + 1) * PAIR)
            query = pair_rows(q_ref[rows, lanes], left, SCALE)
            grad = pair_rows(do_ref[rows, lanes], left)
            keys = slot_rows(k_ref, slots, lanes)
            values = slot_rows(v_ref, slots, lanes)
            scores = dot_nt(keys, query) + bias
            probs = jnp.exp(scores - lse_ref[block, pl.ds(pair, 1), :])
            g_probs = dot_nt(values, grad)
            terms = probs * g_probs
            g_scores = (terms - probs * jnp.sum(terms, 0, keepdims=True)).astype(jnp.bfloat16)
            dv = dot_nn(probs.astype(jnp.bfloat16), grad)
            dk = dot_nn(g_scores, query)
            both = dot_tn(g_scores, keys)
            dq_ref[rows, lanes] = (jnp.where(left, both[:BLK], both[BLK:]) * SCALE).astype(
                dq_ref.dtype
            )
            for slot in range(SLOTS):
                spot = block_rows(slots[slot])
                part = slice(slot * BLK, (slot + 1) * BLK)
                dk_sum[spot, lanes] += dk[part]
                dv_sum[spot, lanes] += dv[part]
        return carry

    lax.fori_loop(0, count, narrow, 0, unroll=BACK_LEAP if count % BACK_LEAP == 0 else 1)

    def wide_step(which, nothing):
        block = jnp.where(which == 0, wide[0], wide[1])
        rows = block_rows(block)
        code = query_code[pl.ds(block, 1), :]

        def pieces(chunk, pair, bias):
            keys_at = pl.ds(pl.multiple_of(chunk * WIDE, WIDE), WIDE)
            lanes = slice(pair * PAIR, (pair + 1) * PAIR)
            query = pair_rows(q_ref[rows, lanes], left, SCALE)
            grad = pair_rows(do_ref[rows, lanes], left)
            keys = wide_rows(k_ref, chunk, lanes)
            scores = dot_nt(keys, query) + bias
            probs = jnp.exp(scores - lse_ref[block, pl.ds(pair, 1), :])
            return keys_at, lanes, query, grad, keys, probs, probs * dot_nt(wide_rows(v_ref, chunk, lanes), grad)

        def first(chunk, carry):
            bias = wide_bias(key_code, code, block, chunk)
            return tuple(
                carry[pair] + jnp.sum(pieces(chunk, pair, bias)[-1], 0, keepdims=True)
                for pair in range(pairs)
            )

        deltas = lax.fori_loop(
            0, length // WIDE, first, (jnp.zeros((1, PAIR), jnp.float32),) * pairs
        )
        dq_acc[...] = jnp.zeros_like(dq_acc)

        def second(chunk, carry):
            bias = wide_bias(key_code, code, block, chunk)
            for pair in range(pairs):
                keys_at, lanes, query, grad, keys, probs, terms = pieces(chunk, pair, bias)
                g_scores = (terms - probs * carry[pair]).astype(jnp.bfloat16)
                dv_sum[keys_at, lanes] += dot_nn(probs.astype(jnp.bfloat16), grad)
                dk_sum[keys_at, lanes] += dot_nn(g_scores, query)
                dq_acc[pair] += dot_tn(g_scores, keys)
            return carry

        lax.fori_loop(0, length // WIDE, second, deltas)
        for pair in range(pairs):
            lanes = slice(pair * PAIR, (pair + 1) * PAIR)
            both = dq_acc[pair]
            dq_ref[rows, lanes] = (jnp.where(left, both[:BLK], both[BLK:]) * SCALE).astype(
                dq_ref.dtype
            )
        return nothing

    lax.fori_loop(0, 2, wide_step, 0)
    dk_ref[...] = dk_sum[...].astype(dk_ref.dtype)
    dv_ref[...] = dv_sum[...].astype(dv_ref.dtype)


def in_blocks(rows):
    return rows.reshape(-1, BLK, rows.shape[-1])


VMEM_SPEC = pl.BlockSpec(memory_space=pltpu.VMEM)
SMEM_SPEC = pl.BlockSpec(memory_space=pltpu.SMEM)
ROOM = pltpu.CompilerParams(vmem_limit_bytes=60 * 1024 * 1024)


def attend(table, wide, q, k, v, key_code, query_code):
    length, width = q.shape
    return pl.pallas_call(
        attend_kernel,
        out_shape=(
            jax.ShapeDtypeStruct((length, width), jnp.bfloat16),
            jax.ShapeDtypeStruct((length // BLK, 8, PAIR), jnp.float32),
        ),
        in_specs=[SMEM_SPEC] * 2 + [VMEM_SPEC] * 5,
        out_specs=(VMEM_SPEC, VMEM_SPEC),
        scratch_shapes=[pltpu.VMEM((width // PAIR, PAIR, PAIR), jnp.float32)],
        compiler_params=ROOM,
        cost_estimate=pl.CostEstimate(
            flops=length * width * 1024 * 60, bytes_accessed=length * width * 8,
            transcendentals=length * width * 8,
        ),
        name="attend",
    )(table, wide, q, in_blocks(k), in_blocks(v), in_blocks(key_code), query_code)


def attend_back(table, wide, q, k, v, do, key_code, query_code, lse):
    length, width = q.shape
    shape = jax.ShapeDtypeStruct((length, width), jnp.bfloat16)
    return pl.pallas_call(
        attend_back_kernel,
        out_shape=(shape, shape, shape),
        in_specs=[SMEM_SPEC] * 2 + [VMEM_SPEC] * 7,
        out_specs=(VMEM_SPEC,) * 3,
        scratch_shapes=[
            pltpu.VMEM((length, width), jnp.float32),
            pltpu.VMEM((length, width), jnp.float32),
            pltpu.VMEM((width // PAIR, PAIR, PAIR), jnp.float32),
        ],
        compiler_params=ROOM,
        cost_estimate=pl.CostEstimate(
            flops=length * width * 1024 * 70, bytes_accessed=length * width * 14,
            transcendentals=length * width * 8,
        ),
        name="attend_back",
    )(table, wide, q, in_blocks(k), in_blocks(v), do, in_blocks(key_code), query_code, lse)


GROUPS = 8
DUOS = GROUPS // 2
TILE = 256
FRONT = 512
ANY_SPEC = pl.BlockSpec(memory_space=pl.ANY)
DMA = pltpu.SemaphoreType.DMA
WIDE_ROOM = pltpu.CompilerParams(vmem_limit_bytes=63 * 1024 * 1024)


def normalize(values):
    row_mean = jnp.mean(values, -1, keepdims=True)
    centered = values - row_mean
    row_var = jnp.mean(centered * centered, -1, keepdims=True)
    inverse = lax.rsqrt(row_var + EPSILON)
    return centered * inverse, inverse


def normalize_back(grad, unit, inverse):
    return inverse * (
        grad
        - jnp.mean(grad, -1, keepdims=True)
        - unit * jnp.mean(grad * unit, -1, keepdims=True)
    )


def gelu_both(u):
    root = 0.7978845608028654
    square = u * u
    inner = jnp.tanh(u * (root + (root * 0.044715) * square))
    half = 0.5 + 0.5 * inner
    slope = half + u * (0.5 - 0.5 * (inner * inner)) * (root + (3.0 * root * 0.044715) * square)
    return u * half, slope


def start_copies(pairs, sem):
    copies = [pltpu.make_async_copy(src, dst, sem.at[i]) for i, (src, dst) in enumerate(pairs)]
    for copy in copies:
        copy.start()
    return copies


def wait_copies(copies):
    for copy in copies:
        copy.wait()


def row_of(ref):
    return ref[...].astype(jnp.float32).reshape(1, ref.shape[0])


def my_spot():
    place = lax.axis_index("context")
    return lax.axis_index("tensor"), place // 2, place % 2


def group_homes():
    half, turn, share = my_spot()
    return [
        ((half + h) % 2, ((turn + t) % 2) * 2 + (share + s) % 2)
        for s in range(2)
        for h in range(2)
        for t in range(2)
    ]


def lanes_of(g, cols):
    return pl.ds((g % 2) * cols, cols)


def place_block(block, per):
    half, turn, share = my_spot()
    chunk = block // per
    spot = ((share + chunk) % 2) * 2 + (turn + chunk // 2) % 2
    return spot * per + block % per


def computed(random, per, blocks):
    def find(row):
        block = row + 2
        ids = [block - 1, block, (block + 1) % blocks]
        slots = [place_block(i, per) for i in ids]
        slots += [place_block(jnp.int32(i), per) for i in range(2)]
        slots += [random[block * 3 + i] for i in range(3)]
        return slots[1], slots, block >= 3, block <= blocks - 2

    return find, [place_block(jnp.int32(i), per) for i in range(2)]


def write_codes(segments, live, key_code, query_code, span):
    half, turn, share = my_spot()
    row = pl.ds(half * 2 + turn, 1)
    left = lax.broadcasted_iota(jnp.int32, (1, PAIR), 1) < HD
    per = span // BLK
    for spot in range(4):
        chunk = ((turn + spot) % 2) * 2 + (share + spot // 2) % 2
        lanes = pl.ds(pl.multiple_of(chunk * span, span), span)
        seg = segments[row, lanes]
        code = jnp.where(live[row, lanes] == 1, seg, -1)
        key_code[pl.ds(spot * per, per)] = jnp.broadcast_to(code, (PAIR, span)).T.reshape(
            per, BLK, PAIR
        )
        for two in range(per // 2):
            both = seg[:, two * PAIR : (two + 1) * PAIR]
            turned = pltpu.roll(both, HD, 1)
            at = spot * per + 2 * two
            query_code[at : at + 1, :] = jnp.where(left, both, turned)
            query_code[at + 1 : at + 2, :] = jnp.where(left, turned, both)


def project_attend_kernel(
    random, hidden, x_in, q_all, f_deep, n1_in, n2_in, segments, live, b_q, b_v, far_q, far_v,
    own_ref, other_home, q_home, k_home, v_home, w_home,
    n1, n2, n3, f0, f1, f2, f3, lse_ref, key_code, query_code,
    x_v, q_v, k_v, v_v, o_v, w_v, acc, in_sem, out_sem, w_sem, send_sem, recv_sem,
):
    span = hidden.shape[1]
    length, width = q_v.shape
    depth = f_deep.shape[0]
    half, turn, share = my_spot()
    across, beside, partner = neighbours()
    weights = start_copies(
        [(q_all.at[share, t, s], w_v.at[:, t, s]) for t in range(2) for s in range(2)], w_sem
    )
    chunks = [hidden.at[half * 2 + turn]] + [x_in.at[i] for i in range(3)]
    loads = start_copies(
        [(x, x_v.at[pl.ds(i * span, span)]) for i, x in enumerate(chunks)], in_sem
    )
    deep = lax.axis_index("dp")
    deeps = [{"dp": (deep + j) % depth} for j in range(1, depth)]
    signal_all([across, beside, partner] + deeps)
    ids = iter(range(send_sem.shape[0]))
    started = []

    def go(src, dst, device):
        i = next(ids)
        copy = remote(src, dst, send_sem.at[i], recv_sem.at[i], device)
        copy.start()
        started.append(copy)
        return copy

    at = [(deep + j) % depth for j in range(depth)]
    ends = []

    def share_out(home, landing, j):
        ends.append(go(home.at[at[j]], landing.at[at[j]], partner))

    corner = {0: go(n2.at[at[0]], n3.at[at[0]], beside)}
    to_across, along = {}, {}
    for j in range(1, depth):
        to_across[j] = go(f_deep.at[at[j]], n2.at[at[j]], across)
        along[depth - j] = go(n1.at[deep], n1.at[deep], deeps[j - 1])
    for j in range(depth):
        share_out(f_deep, f0, j)
    share_out(n1, f1, 0)
    share_out(n2, f2, 0)

    def from_side(j):
        along[j].wait_recv()
        share_out(n1, f1, j)

    def from_far(j):
        to_across[j].wait_recv()
        share_out(n2, f2, j)
        corner[j] = go(n2.at[at[j]], n3.at[at[j]], beside)

    def from_corner(j):
        corner[j].wait_recv()
        share_out(n3, f3, j)

    steps = [[(from_far, j)] for j in range(1, depth)]
    steps[0].append((from_corner, 0))
    steps += [[(from_side, j) for j in range(1, depth)] + [(from_corner, 1)]]
    steps += [[(from_corner, j)] for j in range(2, depth)]

    def next_step():
        if steps:
            for action, j in steps.pop(0):
                action(j)

    write_codes(segments, live, key_code, query_code, span)
    same = half == share
    bias = jnp.concatenate(
        [
            jnp.where(same, row_of(b_q), row_of(far_q)),
            jnp.zeros((1, width), jnp.float32),
            jnp.where(same, row_of(b_v), row_of(far_v)),
        ],
        1,
    )
    wait_copies(weights)
    wait_copies(loads)
    per = span // BLK

    def project(i, carry):
        at = pl.ds(pl.multiple_of(i * span, span), span)
        w_qkv = w_v[...].reshape(x_v.shape[1], 3 * width)
        value = (dot_nn(x_v[at, :], w_qkv) + bias).astype(jnp.bfloat16)
        q_v[at, :] = value[:, :width]
        k_v[pl.ds(i * per, per)] = value[:, width : 2 * width].reshape(per, BLK, width)
        v_v[pl.ds(i * per, per)] = value[:, 2 * width :].reshape(per, BLK, width)
        return carry

    lax.fori_loop(0, 4, project, 0)
    stores = start_copies([(q_v, q_home), (k_v, k_home), (v_v, v_home), (w_v, w_home)], out_sem)
    blocks = length // BLK
    find, wide = computed(random, span // BLK, blocks)
    count = blocks - 2
    leg = -(-count // 5)
    legs = [(start, min(start + leg, count), next_step) for start in range(0, count, leg)]
    attend_blocks(
        find, wide, legs, q_v, k_v, v_v, key_code, query_code, o_v, lse_ref, acc,
        pause=lambda step: next_step() if step else None,
    )
    own_ref[...] = o_v[: length // 2, :]
    swap = go(o_v.at[pl.ds(length // 2, length // 2)], other_home, partner)
    while steps:
        next_step()
    for copy in ends + [swap]:
        copy.wait_recv()
    for copy in started:
        copy.wait_send()
    wait_copies(stores)


def project_attend(
    random, hidden, x_in, q_all, f_deep, n1, n2, segments, live, b_q, b_v, far_q, far_v
):
    span, features = hidden.shape[1:]
    length = 4 * span
    depth, slim, cols = q_all.shape[3:]
    width = cols // 3
    bf16, shape = jnp.bfloat16, jax.ShapeDtypeStruct
    piece = shape(f_deep.shape, bf16)
    outs = pl.pallas_call(
        project_attend_kernel,
        out_shape=(shape((length // 2, width), bf16),) * 2
        + (shape((length, width), bf16),)
        + (shape((length // BLK, BLK, width), bf16),) * 2
        + (shape((depth, 2, 2, slim, cols), bf16),)
        + (piece,) * 7
        + (
            shape((length // BLK, 8, PAIR), jnp.float32),
            shape((length // BLK, BLK, PAIR), jnp.int32),
            shape((length // BLK, PAIR), jnp.int32),
        ),
        in_specs=[SMEM_SPEC] + [ANY_SPEC] * 6 + [VMEM_SPEC] * 6,
        out_specs=(VMEM_SPEC,) + (ANY_SPEC,) * 12 + (VMEM_SPEC,) * 3,
        scratch_shapes=[pltpu.VMEM((length, features), bf16)]
        + [pltpu.VMEM((length, width), bf16)]
        + [pltpu.VMEM((length // BLK, BLK, width), bf16)] * 2
        + [pltpu.VMEM((length, width), bf16)]
        + [
            pltpu.VMEM((depth, 2, 2, slim, cols), bf16),
            pltpu.VMEM((width // PAIR, PAIR, PAIR), jnp.float32),
            DMA((4,)), DMA((4,)), DMA((4,)), DMA((8 * depth + 2,)), DMA((8 * depth + 2,)),
        ],
        input_output_aliases={5: 6, 6: 7},
        compiler_params=pltpu.CompilerParams(
            vmem_limit_bytes=63 * 1024 * 1024, collective_id=3, has_side_effects=True
        ),
        cost_estimate=pl.CostEstimate(
            flops=length * width * 1024 * 65, bytes_accessed=length * width * 16,
            transcendentals=length * width * 8,
        ),
        name="project_attend",
    )(
        random, hidden, x_in, q_all, f_deep, n1, n2, segments, live, b_q, b_v, far_q, far_v
    )
    att0, att1, q, k, v, w_qkv, *pieces, lse, key_code, query_code = outs
    w_qkv = w_qkv.reshape(features, cols)
    return att0, att1, q, k, v, lse, w_qkv, [f_deep] + pieces, key_code, query_code


def attend_grad_kernel(
    random, do0, do1, q_in, k_in, v_in, layer, key_code, query_code, lse_ref,
    d_ref, layer_home, sums,
    layer_v, layer_sem, q_v, k_v, v_v, do_v, dk_sum, dv_sum, acc, in_sem,
):
    f32 = jnp.float32
    length, width = q_v.shape
    half_length = length // 2
    loads = start_copies(
        [
            (q_in, q_v), (k_in, k_v), (v_in, v_v),
            (do0, do_v.at[pl.ds(0, half_length)]),
            (do1, do_v.at[pl.ds(half_length, half_length)]),
        ],
        in_sem,
    )
    take = pltpu.make_async_copy(layer, layer_v, layer_sem.at[0])
    put = pltpu.make_async_copy(layer_v, layer_home, layer_sem.at[1])
    take.start()
    wait_copies(loads)
    take.wait()
    put.start()
    parts = [d_ref.at[:, pl.ds(i * width, width)] for i in range(3)]
    blocks = length // BLK
    find, wide = computed(random, blocks // 4, blocks)
    attend_back_blocks(
        find, wide, blocks - 2, q_v, k_v, v_v, do_v, key_code, query_code, lse_ref,
        *parts, dk_sum, dv_sum, acc,
    )
    share = my_spot()[2]
    sums[...] = jnp.zeros_like(sums)
    for s in range(2):

        @pl.when(share == s)
        def _():
            lanes = slice(s * width, (s + 1) * width)
            sums[0:1, lanes] = jnp.sum(d_ref[:, :width].astype(f32), 0, keepdims=True)
            sums[1:2, lanes] = jnp.sum(d_ref[:, 2 * width :].astype(f32), 0, keepdims=True)
    put.wait()


def attend_grad(random, do0, do1, q, k, v, layer, key_code, query_code, lse):
    length, width = q.shape
    f32, bf16, shape = jnp.float32, jnp.bfloat16, jax.ShapeDtypeStruct
    return pl.pallas_call(
        attend_grad_kernel,
        out_shape=(
            shape((length, 3 * width), bf16), shape(layer.shape, bf16), shape((8, 2 * width), f32)
        ),
        in_specs=[SMEM_SPEC] + [ANY_SPEC] * 6 + [VMEM_SPEC] * 3,
        out_specs=(VMEM_SPEC, ANY_SPEC, VMEM_SPEC),
        scratch_shapes=[pltpu.VMEM(layer.shape, bf16), DMA((2,))]
        + [pltpu.VMEM((length, width), bf16)]
        + [pltpu.VMEM((length // BLK, BLK, width), bf16)] * 2
        + [pltpu.VMEM((length, width), bf16)]
        + [pltpu.VMEM((length, width), f32)] * 2
        + [pltpu.VMEM((width // PAIR, PAIR, PAIR), f32), DMA((5,))],
        compiler_params=WIDE_ROOM,
        cost_estimate=pl.CostEstimate(
            flops=length * width * 1024 * 75, bytes_accessed=length * width * 30,
            transcendentals=length * width * 8,
        ),
        name="attend_grad",
    )(random, do0, do1, q, k, v, layer, key_code, query_code, lse)


def load_weights(groups, w_up, w_dn, w_out, up_sem, dn_sem, wo_sem):
    depth, deep, cols = groups[0].shape
    thin = w_up.shape[2]
    slim = deep - 2 * thin
    homes = group_homes()
    out_loads = []
    for g in range(GROUPS):
        half, at = homes[g]
        for d in range(depth):
            spot = pl.ds(pl.multiple_of(d * thin + at * slim, 16), slim)
            out_loads.append(
                pltpu.make_async_copy(
                    groups[g].at[d, pl.ds(2 * thin, slim)], w_out.at[half, spot], wo_sem.at[g, d]
                )
            )
    up_loads = [
        pltpu.make_async_copy(
            groups[g].at[:, pl.ds(0, thin)], w_up.at[g // 2, :, :, lanes_of(g, cols)], up_sem.at[g]
        )
        for g in range(GROUPS)
    ]
    dn_loads = [
        pltpu.make_async_copy(
            groups[g].at[:, pl.ds(thin, thin)],
            w_dn.at[g // 2, :, :, lanes_of(g, cols)],
            dn_sem.at[g],
        )
        for g in range(GROUPS)
    ]
    return out_loads, up_loads, dn_loads


def whole(ref, g):
    depth, thin, cols = ref.shape[1:]
    return ref[g].reshape(depth * thin, cols)


def ffn_front_kernel(att0, att1, hidden, x_in, g_all, *rest):
    groups = rest[:GROUPS]
    (
        key_code, v_out, v_gain1, v_shift1, v_down, v_gain2, v_shift2, b_near, b_far,
        out0_home, out1_home, slope_home, g_second_home, unit_home, norm_t_home, down_home,
        inverse_ref, sums,
        att_v, x_v, g_v, w_up, w_dn, w_out, act, slope, normed_low,
        out_v, g_second_v, unit_v, norm_t, g_ffn_t, stage, b_up, b_all,
        in_sem, up_sem, dn_sem, wo_sem, stage_sem, home_sem, end_sem, g_sem,
    ) = rest[GROUPS:]
    f32, bf16 = jnp.float32, jnp.bfloat16
    rows, width = x_v.shape
    span = hidden.shape[1]
    depth, deep, cols = groups[0].shape
    half, turn, share = my_spot()
    x_chunks = (hidden.at[half * 2 + turn], x_in.at[0])
    g_chunks = (g_all.at[half * 2 + turn],)
    other = (share + 1) % 2
    out_loads, up_loads, dn_loads = load_weights(groups, w_up, w_dn, w_out, up_sem, dn_sem, wo_sem)
    loads = start_copies(
        [(a, att_v.at[:, lanes_of(i, cols)]) for i, a in enumerate((att0, att1))]
        + [(x, x_v.at[pl.ds(i * span, span)]) for i, x in enumerate(x_chunks)]
        + [(g, g_v.at[pl.ds(i * span, span)]) for i, g in enumerate(g_chunks)],
        in_sem,
    )
    for copy in out_loads + up_loads + dn_loads:
        copy.start()
    beside = neighbours()[1]
    signal_all([beside])
    g_next = remote(
        g_all.at[half * 2 + (turn + 1) % 2], g_v.at[pl.ds(span, span)], g_sem.at[0], g_sem.at[1],
        beside,
    )
    g_next.start()
    sums[...] = jnp.zeros_like(sums)
    b_all[0:1, :] = row_of(b_near)
    b_all[1:2, :] = row_of(b_far)
    for g in range(GROUPS):
        at = group_homes()[g][1]
        lanes = pl.ds(pl.multiple_of(at * cols, PAIR), cols)
        value = b_all[g // 2 % 2 : g // 2 % 2 + 1, lanes]
        b_up[g // 2 : g // 2 + 1, (g % 2) * cols : (g % 2 + 1) * cols] = value
    wait_copies(loads + out_loads)
    b_out, gain1, shift1, b_down, gain2, shift2 = (
        row_of(ref) for ref in (v_out, v_gain1, v_shift1, v_down, v_gain2, v_shift2)
    )

    def add_sum(index, value):
        sums[index : index + 1, :] += jnp.sum(value, 0, keepdims=True)

    def homes(tile):
        at = pl.ds(pl.multiple_of(tile * FRONT, FRONT), FRONT)
        return [
            pltpu.make_async_copy(src, dst, home_sem.at[i, tile])
            for i, (src, dst) in enumerate(
                [
                    (slope.at[:, at], slope_home.at[:, at]),
                    (g_second_v.at[at], g_second_home.at[at]),
                    (unit_v.at[at], unit_home.at[at]),
                ]
            )
        ]

    def tile_step(tile, carry):
        at = pl.ds(pl.multiple_of(tile * FRONT, FRONT), FRONT)
        live = (key_code[at, :1] >= 0).astype(f32)
        add_sum(11, jnp.broadcast_to(live, (FRONT, width)))
        attn = b_out + dot_nt(att_v[at, :], jnp.concatenate([w_out[share], w_out[other]], 1))
        x = x_v[at, :].astype(f32)
        first = x + attn
        add_sum(6, live * (x * x))
        add_sum(7, live * (first * first))
        add_sum(9, live * (attn * attn))
        unit1, inverse1 = normalize(first)
        unit_v[at, :] = unit1
        inverse_ref[at, :] = inverse1
        normed = unit1 * gain1 + shift1
        low = normed.astype(bf16)
        normed_low[...] = low
        norm_t[:, at] = low.T

        @pl.when(tile == 0)
        def _():
            wait_copies(up_loads + dn_loads)

        @pl.when(tile == span // FRONT)
        def _():
            g_next.wait_recv()

        def up_step(g, ffn):
            pre = dot_nn(normed_low[...], whole(w_up, g)) + b_up[pl.ds(g, 1), :]
            value, rise = gelu_both(pre)
            value = value.astype(bf16)
            act[g, at, :] = value
            slope[g, at, :] = rise.astype(bf16)
            return ffn + dot_nt(value, whole(w_dn, g))

        ffn = lax.fori_loop(0, DUOS, up_step, jnp.broadcast_to(b_down, (FRONT, width)))
        second = normed + ffn
        add_sum(8, live * (second * second))
        add_sum(10, live * (ffn * ffn))
        unit2, inverse2 = normalize(second)
        out_v[at, :] = (unit2 * gain2 + shift2).astype(bf16)
        g_out = g_v[at, :].astype(f32)
        add_sum(4, g_out * unit2)
        add_sum(5, g_out)
        g_second = normalize_back(g_out * gain2, unit2, inverse2)
        g_second_v[at, :] = g_second
        g_ffn = g_second.astype(bf16)
        add_sum(3, g_ffn.astype(f32))
        g_ffn_t[:, at] = g_ffn.T
        for copy in homes(tile):
            copy.start()
        return carry

    lax.fori_loop(0, rows // FRONT, tile_step, 0)
    last = start_copies(
        [
            (norm_t, norm_t_home),
            (out_v.at[pl.ds(0, span)], out0_home),
            (out_v.at[pl.ds(span, span)], out1_home),
        ],
        end_sem,
    )

    def leave(g):
        return pltpu.make_async_copy(stage.at[g], down_home.at[g], stage_sem.at[g])

    def down_step(duo, carry):
        down = dot_nn(g_ffn_t[...], act[duo]).astype(bf16).reshape(depth, -1, 2 * cols)
        for i in range(2):
            stage[2 * duo + i] = down[:, :, i * cols : (i + 1) * cols]
            leave(2 * duo + i).start()
        return carry

    lax.fori_loop(0, DUOS, down_step, 0)
    for tile in range(rows // FRONT):
        wait_copies(homes(tile))
    wait_copies([leave(g) for g in range(GROUPS)] + last)
    g_next.wait_send()


def ffn_front(att0, att1, hidden, x_in, g_all, groups, key_code, vectors, b_near, b_far):
    rows, part = att0.shape
    width = hidden.shape[2]
    depth, deep, cols = groups[0].shape
    thin = width // depth
    f32, bf16, shape = jnp.float32, jnp.bfloat16, jax.ShapeDtypeStruct
    weights = pltpu.VMEM((DUOS, depth, thin, 2 * cols), bf16)
    flat = pltpu.VMEM((rows, width), bf16)
    tall = pltpu.VMEM((rows, width), f32)
    deep_rows = pltpu.VMEM((DUOS, rows, 2 * cols), bf16)
    turned = pltpu.VMEM((width, rows), bf16)
    return pl.pallas_call(
        ffn_front_kernel,
        out_shape=(
            shape((rows // 2, width), bf16), shape((rows // 2, width), bf16),
            shape((DUOS, rows, 2 * cols), bf16),
            shape((rows, width), f32), shape((rows, width), f32), shape((width, rows), bf16),
            shape((GROUPS, depth, thin, cols), bf16), shape((rows, 1), f32), shape((16, width), f32),
        ),
        in_specs=[ANY_SPEC] * (5 + GROUPS) + [VMEM_SPEC] * 9,
        out_specs=(ANY_SPEC,) * 7 + (VMEM_SPEC,) * 2,
        scratch_shapes=[
            flat, flat, flat, weights, weights, pltpu.VMEM((2, width, part), bf16),
            deep_rows, deep_rows, pltpu.VMEM((FRONT, width), bf16),
            flat, tall, tall, turned, turned, pltpu.VMEM((GROUPS, depth, thin, cols), bf16),
            pltpu.VMEM((DUOS, 2 * cols), f32), pltpu.VMEM((2, 4 * cols), f32),
            DMA((6,)), DMA((GROUPS,)), DMA((GROUPS,)), DMA((GROUPS, depth)), DMA((GROUPS,)),
            DMA((3, rows // FRONT)), DMA((3,)), DMA((2,)),
        ],
        compiler_params=pltpu.CompilerParams(
            vmem_limit_bytes=63 * 1024 * 1024, collective_id=4, has_side_effects=True
        ),
        cost_estimate=pl.CostEstimate(
            flops=38 * 10**9, bytes_accessed=40 * 10**6, transcendentals=rows * GROUPS * cols
        ),
        name="ffn_front",
    )(att0, att1, hidden, x_in, g_all, *groups, key_code, *vectors, b_near, b_far)


def ffn_rear_kernel(
    att0, att1, slope_in, g_second_in, unit_in, norm_t_in, out0, out1, downs, *rest
):
    groups = rest[:GROUPS]
    (
        inverse_ref, v_gain1,
        g_first_home, do_own, do_far, layer_home, *totals
    ) = rest[GROUPS : GROUPS + 5 + DUOS + groups[0].shape[0]]
    corners = totals[DUOS - 1 :]
    (
        sums, up_sums,
        att_v, slope, g_second_v, unit_v, norm_t, w_up, w_dn, w_out, g_pre,
        g_first_v, g_att_v, g_attn_t, out_v, far_v, got_v, got_dn, near_v, stage,
        in_sem, up_sem, dn_sem, wo_sem, stage_sem, home_sem, out_sem,
        l_send, l_recv, a_send, a_recv, u_send, u_recv, corner_sem,
    ) = rest[GROUPS + 5 + DUOS + len(corners) :]
    f32, bf16 = jnp.float32, jnp.bfloat16
    rows, width = unit_v.shape
    span = out0.shape[0]
    depth, deep, cols = groups[0].shape
    thin = w_up.shape[2]
    slim = deep - 2 * thin
    half, turn, share = my_spot()
    other = (share + 1) % 2
    across, beside, partner = neighbours()
    out_loads, up_loads, dn_loads = load_weights(groups, w_up, w_dn, w_out, up_sem, dn_sem, wo_sem)
    wait_order = [
        pltpu.make_async_copy(src, dst, in_sem.at[i])
        for i, (src, dst) in enumerate(
            [
                (g_second_in, g_second_v), (slope_in, slope), (unit_in, unit_v),
                (norm_t_in, norm_t), (att0, att_v.at[:, lanes_of(0, cols)]),
                (att1, att_v.at[:, lanes_of(1, cols)]),
            ]
        )
    ]
    for copy in wait_order[:1] + dn_loads + wait_order[1:2] + up_loads + wait_order[2:3]:
        copy.start()
    for copy in out_loads + wait_order[3:]:
        copy.start()
    late = start_copies([(out0, out_v), (downs.at[pl.ds(0, DUOS)], near_v)], out_sem)
    signal_all([across, beside, partner])
    mine = layer_home.at[half * 2 + turn]
    theirs = layer_home.at[half * 2 + (turn + 1) % 2]
    parts = [pl.ds(i * (span // 2), span // 2) for i in range(2)]
    layer = [
        remote(out1.at[parts[0]], mine.at[parts[0]], l_send.at[0], l_recv.at[0], beside),
        remote(out0, mine, l_send.at[1], l_recv.at[1], across),
        remote(theirs.at[parts[0]], theirs.at[parts[0]], l_send.at[2], l_recv.at[2], across),
        remote(downs.at[pl.ds(DUOS, DUOS)], got_dn, l_send.at[3], l_recv.at[3], partner),
        remote(out1.at[parts[1]], mine.at[parts[1]], l_send.at[4], l_recv.at[4], beside),
        remote(theirs.at[parts[1]], theirs.at[parts[1]], l_send.at[5], l_recv.at[5], across),
    ]
    for i in (0, 4, 1, 3):
        layer[i].start()
    sums[...] = jnp.zeros_like(sums)
    up_sums[...] = jnp.zeros_like(up_sums)
    gain1 = row_of(v_gain1)
    wait_copies(wait_order[:1] + dn_loads + wait_order[1:2])
    out_weight = lambda: jnp.concatenate([w_out[share], w_out[other]], 1)

    def add_sum(index, value):
        sums[index : index + 1, :] += jnp.sum(value, 0, keepdims=True)

    def tile_rows(tile):
        return pl.ds(pl.multiple_of(tile * TILE, TILE), TILE)

    def give(tile):
        at = tile_rows(tile)
        return remote(g_att_v.at[1, at], do_far.at[at], a_send.at[tile], a_recv.at[tile], partner)

    tiles = rows // TILE

    def tile_step(tile, carry):
        at = tile_rows(tile)

        @pl.when(tile == 0)
        def _():
            wait_copies(up_loads + wait_order[2:] + out_loads)

        for late_tile, i in ((tiles - 2, 0), (tiles - 1, 1)):

            @pl.when(tile == late_tile)
            def _():
                layer[(0, 4)[i]].wait_recv()
                layer[(2, 5)[i]].start()

        g_second = g_second_v[at, :]
        g_ffn = g_second.astype(bf16)

        def back_step(g, total):
            grad = (dot_nn(g_ffn, whole(w_dn, g)) * slope[g, at, :].astype(f32)).astype(bf16)
            g_pre[g, at, :] = grad
            up_sums[pl.ds(g, 1), :] += jnp.sum(grad.astype(f32), 0, keepdims=True)
            return total + dot_nt(grad, whole(w_up, g))

        g_normed = lax.fori_loop(0, DUOS, back_step, g_second)
        unit1 = unit_v[at, :]
        add_sum(1, g_normed * unit1)
        add_sum(2, g_normed)
        g_first = normalize_back(g_normed * gain1, unit1, inverse_ref[at, :])
        g_first_v[at, :] = g_first
        g_attn = g_first.astype(bf16)
        add_sum(0, g_attn.astype(f32))
        g_attn_t[:, at] = g_attn.T
        both = dot_nn(g_attn, out_weight()).astype(bf16)
        g_att_v[0, at, :] = both[:, :cols]
        g_att_v[1, at, :] = both[:, cols:]
        give(tile).start()
        return carry

    lax.fori_loop(0, tiles, tile_step, 0)
    homes = start_copies([(g_att_v.at[0], do_own), (g_first_v, g_first_home)], home_sem)
    wait_copies(late)
    own_out = pltpu.make_async_copy(out_v, mine, out_sem.at[0])
    own_out.start()
    both = dot_nn(g_attn_t[...], att_v[...]).astype(bf16)
    w_out[share] = both[:, :cols]
    w_out[other] = both[:, cols:]

    def out_rows(g, d):
        where = (half + g // 2) % 2
        at = ((turn + g) % 2) * 2 + (share + g // 4) % 2
        return w_out[where, pl.ds(pl.multiple_of(d * thin + at * slim, 16), slim), :]

    def up_of(duo):
        up = dot_nn(norm_t[...], g_pre[duo]).astype(bf16).reshape(depth, thin, 2 * cols)
        return [(2 * duo + i, up[:, :, i * cols : (i + 1) * cols]) for i in range(2)]

    def pass_on(i):
        return remote(far_v.at[i], got_v.at[i], u_send.at[i], u_recv.at[i], partner)

    def far_step(duo, carry):
        for g, up in up_of(duo):
            i = g - DUOS
            far_v[i, :, pl.ds(0, thin), :] = up
            for d in range(depth):
                far_v[i, d, pl.ds(thin, slim), :] = out_rows(g, d)
            pass_on(i).start()
        return carry

    lax.fori_loop(DUOS // 2, DUOS, far_step, 0)
    sends = [pass_on(i) for i in range(DUOS)]
    layer[3].wait_recv()
    add = lambda a, b: (a.astype(f32) + b.astype(f32)).astype(bf16)
    stores = [None] * DUOS
    for duo in range(DUOS // 2):
        for g, up in up_of(duo):
            slot = g % 2
            if g >= 2:
                stores[g - 2].wait()
            sends[g].wait_recv()
            stage[slot, :, pl.ds(0, thin), :] = add(up, got_v[g, :, pl.ds(0, thin), :])
            stage[slot, :, pl.ds(thin, thin), :] = add(near_v[g], got_dn[g])
            for d in range(depth):
                stage[slot, d, pl.ds(2 * thin, slim), :] = add(
                    out_rows(g, d), got_v[g, d, pl.ds(thin, slim), :]
                )
            if g == DUOS - 1:
                deep_at = lax.axis_index("dp")
                rounds = start_copies(
                    [
                        (stage.at[slot, (deep_at + j) % depth], home)
                        for j, home in enumerate(corners)
                    ],
                    corner_sem,
                )
                continue
            stores[g] = pltpu.make_async_copy(stage.at[slot], totals[g], stage_sem.at[slot])
            stores[g].start()
    for tile in range(tiles):
        give(tile).wait()
    for i in (1, 2, 5):
        layer[i].wait_recv()
    for copy in layer + sends:
        copy.wait_send()
    wait_copies(stores[-2:-1] + rounds + homes + [own_out])


def ffn_rear(
    att0, att1, slope, g_second, unit, norm_t, out0, out1, downs_in, groups, inverse, gain1
):
    rows, part = att0.shape
    span, width = out0.shape
    depth, deep, cols = groups[0].shape
    thin = width // depth
    f32, bf16, shape, v = jnp.float32, jnp.bfloat16, jax.ShapeDtypeStruct, pltpu.VMEM
    weights = v((DUOS, depth, thin, 2 * cols), bf16)
    flat = v((rows, width), bf16)
    tall = v((rows, width), f32)
    deep_rows = v((DUOS, rows, 2 * cols), bf16)
    turned = v((width, rows), bf16)
    mixed = v((DUOS, depth, deep - thin, cols), bf16)
    downs = v((DUOS, depth, thin, cols), bf16)
    tiles = rows // TILE
    return pl.pallas_call(
        ffn_rear_kernel,
        out_shape=(
            shape((rows, width), f32), shape((rows, part), bf16), shape((rows, part), bf16),
            shape((4, span, width), bf16),
        )
        + (shape((depth, deep, cols), bf16),) * (DUOS - 1)
        + (shape((deep, cols), bf16),) * depth
        + (shape((16, width), f32), shape((DUOS, 2 * cols), f32)),
        in_specs=[ANY_SPEC] * (9 + GROUPS) + [VMEM_SPEC] * 2,
        out_specs=(ANY_SPEC,) * (3 + DUOS + depth) + (VMEM_SPEC,) * 2,
        scratch_shapes=[
            flat, deep_rows, tall, tall, turned, weights, weights,
            v((2, width, part), bf16), deep_rows, tall, v((2, rows, part), bf16), turned,
            v((span, width), bf16), mixed, mixed, downs, downs, v((2, depth, deep, cols), bf16),
            DMA((6,)), DMA((GROUPS,)), DMA((GROUPS,)), DMA((GROUPS, depth)), DMA((2,)), DMA((2,)),
            DMA((2,)), DMA((6,)), DMA((6,)), DMA((tiles,)), DMA((tiles,)), DMA((DUOS,)),
            DMA((DUOS,)), DMA((depth,)),
        ],
        compiler_params=pltpu.CompilerParams(
            vmem_limit_bytes=63 * 1024 * 1024, collective_id=2, has_side_effects=True
        ),
        cost_estimate=pl.CostEstimate(
            flops=45 * 10**9, bytes_accessed=40 * 10**6, transcendentals=0
        ),
        name="ffn_rear",
    )(
        att0, att1, slope, g_second, unit, norm_t, out0, out1, downs_in, *groups, inverse, gain1
    )


MESH = pl.DeviceIdType.MESH
CUTS = 8
THIRDS = 3


def signal_all(devices):
    barrier = pltpu.get_barrier_semaphore()
    for device in devices:
        pl.semaphore_signal(barrier, inc=1, device_id=device, device_id_type=MESH)
    pl.semaphore_wait(barrier, len(devices))


def neighbours():
    half, turn, share = my_spot()
    return (
        {"tensor": (half + 1) % 2},
        {"context": ((turn + 1) % 2) * 2 + share},
        {"context": turn * 2 + (share + 1) % 2},
    )


def remote(src, dst, send_sem, recv_sem, device):
    return pltpu.make_async_remote_copy(
        src_ref=src, dst_ref=dst, send_sem=send_sem, recv_sem=recv_sem,
        device_id=device, device_id_type=MESH,
    )


def fetch_kernel(
    hidden, w_q, w_k, w_v, w_up, w_down, w_out, bias_q, bias_v, bias_u,
    x_out, q_all, f_deep, n1, n2, far_q, far_v, far_u,
    qkv, ffn, cut_sem, own_sem, x_send, x_recv, z_send, z_recv, f_send, f_recv,
    h_send, h_recv, t_send, t_recv, c_send, c_recv, b_sem, n_send, n_recv,
):
    half, turn, share = my_spot()
    deep = lax.axis_index("dp")
    depth = f_deep.shape[0]
    across, beside, partner = neighbours()
    up, down = {"dp": (deep + 1) % depth}, {"dp": (deep + depth - 1) % depth}
    slim, thin, cols = qkv.shape[0], w_q.shape[0], w_q.shape[1]
    place = turn * 2 + share
    my_rows = pl.ds(pl.multiple_of(place * slim, 16), slim)
    my_lanes = pl.ds(pl.multiple_of(place * cols, PAIR), cols)
    cuts = start_copies(
        [(w.at[my_rows], qkv.at[:, pl.ds(i * cols, cols)]) for i, w in enumerate((w_q, w_k, w_v))]
        + [(w.at[:, my_lanes], ffn.at[pl.ds(i * thin, thin)]) for i, w in enumerate((w_up, w_down))]
        + [(w_out.at[my_rows], ffn.at[pl.ds(2 * thin, slim)])],
        cut_sem,
    )
    signal_all([across, beside, partner, up, down])
    wait_copies(cuts)

    slot = lambda h, t, d: q_all.at[h, t, share, d]
    own = start_copies([(qkv, slot(half, turn, deep)), (ffn, f_deep.at[deep])], own_sem)

    def to_up(d):
        return remote(slot(half, turn, d), slot(half, turn, d), z_send.at[0, d], z_recv.at[d], up)

    def to_down(d):
        return remote(slot(half, turn, d), slot(half, turn, d), z_send.at[1, d], z_recv.at[d], down)

    third = f_deep.shape[1] // THIRDS

    def f_copies(d, side, device):
        return [
            remote(
                f_deep.at[d, pl.ds(i * third, third)], f_deep.at[d, pl.ds(i * third, third)],
                f_send.at[side, d, i], f_recv.at[d, i], device,
            )
            for i in range(THIRDS)
        ]

    f_up = lambda d: f_copies(d, 0, up)
    f_down = lambda d: f_copies(d, 1, down)

    def to_across(t, d):
        return remote(slot(half, t, d), slot(half, t, d), h_send.at[t, d], h_recv.at[t, d], across)

    def from_across(t, d):
        other = slot((half + 1) % 2, t, d)
        return remote(other, other, h_send.at[t, d], h_recv.at[t, d], across)

    def to_beside(d):
        return remote(slot(half, turn, d), slot(half, turn, d), t_send.at[d], t_recv.at[d], beside)

    def from_beside(d):
        other = slot(half, (turn + 1) % 2, d)
        return remote(other, other, t_send.at[d], t_recv.at[d], beside)

    def to_partner(t, d):
        piece = slot((share + 1) % 2, t, d)
        return remote(piece, piece, c_send.at[t, d], c_recv.at[t, d], partner)

    def from_partner(t, d):
        piece = q_all.at[share, t, (share + 1) % 2, d]
        return remote(piece, piece, c_send.at[t, d], c_recv.at[t, d], partner)

    cut = x_out.shape[1] // CUTS
    piece_rows = lambda i: pl.ds(i * cut, cut)
    x_next = [
        remote(
            hidden.at[half * 2 + (turn + 1) % 2, piece_rows(i)], x_out.at[0, piece_rows(i)],
            x_send.at[0, i], x_recv.at[0, i], beside,
        )
        for i in range(CUTS)
    ]
    x_mine = remote(
        hidden.at[half * 2 + turn], x_out.at[1], x_send.at[1, 0], x_recv.at[1, 0], partner
    )
    x_relay = [
        remote(
            x_out.at[0, piece_rows(i)], x_out.at[2, piece_rows(i)],
            x_send.at[2, i], x_recv.at[2, i], partner,
        )
        for i in range(CUTS)
    ]
    biases = [
        remote(src, dst, b_sem.at[0, i], b_sem.at[1, i], across)
        for i, (src, dst) in enumerate(((bias_q, far_q), (bias_v, far_v), (bias_u, far_u)))
    ]
    wait_copies(own)
    own_turn = (share + 1) % 2 == half

    def spread_own(d):
        to_across(turn, d).start()
        to_beside(d).start()

        @pl.when(own_turn)
        def _():
            to_partner(turn, d).start()

    def when(condition, *copies):
        @pl.when(condition)
        def _():
            for copy in copies:
                copy.start()

    when(deep < depth - 1, to_up(deep))
    when(deep > 0, to_down(deep))
    when(deep < depth - 1, f_up(deep)[0])
    when(deep > 0, f_down(deep)[0])
    spread_own(deep)
    x_next[0].start()
    for copy in biases:
        copy.start()
    x_mine.start()
    for k in range(1, depth):
        low, high = (deep + depth - k) % depth, (deep + k) % depth

        @pl.when(deep >= k)
        def _():
            to_up(low).wait_recv()
            when(deep < depth - 1, to_up(low))
            spread_own(low)

        @pl.when(deep + k < depth)
        def _():
            to_down(high).wait_recv()
            when(deep > 0, to_down(high))
            spread_own(high)

        if k < THIRDS:
            when(deep < depth - 1, f_up(deep)[k])
            when(deep > 0, f_down(deep)[k])
        x_next[k].start()

    for i in range(depth, THIRDS):
        when(deep < depth - 1, f_up(deep)[i])
        when(deep > 0, f_down(deep)[i])
    for copy in x_next[depth:]:
        copy.start()
    for k in range(depth):
        d = (deep + k) % depth
        from_beside(d).wait_recv()
        to_across((turn + 1) % 2, d).start()

        @pl.when(own_turn)
        def _():
            to_partner((turn + 1) % 2, d).start()

    f_side = [
        remote(
            f_deep.at[deep, pl.ds(i * third, third)], home.at[deep, pl.ds(i * third, third)],
            n_send.at[j, i], n_recv.at[j, i], device,
        )
        for i in range(THIRDS)
        for j, (home, device) in enumerate(((n1, beside), (n2, across)))
    ]
    for copy in f_side:
        copy.start()

    def f_step(k):
        low, high = (deep + depth - k) % depth, (deep + k) % depth

        @pl.when(deep >= k)
        def _():
            for copy in f_up(low):
                copy.wait_recv()
                when(deep < depth - 1, copy)

        @pl.when(deep + k < depth)
        def _():
            for copy in f_down(high):
                copy.wait_recv()
                when(deep > 0, copy)

    def x_step(step):
        for i in range(step * CUTS // (depth + 1), (step + 1) * CUTS // (depth + 1)):
            x_next[i].wait_recv()
            x_relay[i].start()

    f_step(1)
    for step, t in enumerate((turn, (turn + 1) % 2)):
        for k in range(depth):
            d = (deep + k) % depth
            from_across(t, d).wait_recv()

            @pl.when(jnp.logical_not(own_turn))
            def _():
                to_partner(t, d).start()

        x_step(step)
        if step == 0 and depth > 2:
            f_step(2)
    for k in range(3, depth):
        x_step(k - 1)
        f_step(k)
    for step in range(max(2, depth - 1), depth + 1):
        x_step(step)

    for t in range(2):
        for d in range(depth):
            from_partner(t, d).wait_recv()
    x_mine.wait_recv()
    for copy in x_relay + biases + f_side:
        copy.wait_recv()
    for d in range(depth):
        for copy in (to_across(0, d), to_across(1, d), to_beside(d), to_partner(0, d), to_partner(1, d)):
            copy.wait_send()

        @pl.when(jnp.logical_and(deep < depth - 1, deep >= d))
        def _():
            for copy in [to_up(d)] + f_up(d):
                copy.wait_send()

        @pl.when(jnp.logical_and(deep > 0, deep <= d))
        def _():
            for copy in [to_down(d)] + f_down(d):
                copy.wait_send()

    for copy in x_next + x_relay + [x_mine] + biases + f_side:
        copy.wait_send()


def fetch(hidden_in, weights, biases, depth):
    span, width = hidden_in.shape[1:]
    thin, cols = weights[0].shape
    slim = thin // 4
    bf16, shape = jnp.bfloat16, jax.ShapeDtypeStruct
    pair = DMA((2, depth))
    return pl.pallas_call(
        fetch_kernel,
        out_shape=(
            shape((3, span, width), bf16),
            shape((2, 2, 2, depth, slim, 3 * cols), bf16),
            *(shape((depth, 2 * thin + slim, cols), bf16) for _ in range(3)),
            *(shape(b.shape, bf16) for b in biases),
        ),
        in_specs=[ANY_SPEC] * 7 + [VMEM_SPEC] * 3,
        out_specs=(ANY_SPEC, VMEM_SPEC) + (ANY_SPEC,) * 3 + (VMEM_SPEC,) * 3,
        scratch_shapes=[
            pltpu.VMEM((slim, 3 * cols), bf16), pltpu.VMEM((2 * thin + slim, cols), bf16),
            DMA((6,)), DMA((2,)), DMA((3, CUTS)), DMA((3, CUTS)), pair, DMA((depth,)),
            DMA((2, depth, THIRDS)), DMA((depth, THIRDS)),
            pair, pair, DMA((depth,)), DMA((depth,)), pair, pair, DMA((2, 3)),
            DMA((2, THIRDS)), DMA((2, THIRDS)),
        ],
        compiler_params=pltpu.CompilerParams(
            vmem_limit_bytes=63 * 1024 * 1024, collective_id=0, has_side_effects=True
        ),
        cost_estimate=pl.CostEstimate(
            flops=30 * 10**9, bytes_accessed=10 * 10**6, transcendentals=0
        ),
        name="fetch",
    )(hidden_in, *weights, *biases)


SUBS = 4


def settle_kernel(
    parts_depth, hidden, x_in, dqkv, w_qkv, g_first, front_sums, rear_sums, up_sums, head_sums,
    *rest,
):
    f32, bf16 = jnp.float32, jnp.bfloat16
    parts, corners = rest[:3], rest[3 : 3 + parts_depth]
    (
        out, qkv_out, f_out, small_out,
        x_v, d_v, w_v, first_v, part_v, small_v, small_got,
        back_v, got_v, fin_v, land_v, tot_v, zf_v, ff_v,
        corner_v, corner_out, corner_in, grad_v, swap_v, pq_v, yl_v, xs_v, xl_v, rs_v, zq_v, qf_v,
        in_sem, out_sem, send_sem, recv_sem,
    ) = rest[3 + parts_depth :]
    half, turn, share = my_spot()
    deep = lax.axis_index("dp")
    depth = tot_v.shape[0]
    span = hidden.shape[1]
    sub = span // SUBS
    other = (share + 1) % 2
    far_half, far_turn = (half + 1) % 2, (turn + 1) % 2
    across, beside, partner = neighbours()
    deeps = [{"dp": (deep + k) % depth} for k in range(1, depth)]
    ids = iter(range(send_sem.shape[0]))
    started = []

    def link(src, dst, device):
        i = next(ids)
        copy = remote(src, dst, send_sem.at[i], recv_sem.at[i], device)
        started.append(copy)
        return copy

    def go(src, dst, device):
        copy = link(src, dst, device)
        copy.start()
        return copy

    chunk = lambda i: pl.ds(i * span, span)
    chunks = [hidden.at[half * 2 + turn]] + [x_in.at[i] for i in range(3)]
    loads = [
        pltpu.make_async_copy(src, dst, in_sem.at[i])
        for i, (src, dst) in enumerate(
            [(w_qkv, w_v)]
            + [(dqkv.at[chunk(i)], d_v.at[chunk(i)]) for i in (2, 3, 0, 1)]
            + [(p, part_v.at[i]) for i, p in enumerate(parts)]
            + [(g_first, first_v)]
            + [(c, x_v.at[chunk(i)]) for i, c in enumerate(chunks)]
        )
    ]
    corner_loads = start_copies(
        [(c, corner_v.at[i]) for i, c in enumerate(corners)], out_sem
    )
    for copy in loads:
        copy.start()
    diagonal = {"tensor": far_half, "context": far_turn * 2 + share}
    signal_all([across, beside, partner, diagonal] + deeps)
    wait_copies(corner_loads)
    corner_out[...] = sum(
        [corner_v[i].astype(f32) for i in range(1, depth)], corner_v[0].astype(f32)
    ).astype(bf16)
    corner = go(corner_out, corner_in, diagonal)
    small_v[...] = jnp.zeros_like(small_v)
    cols = up_sums.shape[1] // 2
    for g, (where, at) in enumerate(group_homes()):
        row = pl.ds(where * 2 + at // 2, 1)
        lanes = pl.ds(pl.multiple_of((at % 2) * cols, PAIR), cols)
        small_v[row, lanes] = up_sums[g // 2 : g // 2 + 1, (g % 2) * cols : (g % 2 + 1) * cols]
    small_v[4:7, :] = rear_sums[0:3, :]
    small_v[7:10, :] = front_sums[3:6, :]
    lane = lax.broadcasted_iota(jnp.int32, (1, small_v.shape[1]), 1)
    stats = jnp.where(lane == 5, front_sums[11:12, :], 0.0)
    for i in range(5):
        stats = jnp.where(lane == i, jnp.sum(front_sums[6 + i : 7 + i, :], 1, keepdims=True), stats)
    small_v[10:11, :] = stats
    small_v[11:13, :] = head_sums[0:2, :]

    s0 = go(small_v, small_got.at[0], partner)
    wait_copies(loads[:3])
    back = []
    for i in range(2):
        back_v[i] = dot_nt(d_v[chunk(2 + i), :], w_v[...]).astype(bf16)
        back.append(go(back_v.at[i], got_v.at[i], partner))
    wait_copies(loads[3:5] + loads[8:9])
    outs = []

    def own_back(i):
        value = dot_nt(d_v[chunk(i), :], w_v[...]) + first_v[chunk(i), :]
        back[i].wait_recv()
        fin_v[i] = (value + got_v[i].astype(f32)).astype(bf16)

    rows = lambda j: pl.ds(j * sub, sub)

    def put(ref, h, t):
        copy = pltpu.make_async_copy(ref, out.at[h * 2 + t], out_sem.at[len(outs)])
        copy.start()
        outs.append(copy)

    own_back(0)
    x_subs = [go(fin_v.at[0, rows(j)], land_v.at[1, rows(j)], across) for j in range(SUBS)]
    put(fin_v.at[0], half, turn)
    own_back(1)
    y_subs = [go(fin_v.at[1, rows(j)], land_v.at[0, rows(j)], beside) for j in range(SUBS // 2)]
    wait_copies(loads[5:8])
    tot_v[...] = (
        part_v[0].astype(f32) + part_v[1].astype(f32) + part_v[2].astype(f32)
    ).astype(bf16)
    z_f = [
        go(tot_v.at[(deep + k + 1) % depth], zf_v.at[k], device) for k, device in enumerate(deeps)
    ]


    s0.wait_recv()
    s0.wait_send()
    small_v[...] += small_got[0]
    s1 = go(small_v, small_got.at[1], beside)
    wait_copies(loads[9:])
    third = grad_v.shape[0] // 3

    def grad_step(i, carry):
        at = pl.ds(pl.multiple_of(i * third, PAIR), third)
        grad_v[at, :] = dot_tn(x_v[:, at], d_v[...]).astype(bf16)
        return carry

    lax.fori_loop(0, 3, grad_step, 0)
    slim = swap_v.shape[2]

    def grad_rows(d, t, s):
        return grad_v[pl.ds(pl.multiple_of((d * 4 + t * 2 + s) * slim, 16), slim), :]

    for d in range(depth):
        for t in range(2):
            swap_v[d, t] = grad_rows(d, t, other)
    swap = go(swap_v, pq_v.at[share], partner)
    for d in range(depth):
        for t in range(2):
            pq_v[share, d, t] = grad_rows(d, t, share)
    s1.wait_recv()
    s1.wait_send()
    small_v[...] += small_got[1]
    s2 = go(small_v, small_got.at[2], across)
    swap.wait_recv()
    keep_v = lambda h, t: pq_v[h, :, t]
    q1 = go(pq_v.at[far_half, :, far_turn], yl_v.at[0], beside)
    q2 = go(pq_v.at[half, :, far_turn], yl_v.at[1], beside)
    y_subs += [
        go(fin_v.at[1, rows(j)], land_v.at[0, rows(j)], beside) for j in range(SUBS // 2, SUBS)
    ]
    s2.wait_recv()
    s2.wait_send()
    small_v[...] += small_got[2]
    s3 = [go(small_v, small_got.at[3 + k], device) for k, device in enumerate(deeps)]
    relays = []

    def relay(j):
        y_subs[j].wait_recv()
        relays.append(go(land_v.at[0, rows(j)], land_v.at[2, rows(j)], across))

    for j in range(SUBS // 2):
        relay(j)
    q1.wait_recv()
    xs_v[...] = (keep_v(far_half, turn).astype(f32) + yl_v[0].astype(f32)).astype(bf16)
    qx = go(xs_v, xl_v, across)

    for copy in z_f:
        copy.wait_recv()
    ranks = range(depth - 1)
    spread = lambda ref, got: sum([got[k].astype(f32) for k in ranks], ref[deep].astype(f32))
    corner.wait_recv()
    ff_v[turn, share] = (spread(tot_v, zf_v) + corner_in[...].astype(f32)).astype(bf16)

    def gather_first(ref):
        piece = ref.at[turn, share]
        return go(piece, piece, beside), go(piece, piece, partner)

    def gather_next(ref, first):
        first.wait_recv()
        piece = ref.at[far_turn, share]
        return go(piece, piece, partner)

    f_first = gather_first(ff_v)
    q2.wait_recv()
    for j in range(SUBS // 2, SUBS):
        relay(j)
    qx.wait_recv()
    rs_v[...] = (
        keep_v(half, turn).astype(f32) + yl_v[1].astype(f32) + xl_v[...].astype(f32)
    ).astype(bf16)
    z_q = [
        go(rs_v.at[(deep + k + 1) % depth], zq_v.at[k], device) for k, device in enumerate(deeps)
    ]
    for copy in s3:
        copy.wait_recv()
    small_out[...] = small_v[...] + sum([small_got[4 + k] for k in range(depth - 2)], small_got[3])
    f_next = gather_next(ff_v, f_first[0])
    for copy in z_q:
        copy.wait_recv()
    qf_v[turn, share] = spread(rs_v, zq_v).astype(bf16)
    q_first = gather_first(qf_v)
    put(land_v.at[0], half, far_turn)
    for copy in x_subs:
        copy.wait_recv()
    put(land_v.at[1], far_half, turn)
    f_first[1].wait_recv()
    f_next.wait_recv()
    ends = start_copies([(ff_v, f_out)], in_sem)
    q_next = gather_next(qf_v, q_first[0])
    for copy in relays:
        copy.wait_recv()
    put(land_v.at[2], far_half, far_turn)
    q_first[1].wait_recv()
    q_next.wait_recv()
    last = pltpu.make_async_copy(qf_v, qkv_out, in_sem.at[2])
    last.start()
    wait_copies(ends + [last] + outs)
    waited = [s0, s1, s2]
    for copy in started:
        if not any(copy is w for w in waited):
            copy.wait_send()


def settle(hidden_in, x_in, dqkv, w_qkv, g_first, sums, parts, corners):
    rows, width = g_first.shape
    span = hidden_in.shape[1]
    depth, tall, cols = parts[0].shape
    wide = dqkv.shape[1]
    slim = width // depth // 4
    f32, bf16, shape = jnp.float32, jnp.bfloat16, jax.ShapeDtypeStruct
    v = pltpu.VMEM
    count = 80
    return pl.pallas_call(
        functools.partial(settle_kernel, depth),
        out_shape=(
            shape((4, span, width), bf16), shape((2, 2, slim, wide), bf16),
            shape((2, 2, tall, cols), bf16), shape((16, width), f32),
        ),
        in_specs=[ANY_SPEC] * 5 + [VMEM_SPEC] * 4 + [ANY_SPEC] * (3 + depth),
        out_specs=(ANY_SPEC,) * 3 + (VMEM_SPEC,),
        scratch_shapes=[
            v((2 * rows, width), bf16), v((2 * rows, wide), bf16), v((width, wide), bf16),
            v((rows, width), f32), v((3, depth, tall, cols), bf16), v((16, width), f32),
            v((2 + depth, 16, width), f32),
            v((2, span, width), bf16), v((2, span, width), bf16), v((2, span, width), bf16),
            v((3, span, width), bf16),
            v((depth, tall, cols), bf16), v((depth - 1, tall, cols), bf16),
            v((2, 2, tall, cols), bf16),
            v((depth, tall, cols), bf16), v((tall, cols), bf16), v((tall, cols), bf16),
            v((width, wide), bf16), v((depth, 2, slim, wide), bf16),
            v((2, depth, 2, slim, wide), bf16), v((2, depth, slim, wide), bf16),
            v((depth, slim, wide), bf16), v((depth, slim, wide), bf16),
            v((depth, slim, wide), bf16), v((depth - 1, slim, wide), bf16),
            v((2, 2, slim, wide), bf16),
            DMA((20,)), DMA((max(4, depth),)), DMA((count,)), DMA((count,)),
        ],
        compiler_params=pltpu.CompilerParams(
            vmem_limit_bytes=63 * 1024 * 1024, collective_id=1, has_side_effects=True
        ),
        cost_estimate=pl.CostEstimate(
            flops=60 * 10**9, bytes_accessed=30 * 10**6, transcendentals=0
        ),
        name="settle",
    )(hidden_in, x_in, dqkv, w_qkv, g_first, *sums, *parts, *corners)


def finish_kernel(
    grad, qkv, ffn, small,
    grad_home, o_q, o_bq, o_k, o_v, o_bv, o_o, o_bo, o_g1, o_s1, o_up, o_bup, o_down, o_bdown,
    o_g2, o_s2, o_rms,
    grad_in, grad_out, in_sem, out_sem,
):
    f32 = jnp.float32
    seqs, span, width = grad.shape
    half = my_spot()[0]
    thin = o_q.shape[0]
    cols = o_q.shape[1]
    loads = start_copies([(grad.at[i], grad_in.at[i]) for i in range(seqs)], in_sem)
    stores = []
    for i in range(seqs):
        loads[i].wait()
        grad_out[i] = grad_in[i].astype(f32)
        stores.append(pltpu.make_async_copy(grad_out.at[i], grad_home.at[i], out_sem.at[i]))
        stores[i].start()
    for i, ref in enumerate((o_q, o_k, o_v)):
        ref[...] = qkv[:, i * cols : (i + 1) * cols].astype(f32)
    slim = ffn.shape[1] - 2 * thin
    for p in range(4):
        at = slice(p * cols, (p + 1) * cols)
        o_up[:, at] = ffn[p, :thin, :].astype(f32)
        o_down[:, at] = ffn[p, thin : 2 * thin, :].astype(f32)
        o_o[p * slim : (p + 1) * slim, :] = ffn[p, 2 * thin :, :].astype(f32)
    flat = lambda row: row.reshape(row.shape[1])
    up = [small[pl.ds(half * 2 + i, 1), :] for i in range(2)]
    o_bup[...] = flat(jnp.concatenate(up, 1))
    for i, ref in enumerate((o_bo, o_g1, o_s1, o_bdown, o_g2, o_s2)):
        ref[...] = flat(small[4 + i : 5 + i, :])
    own = pl.ds(pl.multiple_of(half * cols, PAIR), cols)
    o_bq[...] = flat(small[11:12, own])
    o_bv[...] = flat(small[12:13, own])
    stats = small[10:11, :]
    o_rms[...] = jnp.sqrt(stats / (jnp.maximum(stats[:, 5:6], 1.0) * width))[:, :PAIR]
    wait_copies(stores)


def finish_all(grad, qkv, ffn, small):
    seqs, span, width = grad.shape
    thin, cols = qkv.shape[0], qkv.shape[1] // 3
    f32 = jnp.float32
    shape = lambda *s: jax.ShapeDtypeStruct(s, f32)
    outs = pl.pallas_call(
        finish_kernel,
        out_shape=(
            shape(seqs, span, width),
            shape(thin, cols), shape(cols), shape(thin, cols),
            shape(thin, cols), shape(cols), shape(thin, cols), shape(width), shape(width),
            shape(width), shape(thin, 4 * cols), shape(4 * cols), shape(thin, 4 * cols),
            shape(width), shape(width), shape(width), shape(1, PAIR),
        ),
        in_specs=[ANY_SPEC] + [VMEM_SPEC] * 3,
        out_specs=(ANY_SPEC,) + (VMEM_SPEC,) * 16,
        scratch_shapes=[
            pltpu.VMEM((seqs, span, width), grad.dtype), pltpu.VMEM((seqs, span, width), f32),
            DMA((seqs,)), DMA((seqs,)),
        ],
        compiler_params=WIDE_ROOM,
        name="finish_all",
    )(grad, qkv, ffn, small)
    outs = list(outs)
    outs[6], outs[12] = outs[6].T, outs[12].T
    return (*outs[:-1], outs[-1][0, :5])


def layer_norm(values, norm_gain, norm_shift):
    row_mean = jnp.mean(values, -1, keepdims=True)
    centered = values - row_mean
    row_var = jnp.mean(centered * centered, -1, keepdims=True)
    return centered * lax.rsqrt(row_var + EPSILON) * norm_gain + norm_shift


def gelu_tanh(values):
    return jax.nn.gelu(values, approximate=True)


def block_tables(random_seq, all_blocks, place):
    block = jnp.arange(2, all_blocks, dtype=jnp.int32)
    last = all_blocks - 1
    zero = jnp.zeros_like(block)
    true_ids = jnp.stack(
        [block, block - 1, block, jnp.minimum(block + 1, last), zero, zero + 1], -1
    )
    true_ids = jnp.concatenate([true_ids, random_seq[2:]], -1)
    flags = jnp.stack([block >= 3, block <= last - 1], -1).astype(jnp.int32)
    return (
        jnp.concatenate([place(true_ids), flags], -1).astype(jnp.int32),
        place(jnp.arange(2, dtype=jnp.int32)),
    )


def local(
    hidden_in, out_grad, segment_ids, token_valid, random_blocks,
    query_weight, query_bias, key_weight, value_weight, value_bias,
    output_weight, output_bias, norm1_gain, norm1_shift,
    up_weight, up_bias, down_weight, down_bias, norm2_gain, norm2_shift,
):
    f32, bf16 = jnp.float32, jnp.bfloat16
    seqs, span, width = hidden_in.shape
    length = segment_ids.shape[1]
    places = length // span
    halves = lax.axis_size("tensor")
    depth = lax.axis_size("dp")
    turns = seqs // halves
    shares = places // turns
    my_half = lax.axis_index("tensor")
    my_place = lax.axis_index("context")
    my_depth = lax.axis_index("dp")
    my_turn, my_share = my_place // shares, my_place % shares
    my_seq = my_half * turns + my_turn
    blocks = length // BLK
    rows = turns * span
    spots = [(h, t) for h in range(halves) for t in range(turns)]

    def send(value, half=0, turn=0, share=0):
        if half % halves == 0 and turn % turns == 0 and share % shares == 0:
            return value
        pairs = []
        for h in range(halves):
            for t in range(turns):
                for s in range(shares):
                    to_place = (t + turn) % turns * shares + (s + share) % shares
                    pairs.append(
                        ((t * shares + s) * halves + h, to_place * halves + (h + half) % halves)
                    )
        return lax.ppermute(value, ("context", "tensor"), pairs)

    def send_deep(value, step):
        return lax.ppermute(value, "dp", [(i, (i + step) % depth) for i in range(depth)])

    def pick(value, index, axis=0):
        return lax.dynamic_index_in_dim(value, index, axis, keepdims=False)

    def own_slice(value, count, which, axis):
        size = value.shape[axis] // count
        return lax.dynamic_slice_in_dim(value, which * size, size, axis)

    def gather_deep(value):
        if depth > 4:
            return lax.all_gather(value, "dp", axis=0)
        got = [value] + [send_deep(value, k) for k in range(1, depth)]
        ring = jnp.stack([got[depth - 1 - i % depth] for i in range(2 * depth - 1)])
        return lax.dynamic_slice_in_dim(ring, depth - 1 - my_depth, depth, 0)

    def reduce_deep(value):
        if depth > 4:
            return lax.psum_scatter(value, "dp", scatter_dimension=0)
        total = pick(value, my_depth).astype(f32)
        for k in range(1, depth):
            total = total + send_deep(pick(value, (my_depth + k) % depth), k).astype(f32)
        return total.astype(bf16)

    def gather_square(value):
        near = {spot: send(value, *spot) for spot in spots}
        near = jnp.stack([near[spot] for spot in spots])
        return [near] + [send(near, 0, 0, s) for s in range(1, shares)]

    def reduce_square(value):
        total = value[0].astype(f32)
        for i, (h, t) in enumerate(spots[1:], 1):
            total = total + send(value[i], -h, -t).astype(f32)
        return total.astype(bf16)

    def gather_places(value):
        near = [send(value, 0, t) for t in range(turns)]
        near = jnp.stack(near)
        far = jnp.stack([near] + [send(near, 0, 0, s) for s in range(1, shares)])
        return jnp.stack(
            [
                pick(pick(far, (my_share - s) % shares), (my_turn - t) % turns)
                for t in range(turns)
                for s in range(shares)
            ]
        )

    def sum_all(value):
        for step in range(halves.bit_length() - 1):
            value = value + send(value, 1 << step)
        size = 1
        while size < places:
            value = value + lax.ppermute(value, "context", [(i, i ^ size) for i in range(places)])
            size *= 2
        size = 1
        while size < depth:
            value = value + lax.ppermute(value, "dp", [(i, i ^ size) for i in range(depth)])
            size *= 2
        return value

    def bring(value):
        return jnp.concatenate(
            [
                send(pick(value, my_half * turns + (my_turn + k) % turns), 0, k)
                for k in range(turns)
            ],
            0,
        )

    def deliver(value):
        value = value.reshape(turns, span, width)
        got = jnp.stack([send(value[t], h, -t) for h, t in spots])
        return jnp.stack(
            [
                pick(got, (my_half - h) % halves * turns + (t - my_turn) % turns)
                for h in range(halves)
                for t in range(turns)
            ]
        )

    def after(value, *earlier):
        return lax.optimization_barrier((value, *earlier))[0]

    per = span // BLK

    def place(block_ids):
        chunk = block_ids // per
        turn, share = chunk // shares, chunk % shares
        spot = ((my_share - share) % shares) * turns + (my_turn - turn) % turns
        return spot * per + block_ids % per

    def in_order(row):
        return jnp.concatenate(
            [
                lax.dynamic_slice_in_dim(
                    row,
                    (((my_turn - k) % turns) * shares + (my_share - s) % shares) * span,
                    span,
                )
                for s in range(shares)
                for k in range(turns)
            ]
        )

    half_width = query_weight.shape[1]
    thin = query_weight.shape[0]
    slim = thin // places
    hidden = up_weight.shape[1] // places
    biases = jnp.concatenate([query_bias, value_bias, up_bias])

    def split_biases(by_half):
        by_half = jnp.stack([pick(by_half, (my_half - h) % halves) for h in range(halves)])
        return (
            by_half[:, at : at + b.shape[0]].reshape(-1)
            for b, at in ((query_bias, 0), (value_bias, half_width), (up_bias, 2 * half_width))
        )

    def spread(value, which, count):
        return lax.dynamic_update_slice_in_dim(
            jnp.zeros((value.shape[0] * count,), value.dtype), value, which * value.shape[0], 0
        )

    def small_rows(up_sums, group_at, norm_sums, stats):
        up_natural = jnp.zeros_like(up_sums)
        for i, at in enumerate(group_at):
            up_natural = lax.dynamic_update_slice_in_dim(
                up_natural, up_sums[i * hidden : (i + 1) * hidden], at * hidden, 0
            )
        stats = jnp.pad(stats, (0, width - stats.shape[0]))
        return jnp.concatenate(
            [up_natural.reshape(-1, width), *(row[None] for row in norm_sums), stats[None]], 0
        )

    def finish(layer_out, input_grad, qkv_shard, up_part, down_part, out_part, small):
        deep = up_weight.shape[1] * halves // width
        s_up, (s_o, s_g1, s_s1, s_down, s_g2, s_s2, stats, s_q, s_v) = (
            small[:deep].reshape(-1), small[deep : deep + 9]
        )
        s_q, s_v, s_up = (own_slice(value, halves, my_half, 0) for value in (s_q, s_v, s_up))
        input_rms = jnp.sqrt(stats[:5] / (jnp.maximum(stats[5], 1.0) * width))
        join = lambda w: jnp.moveaxis(w, 0, 1).reshape(thin, -1).astype(f32)
        shard_o = out_part.reshape(thin, -1)[:, :half_width].astype(f32).T
        shard_q, shard_k, shard_v = (qkv_shard[:, i].astype(f32) for i in range(3))
        return (
            layer_out, input_grad, shard_q, s_q, shard_k, shard_v, s_v, shard_o, s_o,
            s_g1, s_s1, join(up_part), s_up, join(down_part).T, s_down, s_g2, s_s2, input_rms,
        )

    if (turns, shares, halves) == (2, 2, 2) and depth <= 4 and rows % TILE == 0:
        near_b = [query_bias, value_bias, up_bias]
        x_in, q_all, f_deep, n1, n2, *far_b = fetch(
            hidden_in,
            [query_weight, key_weight, value_weight, up_weight, down_weight.T, output_weight.T],
            near_b, depth,
        )
        random = place(pick(random_blocks, my_seq)).reshape(-1)
        (
            att0, att1, q, k, v, lse, w_qkv, groups, key_code, query_code
        ) = project_attend(
            random, hidden_in, x_in, q_all, f_deep, n1, n2, segment_ids, token_valid,
            near_b[0], near_b[1], far_b[0], far_b[1],
        )
        vectors = [output_bias, norm1_gain, norm1_shift, down_bias, norm2_gain, norm2_shift]
        out0, out1, slope, g_second, unit, norm_t, downs, inverse, front_sums = ffn_front(
            att0, att1, hidden_in, x_in, out_grad, groups,
            key_code.reshape(length, PAIR), vectors, near_b[2], far_b[2],
        )
        g_first, do_own, do_far, layer_out, kept, turned, crossed, *corners, rear_sums, up_sums = ffn_rear(
            att0, att1, slope, g_second, unit, norm_t, out0, out1, downs, groups, inverse,
            norm1_gain,
        )
        parts = [kept, send(turned, 0, 1), send(crossed, 1)]
        corners = [send_deep(c, i) if i else c for i, c in enumerate(corners)]
        dqkv, layer_out, head_sums = attend_grad(
            random, do_own, do_far, q, k, v, layer_out, key_code, query_code, lse
        )
        dqkv, head_sums, parts, corners = lax.optimization_barrier(
            (dqkv, head_sums, parts, corners)
        )
        input_grad, qkv_shard, ffn_shard, small = settle(
            hidden_in, x_in, dqkv, w_qkv, g_first, (front_sums, rear_sums, up_sums, head_sums), parts,
            corners,
        )
        return (
            layer_out,
            *finish_all(
                input_grad, qkv_shard.reshape(thin, -1),
                ffn_shard.reshape((places,) + ffn_shard.shape[2:]), small,
            ),
        )

    seg = in_order(pick(segment_ids, my_seq))
    live = in_order(pick(token_valid, my_seq))
    random_seq = pick(random_blocks, my_seq)
    table, wide = block_tables(random_seq, blocks, place)
    key_code = jnp.broadcast_to(jnp.where(live == 1, seg, -1)[:, None], (length, PAIR))
    query_code = jnp.tile(seg.reshape(blocks, BLK), (1, PAIR // BLK))
    part = width // shares
    padded = -(-part // PAIR) * PAIR
    x_own = bring(hidden_in)
    qkv_piece = own_slice(
        jnp.concatenate([query_weight, key_weight, value_weight], 1), places, my_place, 0
    )
    qkv_all = jnp.stack(gather_square(gather_deep(qkv_piece)))
    per_half = shares // halves
    target = my_share // per_half
    qkv_all = jnp.stack(
        [
            pick(
                pick(qkv_all, (my_share - s) % shares),
                (my_half - target) % halves * turns + (my_turn - t) % turns,
            )
            for t in range(turns)
            for s in range(shares)
        ],
        1,
    ).reshape(width, 3, half_width)
    pad_cols = lambda w: jnp.pad(w, [(0, 0)] * (w.ndim - 1) + [(0, padded - part)])
    mine = lambda w: pad_cols(own_slice(w, per_half, my_share % per_half, w.ndim - 1))
    w_qkv = mine(qkv_all).reshape(width, 3 * padded)
    b_q, b_v, b_up = split_biases(jnp.stack([send(biases, h) for h in range(halves)]))
    mine_b = lambda b: pad_cols(own_slice(b, shares, my_share, 0))
    b_qkv = jnp.concatenate([mine_b(b_q), jnp.zeros((padded,), bf16), mine_b(b_v)]).astype(f32)

    ffn_piece = jnp.concatenate(
        [
            own_slice(up_weight, places, my_place, 1),
            own_slice(down_weight, places, my_place, 0).T,
            jnp.pad(
                own_slice(output_weight.T, places, my_place, 0),
                [(0, 0), (0, max(0, hidden - half_width))],
            ).reshape(-1, hidden),
        ],
        0,
    )
    ffn_all = gather_square(gather_deep(ffn_piece))
    groups = [
        (s, i, ffn_all[s][i]) for s in range(shares) for i in range(len(spots))
    ]
    w_up = jnp.concatenate([g[:, :thin].reshape(width, hidden) for _, _, g in groups], 1)
    w_down_t = jnp.concatenate(
        [g[:, thin : 2 * thin].reshape(width, hidden) for _, _, g in groups], 1
    )
    out_all = jnp.stack(
        [jnp.stack([g[:, 2 * thin :] for g in ffn_all[s]]) for s in range(shares)]
    )
    w_out_t = jnp.stack(
        [
            jnp.stack(
                [
                    pick(
                        pick(out_all, (my_share - s) % shares),
                        (my_half - h) % halves * turns + (my_turn - t) % turns,
                    )
                    for t in range(turns)
                    for s in range(shares)
                ],
                1,
            ).reshape(width, half_width)
            for h in range(halves)
        ],
        1,
    ).reshape(width, width)
    w_out_t = jnp.concatenate(
        [own_slice(w_out_t, shares, (my_share + k) % shares, 1) for k in range(shares)], 1
    )
    group_at = [
        ((my_half - spots[i][0]) % halves * places
         + (my_turn - spots[i][1]) % turns * shares + (my_share - s) % shares)
        for s, i, _ in groups
    ]
    b_up = jnp.concatenate(
        [lax.dynamic_slice_in_dim(b_up, at * hidden, hidden) for at in group_at]
    ).astype(f32)

    g_out = bring(out_grad).astype(f32)
    x_seq = jnp.concatenate([send(x_own, 0, 0, k) for k in range(shares)], 0)
    q, k, v = (
        (
            jnp.dot(x_seq, w_qkv[:, i * padded : (i + 1) * padded], preferred_element_type=f32)
            + b_qkv[i * padded : (i + 1) * padded]
        ).astype(bf16)
        for i in range(3)
    )
    att, lse = attend(table, wide, q, k, v, key_code, query_code)
    att = att[:, :part].reshape(shares, rows, part)
    att_own = jnp.concatenate([send(att[s], 0, 0, -s) for s in range(shares)], 1)
    attn_out = lax.dot_general(
        att_own, w_out_t, (((1,), (1,)), ((), ())), preferred_element_type=f32
    ) + output_bias.astype(f32)
    x_full = x_own.astype(f32)
    first_sum = x_full + attn_out
    gain_one, shift_one = norm1_gain.astype(f32), norm1_shift.astype(f32)
    normed = layer_norm(first_sum, gain_one, shift_one)
    normed_low = normed.astype(bf16)
    pre_act = jnp.dot(normed_low, w_up, preferred_element_type=f32) + b_up
    act_low = gelu_tanh(pre_act).astype(bf16)
    ffn_out = lax.dot_general(
        act_low, w_down_t, (((1,), (1,)), ((), ())), preferred_element_type=f32
    ) + down_bias.astype(f32)
    second_sum = normed + ffn_out
    gain_two, shift_two = norm2_gain.astype(f32), norm2_shift.astype(f32)
    layer_out, norm_back = jax.vjp(layer_norm, second_sum, gain_two, shift_two)
    g_second, gain_two_grad, shift_two_grad = norm_back(g_out)
    layer_out = deliver(layer_out.astype(bf16))
    g_ffn = g_second.astype(bf16)
    g_act = jnp.dot(g_ffn, w_down_t, preferred_element_type=f32)
    g_pre = jax.vjp(gelu_tanh, pre_act)[1](g_act)[0].astype(bf16)
    up_part = jnp.dot(normed_low.T, g_pre, preferred_element_type=f32).astype(bf16)
    down_part_t = jnp.dot(g_ffn.T, act_low, preferred_element_type=f32).astype(bf16)
    g_normed = g_second + jnp.dot(g_pre, w_up.T, preferred_element_type=f32)
    g_first, gain_one_grad, shift_one_grad = jax.vjp(layer_norm, first_sum, gain_one, shift_one)[1](
        g_normed
    )
    g_attn = g_first.astype(bf16)
    out_part_t = jnp.dot(g_attn.T, att_own, preferred_element_type=f32).astype(bf16)
    g_att = jnp.dot(g_attn, w_out_t, preferred_element_type=f32).astype(bf16)
    do = jnp.concatenate(
        [send(own_slice(g_att, shares, s, 1), 0, 0, s) for s in range(shares)], 0
    )
    dq, dk, dv = attend_back(table, wide, q, k, v, pad_cols(do), key_code, query_code, lse)

    out_natural = jnp.concatenate(
        [own_slice(out_part_t, shares, (s - my_share) % shares, 1) for s in range(shares)], 1
    ).reshape(depth, turns, shares, slim, halves, half_width)

    def ffn_group(s, i):
        h, t = spots[i]
        at = (s * len(spots) + i) * hidden
        out = pick(out_natural, (my_half - h) % halves, 4)
        out = pick(pick(out, (my_turn - t) % turns, 1), (my_share - s) % shares, 1)
        out = jnp.pad(out, [(0, 0), (0, 0), (0, max(0, hidden - half_width))])
        cut = lambda w: w[:, at : at + hidden].reshape(depth, thin, hidden)
        return jnp.concatenate(
            [cut(up_part), cut(down_part_t), out.reshape(depth, -1, hidden)], 1
        )

    ffn_grads = [
        jnp.stack([ffn_group(s, i) for i in range(len(spots))]) for s in range(shares)
    ]
    total = ffn_grads[0].astype(f32)
    for s in range(1, shares):
        total = total + send(ffn_grads[s], 0, 0, -s).astype(f32)
    ffn_shard = gather_places(reduce_deep(reduce_square(total.astype(bf16))))
    dqkv = jnp.concatenate([dq, dk, dv], 1)
    qkv_part = (
        jnp.dot(x_seq.T, dqkv, preferred_element_type=f32)
        .astype(bf16)
        .reshape(depth, turns, shares, slim, 3, padded)[..., :part]
    )
    got = jnp.stack(
        [send(pick(qkv_part, (my_share + s) % shares, 2), 0, 0, s) for s in range(shares)]
    )
    got = jnp.stack([pick(got, (my_share - s) % shares) for s in range(shares)], 4)
    got = got.reshape(depth, turns, slim, 3, halves, half_width)
    square = jnp.stack(
        [
            pick(pick(got, (my_half - h) % halves, 4), (my_turn - t) % turns, 1)
            for h, t in spots
        ]
    ).reshape(len(spots), depth, slim, 3 * half_width)
    qkv_shard = gather_places(reduce_deep(reduce_square(square))).reshape(thin, 3, half_width)
    back = jnp.dot(dqkv, w_qkv.T, preferred_element_type=f32).reshape(shares, rows, width)
    back_own = back[0]
    for s in range(1, shares):
        back_own = back_own + send(back[s].astype(bf16), 0, 0, -s).astype(f32)
    input_grad = deliver((g_first + back_own).astype(bf16)).astype(f32)

    sums = lambda value: jnp.sum(value.astype(f32), 0)
    valid = live[:rows].astype(f32)
    squares = lambda member: jnp.sum(valid * jnp.sum(member * member, -1))
    stats = jnp.stack(
        [squares(m) for m in (x_full, first_sum, second_sum, attn_out, ffn_out)]
        + [jnp.sum(valid), 0.0, 0.0]
    )
    up_sums = sums(g_pre)
    norm_sums = [
        sums(g_attn), gain_one_grad, shift_one_grad, sums(g_ffn), gain_two_grad, shift_two_grad
    ]
    small = small_rows(up_sums, group_at, norm_sums, stats)
    heads = [spread(sums(d)[:part], my_share, shares)[None] for d in (dq, dv)]
    small = sum_all(jnp.concatenate([small, *heads], 0))
    return finish(
        layer_out, input_grad, qkv_shard, ffn_shard[:, :thin], ffn_shard[:, thin : 2 * thin],
        ffn_shard[:, 2 * thin :], small,
    )


def solution(mesh):
    rows, plain = P("dp", "context", None), P()
    columns, across, halves = P("dp", "tensor"), P("tensor", "dp"), P("tensor")
    return jax.shard_map(
        local,
        mesh=mesh,
        in_specs=(
            rows, rows, P("dp", None), P("dp", None), P("dp", None, None),
            columns, halves, columns, columns, halves, across, plain, plain, plain,
            columns, halves, across, plain, plain, plain,
        ),
        out_specs=(
            rows, rows, columns, halves, columns, columns, halves, across, plain,
            plain, plain, columns, halves, across, plain, plain, plain, plain,
        ),
        check_vma=False,
    )
```

```python
import functools

import jax
import jax.numpy as jnp
from jax import lax
from jax.experimental import pallas as pl
from jax.experimental.pallas import tpu as pltpu
from jax.sharding import PartitionSpec as P

HD = 64
BLK = 64
PAIR = 128
SLOTS = 8
WIDE = 512
SCALE = HD ** (-0.5)
EPSILON = 1e-06


NEG_FILL = -1e30
LEAP = 3
BACK_LEAP = 3


def pair_rows(block, left, scale=None):
    if scale is not None:
        block = block * jnp.asarray(scale, block.dtype)
    zero = jnp.zeros_like(block)
    return jnp.concatenate([jnp.where(left, block, zero), jnp.where(left, zero, block)], 0)


def lane_left(rows):
    return lax.broadcasted_iota(jnp.int32, (rows, PAIR), 1) < HD


def eye_pair():
    lanes = lax.broadcasted_iota(jnp.int32, (BLK, PAIR), 1)
    rows = lax.broadcasted_iota(jnp.int32, (BLK, PAIR), 0)
    return rows == lanes % BLK


def block_rows(index):
    return pl.ds(pl.multiple_of(index * BLK, BLK), BLK)


def slot_bias(slots, first_ok, third_ok, key_code, query_code, own):
    pieces = []
    for slot in range(SLOTS):
        code = query_code
        if slot == 0:
            code = jnp.where(first_ok, query_code, -2)
        if slot == 2:
            code = jnp.where(third_ok, query_code, -2)
        same = key_code[slots[slot]] == code
        if slot == 1:
            same = same | own
        pieces.append(jnp.where(same, 0.0, NEG_FILL))
    return jnp.concatenate(pieces, 0)


def slot_rows(ref, slots, lanes):
    return jnp.concatenate([ref[slot, :, lanes] for slot in slots], 0)


def wide_rows(ref, chunk, lanes):
    count = WIDE // BLK
    return ref[pl.ds(chunk * count, count), :, lanes].reshape(WIDE, PAIR)


def listed(table):
    def find(row):
        slots = [table[row, 1 + slot] for slot in range(SLOTS)]
        return table[row, 0], slots, table[row, 9] == 1, table[row, 10] == 1

    return find


def wide_bias(key_code, query_code, block, chunk):
    same = wide_rows(key_code, chunk, slice(0, PAIR)) == query_code
    key_pos = chunk * WIDE + lax.broadcasted_iota(jnp.int32, (WIDE, PAIR), 0)
    query_pos = block * BLK + lax.broadcasted_iota(jnp.int32, (WIDE, PAIR), 1) % BLK
    return jnp.where(same | (key_pos == query_pos), 0.0, NEG_FILL)


def dot_nt(left, right):
    return lax.dot_general(
        left, right, (((1,), (1,)), ((), ())), preferred_element_type=jnp.float32
    )


def dot_tn(left, right):
    return lax.dot_general(
        left, right, (((0,), (0,)), ((), ())), preferred_element_type=jnp.float32
    )


def dot_nn(left, right):
    return jnp.dot(left, right, preferred_element_type=jnp.float32)


def attend_kernel(table, wide, *refs):
    attend_blocks(listed(table), [wide[0], wide[1]], table.shape[0], [], *refs)


def attend_blocks(
    find, wide, count, marks, q_ref, k_ref, v_ref, key_code, query_code, o_ref, lse_ref, acc
):
    length, width = q_ref.shape
    pairs = width // PAIR
    left = lane_left(BLK)
    own = eye_pair()

    def narrow(row, carry):
        block, slots, first_ok, third_ok = find(row)
        rows = block_rows(block)
        code = query_code[pl.ds(block, 1), :]
        bias = slot_bias(slots, first_ok, third_ok, key_code, code, own)
        for pair in range(pairs):
            lanes = slice(pair * PAIR, (pair + 1) * PAIR)
            query = pair_rows(q_ref[rows, lanes], left, SCALE)
            scores = dot_nt(slot_rows(k_ref, slots, lanes), query) + bias
            top = jnp.max(scores, 0, keepdims=True)
            weight = jnp.exp(scores - top)
            total = jnp.sum(weight, 0, keepdims=True)
            probs = (weight * (1.0 / total)).astype(jnp.bfloat16)
            lse_ref[block, pl.ds(pair, 1), :] = top + jnp.log(total)
            both = dot_tn(probs, slot_rows(v_ref, slots, lanes))
            o_ref[rows, lanes] = jnp.where(left, both[:BLK], both[BLK:]).astype(o_ref.dtype)
        return carry

    leap = LEAP if count % LEAP == 0 else 1

    def stride(i, carry):
        for j in range(leap):
            narrow(i * leap + j, 0)
        for mark, action in marks:

            @pl.when(i == mark)
            def _():
                action()

        return carry

    lax.fori_loop(0, count // leap, stride, 0)

    def wide_step(which, nothing):
        block = wide[0] + which * (wide[1] - wide[0])
        rows = block_rows(block)
        code = query_code[pl.ds(block, 1), :]

        def first(chunk, carry):
            bias = wide_bias(key_code, code, block, chunk)
            out = []
            for pair in range(pairs):
                lanes = slice(pair * PAIR, (pair + 1) * PAIR)
                query = pair_rows(q_ref[rows, lanes], left, SCALE)
                scores = dot_nt(wide_rows(k_ref, chunk, lanes), query) + bias
                top_old, total_old = carry[pair]
                top = jnp.maximum(top_old, jnp.max(scores, 0, keepdims=True))
                total = total_old * jnp.exp(top_old - top) + jnp.sum(
                    jnp.exp(scores - top), 0, keepdims=True
                )
                out.append((top, total))
            return tuple(out)

        start = (jnp.full((1, PAIR), NEG_FILL), jnp.zeros((1, PAIR), jnp.float32))
        ends = lax.fori_loop(0, length // WIDE, first, (start,) * pairs, unroll=2)
        for pair in range(pairs):
            lse_ref[block, pl.ds(pair, 1), :] = ends[pair][0] + jnp.log(ends[pair][1])
        acc[...] = jnp.zeros_like(acc)

        def second(chunk, carry):
            bias = wide_bias(key_code, code, block, chunk)
            for pair in range(pairs):
                lanes = slice(pair * PAIR, (pair + 1) * PAIR)
                query = pair_rows(q_ref[rows, lanes], left, SCALE)
                scores = dot_nt(wide_rows(k_ref, chunk, lanes), query) + bias
                probs = jnp.exp(scores - lse_ref[block, pl.ds(pair, 1), :]).astype(jnp.bfloat16)
                acc[pair] += dot_tn(probs, wide_rows(v_ref, chunk, lanes))
            return carry

        lax.fori_loop(0, length // WIDE, second, 0, unroll=2)
        for pair in range(pairs):
            lanes = slice(pair * PAIR, (pair + 1) * PAIR)
            both = acc[pair]
            o_ref[rows, lanes] = jnp.where(left, both[:BLK], both[BLK:]).astype(o_ref.dtype)
        return nothing

    lax.fori_loop(0, 2, wide_step, 0)


def attend_back_kernel(table, wide, *refs):
    attend_back_blocks(listed(table), [wide[0], wide[1]], table.shape[0], *refs)


def attend_back_blocks(
    find, wide, count, q_ref, k_ref, v_ref, do_ref, key_code, query_code, lse_ref,
    dq_ref, dk_ref, dv_ref, dk_sum, dv_sum, dq_acc,
):
    length, width = q_ref.shape
    pairs = width // PAIR
    left = lane_left(BLK)
    own = eye_pair()
    dk_sum[...] = jnp.zeros_like(dk_sum)
    dv_sum[...] = jnp.zeros_like(dv_sum)

    def narrow(row, carry):
        block, slots, first_ok, third_ok = find(row)
        rows = block_rows(block)
        code = query_code[pl.ds(block, 1), :]
        bias = slot_bias(slots, first_ok, third_ok, key_code, code, own)
        for pair in range(pairs):
            lanes = slice(pair * PAIR, (pair + 1) * PAIR)
            query = pair_rows(q_ref[rows, lanes], left, SCALE)
            grad = pair_rows(do_ref[rows, lanes], left)
            keys = slot_rows(k_ref, slots, lanes)
            values = slot_rows(v_ref, slots, lanes)
            scores = dot_nt(keys, query) + bias
            probs = jnp.exp(scores - lse_ref[block, pl.ds(pair, 1), :])
            g_probs = dot_nt(values, grad)
            terms = probs * g_probs
            g_scores = (terms - probs * jnp.sum(terms, 0, keepdims=True)).astype(jnp.bfloat16)
            dv = dot_nn(probs.astype(jnp.bfloat16), grad)
            dk = dot_nn(g_scores, query)
            both = dot_tn(g_scores, keys)
            dq_ref[rows, lanes] = (jnp.where(left, both[:BLK], both[BLK:]) * SCALE).astype(
                dq_ref.dtype
            )
            for slot in range(SLOTS):
                spot = block_rows(slots[slot])
                part = slice(slot * BLK, (slot + 1) * BLK)
                dk_sum[spot, lanes] += dk[part]
                dv_sum[spot, lanes] += dv[part]
        return carry

    lax.fori_loop(0, count, narrow, 0, unroll=BACK_LEAP if count % BACK_LEAP == 0 else 1)

    def wide_step(which, nothing):
        block = wide[0] + which * (wide[1] - wide[0])
        rows = block_rows(block)
        code = query_code[pl.ds(block, 1), :]

        def pieces(chunk, pair, bias):
            keys_at = pl.ds(pl.multiple_of(chunk * WIDE, WIDE), WIDE)
            lanes = slice(pair * PAIR, (pair + 1) * PAIR)
            query = pair_rows(q_ref[rows, lanes], left, SCALE)
            grad = pair_rows(do_ref[rows, lanes], left)
            keys = wide_rows(k_ref, chunk, lanes)
            scores = dot_nt(keys, query) + bias
            probs = jnp.exp(scores - lse_ref[block, pl.ds(pair, 1), :])
            return keys_at, lanes, query, grad, keys, probs, probs * dot_nt(wide_rows(v_ref, chunk, lanes), grad)

        def first(chunk, carry):
            bias = wide_bias(key_code, code, block, chunk)
            return tuple(
                carry[pair] + jnp.sum(pieces(chunk, pair, bias)[-1], 0, keepdims=True)
                for pair in range(pairs)
            )

        deltas = lax.fori_loop(
            0, length // WIDE, first, (jnp.zeros((1, PAIR), jnp.float32),) * pairs
        )
        dq_acc[...] = jnp.zeros_like(dq_acc)

        def second(chunk, carry):
            bias = wide_bias(key_code, code, block, chunk)
            for pair in range(pairs):
                keys_at, lanes, query, grad, keys, probs, terms = pieces(chunk, pair, bias)
                g_scores = (terms - probs * carry[pair]).astype(jnp.bfloat16)
                dv_sum[keys_at, lanes] += dot_nn(probs.astype(jnp.bfloat16), grad)
                dk_sum[keys_at, lanes] += dot_nn(g_scores, query)
                dq_acc[pair] += dot_tn(g_scores, keys)
            return carry

        lax.fori_loop(0, length // WIDE, second, deltas)
        for pair in range(pairs):
            lanes = slice(pair * PAIR, (pair + 1) * PAIR)
            both = dq_acc[pair]
            dq_ref[rows, lanes] = (jnp.where(left, both[:BLK], both[BLK:]) * SCALE).astype(
                dq_ref.dtype
            )
        return nothing

    lax.fori_loop(0, 2, wide_step, 0)
    dk_ref[...] = dk_sum[...].astype(dk_ref.dtype)
    dv_ref[...] = dv_sum[...].astype(dv_ref.dtype)


def in_blocks(rows):
    return rows.reshape(-1, BLK, rows.shape[-1])


VMEM_SPEC = pl.BlockSpec(memory_space=pltpu.VMEM)
SMEM_SPEC = pl.BlockSpec(memory_space=pltpu.SMEM)
ROOM = pltpu.CompilerParams(vmem_limit_bytes=60 * 1024 * 1024)


def attend(table, wide, q, k, v, key_code, query_code):
    length, width = q.shape
    return pl.pallas_call(
        attend_kernel,
        out_shape=(
            jax.ShapeDtypeStruct((length, width), jnp.bfloat16),
            jax.ShapeDtypeStruct((length // BLK, 8, PAIR), jnp.float32),
        ),
        in_specs=[SMEM_SPEC] * 2 + [VMEM_SPEC] * 5,
        out_specs=(VMEM_SPEC, VMEM_SPEC),
        scratch_shapes=[pltpu.VMEM((width // PAIR, PAIR, PAIR), jnp.float32)],
        compiler_params=ROOM,
        cost_estimate=pl.CostEstimate(
            flops=length * width * 1024 * 60, bytes_accessed=length * width * 8,
            transcendentals=length * width * 8,
        ),
        name="attend",
    )(table, wide, q, in_blocks(k), in_blocks(v), in_blocks(key_code), query_code)


def attend_back(table, wide, q, k, v, do, key_code, query_code, lse):
    length, width = q.shape
    shape = jax.ShapeDtypeStruct((length, width), jnp.bfloat16)
    return pl.pallas_call(
        attend_back_kernel,
        out_shape=(shape, shape, shape),
        in_specs=[SMEM_SPEC] * 2 + [VMEM_SPEC] * 7,
        out_specs=(VMEM_SPEC,) * 3,
        scratch_shapes=[
            pltpu.VMEM((length, width), jnp.float32),
            pltpu.VMEM((length, width), jnp.float32),
            pltpu.VMEM((width // PAIR, PAIR, PAIR), jnp.float32),
        ],
        compiler_params=ROOM,
        cost_estimate=pl.CostEstimate(
            flops=length * width * 1024 * 70, bytes_accessed=length * width * 14,
            transcendentals=length * width * 8,
        ),
        name="attend_back",
    )(table, wide, q, in_blocks(k), in_blocks(v), do, in_blocks(key_code), query_code, lse)


GROUPS = 8
DUOS = GROUPS // 2
TILE = 256
FRONT = 512
ANY_SPEC = pl.BlockSpec(memory_space=pl.ANY)
DMA = pltpu.SemaphoreType.DMA
WIDE_ROOM = pltpu.CompilerParams(vmem_limit_bytes=63 * 1024 * 1024)


def normalize(values):
    row_mean = jnp.mean(values, -1, keepdims=True)
    centered = values - row_mean
    row_var = jnp.mean(centered * centered, -1, keepdims=True)
    inverse = lax.rsqrt(row_var + EPSILON)
    return centered * inverse, inverse


def normalize_back(grad, unit, inverse):
    return inverse * (
        grad
        - jnp.mean(grad, -1, keepdims=True)
        - unit * jnp.mean(grad * unit, -1, keepdims=True)
    )


def gelu_both(u):
    root = 0.7978845608028654
    square = u * u
    inner = jnp.tanh(u * (root + (root * 0.044715) * square))
    half = 0.5 + 0.5 * inner
    slope = half + u * (0.5 - 0.5 * (inner * inner)) * (root + (3.0 * root * 0.044715) * square)
    return u * half, slope


def start_copies(pairs, sem):
    copies = [pltpu.make_async_copy(src, dst, sem.at[i]) for i, (src, dst) in enumerate(pairs)]
    for copy in copies:
        copy.start()
    return copies


def wait_copies(copies):
    for copy in copies:
        copy.wait()


def row_of(ref):
    return ref[...].astype(jnp.float32).reshape(1, ref.shape[0])


def my_spot():
    place = lax.axis_index("context")
    return lax.axis_index("tensor"), place // 2, place % 2


def group_homes():
    half, turn, share = my_spot()
    return [
        ((half + h) % 2, ((turn + t) % 2) * 2 + (share + s) % 2)
        for s in range(2)
        for h in range(2)
        for t in range(2)
    ]


def lanes_of(g, cols):
    return pl.ds((g % 2) * cols, cols)


def place_block(block, per):
    half, turn, share = my_spot()
    chunk = block // per
    spot = ((share + chunk) % 2) * 2 + (turn + chunk // 2) % 2
    return spot * per + block % per


def computed(random, per, blocks):
    def find(row):
        block = row + 2
        ids = [block - 1, block, (block + 1) % blocks]
        slots = [place_block(i, per) for i in ids]
        slots += [place_block(jnp.int32(i), per) for i in range(2)]
        slots += [random[block * 3 + i] for i in range(3)]
        return slots[1], slots, block >= 3, block <= blocks - 2

    return find, [place_block(jnp.int32(i), per) for i in range(2)]


def write_codes(segments, live, key_code, query_code, span):
    half, turn, share = my_spot()
    row = pl.ds(half * 2 + turn, 1)
    left = lax.broadcasted_iota(jnp.int32, (1, PAIR), 1) < HD
    per = span // BLK
    for spot in range(4):
        chunk = ((turn + spot) % 2) * 2 + (share + spot // 2) % 2
        lanes = pl.ds(pl.multiple_of(chunk * span, span), span)
        seg = segments[row, lanes]
        code = jnp.where(live[row, lanes] == 1, seg, -1)
        key_code[pl.ds(spot * per, per)] = jnp.broadcast_to(code, (PAIR, span)).T.reshape(
            per, BLK, PAIR
        )
        for two in range(per // 2):
            both = seg[:, two * PAIR : (two + 1) * PAIR]
            turned = pltpu.roll(both, HD, 1)
            at = spot * per + 2 * two
            query_code[at : at + 1, :] = jnp.where(left, both, turned)
            query_code[at + 1 : at + 2, :] = jnp.where(left, turned, both)


def project_attend_kernel(
    random, hidden, x_in, q_all, f_deep, n1_in, n2_in, segments, live, b_q, b_v, far_q, far_v,
    own_ref, other_home, q_home, k_home, v_home, w_home,
    n1, n2, n3, f0, f1, f2, f3, lse_ref, key_code, query_code,
    x_v, q_v, k_v, v_v, o_v, w_v, acc, in_sem, out_sem, w_sem, send_sem, recv_sem,
):
    span = hidden.shape[1]
    length, width = q_v.shape
    depth = f_deep.shape[0]
    half, turn, share = my_spot()
    across, beside, partner = neighbours()
    weights = start_copies(
        [(q_all.at[share, t, s], w_v.at[:, t, s]) for t in range(2) for s in range(2)], w_sem
    )
    chunks = [hidden.at[half * 2 + turn]] + [x_in.at[i] for i in range(3)]
    loads = start_copies(
        [(x, x_v.at[pl.ds(i * span, span)]) for i, x in enumerate(chunks)], in_sem
    )
    deep = lax.axis_index("dp")
    deeps = [{"dp": (deep + j) % depth} for j in range(1, depth)]
    signal_all([across, beside, partner] + deeps)
    ids = iter(range(send_sem.shape[0]))
    started = []

    def link(src, dst, device):
        i = next(ids)
        started.append(remote(src, dst, send_sem.at[i], recv_sem.at[i], device))
        return started[-1]

    at = [(deep + j) % depth for j in range(depth)]
    rest_of = range(1, depth)
    corner = [link(n2.at[at[j]], n3.at[at[j]], beside) for j in range(depth)]
    to_across = {j: link(f_deep.at[at[j]], n2.at[at[j]], across) for j in rest_of}
    along = {depth - j: link(n1.at[deep], n1.at[deep], deeps[j - 1]) for j in rest_of}
    ends = [
        [link(home.at[at[j]], landing.at[at[j]], partner) for j in range(depth)]
        for home, landing in ((f_deep, f0), (n1, f1), (n2, f2), (n3, f3))
    ]
    swap = link(o_v.at[pl.ds(length // 2, length // 2)], other_home, partner)
    corner[0].start()
    for j in rest_of:
        to_across[j].start()
        along[depth - j].start()
    for copy in ends[0] + [ends[1][0], ends[2][0]]:
        copy.start()

    def from_side(j):
        along[j].wait_recv()
        ends[1][j].start()

    def from_far(j):
        to_across[j].wait_recv()
        ends[2][j].start()
        corner[j].start()

    def from_corner(j):
        corner[j].wait_recv()
        ends[3][j].start()

    steps = [[(from_far, j)] for j in rest_of]
    steps[0].append((from_corner, 0))
    steps += [[(from_side, j) for j in rest_of] + [(from_corner, 1)]]
    steps += [[(from_corner, j)] for j in range(2, depth)]

    def take_step(index):
        for action, j in steps[index]:
            action(j)

    write_codes(segments, live, key_code, query_code, span)
    same = half == share
    bias = jnp.concatenate(
        [
            jnp.where(same, row_of(b_q), row_of(far_q)),
            jnp.zeros((1, width), jnp.float32),
            jnp.where(same, row_of(b_v), row_of(far_v)),
        ],
        1,
    )
    wait_copies(weights)
    wait_copies(loads)
    per = span // BLK

    def project(i, carry):
        at = pl.ds(pl.multiple_of(i * span, span), span)
        w_qkv = w_v[...].reshape(x_v.shape[1], 3 * width)
        value = (dot_nn(x_v[at, :], w_qkv) + bias).astype(jnp.bfloat16)
        q_v[at, :] = value[:, :width]
        k_v[pl.ds(i * per, per)] = value[:, width : 2 * width].reshape(per, BLK, width)
        v_v[pl.ds(i * per, per)] = value[:, 2 * width :].reshape(per, BLK, width)
        return carry

    lax.fori_loop(0, 4, project, 0)
    stores = start_copies([(q_v, q_home), (k_v, k_home), (v_v, v_home), (w_v, w_home)], out_sem)
    blocks = length // BLK
    find, wide = computed(random, span // BLK, blocks)
    count = blocks - 2
    early = min(5, count // LEAP // 2, len(steps))
    marks = [(2 * i + 1, functools.partial(take_step, i)) for i in range(early)]
    attend_blocks(
        find, wide, count, marks, q_v, k_v, v_v, key_code, query_code, o_v, lse_ref, acc
    )
    own_ref[...] = o_v[: length // 2, :]
    swap.start()
    for index in range(early, len(steps)):
        take_step(index)
    for copy in ends[0] + ends[1] + ends[2] + ends[3] + [swap]:
        copy.wait_recv()
    for copy in started:
        copy.wait_send()
    wait_copies(stores)


def project_attend(
    random, hidden, x_in, q_all, f_deep, n1, n2, segments, live, b_q, b_v, far_q, far_v
):
    span, features = hidden.shape[1:]
    length = 4 * span
    depth, slim, cols = q_all.shape[3:]
    width = cols // 3
    bf16, shape = jnp.bfloat16, jax.ShapeDtypeStruct
    piece = shape(f_deep.shape, bf16)
    outs = pl.pallas_call(
        project_attend_kernel,
        out_shape=(shape((length // 2, width), bf16),) * 2
        + (shape((length, width), bf16),)
        + (shape((length // BLK, BLK, width), bf16),) * 2
        + (shape((depth, 2, 2, slim, cols), bf16),)
        + (piece,) * 7
        + (
            shape((length // BLK, 8, PAIR), jnp.float32),
            shape((length // BLK, BLK, PAIR), jnp.int32),
            shape((length // BLK, PAIR), jnp.int32),
        ),
        in_specs=[SMEM_SPEC] + [ANY_SPEC] * 6 + [VMEM_SPEC] * 6,
        out_specs=(VMEM_SPEC,) + (ANY_SPEC,) * 12 + (VMEM_SPEC,) * 3,
        scratch_shapes=[pltpu.VMEM((length, features), bf16)]
        + [pltpu.VMEM((length, width), bf16)]
        + [pltpu.VMEM((length // BLK, BLK, width), bf16)] * 2
        + [pltpu.VMEM((length, width), bf16)]
        + [
            pltpu.VMEM((depth, 2, 2, slim, cols), bf16),
            pltpu.VMEM((width // PAIR, PAIR, PAIR), jnp.float32),
            DMA((4,)), DMA((4,)), DMA((4,)), DMA((8 * depth + 2,)), DMA((8 * depth + 2,)),
        ],
        input_output_aliases={5: 6, 6: 7},
        compiler_params=pltpu.CompilerParams(
            vmem_limit_bytes=63 * 1024 * 1024, collective_id=3, has_side_effects=True
        ),
        cost_estimate=pl.CostEstimate(
            flops=length * width * 1024 * 65, bytes_accessed=length * width * 16,
            transcendentals=length * width * 8,
        ),
        name="project_attend",
    )(
        random, hidden, x_in, q_all, f_deep, n1, n2, segments, live, b_q, b_v, far_q, far_v
    )
    att0, att1, q, k, v, w_qkv, *pieces, lse, key_code, query_code = outs
    w_qkv = w_qkv.reshape(features, cols)
    return att0, att1, q, k, v, lse, w_qkv, [f_deep] + pieces, key_code, query_code


def attend_grad_kernel(
    random, do0, do1, q_in, k_in, v_in, layer, key_code, query_code, lse_ref,
    d_ref, layer_home, sums,
    layer_v, layer_sem, q_v, k_v, v_v, do_v, dk_sum, dv_sum, acc, in_sem,
):
    f32 = jnp.float32
    length, width = q_v.shape
    half_length = length // 2
    loads = start_copies(
        [
            (q_in, q_v), (k_in, k_v), (v_in, v_v),
            (do0, do_v.at[pl.ds(0, half_length)]),
            (do1, do_v.at[pl.ds(half_length, half_length)]),
        ],
        in_sem,
    )
    take = pltpu.make_async_copy(layer, layer_v, layer_sem.at[0])
    put = pltpu.make_async_copy(layer_v, layer_home, layer_sem.at[1])
    take.start()
    wait_copies(loads)
    take.wait()
    put.start()
    parts = [d_ref.at[:, pl.ds(i * width, width)] for i in range(3)]
    blocks = length // BLK
    find, wide = computed(random, blocks // 4, blocks)
    attend_back_blocks(
        find, wide, blocks - 2, q_v, k_v, v_v, do_v, key_code, query_code, lse_ref,
        *parts, dk_sum, dv_sum, acc,
    )
    share = my_spot()[2]
    sums[...] = jnp.zeros_like(sums)
    for s in range(2):

        @pl.when(share == s)
        def _():
            lanes = slice(s * width, (s + 1) * width)
            sums[0:1, lanes] = jnp.sum(d_ref[:, :width].astype(f32), 0, keepdims=True)
            sums[1:2, lanes] = jnp.sum(d_ref[:, 2 * width :].astype(f32), 0, keepdims=True)
    put.wait()


def attend_grad(random, do0, do1, q, k, v, layer, key_code, query_code, lse):
    length, width = q.shape
    f32, bf16, shape = jnp.float32, jnp.bfloat16, jax.ShapeDtypeStruct
    return pl.pallas_call(
        attend_grad_kernel,
        out_shape=(
            shape((length, 3 * width), bf16), shape(layer.shape, bf16), shape((8, 2 * width), f32)
        ),
        in_specs=[SMEM_SPEC] + [ANY_SPEC] * 6 + [VMEM_SPEC] * 3,
        out_specs=(VMEM_SPEC, ANY_SPEC, VMEM_SPEC),
        scratch_shapes=[pltpu.VMEM(layer.shape, bf16), DMA((2,))]
        + [pltpu.VMEM((length, width), bf16)]
        + [pltpu.VMEM((length // BLK, BLK, width), bf16)] * 2
        + [pltpu.VMEM((length, width), bf16)]
        + [pltpu.VMEM((length, width), f32)] * 2
        + [pltpu.VMEM((width // PAIR, PAIR, PAIR), f32), DMA((5,))],
        compiler_params=WIDE_ROOM,
        cost_estimate=pl.CostEstimate(
            flops=length * width * 1024 * 75, bytes_accessed=length * width * 30,
            transcendentals=length * width * 8,
        ),
        name="attend_grad",
    )(random, do0, do1, q, k, v, layer, key_code, query_code, lse)


def load_weights(groups, w_up, w_dn, w_out, up_sem, dn_sem, wo_sem):
    depth, deep, cols = groups[0].shape
    thin = w_up.shape[2]
    slim = deep - 2 * thin
    homes = group_homes()
    out_loads = []
    for g in range(GROUPS):
        half, at = homes[g]
        for d in range(depth):
            spot = pl.ds(pl.multiple_of(d * thin + at * slim, 16), slim)
            out_loads.append(
                pltpu.make_async_copy(
                    groups[g].at[d, pl.ds(2 * thin, slim)], w_out.at[half, spot], wo_sem.at[g, d]
                )
            )
    up_loads = [
        pltpu.make_async_copy(
            groups[g].at[:, pl.ds(0, thin)], w_up.at[g // 2, :, :, lanes_of(g, cols)], up_sem.at[g]
        )
        for g in range(GROUPS)
    ]
    dn_loads = [
        pltpu.make_async_copy(
            groups[g].at[:, pl.ds(thin, thin)],
            w_dn.at[g // 2, :, :, lanes_of(g, cols)],
            dn_sem.at[g],
        )
        for g in range(GROUPS)
    ]
    return out_loads, up_loads, dn_loads


def whole(ref, g):
    depth, thin, cols = ref.shape[1:]
    return ref[g].reshape(depth * thin, cols)


def ffn_front_kernel(att0, att1, hidden, x_in, g_all, *rest):
    groups = rest[:GROUPS]
    (
        key_code, v_out, v_gain1, v_shift1, v_down, v_gain2, v_shift2, b_near, b_far,
        out0_home, out1_home, slope_home, g_second_home, unit_home, norm_t_home, down_home,
        inverse_ref, sums,
        att_v, x_v, g_v, w_up, w_dn, w_out, act, slope, normed_low,
        out_v, g_second_v, unit_v, norm_t, g_ffn_t, stage, b_up, b_all,
        in_sem, up_sem, dn_sem, wo_sem, stage_sem, home_sem, end_sem, g_sem,
    ) = rest[GROUPS:]
    f32, bf16 = jnp.float32, jnp.bfloat16
    rows, width = x_v.shape
    span = hidden.shape[1]
    depth, deep, cols = groups[0].shape
    half, turn, share = my_spot()
    x_chunks = (hidden.at[half * 2 + turn], x_in.at[0])
    g_chunks = (g_all.at[half * 2 + turn],)
    other = (share + 1) % 2
    out_loads, up_loads, dn_loads = load_weights(groups, w_up, w_dn, w_out, up_sem, dn_sem, wo_sem)
    loads = start_copies(
        [(a, att_v.at[:, lanes_of(i, cols)]) for i, a in enumerate((att0, att1))]
        + [(x, x_v.at[pl.ds(i * span, span)]) for i, x in enumerate(x_chunks)]
        + [(g, g_v.at[pl.ds(i * span, span)]) for i, g in enumerate(g_chunks)],
        in_sem,
    )
    for copy in out_loads + up_loads + dn_loads:
        copy.start()
    beside = neighbours()[1]
    signal_all([beside])
    g_next = remote(
        g_all.at[half * 2 + (turn + 1) % 2], g_v.at[pl.ds(span, span)], g_sem.at[0], g_sem.at[1],
        beside,
    )
    g_next.start()
    sums[...] = jnp.zeros_like(sums)
    b_all[0:1, :] = row_of(b_near)
    b_all[1:2, :] = row_of(b_far)
    for g in range(GROUPS):
        at = group_homes()[g][1]
        lanes = pl.ds(pl.multiple_of(at * cols, PAIR), cols)
        value = b_all[g // 2 % 2 : g // 2 % 2 + 1, lanes]
        b_up[g // 2 : g // 2 + 1, (g % 2) * cols : (g % 2 + 1) * cols] = value
    wait_copies(loads + out_loads)
    b_out, gain1, shift1, b_down, gain2, shift2 = (
        row_of(ref) for ref in (v_out, v_gain1, v_shift1, v_down, v_gain2, v_shift2)
    )

    def add_sum(index, value):
        sums[index : index + 1, :] += jnp.sum(value, 0, keepdims=True)

    def homes(tile):
        at = pl.ds(pl.multiple_of(tile * FRONT, FRONT), FRONT)
        return [
            pltpu.make_async_copy(src, dst, home_sem.at[i, tile])
            for i, (src, dst) in enumerate(
                [
                    (slope.at[:, at], slope_home.at[:, at]),
                    (g_second_v.at[at], g_second_home.at[at]),
                    (unit_v.at[at], unit_home.at[at]),
                ]
            )
        ]

    def tile_step(tile, carry):
        at = pl.ds(pl.multiple_of(tile * FRONT, FRONT), FRONT)
        live = (key_code[at, :1] >= 0).astype(f32)
        add_sum(11, jnp.broadcast_to(live, (FRONT, width)))
        attn = b_out + dot_nt(att_v[at, :], jnp.concatenate([w_out[share], w_out[other]], 1))
        x = x_v[at, :].astype(f32)
        first = x + attn
        add_sum(6, live * (x * x))
        add_sum(7, live * (first * first))
        add_sum(9, live * (attn * attn))
        unit1, inverse1 = normalize(first)
        unit_v[at, :] = unit1
        inverse_ref[at, :] = inverse1
        normed = unit1 * gain1 + shift1
        low = normed.astype(bf16)
        normed_low[...] = low
        norm_t[:, at] = low.T

        @pl.when(tile == 0)
        def _():
            wait_copies(up_loads + dn_loads)

        @pl.when(tile == span // FRONT)
        def _():
            g_next.wait_recv()

        def up_step(g, ffn):
            pre = dot_nn(normed_low[...], whole(w_up, g)) + b_up[pl.ds(g, 1), :]
            value, rise = gelu_both(pre)
            value = value.astype(bf16)
            act[g, at, :] = value
            slope[g, at, :] = rise.astype(bf16)
            return ffn + dot_nt(value, whole(w_dn, g))

        ffn = lax.fori_loop(0, DUOS, up_step, jnp.broadcast_to(b_down, (FRONT, width)))
        second = normed + ffn
        add_sum(8, live * (second * second))
        add_sum(10, live * (ffn * ffn))
        unit2, inverse2 = normalize(second)
        out_v[at, :] = (unit2 * gain2 + shift2).astype(bf16)
        g_out = g_v[at, :].astype(f32)
        add_sum(4, g_out * unit2)
        add_sum(5, g_out)
        g_second = normalize_back(g_out * gain2, unit2, inverse2)
        g_second_v[at, :] = g_second
        g_ffn = g_second.astype(bf16)
        add_sum(3, g_ffn.astype(f32))
        g_ffn_t[:, at] = g_ffn.T
        for copy in homes(tile):
            copy.start()
        return carry

    lax.fori_loop(0, rows // FRONT, tile_step, 0)
    last = start_copies(
        [
            (norm_t, norm_t_home),
            (out_v.at[pl.ds(0, span)], out0_home),
            (out_v.at[pl.ds(span, span)], out1_home),
        ],
        end_sem,
    )

    def leave(g):
        return pltpu.make_async_copy(stage.at[g], down_home.at[g], stage_sem.at[g])

    def down_step(duo, carry):
        down = dot_nn(g_ffn_t[...], act[duo]).astype(bf16).reshape(depth, -1, 2 * cols)
        for i in range(2):
            stage[2 * duo + i] = down[:, :, i * cols : (i + 1) * cols]
            leave(2 * duo + i).start()
        return carry

    lax.fori_loop(0, DUOS, down_step, 0)
    for tile in range(rows // FRONT):
        wait_copies(homes(tile))
    wait_copies([leave(g) for g in range(GROUPS)] + last)
    g_next.wait_send()


def ffn_front(att0, att1, hidden, x_in, g_all, groups, key_code, vectors, b_near, b_far):
    rows, part = att0.shape
    width = hidden.shape[2]
    depth, deep, cols = groups[0].shape
    thin = width // depth
    f32, bf16, shape = jnp.float32, jnp.bfloat16, jax.ShapeDtypeStruct
    weights = pltpu.VMEM((DUOS, depth, thin, 2 * cols), bf16)
    flat = pltpu.VMEM((rows, width), bf16)
    tall = pltpu.VMEM((rows, width), f32)
    deep_rows = pltpu.VMEM((DUOS, rows, 2 * cols), bf16)
    turned = pltpu.VMEM((width, rows), bf16)
    return pl.pallas_call(
        ffn_front_kernel,
        out_shape=(
            shape((rows // 2, width), bf16), shape((rows // 2, width), bf16),
            shape((DUOS, rows, 2 * cols), bf16),
            shape((rows, width), f32), shape((rows, width), f32), shape((width, rows), bf16),
            shape((GROUPS, depth, thin, cols), bf16), shape((rows, 1), f32), shape((16, width), f32),
        ),
        in_specs=[ANY_SPEC] * (5 + GROUPS) + [VMEM_SPEC] * 9,
        out_specs=(ANY_SPEC,) * 7 + (VMEM_SPEC,) * 2,
        scratch_shapes=[
            flat, flat, flat, weights, weights, pltpu.VMEM((2, width, part), bf16),
            deep_rows, deep_rows, pltpu.VMEM((FRONT, width), bf16),
            flat, tall, tall, turned, turned, pltpu.VMEM((GROUPS, depth, thin, cols), bf16),
            pltpu.VMEM((DUOS, 2 * cols), f32), pltpu.VMEM((2, 4 * cols), f32),
            DMA((6,)), DMA((GROUPS,)), DMA((GROUPS,)), DMA((GROUPS, depth)), DMA((GROUPS,)),
            DMA((3, rows // FRONT)), DMA((3,)), DMA((2,)),
        ],
        compiler_params=pltpu.CompilerParams(
            vmem_limit_bytes=63 * 1024 * 1024, collective_id=4, has_side_effects=True
        ),
        cost_estimate=pl.CostEstimate(
            flops=38 * 10**9, bytes_accessed=40 * 10**6, transcendentals=rows * GROUPS * cols
        ),
        name="ffn_front",
    )(att0, att1, hidden, x_in, g_all, *groups, key_code, *vectors, b_near, b_far)


def ffn_rear_kernel(
    att0, att1, slope_in, g_second_in, unit_in, norm_t_in, out0, out1, downs, *rest
):
    groups = rest[:GROUPS]
    (
        inverse_ref, v_gain1,
        g_first_home, do_own, do_far, layer_home, *totals
    ) = rest[GROUPS : GROUPS + 5 + DUOS + groups[0].shape[0]]
    corners = totals[DUOS - 1 :]
    (
        sums, up_sums,
        att_v, slope, g_second_v, unit_v, norm_t, w_up, w_dn, w_out, g_pre,
        g_first_v, g_att_v, g_attn_t, out_v, far_v, got_v, got_dn, near_v, stage,
        in_sem, up_sem, dn_sem, wo_sem, stage_sem, home_sem, out_sem,
        l_send, l_recv, a_send, a_recv, u_send, u_recv, corner_sem,
    ) = rest[GROUPS + 5 + DUOS + len(corners) :]
    f32, bf16 = jnp.float32, jnp.bfloat16
    rows, width = unit_v.shape
    span = out0.shape[0]
    depth, deep, cols = groups[0].shape
    thin = w_up.shape[2]
    slim = deep - 2 * thin
    half, turn, share = my_spot()
    other = (share + 1) % 2
    across, beside, partner = neighbours()
    out_loads, up_loads, dn_loads = load_weights(groups, w_up, w_dn, w_out, up_sem, dn_sem, wo_sem)
    wait_order = [
        pltpu.make_async_copy(src, dst, in_sem.at[i])
        for i, (src, dst) in enumerate(
            [
                (g_second_in, g_second_v), (slope_in, slope), (unit_in, unit_v),
                (norm_t_in, norm_t), (att0, att_v.at[:, lanes_of(0, cols)]),
                (att1, att_v.at[:, lanes_of(1, cols)]),
            ]
        )
    ]
    for copy in wait_order[:1] + dn_loads + wait_order[1:2] + up_loads + wait_order[2:3]:
        copy.start()
    for copy in out_loads + wait_order[3:]:
        copy.start()
    late = start_copies([(out0, out_v), (downs.at[pl.ds(0, DUOS)], near_v)], out_sem)
    signal_all([across, beside, partner])
    mine = layer_home.at[half * 2 + turn]
    theirs = layer_home.at[half * 2 + (turn + 1) % 2]
    parts = [pl.ds(i * (span // 2), span // 2) for i in range(2)]
    layer = [
        remote(out1.at[parts[0]], mine.at[parts[0]], l_send.at[0], l_recv.at[0], beside),
        remote(out0, mine, l_send.at[1], l_recv.at[1], across),
        remote(theirs.at[parts[0]], theirs.at[parts[0]], l_send.at[2], l_recv.at[2], across),
        remote(downs.at[pl.ds(DUOS, DUOS)], got_dn, l_send.at[3], l_recv.at[3], partner),
        remote(out1.at[parts[1]], mine.at[parts[1]], l_send.at[4], l_recv.at[4], beside),
        remote(theirs.at[parts[1]], theirs.at[parts[1]], l_send.at[5], l_recv.at[5], across),
    ]
    for i in (0, 4, 1, 3):
        layer[i].start()
    sums[...] = jnp.zeros_like(sums)
    up_sums[...] = jnp.zeros_like(up_sums)
    gain1 = row_of(v_gain1)
    wait_copies(wait_order[:1] + dn_loads + wait_order[1:2])
    out_weight = lambda: jnp.concatenate([w_out[share], w_out[other]], 1)

    def add_sum(index, value):
        sums[index : index + 1, :] += jnp.sum(value, 0, keepdims=True)

    def tile_rows(tile):
        return pl.ds(pl.multiple_of(tile * TILE, TILE), TILE)

    def give(tile):
        at = tile_rows(tile)
        return remote(g_att_v.at[1, at], do_far.at[at], a_send.at[tile], a_recv.at[tile], partner)

    tiles = rows // TILE

    def tile_step(tile, carry):
        at = tile_rows(tile)

        @pl.when(tile == 0)
        def _():
            wait_copies(up_loads + wait_order[2:] + out_loads)

        for late_tile, i in ((tiles - 2, 0), (tiles - 1, 1)):

            @pl.when(tile == late_tile)
            def _():
                layer[(0, 4)[i]].wait_recv()
                layer[(2, 5)[i]].start()

        g_second = g_second_v[at, :]
        g_ffn = g_second.astype(bf16)

        def back_step(g, total):
            grad = (dot_nn(g_ffn, whole(w_dn, g)) * slope[g, at, :].astype(f32)).astype(bf16)
            g_pre[g, at, :] = grad
            up_sums[pl.ds(g, 1), :] += jnp.sum(grad.astype(f32), 0, keepdims=True)
            return total + dot_nt(grad, whole(w_up, g))

        g_normed = lax.fori_loop(0, DUOS, back_step, g_second)
        unit1 = unit_v[at, :]
        add_sum(1, g_normed * unit1)
        add_sum(2, g_normed)
        g_first = normalize_back(g_normed * gain1, unit1, inverse_ref[at, :])
        g_first_v[at, :] = g_first
        g_attn = g_first.astype(bf16)
        add_sum(0, g_attn.astype(f32))
        g_attn_t[:, at] = g_attn.T
        both = dot_nn(g_attn, out_weight()).astype(bf16)
        g_att_v[0, at, :] = both[:, :cols]
        g_att_v[1, at, :] = both[:, cols:]
        give(tile).start()
        return carry

    lax.fori_loop(0, tiles, tile_step, 0)
    homes = start_copies([(g_att_v.at[0], do_own), (g_first_v, g_first_home)], home_sem)
    wait_copies(late)
    own_out = pltpu.make_async_copy(out_v, mine, out_sem.at[0])
    own_out.start()
    both = dot_nn(g_attn_t[...], att_v[...]).astype(bf16)
    w_out[share] = both[:, :cols]
    w_out[other] = both[:, cols:]

    def out_rows(g, d):
        where = (half + g // 2) % 2
        at = ((turn + g) % 2) * 2 + (share + g // 4) % 2
        return w_out[where, pl.ds(pl.multiple_of(d * thin + at * slim, 16), slim), :]

    def up_of(duo):
        up = dot_nn(norm_t[...], g_pre[duo]).astype(bf16).reshape(depth, thin, 2 * cols)
        return [(2 * duo + i, up[:, :, i * cols : (i + 1) * cols]) for i in range(2)]

    def pass_on(i):
        return remote(far_v.at[i], got_v.at[i], u_send.at[i], u_recv.at[i], partner)

    def far_step(duo, carry):
        for g, up in up_of(duo):
            i = g - DUOS
            far_v[i, :, pl.ds(0, thin), :] = up
            for d in range(depth):
                far_v[i, d, pl.ds(thin, slim), :] = out_rows(g, d)
            pass_on(i).start()
        return carry

    lax.fori_loop(DUOS // 2, DUOS, far_step, 0)
    sends = [pass_on(i) for i in range(DUOS)]
    layer[3].wait_recv()
    add = lambda a, b: (a.astype(f32) + b.astype(f32)).astype(bf16)
    stores = [None] * DUOS
    for duo in range(DUOS // 2):
        for g, up in up_of(duo):
            slot = g % 2
            if g >= 2:
                stores[g - 2].wait()
            sends[g].wait_recv()
            stage[slot, :, pl.ds(0, thin), :] = add(up, got_v[g, :, pl.ds(0, thin), :])
            stage[slot, :, pl.ds(thin, thin), :] = add(near_v[g], got_dn[g])
            for d in range(depth):
                stage[slot, d, pl.ds(2 * thin, slim), :] = add(
                    out_rows(g, d), got_v[g, d, pl.ds(thin, slim), :]
                )
            if g == DUOS - 1:
                deep_at = lax.axis_index("dp")
                rounds = start_copies(
                    [
                        (stage.at[slot, (deep_at + j) % depth], home)
                        for j, home in enumerate(corners)
                    ],
                    corner_sem,
                )
                continue
            stores[g] = pltpu.make_async_copy(stage.at[slot], totals[g], stage_sem.at[slot])
            stores[g].start()
    for tile in range(tiles):
        give(tile).wait()
    for i in (1, 2, 5):
        layer[i].wait_recv()
    for copy in layer + sends:
        copy.wait_send()
    wait_copies(stores[-2:-1] + rounds + homes + [own_out])


def ffn_rear(
    att0, att1, slope, g_second, unit, norm_t, out0, out1, downs_in, groups, inverse, gain1
):
    rows, part = att0.shape
    span, width = out0.shape
    depth, deep, cols = groups[0].shape
    thin = width // depth
    f32, bf16, shape, v = jnp.float32, jnp.bfloat16, jax.ShapeDtypeStruct, pltpu.VMEM
    weights = v((DUOS, depth, thin, 2 * cols), bf16)
    flat = v((rows, width), bf16)
    tall = v((rows, width), f32)
    deep_rows = v((DUOS, rows, 2 * cols), bf16)
    turned = v((width, rows), bf16)
    mixed = v((DUOS, depth, deep - thin, cols), bf16)
    downs = v((DUOS, depth, thin, cols), bf16)
    tiles = rows // TILE
    return pl.pallas_call(
        ffn_rear_kernel,
        out_shape=(
            shape((rows, width), f32), shape((rows, part), bf16), shape((rows, part), bf16),
            shape((4, span, width), bf16),
        )
        + (shape((depth, deep, cols), bf16),) * (DUOS - 1)
        + (shape((deep, cols), bf16),) * depth
        + (shape((16, width), f32), shape((DUOS, 2 * cols), f32)),
        in_specs=[ANY_SPEC] * (9 + GROUPS) + [VMEM_SPEC] * 2,
        out_specs=(ANY_SPEC,) * (3 + DUOS + depth) + (VMEM_SPEC,) * 2,
        scratch_shapes=[
            flat, deep_rows, tall, tall, turned, weights, weights,
            v((2, width, part), bf16), deep_rows, tall, v((2, rows, part), bf16), turned,
            v((span, width), bf16), mixed, mixed, downs, downs, v((2, depth, deep, cols), bf16),
            DMA((6,)), DMA((GROUPS,)), DMA((GROUPS,)), DMA((GROUPS, depth)), DMA((2,)), DMA((2,)),
            DMA((2,)), DMA((6,)), DMA((6,)), DMA((tiles,)), DMA((tiles,)), DMA((DUOS,)),
            DMA((DUOS,)), DMA((depth,)),
        ],
        compiler_params=pltpu.CompilerParams(
            vmem_limit_bytes=63 * 1024 * 1024, collective_id=2, has_side_effects=True
        ),
        cost_estimate=pl.CostEstimate(
            flops=45 * 10**9, bytes_accessed=40 * 10**6, transcendentals=0
        ),
        name="ffn_rear",
    )(
        att0, att1, slope, g_second, unit, norm_t, out0, out1, downs_in, *groups, inverse, gain1
    )


MESH = pl.DeviceIdType.MESH
CUTS = 8
THIRDS = 3


def signal_all(devices):
    barrier = pltpu.get_barrier_semaphore()
    for device in devices:
        pl.semaphore_signal(barrier, inc=1, device_id=device, device_id_type=MESH)
    pl.semaphore_wait(barrier, len(devices))


def neighbours():
    half, turn, share = my_spot()
    return (
        {"tensor": (half + 1) % 2},
        {"context": ((turn + 1) % 2) * 2 + share},
        {"context": turn * 2 + (share + 1) % 2},
    )


def remote(src, dst, send_sem, recv_sem, device):
    return pltpu.make_async_remote_copy(
        src_ref=src, dst_ref=dst, send_sem=send_sem, recv_sem=recv_sem,
        device_id=device, device_id_type=MESH,
    )


def fetch_kernel(
    hidden, w_q, w_k, w_v, w_up, w_down, w_out, bias_q, bias_v, bias_u,
    x_out, q_all, f_deep, n1, n2, far_q, far_v, far_u,
    qkv, ffn, cut_sem, own_sem, x_send, x_recv, z_send, z_recv, f_send, f_recv,
    h_send, h_recv, t_send, t_recv, c_send, c_recv, b_sem, n_send, n_recv,
):
    half, turn, share = my_spot()
    deep = lax.axis_index("dp")
    depth = f_deep.shape[0]
    across, beside, partner = neighbours()
    up, down = {"dp": (deep + 1) % depth}, {"dp": (deep + depth - 1) % depth}
    slim, thin, cols = qkv.shape[0], w_q.shape[0], w_q.shape[1]
    place = turn * 2 + share
    my_rows = pl.ds(pl.multiple_of(place * slim, 16), slim)
    my_lanes = pl.ds(pl.multiple_of(place * cols, PAIR), cols)
    cuts = start_copies(
        [(w.at[my_rows], qkv.at[:, pl.ds(i * cols, cols)]) for i, w in enumerate((w_q, w_k, w_v))]
        + [(w.at[:, my_lanes], ffn.at[pl.ds(i * thin, thin)]) for i, w in enumerate((w_up, w_down))]
        + [(w_out.at[my_rows], ffn.at[pl.ds(2 * thin, slim)])],
        cut_sem,
    )
    signal_all([across, beside, partner, up, down])
    wait_copies(cuts)

    slot = lambda h, t, d: q_all.at[h, t, share, d]
    own = start_copies([(qkv, slot(half, turn, deep)), (ffn, f_deep.at[deep])], own_sem)

    def to_up(d):
        return remote(slot(half, turn, d), slot(half, turn, d), z_send.at[0, d], z_recv.at[d], up)

    def to_down(d):
        return remote(slot(half, turn, d), slot(half, turn, d), z_send.at[1, d], z_recv.at[d], down)

    third = f_deep.shape[1] // THIRDS

    def f_copies(d, side, device):
        return [
            remote(
                f_deep.at[d, pl.ds(i * third, third)], f_deep.at[d, pl.ds(i * third, third)],
                f_send.at[side, d, i], f_recv.at[d, i], device,
            )
            for i in range(THIRDS)
        ]

    f_up = lambda d: f_copies(d, 0, up)
    f_down = lambda d: f_copies(d, 1, down)

    def to_across(t, d):
        return remote(slot(half, t, d), slot(half, t, d), h_send.at[t, d], h_recv.at[t, d], across)

    def from_across(t, d):
        other = slot((half + 1) % 2, t, d)
        return remote(other, other, h_send.at[t, d], h_recv.at[t, d], across)

    def to_beside(d):
        return remote(slot(half, turn, d), slot(half, turn, d), t_send.at[d], t_recv.at[d], beside)

    def from_beside(d):
        other = slot(half, (turn + 1) % 2, d)
        return remote(other, other, t_send.at[d], t_recv.at[d], beside)

    def to_partner(t, d):
        piece = slot((share + 1) % 2, t, d)
        return remote(piece, piece, c_send.at[t, d], c_recv.at[t, d], partner)

    def from_partner(t, d):
        piece = q_all.at[share, t, (share + 1) % 2, d]
        return remote(piece, piece, c_send.at[t, d], c_recv.at[t, d], partner)

    cut = x_out.shape[1] // CUTS
    piece_rows = lambda i: pl.ds(i * cut, cut)
    x_next = [
        remote(
            hidden.at[half * 2 + (turn + 1) % 2, piece_rows(i)], x_out.at[0, piece_rows(i)],
            x_send.at[0, i], x_recv.at[0, i], beside,
        )
        for i in range(CUTS)
    ]
    x_mine = remote(
        hidden.at[half * 2 + turn], x_out.at[1], x_send.at[1, 0], x_recv.at[1, 0], partner
    )
    x_relay = [
        remote(
            x_out.at[0, piece_rows(i)], x_out.at[2, piece_rows(i)],
            x_send.at[2, i], x_recv.at[2, i], partner,
        )
        for i in range(CUTS)
    ]
    biases = [
        remote(src, dst, b_sem.at[0, i], b_sem.at[1, i], across)
        for i, (src, dst) in enumerate(((bias_q, far_q), (bias_v, far_v), (bias_u, far_u)))
    ]
    wait_copies(own)
    own_turn = (share + 1) % 2 == half

    def spread_own(d):
        to_across(turn, d).start()
        to_beside(d).start()

        @pl.when(own_turn)
        def _():
            to_partner(turn, d).start()

    def when(condition, *copies):
        @pl.when(condition)
        def _():
            for copy in copies:
                copy.start()

    when(deep < depth - 1, to_up(deep))
    when(deep > 0, to_down(deep))
    when(deep < depth - 1, f_up(deep)[0])
    when(deep > 0, f_down(deep)[0])
    spread_own(deep)
    x_next[0].start()
    for copy in biases:
        copy.start()
    x_mine.start()
    for k in range(1, depth):
        low, high = (deep + depth - k) % depth, (deep + k) % depth

        @pl.when(deep >= k)
        def _():
            to_up(low).wait_recv()
            when(deep < depth - 1, to_up(low))
            spread_own(low)

        @pl.when(deep + k < depth)
        def _():
            to_down(high).wait_recv()
            when(deep > 0, to_down(high))
            spread_own(high)

        if k < THIRDS:
            when(deep < depth - 1, f_up(deep)[k])
            when(deep > 0, f_down(deep)[k])
        x_next[k].start()

    for i in range(depth, THIRDS):
        when(deep < depth - 1, f_up(deep)[i])
        when(deep > 0, f_down(deep)[i])
    for copy in x_next[depth:]:
        copy.start()
    for k in range(depth):
        d = (deep + k) % depth
        from_beside(d).wait_recv()
        to_across((turn + 1) % 2, d).start()

        @pl.when(own_turn)
        def _():
            to_partner((turn + 1) % 2, d).start()

    f_side = [
        remote(
            f_deep.at[deep, pl.ds(i * third, third)], home.at[deep, pl.ds(i * third, third)],
            n_send.at[j, i], n_recv.at[j, i], device,
        )
        for i in range(THIRDS)
        for j, (home, device) in enumerate(((n1, beside), (n2, across)))
    ]
    for copy in f_side:
        copy.start()

    def f_step(k):
        low, high = (deep + depth - k) % depth, (deep + k) % depth

        @pl.when(deep >= k)
        def _():
            for copy in f_up(low):
                copy.wait_recv()
                when(deep < depth - 1, copy)

        @pl.when(deep + k < depth)
        def _():
            for copy in f_down(high):
                copy.wait_recv()
                when(deep > 0, copy)

    def x_step(step):
        for i in range(step * CUTS // (depth + 1), (step + 1) * CUTS // (depth + 1)):
            x_next[i].wait_recv()
            x_relay[i].start()

    f_step(1)
    for step, t in enumerate((turn, (turn + 1) % 2)):
        for k in range(depth):
            d = (deep + k) % depth
            from_across(t, d).wait_recv()

            @pl.when(jnp.logical_not(own_turn))
            def _():
                to_partner(t, d).start()

        x_step(step)
        if step == 0 and depth > 2:
            f_step(2)
    for k in range(3, depth):
        x_step(k - 1)
        f_step(k)
    for step in range(max(2, depth - 1), depth + 1):
        x_step(step)

    for t in range(2):
        for d in range(depth):
            from_partner(t, d).wait_recv()
    x_mine.wait_recv()
    for copy in x_relay + biases + f_side:
        copy.wait_recv()
    for d in range(depth):
        for copy in (to_across(0, d), to_across(1, d), to_beside(d), to_partner(0, d), to_partner(1, d)):
            copy.wait_send()

        @pl.when(jnp.logical_and(deep < depth - 1, deep >= d))
        def _():
            for copy in [to_up(d)] + f_up(d):
                copy.wait_send()

        @pl.when(jnp.logical_and(deep > 0, deep <= d))
        def _():
            for copy in [to_down(d)] + f_down(d):
                copy.wait_send()

    for copy in x_next + x_relay + [x_mine] + biases + f_side:
        copy.wait_send()


def fetch(hidden_in, weights, biases, depth):
    span, width = hidden_in.shape[1:]
    thin, cols = weights[0].shape
    slim = thin // 4
    bf16, shape = jnp.bfloat16, jax.ShapeDtypeStruct
    pair = DMA((2, depth))
    return pl.pallas_call(
        fetch_kernel,
        out_shape=(
            shape((3, span, width), bf16),
            shape((2, 2, 2, depth, slim, 3 * cols), bf16),
            *(shape((depth, 2 * thin + slim, cols), bf16) for _ in range(3)),
            *(shape(b.shape, bf16) for b in biases),
        ),
        in_specs=[ANY_SPEC] * 7 + [VMEM_SPEC] * 3,
        out_specs=(ANY_SPEC, VMEM_SPEC) + (ANY_SPEC,) * 3 + (VMEM_SPEC,) * 3,
        scratch_shapes=[
            pltpu.VMEM((slim, 3 * cols), bf16), pltpu.VMEM((2 * thin + slim, cols), bf16),
            DMA((6,)), DMA((2,)), DMA((3, CUTS)), DMA((3, CUTS)), pair, DMA((depth,)),
            DMA((2, depth, THIRDS)), DMA((depth, THIRDS)),
            pair, pair, DMA((depth,)), DMA((depth,)), pair, pair, DMA((2, 3)),
            DMA((2, THIRDS)), DMA((2, THIRDS)),
        ],
        compiler_params=pltpu.CompilerParams(
            vmem_limit_bytes=63 * 1024 * 1024, collective_id=0, has_side_effects=True
        ),
        cost_estimate=pl.CostEstimate(
            flops=30 * 10**9, bytes_accessed=10 * 10**6, transcendentals=0
        ),
        name="fetch",
    )(hidden_in, *weights, *biases)


SUBS = 4


def settle_kernel(
    parts_depth, hidden, x_in, dqkv, w_qkv, g_first, front_sums, rear_sums, up_sums, head_sums,
    *rest,
):
    f32, bf16 = jnp.float32, jnp.bfloat16
    parts, corners = rest[:3], rest[3 : 3 + parts_depth]
    (
        out, qkv_out, f_out, small_out,
        x_v, d_v, w_v, first_v, part_v, small_v, small_got,
        back_v, got_v, fin_v, land_v, tot_v, zf_v, ff_v,
        corner_v, corner_out, corner_in, grad_v, swap_v, pq_v, yl_v, xs_v, xl_v, rs_v, zq_v, qf_v,
        in_sem, out_sem, send_sem, recv_sem,
    ) = rest[3 + parts_depth :]
    half, turn, share = my_spot()
    deep = lax.axis_index("dp")
    depth = tot_v.shape[0]
    span = hidden.shape[1]
    sub = span // SUBS
    other = (share + 1) % 2
    far_half, far_turn = (half + 1) % 2, (turn + 1) % 2
    across, beside, partner = neighbours()
    deeps = [{"dp": (deep + k) % depth} for k in range(1, depth)]
    ids = iter(range(send_sem.shape[0]))
    started = []

    def link(src, dst, device):
        i = next(ids)
        copy = remote(src, dst, send_sem.at[i], recv_sem.at[i], device)
        started.append(copy)
        return copy

    def go(src, dst, device):
        copy = link(src, dst, device)
        copy.start()
        return copy

    chunk = lambda i: pl.ds(i * span, span)
    chunks = [hidden.at[half * 2 + turn]] + [x_in.at[i] for i in range(3)]
    loads = [
        pltpu.make_async_copy(src, dst, in_sem.at[i])
        for i, (src, dst) in enumerate(
            [(w_qkv, w_v)]
            + [(dqkv.at[chunk(i)], d_v.at[chunk(i)]) for i in (2, 3, 0, 1)]
            + [(p, part_v.at[i]) for i, p in enumerate(parts)]
            + [(g_first, first_v)]
            + [(c, x_v.at[chunk(i)]) for i, c in enumerate(chunks)]
        )
    ]
    corner_loads = start_copies(
        [(c, corner_v.at[i]) for i, c in enumerate(corners)], out_sem
    )
    for copy in loads:
        copy.start()
    diagonal = {"tensor": far_half, "context": far_turn * 2 + share}
    signal_all([across, beside, partner, diagonal] + deeps)
    wait_copies(corner_loads)
    corner_out[...] = sum(
        [corner_v[i].astype(f32) for i in range(1, depth)], corner_v[0].astype(f32)
    ).astype(bf16)
    corner = go(corner_out, corner_in, diagonal)
    small_v[...] = jnp.zeros_like(small_v)
    cols = up_sums.shape[1] // 2
    for g, (where, at) in enumerate(group_homes()):
        row = pl.ds(where * 2 + at // 2, 1)
        lanes = pl.ds(pl.multiple_of((at % 2) * cols, PAIR), cols)
        small_v[row, lanes] = up_sums[g // 2 : g // 2 + 1, (g % 2) * cols : (g % 2 + 1) * cols]
    small_v[4:7, :] = rear_sums[0:3, :]
    small_v[7:10, :] = front_sums[3:6, :]
    lane = lax.broadcasted_iota(jnp.int32, (1, small_v.shape[1]), 1)
    stats = jnp.where(lane == 5, front_sums[11:12, :], 0.0)
    for i in range(5):
        stats = jnp.where(lane == i, jnp.sum(front_sums[6 + i : 7 + i, :], 1, keepdims=True), stats)
    small_v[10:11, :] = stats
    small_v[11:13, :] = head_sums[0:2, :]

    s0 = go(small_v, small_got.at[0], partner)
    wait_copies(loads[:5] + loads[8:9])
    outs = []
    first_id = next(ids)
    next(ids)

    def give(i):
        return remote(
            back_v.at[i], got_v.at[i], send_sem.at[first_id + i], recv_sem.at[first_id + i], partner
        )

    rows = lambda j: pl.ds(j * sub, sub)

    def put(ref, h, t):
        copy = pltpu.make_async_copy(ref, out.at[h * 2 + t], out_sem.at[len(outs)])
        copy.start()
        outs.append(copy)

    own_put = pltpu.make_async_copy(fin_v.at[0], out.at[half * 2 + turn], out_sem.at[0])
    outs.append(own_put)
    x_subs = [link(fin_v.at[0, rows(j)], land_v.at[1, rows(j)], across) for j in range(SUBS)]
    y_subs = [link(fin_v.at[1, rows(j)], land_v.at[0, rows(j)], beside) for j in range(SUBS // 2)]

    def back_step(i, carry):
        at = pl.ds(pl.multiple_of((i + 2) % 4 * span, span), span)
        value = dot_nt(d_v[at, :], w_v[...])

        @pl.when(i < 2)
        def _():
            back_v[i] = value.astype(bf16)
            give(i).start()

        @pl.when(i >= 2)
        def _():
            give(i - 2).wait_recv()
            whole_sum = value + first_v[at, :] + got_v[i - 2].astype(f32)
            fin_v[i - 2] = whole_sum.astype(bf16)

        @pl.when(i == 2)
        def _():
            for copy in x_subs + [own_put]:
                copy.start()

        @pl.when(i == 3)
        def _():
            for copy in y_subs:
                copy.start()

        return carry

    lax.fori_loop(0, 4, back_step, 0)
    started += [give(0), give(1)]
    wait_copies(loads[5:8])
    tot_v[...] = (
        part_v[0].astype(f32) + part_v[1].astype(f32) + part_v[2].astype(f32)
    ).astype(bf16)
    z_f = [
        go(tot_v.at[(deep + k + 1) % depth], zf_v.at[k], device) for k, device in enumerate(deeps)
    ]


    s0.wait_recv()
    s0.wait_send()
    small_v[...] += small_got[0]
    s1 = go(small_v, small_got.at[1], beside)
    wait_copies(loads[9:])
    third = grad_v.shape[0] // 3

    def grad_step(i, carry):
        at = pl.ds(pl.multiple_of(i * third, PAIR), third)
        grad_v[at, :] = dot_tn(x_v[:, at], d_v[...]).astype(bf16)
        return carry

    lax.fori_loop(0, 3, grad_step, 0)
    slim = swap_v.shape[2]

    def grad_rows(d, t, s):
        return grad_v[pl.ds(pl.multiple_of((d * 4 + t * 2 + s) * slim, 16), slim), :]

    for d in range(depth):
        for t in range(2):
            swap_v[d, t] = grad_rows(d, t, other)
    swap = go(swap_v, pq_v.at[share], partner)
    for d in range(depth):
        for t in range(2):
            pq_v[share, d, t] = grad_rows(d, t, share)
    s1.wait_recv()
    s1.wait_send()
    small_v[...] += small_got[1]
    s2 = go(small_v, small_got.at[2], across)
    swap.wait_recv()
    keep_v = lambda h, t: pq_v[h, :, t]
    q1 = go(pq_v.at[far_half, :, far_turn], yl_v.at[0], beside)
    q2 = go(pq_v.at[half, :, far_turn], yl_v.at[1], beside)
    y_subs += [
        go(fin_v.at[1, rows(j)], land_v.at[0, rows(j)], beside) for j in range(SUBS // 2, SUBS)
    ]
    s2.wait_recv()
    s2.wait_send()
    small_v[...] += small_got[2]
    s3 = [go(small_v, small_got.at[3 + k], device) for k, device in enumerate(deeps)]
    relays = []

    def relay(j):
        y_subs[j].wait_recv()
        relays.append(go(land_v.at[0, rows(j)], land_v.at[2, rows(j)], across))

    for j in range(SUBS // 2):
        relay(j)
    q1.wait_recv()
    xs_v[...] = (keep_v(far_half, turn).astype(f32) + yl_v[0].astype(f32)).astype(bf16)
    qx = go(xs_v, xl_v, across)

    for copy in z_f:
        copy.wait_recv()
    ranks = range(depth - 1)
    spread = lambda ref, got: sum([got[k].astype(f32) for k in ranks], ref[deep].astype(f32))
    corner.wait_recv()
    ff_v[turn, share] = (spread(tot_v, zf_v) + corner_in[...].astype(f32)).astype(bf16)

    def gather_first(ref):
        piece = ref.at[turn, share]
        return go(piece, piece, beside), go(piece, piece, partner)

    def gather_next(ref, first):
        first.wait_recv()
        piece = ref.at[far_turn, share]
        return go(piece, piece, partner)

    f_first = gather_first(ff_v)
    q2.wait_recv()
    for j in range(SUBS // 2, SUBS):
        relay(j)
    qx.wait_recv()
    rs_v[...] = (
        keep_v(half, turn).astype(f32) + yl_v[1].astype(f32) + xl_v[...].astype(f32)
    ).astype(bf16)
    z_q = [
        go(rs_v.at[(deep + k + 1) % depth], zq_v.at[k], device) for k, device in enumerate(deeps)
    ]
    for copy in s3:
        copy.wait_recv()
    small_out[...] = small_v[...] + sum([small_got[4 + k] for k in range(depth - 2)], small_got[3])
    f_next = gather_next(ff_v, f_first[0])
    for copy in z_q:
        copy.wait_recv()
    qf_v[turn, share] = spread(rs_v, zq_v).astype(bf16)
    q_first = gather_first(qf_v)
    put(land_v.at[0], half, far_turn)
    for copy in x_subs:
        copy.wait_recv()
    put(land_v.at[1], far_half, turn)
    f_first[1].wait_recv()
    f_next.wait_recv()
    ends = start_copies([(ff_v, f_out)], in_sem)
    q_next = gather_next(qf_v, q_first[0])
    for copy in relays:
        copy.wait_recv()
    put(land_v.at[2], far_half, far_turn)
    q_first[1].wait_recv()
    q_next.wait_recv()
    last = pltpu.make_async_copy(qf_v, qkv_out, in_sem.at[2])
    last.start()
    wait_copies(ends + [last] + outs)
    waited = [s0, s1, s2]
    for copy in started:
        if not any(copy is w for w in waited):
            copy.wait_send()


def settle(hidden_in, x_in, dqkv, w_qkv, g_first, sums, parts, corners):
    rows, width = g_first.shape
    span = hidden_in.shape[1]
    depth, tall, cols = parts[0].shape
    wide = dqkv.shape[1]
    slim = width // depth // 4
    f32, bf16, shape = jnp.float32, jnp.bfloat16, jax.ShapeDtypeStruct
    v = pltpu.VMEM
    count = 80
    return pl.pallas_call(
        functools.partial(settle_kernel, depth),
        out_shape=(
            shape((4, span, width), bf16), shape((2, 2, slim, wide), bf16),
            shape((2, 2, tall, cols), bf16), shape((16, width), f32),
        ),
        in_specs=[ANY_SPEC] * 5 + [VMEM_SPEC] * 4 + [ANY_SPEC] * (3 + depth),
        out_specs=(ANY_SPEC,) * 3 + (VMEM_SPEC,),
        scratch_shapes=[
            v((2 * rows, width), bf16), v((2 * rows, wide), bf16), v((width, wide), bf16),
            v((rows, width), f32), v((3, depth, tall, cols), bf16), v((16, width), f32),
            v((2 + depth, 16, width), f32),
            v((2, span, width), bf16), v((2, span, width), bf16), v((2, span, width), bf16),
            v((3, span, width), bf16),
            v((depth, tall, cols), bf16), v((depth - 1, tall, cols), bf16),
            v((2, 2, tall, cols), bf16),
            v((depth, tall, cols), bf16), v((tall, cols), bf16), v((tall, cols), bf16),
            v((width, wide), bf16), v((depth, 2, slim, wide), bf16),
            v((2, depth, 2, slim, wide), bf16), v((2, depth, slim, wide), bf16),
            v((depth, slim, wide), bf16), v((depth, slim, wide), bf16),
            v((depth, slim, wide), bf16), v((depth - 1, slim, wide), bf16),
            v((2, 2, slim, wide), bf16),
            DMA((20,)), DMA((max(4, depth),)), DMA((count,)), DMA((count,)),
        ],
        compiler_params=pltpu.CompilerParams(
            vmem_limit_bytes=63 * 1024 * 1024, collective_id=1, has_side_effects=True
        ),
        cost_estimate=pl.CostEstimate(
            flops=60 * 10**9, bytes_accessed=30 * 10**6, transcendentals=0
        ),
        name="settle",
    )(hidden_in, x_in, dqkv, w_qkv, g_first, *sums, *parts, *corners)


def finish_kernel(
    grad, qkv, ffn, small,
    grad_home, o_q, o_bq, o_k, o_v, o_bv, o_o, o_bo, o_g1, o_s1, o_up, o_bup, o_down, o_bdown,
    o_g2, o_s2, o_rms,
    grad_in, grad_out, in_sem, out_sem,
):
    f32 = jnp.float32
    seqs, span, width = grad.shape
    half = my_spot()[0]
    thin = o_q.shape[0]
    cols = o_q.shape[1]
    loads = start_copies([(grad.at[i], grad_in.at[i]) for i in range(seqs)], in_sem)
    stores = []
    for i in range(seqs):
        loads[i].wait()
        grad_out[i] = grad_in[i].astype(f32)
        stores.append(pltpu.make_async_copy(grad_out.at[i], grad_home.at[i], out_sem.at[i]))
        stores[i].start()
    for i, ref in enumerate((o_q, o_k, o_v)):
        ref[...] = qkv[:, i * cols : (i + 1) * cols].astype(f32)
    slim = ffn.shape[1] - 2 * thin
    for p in range(4):
        at = slice(p * cols, (p + 1) * cols)
        o_up[:, at] = ffn[p, :thin, :].astype(f32)
        o_down[:, at] = ffn[p, thin : 2 * thin, :].astype(f32)
        o_o[p * slim : (p + 1) * slim, :] = ffn[p, 2 * thin :, :].astype(f32)
    flat = lambda row: row.reshape(row.shape[1])
    up = [small[pl.ds(half * 2 + i, 1), :] for i in range(2)]
    o_bup[...] = flat(jnp.concatenate(up, 1))
    for i, ref in enumerate((o_bo, o_g1, o_s1, o_bdown, o_g2, o_s2)):
        ref[...] = flat(small[4 + i : 5 + i, :])
    own = pl.ds(pl.multiple_of(half * cols, PAIR), cols)
    o_bq[...] = flat(small[11:12, own])
    o_bv[...] = flat(small[12:13, own])
    stats = small[10:11, :]
    o_rms[...] = jnp.sqrt(stats / (jnp.maximum(stats[:, 5:6], 1.0) * width))[:, :PAIR]
    wait_copies(stores)


def finish_all(grad, qkv, ffn, small):
    seqs, span, width = grad.shape
    thin, cols = qkv.shape[0], qkv.shape[1] // 3
    f32 = jnp.float32
    shape = lambda *s: jax.ShapeDtypeStruct(s, f32)
    outs = pl.pallas_call(
        finish_kernel,
        out_shape=(
            shape(seqs, span, width),
            shape(thin, cols), shape(cols), shape(thin, cols),
            shape(thin, cols), shape(cols), shape(thin, cols), shape(width), shape(width),
            shape(width), shape(thin, 4 * cols), shape(4 * cols), shape(thin, 4 * cols),
            shape(width), shape(width), shape(width), shape(1, PAIR),
        ),
        in_specs=[ANY_SPEC] + [VMEM_SPEC] * 3,
        out_specs=(ANY_SPEC,) + (VMEM_SPEC,) * 16,
        scratch_shapes=[
            pltpu.VMEM((seqs, span, width), grad.dtype), pltpu.VMEM((seqs, span, width), f32),
            DMA((seqs,)), DMA((seqs,)),
        ],
        compiler_params=WIDE_ROOM,
        name="finish_all",
    )(grad, qkv, ffn, small)
    outs = list(outs)
    outs[6], outs[12] = outs[6].T, outs[12].T
    return (*outs[:-1], outs[-1][0, :5])


def layer_norm(values, norm_gain, norm_shift):
    row_mean = jnp.mean(values, -1, keepdims=True)
    centered = values - row_mean
    row_var = jnp.mean(centered * centered, -1, keepdims=True)
    return centered * lax.rsqrt(row_var + EPSILON) * norm_gain + norm_shift


def gelu_tanh(values):
    return jax.nn.gelu(values, approximate=True)


def block_tables(random_seq, all_blocks, place):
    block = jnp.arange(2, all_blocks, dtype=jnp.int32)
    last = all_blocks - 1
    zero = jnp.zeros_like(block)
    true_ids = jnp.stack(
        [block, block - 1, block, jnp.minimum(block + 1, last), zero, zero + 1], -1
    )
    true_ids = jnp.concatenate([true_ids, random_seq[2:]], -1)
    flags = jnp.stack([block >= 3, block <= last - 1], -1).astype(jnp.int32)
    return (
        jnp.concatenate([place(true_ids), flags], -1).astype(jnp.int32),
        place(jnp.arange(2, dtype=jnp.int32)),
    )


def local(
    hidden_in, out_grad, segment_ids, token_valid, random_blocks,
    query_weight, query_bias, key_weight, value_weight, value_bias,
    output_weight, output_bias, norm1_gain, norm1_shift,
    up_weight, up_bias, down_weight, down_bias, norm2_gain, norm2_shift,
):
    f32, bf16 = jnp.float32, jnp.bfloat16
    seqs, span, width = hidden_in.shape
    length = segment_ids.shape[1]
    places = length // span
    halves = lax.axis_size("tensor")
    depth = lax.axis_size("dp")
    turns = seqs // halves
    shares = places // turns
    my_half = lax.axis_index("tensor")
    my_place = lax.axis_index("context")
    my_depth = lax.axis_index("dp")
    my_turn, my_share = my_place // shares, my_place % shares
    my_seq = my_half * turns + my_turn
    blocks = length // BLK
    rows = turns * span
    spots = [(h, t) for h in range(halves) for t in range(turns)]

    def send(value, half=0, turn=0, share=0):
        if half % halves == 0 and turn % turns == 0 and share % shares == 0:
            return value
        pairs = []
        for h in range(halves):
            for t in range(turns):
                for s in range(shares):
                    to_place = (t + turn) % turns * shares + (s + share) % shares
                    pairs.append(
                        ((t * shares + s) * halves + h, to_place * halves + (h + half) % halves)
                    )
        return lax.ppermute(value, ("context", "tensor"), pairs)

    def send_deep(value, step):
        return lax.ppermute(value, "dp", [(i, (i + step) % depth) for i in range(depth)])

    def pick(value, index, axis=0):
        return lax.dynamic_index_in_dim(value, index, axis, keepdims=False)

    def own_slice(value, count, which, axis):
        size = value.shape[axis] // count
        return lax.dynamic_slice_in_dim(value, which * size, size, axis)

    def gather_deep(value):
        if depth > 4:
            return lax.all_gather(value, "dp", axis=0)
        got = [value] + [send_deep(value, k) for k in range(1, depth)]
        ring = jnp.stack([got[depth - 1 - i % depth] for i in range(2 * depth - 1)])
        return lax.dynamic_slice_in_dim(ring, depth - 1 - my_depth, depth, 0)

    def reduce_deep(value):
        if depth > 4:
            return lax.psum_scatter(value, "dp", scatter_dimension=0)
        total = pick(value, my_depth).astype(f32)
        for k in range(1, depth):
            total = total + send_deep(pick(value, (my_depth + k) % depth), k).astype(f32)
        return total.astype(bf16)

    def gather_square(value):
        near = {spot: send(value, *spot) for spot in spots}
        near = jnp.stack([near[spot] for spot in spots])
        return [near] + [send(near, 0, 0, s) for s in range(1, shares)]

    def reduce_square(value):
        total = value[0].astype(f32)
        for i, (h, t) in enumerate(spots[1:], 1):
            total = total + send(value[i], -h, -t).astype(f32)
        return total.astype(bf16)

    def gather_places(value):
        near = [send(value, 0, t) for t in range(turns)]
        near = jnp.stack(near)
        far = jnp.stack([near] + [send(near, 0, 0, s) for s in range(1, shares)])
        return jnp.stack(
            [
                pick(pick(far, (my_share - s) % shares), (my_turn - t) % turns)
                for t in range(turns)
                for s in range(shares)
            ]
        )

    def sum_all(value):
        for step in range(halves.bit_length() - 1):
            value = value + send(value, 1 << step)
        size = 1
        while size < places:
            value = value + lax.ppermute(value, "context", [(i, i ^ size) for i in range(places)])
            size *= 2
        size = 1
        while size < depth:
            value = value + lax.ppermute(value, "dp", [(i, i ^ size) for i in range(depth)])
            size *= 2
        return value

    def bring(value):
        return jnp.concatenate(
            [
                send(pick(value, my_half * turns + (my_turn + k) % turns), 0, k)
                for k in range(turns)
            ],
            0,
        )

    def deliver(value):
        value = value.reshape(turns, span, width)
        got = jnp.stack([send(value[t], h, -t) for h, t in spots])
        return jnp.stack(
            [
                pick(got, (my_half - h) % halves * turns + (t - my_turn) % turns)
                for h in range(halves)
                for t in range(turns)
            ]
        )

    def after(value, *earlier):
        return lax.optimization_barrier((value, *earlier))[0]

    per = span // BLK

    def place(block_ids):
        chunk = block_ids // per
        turn, share = chunk // shares, chunk % shares
        spot = ((my_share - share) % shares) * turns + (my_turn - turn) % turns
        return spot * per + block_ids % per

    def in_order(row):
        return jnp.concatenate(
            [
                lax.dynamic_slice_in_dim(
                    row,
                    (((my_turn - k) % turns) * shares + (my_share - s) % shares) * span,
                    span,
                )
                for s in range(shares)
                for k in range(turns)
            ]
        )

    half_width = query_weight.shape[1]
    thin = query_weight.shape[0]
    slim = thin // places
    hidden = up_weight.shape[1] // places
    biases = jnp.concatenate([query_bias, value_bias, up_bias])

    def split_biases(by_half):
        by_half = jnp.stack([pick(by_half, (my_half - h) % halves) for h in range(halves)])
        return (
            by_half[:, at : at + b.shape[0]].reshape(-1)
            for b, at in ((query_bias, 0), (value_bias, half_width), (up_bias, 2 * half_width))
        )

    def spread(value, which, count):
        return lax.dynamic_update_slice_in_dim(
            jnp.zeros((value.shape[0] * count,), value.dtype), value, which * value.shape[0], 0
        )

    def small_rows(up_sums, group_at, norm_sums, stats):
        up_natural = jnp.zeros_like(up_sums)
        for i, at in enumerate(group_at):
            up_natural = lax.dynamic_update_slice_in_dim(
                up_natural, up_sums[i * hidden : (i + 1) * hidden], at * hidden, 0
            )
        stats = jnp.pad(stats, (0, width - stats.shape[0]))
        return jnp.concatenate(
            [up_natural.reshape(-1, width), *(row[None] for row in norm_sums), stats[None]], 0
        )

    def finish(layer_out, input_grad, qkv_shard, up_part, down_part, out_part, small):
        deep = up_weight.shape[1] * halves // width
        s_up, (s_o, s_g1, s_s1, s_down, s_g2, s_s2, stats, s_q, s_v) = (
            small[:deep].reshape(-1), small[deep : deep + 9]
        )
        s_q, s_v, s_up = (own_slice(value, halves, my_half, 0) for value in (s_q, s_v, s_up))
        input_rms = jnp.sqrt(stats[:5] / (jnp.maximum(stats[5], 1.0) * width))
        join = lambda w: jnp.moveaxis(w, 0, 1).reshape(thin, -1).astype(f32)
        shard_o = out_part.reshape(thin, -1)[:, :half_width].astype(f32).T
        shard_q, shard_k, shard_v = (qkv_shard[:, i].astype(f32) for i in range(3))
        return (
            layer_out, input_grad, shard_q, s_q, shard_k, shard_v, s_v, shard_o, s_o,
            s_g1, s_s1, join(up_part), s_up, join(down_part).T, s_down, s_g2, s_s2, input_rms,
        )

    if (turns, shares, halves) == (2, 2, 2) and depth <= 4 and rows % TILE == 0:
        near_b = [query_bias, value_bias, up_bias]
        x_in, q_all, f_deep, n1, n2, *far_b = fetch(
            hidden_in,
            [query_weight, key_weight, value_weight, up_weight, down_weight.T, output_weight.T],
            near_b, depth,
        )
        random = place(pick(random_blocks, my_seq)).reshape(-1)
        (
            att0, att1, q, k, v, lse, w_qkv, groups, key_code, query_code
        ) = project_attend(
            random, hidden_in, x_in, q_all, f_deep, n1, n2, segment_ids, token_valid,
            near_b[0], near_b[1], far_b[0], far_b[1],
        )
        vectors = [output_bias, norm1_gain, norm1_shift, down_bias, norm2_gain, norm2_shift]
        out0, out1, slope, g_second, unit, norm_t, downs, inverse, front_sums = ffn_front(
            att0, att1, hidden_in, x_in, out_grad, groups,
            key_code.reshape(length, PAIR), vectors, near_b[2], far_b[2],
        )
        g_first, do_own, do_far, layer_out, kept, turned, crossed, *corners, rear_sums, up_sums = ffn_rear(
            att0, att1, slope, g_second, unit, norm_t, out0, out1, downs, groups, inverse,
            norm1_gain,
        )
        parts = [kept, send(turned, 0, 1), send(crossed, 1)]
        corners = [send_deep(c, i) if i else c for i, c in enumerate(corners)]
        dqkv, layer_out, head_sums = attend_grad(
            random, do_own, do_far, q, k, v, layer_out, key_code, query_code, lse
        )
        dqkv, head_sums, parts, corners = lax.optimization_barrier(
            (dqkv, head_sums, parts, corners)
        )
        input_grad, qkv_shard, ffn_shard, small = settle(
            hidden_in, x_in, dqkv, w_qkv, g_first, (front_sums, rear_sums, up_sums, head_sums), parts,
            corners,
        )
        return (
            layer_out,
            *finish_all(
                input_grad, qkv_shard.reshape(thin, -1),
                ffn_shard.reshape((places,) + ffn_shard.shape[2:]), small,
            ),
        )

    seg = in_order(pick(segment_ids, my_seq))
    live = in_order(pick(token_valid, my_seq))
    random_seq = pick(random_blocks, my_seq)
    table, wide = block_tables(random_seq, blocks, place)
    key_code = jnp.broadcast_to(jnp.where(live == 1, seg, -1)[:, None], (length, PAIR))
    query_code = jnp.tile(seg.reshape(blocks, BLK), (1, PAIR // BLK))
    part = width // shares
    padded = -(-part // PAIR) * PAIR
    x_own = bring(hidden_in)
    qkv_piece = own_slice(
        jnp.concatenate([query_weight, key_weight, value_weight], 1), places, my_place, 0
    )
    qkv_all = jnp.stack(gather_square(gather_deep(qkv_piece)))
    per_half = shares // halves
    target = my_share // per_half
    qkv_all = jnp.stack(
        [
            pick(
                pick(qkv_all, (my_share - s) % shares),
                (my_half - target) % halves * turns + (my_turn - t) % turns,
            )
            for t in range(turns)
            for s in range(shares)
        ],
        1,
    ).reshape(width, 3, half_width)
    pad_cols = lambda w: jnp.pad(w, [(0, 0)] * (w.ndim - 1) + [(0, padded - part)])
    mine = lambda w: pad_cols(own_slice(w, per_half, my_share % per_half, w.ndim - 1))
    w_qkv = mine(qkv_all).reshape(width, 3 * padded)
    b_q, b_v, b_up = split_biases(jnp.stack([send(biases, h) for h in range(halves)]))
    mine_b = lambda b: pad_cols(own_slice(b, shares, my_share, 0))
    b_qkv = jnp.concatenate([mine_b(b_q), jnp.zeros((padded,), bf16), mine_b(b_v)]).astype(f32)

    ffn_piece = jnp.concatenate(
        [
            own_slice(up_weight, places, my_place, 1),
            own_slice(down_weight, places, my_place, 0).T,
            jnp.pad(
                own_slice(output_weight.T, places, my_place, 0),
                [(0, 0), (0, max(0, hidden - half_width))],
            ).reshape(-1, hidden),
        ],
        0,
    )
    ffn_all = gather_square(gather_deep(ffn_piece))
    groups = [
        (s, i, ffn_all[s][i]) for s in range(shares) for i in range(len(spots))
    ]
    w_up = jnp.concatenate([g[:, :thin].reshape(width, hidden) for _, _, g in groups], 1)
    w_down_t = jnp.concatenate(
        [g[:, thin : 2 * thin].reshape(width, hidden) for _, _, g in groups], 1
    )
    out_all = jnp.stack(
        [jnp.stack([g[:, 2 * thin :] for g in ffn_all[s]]) for s in range(shares)]
    )
    w_out_t = jnp.stack(
        [
            jnp.stack(
                [
                    pick(
                        pick(out_all, (my_share - s) % shares),
                        (my_half - h) % halves * turns + (my_turn - t) % turns,
                    )
                    for t in range(turns)
                    for s in range(shares)
                ],
                1,
            ).reshape(width, half_width)
            for h in range(halves)
        ],
        1,
    ).reshape(width, width)
    w_out_t = jnp.concatenate(
        [own_slice(w_out_t, shares, (my_share + k) % shares, 1) for k in range(shares)], 1
    )
    group_at = [
        ((my_half - spots[i][0]) % halves * places
         + (my_turn - spots[i][1]) % turns * shares + (my_share - s) % shares)
        for s, i, _ in groups
    ]
    b_up = jnp.concatenate(
        [lax.dynamic_slice_in_dim(b_up, at * hidden, hidden) for at in group_at]
    ).astype(f32)

    g_out = bring(out_grad).astype(f32)
    x_seq = jnp.concatenate([send(x_own, 0, 0, k) for k in range(shares)], 0)
    q, k, v = (
        (
            jnp.dot(x_seq, w_qkv[:, i * padded : (i + 1) * padded], preferred_element_type=f32)
            + b_qkv[i * padded : (i + 1) * padded]
        ).astype(bf16)
        for i in range(3)
    )
    att, lse = attend(table, wide, q, k, v, key_code, query_code)
    att = att[:, :part].reshape(shares, rows, part)
    att_own = jnp.concatenate([send(att[s], 0, 0, -s) for s in range(shares)], 1)
    attn_out = lax.dot_general(
        att_own, w_out_t, (((1,), (1,)), ((), ())), preferred_element_type=f32
    ) + output_bias.astype(f32)
    x_full = x_own.astype(f32)
    first_sum = x_full + attn_out
    gain_one, shift_one = norm1_gain.astype(f32), norm1_shift.astype(f32)
    normed = layer_norm(first_sum, gain_one, shift_one)
    normed_low = normed.astype(bf16)
    pre_act = jnp.dot(normed_low, w_up, preferred_element_type=f32) + b_up
    act_low = gelu_tanh(pre_act).astype(bf16)
    ffn_out = lax.dot_general(
        act_low, w_down_t, (((1,), (1,)), ((), ())), preferred_element_type=f32
    ) + down_bias.astype(f32)
    second_sum = normed + ffn_out
    gain_two, shift_two = norm2_gain.astype(f32), norm2_shift.astype(f32)
    layer_out, norm_back = jax.vjp(layer_norm, second_sum, gain_two, shift_two)
    g_second, gain_two_grad, shift_two_grad = norm_back(g_out)
    layer_out = deliver(layer_out.astype(bf16))
    g_ffn = g_second.astype(bf16)
    g_act = jnp.dot(g_ffn, w_down_t, preferred_element_type=f32)
    g_pre = jax.vjp(gelu_tanh, pre_act)[1](g_act)[0].astype(bf16)
    up_part = jnp.dot(normed_low.T, g_pre, preferred_element_type=f32).astype(bf16)
    down_part_t = jnp.dot(g_ffn.T, act_low, preferred_element_type=f32).astype(bf16)
    g_normed = g_second + jnp.dot(g_pre, w_up.T, preferred_element_type=f32)
    g_first, gain_one_grad, shift_one_grad = jax.vjp(layer_norm, first_sum, gain_one, shift_one)[1](
        g_normed
    )
    g_attn = g_first.astype(bf16)
    out_part_t = jnp.dot(g_attn.T, att_own, preferred_element_type=f32).astype(bf16)
    g_att = jnp.dot(g_attn, w_out_t, preferred_element_type=f32).astype(bf16)
    do = jnp.concatenate(
        [send(own_slice(g_att, shares, s, 1), 0, 0, s) for s in range(shares)], 0
    )
    dq, dk, dv = attend_back(table, wide, q, k, v, pad_cols(do), key_code, query_code, lse)

    out_natural = jnp.concatenate(
        [own_slice(out_part_t, shares, (s - my_share) % shares, 1) for s in range(shares)], 1
    ).reshape(depth, turns, shares, slim, halves, half_width)

    def ffn_group(s, i):
        h, t = spots[i]
        at = (s * len(spots) + i) * hidden
        out = pick(out_natural, (my_half - h) % halves, 4)
        out = pick(pick(out, (my_turn - t) % turns, 1), (my_share - s) % shares, 1)
        out = jnp.pad(out, [(0, 0), (0, 0), (0, max(0, hidden - half_width))])
        cut = lambda w: w[:, at : at + hidden].reshape(depth, thin, hidden)
        return jnp.concatenate(
            [cut(up_part), cut(down_part_t), out.reshape(depth, -1, hidden)], 1
        )

    ffn_grads = [
        jnp.stack([ffn_group(s, i) for i in range(len(spots))]) for s in range(shares)
    ]
    total = ffn_grads[0].astype(f32)
    for s in range(1, shares):
        total = total + send(ffn_grads[s], 0, 0, -s).astype(f32)
    ffn_shard = gather_places(reduce_deep(reduce_square(total.astype(bf16))))
    dqkv = jnp.concatenate([dq, dk, dv], 1)
    qkv_part = (
        jnp.dot(x_seq.T, dqkv, preferred_element_type=f32)
        .astype(bf16)
        .reshape(depth, turns, shares, slim, 3, padded)[..., :part]
    )
    got = jnp.stack(
        [send(pick(qkv_part, (my_share + s) % shares, 2), 0, 0, s) for s in range(shares)]
    )
    got = jnp.stack([pick(got, (my_share - s) % shares) for s in range(shares)], 4)
    got = got.reshape(depth, turns, slim, 3, halves, half_width)
    square = jnp.stack(
        [
            pick(pick(got, (my_half - h) % halves, 4), (my_turn - t) % turns, 1)
            for h, t in spots
        ]
    ).reshape(len(spots), depth, slim, 3 * half_width)
    qkv_shard = gather_places(reduce_deep(reduce_square(square))).reshape(thin, 3, half_width)
    back = jnp.dot(dqkv, w_qkv.T, preferred_element_type=f32).reshape(shares, rows, width)
    back_own = back[0]
    for s in range(1, shares):
        back_own = back_own + send(back[s].astype(bf16), 0, 0, -s).astype(f32)
    input_grad = deliver((g_first + back_own).astype(bf16)).astype(f32)

    sums = lambda value: jnp.sum(value.astype(f32), 0)
    valid = live[:rows].astype(f32)
    squares = lambda member: jnp.sum(valid * jnp.sum(member * member, -1))
    stats = jnp.stack(
        [squares(m) for m in (x_full, first_sum, second_sum, attn_out, ffn_out)]
        + [jnp.sum(valid), 0.0, 0.0]
    )
    up_sums = sums(g_pre)
    norm_sums = [
        sums(g_attn), gain_one_grad, shift_one_grad, sums(g_ffn), gain_two_grad, shift_two_grad
    ]
    small = small_rows(up_sums, group_at, norm_sums, stats)
    heads = [spread(sums(d)[:part], my_share, shares)[None] for d in (dq, dv)]
    small = sum_all(jnp.concatenate([small, *heads], 0))
    return finish(
        layer_out, input_grad, qkv_shard, ffn_shard[:, :thin], ffn_shard[:, thin : 2 * thin],
        ffn_shard[:, 2 * thin :], small,
    )


def solution(mesh):
    rows, plain = P("dp", "context", None), P()
    columns, across, halves = P("dp", "tensor"), P("tensor", "dp"), P("tensor")
    return jax.shard_map(
        local,
        mesh=mesh,
        in_specs=(
            rows, rows, P("dp", None), P("dp", None), P("dp", None, None),
            columns, halves, columns, columns, halves, across, plain, plain, plain,
            columns, halves, across, plain, plain, plain,
        ),
        out_specs=(
            rows, rows, columns, halves, columns, columns, halves, across, plain,
            plain, plain, columns, halves, across, plain, plain, plain, plain,
        ),
        check_vma=False,
    )
```

```python
import functools

import jax
import jax.numpy as jnp
from jax import lax
from jax.experimental import pallas as pl
from jax.experimental.pallas import tpu as pltpu
from jax.sharding import PartitionSpec as P

HD = 64
BLK = 64
PAIR = 128
SLOTS = 8
WIDE = 512
SCALE = HD ** (-0.5)
EPSILON = 1e-06


NEG_FILL = -1e30
LEAP = 3
BACK_LEAP = 3


def pair_rows(block, left, scale=None):
    if scale is not None:
        block = block * jnp.asarray(scale, block.dtype)
    zero = jnp.zeros_like(block)
    return jnp.concatenate([jnp.where(left, block, zero), jnp.where(left, zero, block)], 0)


def lane_left(rows):
    return lax.broadcasted_iota(jnp.int32, (rows, PAIR), 1) < HD


def eye_pair():
    lanes = lax.broadcasted_iota(jnp.int32, (BLK, PAIR), 1)
    rows = lax.broadcasted_iota(jnp.int32, (BLK, PAIR), 0)
    return rows == lanes % BLK


def block_rows(index):
    return pl.ds(pl.multiple_of(index * BLK, BLK), BLK)


def slot_bias(slots, first_ok, third_ok, key_code, query_code, own):
    pieces = []
    for slot in range(SLOTS):
        code = query_code
        if slot == 0:
            code = jnp.where(first_ok, query_code, -2)
        if slot == 2:
            code = jnp.where(third_ok, query_code, -2)
        same = key_code[slots[slot]] == code
        if slot == 1:
            same = same | own
        pieces.append(jnp.where(same, 0.0, NEG_FILL))
    return jnp.concatenate(pieces, 0)


def slot_rows(ref, slots, lanes):
    return jnp.concatenate([ref[slot, :, lanes] for slot in slots], 0)


def wide_rows(ref, chunk, lanes):
    count = WIDE // BLK
    return ref[pl.ds(chunk * count, count), :, lanes].reshape(WIDE, PAIR)


def listed(table):
    def find(row):
        slots = [table[row, 1 + slot] for slot in range(SLOTS)]
        return table[row, 0], slots, table[row, 9] == 1, table[row, 10] == 1

    return find


def wide_bias(key_code, query_code, block, chunk):
    same = wide_rows(key_code, chunk, slice(0, PAIR)) == query_code
    key_pos = chunk * WIDE + lax.broadcasted_iota(jnp.int32, (WIDE, PAIR), 0)
    query_pos = block * BLK + lax.broadcasted_iota(jnp.int32, (WIDE, PAIR), 1) % BLK
    return jnp.where(same | (key_pos == query_pos), 0.0, NEG_FILL)


def dot_nt(left, right):
    return lax.dot_general(
        left, right, (((1,), (1,)), ((), ())), preferred_element_type=jnp.float32
    )


def dot_tn(left, right):
    return lax.dot_general(
        left, right, (((0,), (0,)), ((), ())), preferred_element_type=jnp.float32
    )


def dot_nn(left, right):
    return jnp.dot(left, right, preferred_element_type=jnp.float32)


def attend_kernel(table, wide, *refs):
    attend_blocks(listed(table), [wide[0], wide[1]], table.shape[0], [], *refs)


def attend_blocks(
    find, wide, count, marks, q_ref, k_ref, v_ref, key_code, query_code, o_ref, lse_ref, acc
):
    length, width = q_ref.shape
    pairs = width // PAIR
    left = lane_left(BLK)
    own = eye_pair()

    def narrow(row, carry):
        block, slots, first_ok, third_ok = find(row)
        rows = block_rows(block)
        code = query_code[pl.ds(block, 1), :]
        bias = slot_bias(slots, first_ok, third_ok, key_code, code, own)
        for pair in range(pairs):
            lanes = slice(pair * PAIR, (pair + 1) * PAIR)
            query = pair_rows(q_ref[rows, lanes], left, SCALE)
            scores = dot_nt(slot_rows(k_ref, slots, lanes), query) + bias
            top = jnp.max(scores, 0, keepdims=True)
            weight = jnp.exp(scores - top)
            total = jnp.sum(weight, 0, keepdims=True)
            probs = (weight * (1.0 / total)).astype(jnp.bfloat16)
            lse_ref[block, pl.ds(pair, 1), :] = top + jnp.log(total)
            both = dot_tn(probs, slot_rows(v_ref, slots, lanes))
            o_ref[rows, lanes] = jnp.where(left, both[:BLK], both[BLK:]).astype(o_ref.dtype)
        return carry

    leap = LEAP if count % LEAP == 0 else 1

    def stride(i, carry):
        for j in range(leap):
            narrow(i * leap + j, 0)
        for mark, action in marks:

            @pl.when(i == mark)
            def _():
                action()

        return carry

    lax.fori_loop(0, count // leap, stride, 0)

    def wide_step(which, nothing):
        block = wide[0] + which * (wide[1] - wide[0])
        rows = block_rows(block)
        code = query_code[pl.ds(block, 1), :]

        def first(chunk, carry):
            bias = wide_bias(key_code, code, block, chunk)
            out = []
            for pair in range(pairs):
                lanes = slice(pair * PAIR, (pair + 1) * PAIR)
                query = pair_rows(q_ref[rows, lanes], left, SCALE)
                scores = dot_nt(wide_rows(k_ref, chunk, lanes), query) + bias
                top_old, total_old = carry[pair]
                top = jnp.maximum(top_old, jnp.max(scores, 0, keepdims=True))
                total = total_old * jnp.exp(top_old - top) + jnp.sum(
                    jnp.exp(scores - top), 0, keepdims=True
                )
                out.append((top, total))
            return tuple(out)

        start = (jnp.full((1, PAIR), NEG_FILL), jnp.zeros((1, PAIR), jnp.float32))
        ends = lax.fori_loop(0, length // WIDE, first, (start,) * pairs, unroll=2)
        for pair in range(pairs):
            lse_ref[block, pl.ds(pair, 1), :] = ends[pair][0] + jnp.log(ends[pair][1])
        acc[...] = jnp.zeros_like(acc)

        def second(chunk, carry):
            bias = wide_bias(key_code, code, block, chunk)
            for pair in range(pairs):
                lanes = slice(pair * PAIR, (pair + 1) * PAIR)
                query = pair_rows(q_ref[rows, lanes], left, SCALE)
                scores = dot_nt(wide_rows(k_ref, chunk, lanes), query) + bias
                probs = jnp.exp(scores - lse_ref[block, pl.ds(pair, 1), :]).astype(jnp.bfloat16)
                acc[pair] += dot_tn(probs, wide_rows(v_ref, chunk, lanes))
            return carry

        lax.fori_loop(0, length // WIDE, second, 0, unroll=2)
        for pair in range(pairs):
            lanes = slice(pair * PAIR, (pair + 1) * PAIR)
            both = acc[pair]
            o_ref[rows, lanes] = jnp.where(left, both[:BLK], both[BLK:]).astype(o_ref.dtype)
        return nothing

    lax.fori_loop(0, 2, wide_step, 0)


def attend_back_kernel(table, wide, *refs):
    attend_back_blocks(listed(table), [wide[0], wide[1]], table.shape[0], *refs)


def attend_back_blocks(
    find, wide, count, q_ref, k_ref, v_ref, do_ref, key_code, query_code, lse_ref,
    dq_ref, dk_ref, dv_ref, dk_sum, dv_sum, dq_acc,
):
    length, width = q_ref.shape
    pairs = width // PAIR
    left = lane_left(BLK)
    own = eye_pair()
    dk_sum[...] = jnp.zeros_like(dk_sum)
    dv_sum[...] = jnp.zeros_like(dv_sum)

    def narrow(row, carry):
        block, slots, first_ok, third_ok = find(row)
        rows = block_rows(block)
        code = query_code[pl.ds(block, 1), :]
        bias = slot_bias(slots, first_ok, third_ok, key_code, code, own)
        for pair in range(pairs):
            lanes = slice(pair * PAIR, (pair + 1) * PAIR)
            query = pair_rows(q_ref[rows, lanes], left, SCALE)
            grad = pair_rows(do_ref[rows, lanes], left)
            keys = slot_rows(k_ref, slots, lanes)
            values = slot_rows(v_ref, slots, lanes)
            scores = dot_nt(keys, query) + bias
            probs = jnp.exp(scores - lse_ref[block, pl.ds(pair, 1), :])
            g_probs = dot_nt(values, grad)
            terms = probs * g_probs
            g_scores = (terms - probs * jnp.sum(terms, 0, keepdims=True)).astype(jnp.bfloat16)
            dv = dot_nn(probs.astype(jnp.bfloat16), grad)
            dk = dot_nn(g_scores, query)
            both = dot_tn(g_scores, keys)
            dq_ref[rows, lanes] = (jnp.where(left, both[:BLK], both[BLK:]) * SCALE).astype(
                dq_ref.dtype
            )
            for slot in range(SLOTS):
                spot = block_rows(slots[slot])
                part = slice(slot * BLK, (slot + 1) * BLK)
                dk_sum[spot, lanes] += dk[part]
                dv_sum[spot, lanes] += dv[part]
        return carry

    lax.fori_loop(0, count, narrow, 0, unroll=BACK_LEAP if count % BACK_LEAP == 0 else 1)

    def wide_step(which, nothing):
        block = wide[0] + which * (wide[1] - wide[0])
        rows = block_rows(block)
        code = query_code[pl.ds(block, 1), :]

        def pieces(chunk, pair, bias):
            keys_at = pl.ds(pl.multiple_of(chunk * WIDE, WIDE), WIDE)
            lanes = slice(pair * PAIR, (pair + 1) * PAIR)
            query = pair_rows(q_ref[rows, lanes], left, SCALE)
            grad = pair_rows(do_ref[rows, lanes], left)
            keys = wide_rows(k_ref, chunk, lanes)
            scores = dot_nt(keys, query) + bias
            probs = jnp.exp(scores - lse_ref[block, pl.ds(pair, 1), :])
            return keys_at, lanes, query, grad, keys, probs, probs * dot_nt(wide_rows(v_ref, chunk, lanes), grad)

        def first(chunk, carry):
            bias = wide_bias(key_code, code, block, chunk)
            return tuple(
                carry[pair] + jnp.sum(pieces(chunk, pair, bias)[-1], 0, keepdims=True)
                for pair in range(pairs)
            )

        deltas = lax.fori_loop(
            0, length // WIDE, first, (jnp.zeros((1, PAIR), jnp.float32),) * pairs, unroll=2
        )
        dq_acc[...] = jnp.zeros_like(dq_acc)

        def second(chunk, carry):
            bias = wide_bias(key_code, code, block, chunk)
            for pair in range(pairs):
                keys_at, lanes, query, grad, keys, probs, terms = pieces(chunk, pair, bias)
                g_scores = (terms - probs * carry[pair]).astype(jnp.bfloat16)
                dv_sum[keys_at, lanes] += dot_nn(probs.astype(jnp.bfloat16), grad)
                dk_sum[keys_at, lanes] += dot_nn(g_scores, query)
                dq_acc[pair] += dot_tn(g_scores, keys)
            return carry

        lax.fori_loop(0, length // WIDE, second, deltas, unroll=2)
        for pair in range(pairs):
            lanes = slice(pair * PAIR, (pair + 1) * PAIR)
            both = dq_acc[pair]
            dq_ref[rows, lanes] = (jnp.where(left, both[:BLK], both[BLK:]) * SCALE).astype(
                dq_ref.dtype
            )
        return nothing

    lax.fori_loop(0, 2, wide_step, 0)
    dk_ref[...] = dk_sum[...].astype(dk_ref.dtype)
    dv_ref[...] = dv_sum[...].astype(dv_ref.dtype)


def in_blocks(rows):
    return rows.reshape(-1, BLK, rows.shape[-1])


VMEM_SPEC = pl.BlockSpec(memory_space=pltpu.VMEM)
SMEM_SPEC = pl.BlockSpec(memory_space=pltpu.SMEM)
ROOM = pltpu.CompilerParams(vmem_limit_bytes=60 * 1024 * 1024)


def attend(table, wide, q, k, v, key_code, query_code):
    length, width = q.shape
    return pl.pallas_call(
        attend_kernel,
        out_shape=(
            jax.ShapeDtypeStruct((length, width), jnp.bfloat16),
            jax.ShapeDtypeStruct((length // BLK, 8, PAIR), jnp.float32),
        ),
        in_specs=[SMEM_SPEC] * 2 + [VMEM_SPEC] * 5,
        out_specs=(VMEM_SPEC, VMEM_SPEC),
        scratch_shapes=[pltpu.VMEM((width // PAIR, PAIR, PAIR), jnp.float32)],
        compiler_params=ROOM,
        cost_estimate=pl.CostEstimate(
            flops=length * width * 1024 * 60, bytes_accessed=length * width * 8,
            transcendentals=length * width * 8,
        ),
        name="attend",
    )(table, wide, q, in_blocks(k), in_blocks(v), in_blocks(key_code), query_code)


def attend_back(table, wide, q, k, v, do, key_code, query_code, lse):
    length, width = q.shape
    shape = jax.ShapeDtypeStruct((length, width), jnp.bfloat16)
    return pl.pallas_call(
        attend_back_kernel,
        out_shape=(shape, shape, shape),
        in_specs=[SMEM_SPEC] * 2 + [VMEM_SPEC] * 7,
        out_specs=(VMEM_SPEC,) * 3,
        scratch_shapes=[
            pltpu.VMEM((length, width), jnp.float32),
            pltpu.VMEM((length, width), jnp.float32),
            pltpu.VMEM((width // PAIR, PAIR, PAIR), jnp.float32),
        ],
        compiler_params=ROOM,
        cost_estimate=pl.CostEstimate(
            flops=length * width * 1024 * 70, bytes_accessed=length * width * 14,
            transcendentals=length * width * 8,
        ),
        name="attend_back",
    )(table, wide, q, in_blocks(k), in_blocks(v), do, in_blocks(key_code), query_code, lse)


GROUPS = 8
DUOS = GROUPS // 2
TILE = 256
FRONT = 512
ANY_SPEC = pl.BlockSpec(memory_space=pl.ANY)
DMA = pltpu.SemaphoreType.DMA
WIDE_ROOM = pltpu.CompilerParams(vmem_limit_bytes=63 * 1024 * 1024)


def normalize(values):
    row_mean = jnp.mean(values, -1, keepdims=True)
    centered = values - row_mean
    row_var = jnp.mean(centered * centered, -1, keepdims=True)
    inverse = lax.rsqrt(row_var + EPSILON)
    return centered * inverse, inverse


def normalize_back(grad, unit, inverse):
    return inverse * (
        grad
        - jnp.mean(grad, -1, keepdims=True)
        - unit * jnp.mean(grad * unit, -1, keepdims=True)
    )


def gelu_both(u):
    root = 0.7978845608028654
    square = u * u
    inner = jnp.tanh(u * (root + (root * 0.044715) * square))
    half = 0.5 + 0.5 * inner
    slope = half + u * (0.5 - 0.5 * (inner * inner)) * (root + (3.0 * root * 0.044715) * square)
    return u * half, slope


def start_copies(pairs, sem):
    copies = [pltpu.make_async_copy(src, dst, sem.at[i]) for i, (src, dst) in enumerate(pairs)]
    for copy in copies:
        copy.start()
    return copies


def wait_copies(copies):
    for copy in copies:
        copy.wait()


def row_of(ref):
    return ref[...].astype(jnp.float32).reshape(1, ref.shape[0])


def my_spot():
    place = lax.axis_index("context")
    return lax.axis_index("tensor"), place // 2, place % 2


def group_homes():
    half, turn, share = my_spot()
    return [
        ((half + h) % 2, ((turn + t) % 2) * 2 + (share + s) % 2)
        for s in range(2)
        for h in range(2)
        for t in range(2)
    ]


def lanes_of(g, cols):
    return pl.ds((g % 2) * cols, cols)


def place_block(block, per):
    half, turn, share = my_spot()
    chunk = block // per
    spot = ((share + chunk) % 2) * 2 + (turn + chunk // 2) % 2
    return spot * per + block % per


def computed(random, per, blocks):
    def find(row):
        block = row + 2
        ids = [block - 1, block, (block + 1) % blocks]
        slots = [place_block(i, per) for i in ids]
        slots += [place_block(jnp.int32(i), per) for i in range(2)]
        slots += [random[block * 3 + i] for i in range(3)]
        return slots[1], slots, block >= 3, block <= blocks - 2

    return find, [place_block(jnp.int32(i), per) for i in range(2)]


def write_codes(segments, live, key_code, query_code, span):
    half, turn, share = my_spot()
    row = pl.ds(half * 2 + turn, 1)
    left = lax.broadcasted_iota(jnp.int32, (1, PAIR), 1) < HD
    per = span // BLK
    for spot in range(4):
        chunk = ((turn + spot) % 2) * 2 + (share + spot // 2) % 2
        lanes = pl.ds(pl.multiple_of(chunk * span, span), span)
        seg = segments[row, lanes]
        code = jnp.where(live[row, lanes] == 1, seg, -1)
        key_code[pl.ds(spot * per, per)] = jnp.broadcast_to(code, (PAIR, span)).T.reshape(
            per, BLK, PAIR
        )
        for two in range(per // 2):
            both = seg[:, two * PAIR : (two + 1) * PAIR]
            turned = pltpu.roll(both, HD, 1)
            at = spot * per + 2 * two
            query_code[at : at + 1, :] = jnp.where(left, both, turned)
            query_code[at + 1 : at + 2, :] = jnp.where(left, turned, both)


def project_attend_kernel(
    random, hidden, x_in, q_all, f_deep, n1_in, n2_in, segments, live, b_q, b_v, far_q, far_v,
    own_ref, other_home, q_home, k_home, v_home, w_home,
    n1, n2, n3, f0, f1, f2, f3, lse_ref, key_code, query_code,
    x_v, q_v, k_v, v_v, o_v, w_v, acc, in_sem, out_sem, w_sem, send_sem, recv_sem,
):
    span = hidden.shape[1]
    length, width = q_v.shape
    depth = f_deep.shape[0]
    half, turn, share = my_spot()
    across, beside, partner = neighbours()
    weights = start_copies(
        [(q_all.at[share, t, s], w_v.at[:, t, s]) for t in range(2) for s in range(2)], w_sem
    )
    chunks = [hidden.at[half * 2 + turn]] + [x_in.at[i] for i in range(3)]
    loads = start_copies(
        [(x, x_v.at[pl.ds(i * span, span)]) for i, x in enumerate(chunks)], in_sem
    )
    deep = lax.axis_index("dp")
    deeps = [{"dp": (deep + j) % depth} for j in range(1, depth)]
    signal_all([across, beside, partner] + deeps)
    ids = iter(range(send_sem.shape[0]))
    started = []

    def link(src, dst, device):
        i = next(ids)
        started.append(remote(src, dst, send_sem.at[i], recv_sem.at[i], device))
        return started[-1]

    at = [(deep + j) % depth for j in range(depth)]
    rest_of = range(1, depth)
    corner = [link(n2.at[at[j]], n3.at[at[j]], beside) for j in range(depth)]
    to_across = {j: link(f_deep.at[at[j]], n2.at[at[j]], across) for j in rest_of}
    along = {depth - j: link(n1.at[deep], n1.at[deep], deeps[j - 1]) for j in rest_of}
    ends = [
        [link(home.at[at[j]], landing.at[at[j]], partner) for j in range(depth)]
        for home, landing in ((f_deep, f0), (n1, f1), (n2, f2), (n3, f3))
    ]
    swap = link(o_v.at[pl.ds(length // 2, length // 2)], other_home, partner)
    corner[0].start()
    for j in rest_of:
        to_across[j].start()
        along[depth - j].start()
    for copy in ends[0] + [ends[1][0], ends[2][0]]:
        copy.start()

    def from_side(j):
        along[j].wait_recv()
        ends[1][j].start()

    def from_far(j):
        to_across[j].wait_recv()
        ends[2][j].start()
        corner[j].start()

    def from_corner(j):
        corner[j].wait_recv()
        ends[3][j].start()

    steps = [[(from_far, j)] for j in rest_of]
    steps[0].append((from_corner, 0))
    steps += [[(from_side, j) for j in rest_of] + [(from_corner, 1)]]
    steps += [[(from_corner, j)] for j in range(2, depth)]

    def take_step(index):
        for action, j in steps[index]:
            action(j)

    write_codes(segments, live, key_code, query_code, span)
    same = half == share
    bias = jnp.concatenate(
        [
            jnp.where(same, row_of(b_q), row_of(far_q)),
            jnp.zeros((1, width), jnp.float32),
            jnp.where(same, row_of(b_v), row_of(far_v)),
        ],
        1,
    )
    wait_copies(weights)
    wait_copies(loads)
    per = span // BLK

    def project(i, carry):
        at = pl.ds(pl.multiple_of(i * span, span), span)
        w_qkv = w_v[...].reshape(x_v.shape[1], 3 * width)
        value = (dot_nn(x_v[at, :], w_qkv) + bias).astype(jnp.bfloat16)
        q_v[at, :] = value[:, :width]
        k_v[pl.ds(i * per, per)] = value[:, width : 2 * width].reshape(per, BLK, width)
        v_v[pl.ds(i * per, per)] = value[:, 2 * width :].reshape(per, BLK, width)
        return carry

    lax.fori_loop(0, 4, project, 0)
    stores = start_copies([(q_v, q_home), (k_v, k_home), (v_v, v_home), (w_v, w_home)], out_sem)
    blocks = length // BLK
    find, wide = computed(random, span // BLK, blocks)
    count = blocks - 2
    early = min(5, count // LEAP // 2, len(steps))
    marks = [(2 * i + 1, functools.partial(take_step, i)) for i in range(early)]
    attend_blocks(
        find, wide, count, marks, q_v, k_v, v_v, key_code, query_code, o_v, lse_ref, acc
    )
    own_ref[...] = o_v[: length // 2, :]
    swap.start()
    for index in range(early, len(steps)):
        take_step(index)
    for copy in ends[0] + ends[1] + ends[2] + ends[3] + [swap]:
        copy.wait_recv()
    for copy in started:
        copy.wait_send()
    wait_copies(stores)


def project_attend(
    random, hidden, x_in, q_all, f_deep, n1, n2, segments, live, b_q, b_v, far_q, far_v
):
    span, features = hidden.shape[1:]
    length = 4 * span
    depth, slim, cols = q_all.shape[3:]
    width = cols // 3
    bf16, shape = jnp.bfloat16, jax.ShapeDtypeStruct
    piece = shape(f_deep.shape, bf16)
    outs = pl.pallas_call(
        project_attend_kernel,
        out_shape=(shape((length // 2, width), bf16),) * 2
        + (shape((length, width), bf16),)
        + (shape((length // BLK, BLK, width), bf16),) * 2
        + (shape((depth, 2, 2, slim, cols), bf16),)
        + (piece,) * 7
        + (
            shape((length // BLK, 8, PAIR), jnp.float32),
            shape((length // BLK, BLK, PAIR), jnp.int32),
            shape((length // BLK, PAIR), jnp.int32),
        ),
        in_specs=[SMEM_SPEC] + [ANY_SPEC] * 6 + [VMEM_SPEC] * 6,
        out_specs=(VMEM_SPEC,) + (ANY_SPEC,) * 12 + (VMEM_SPEC,) * 3,
        scratch_shapes=[pltpu.VMEM((length, features), bf16)]
        + [pltpu.VMEM((length, width), bf16)]
        + [pltpu.VMEM((length // BLK, BLK, width), bf16)] * 2
        + [pltpu.VMEM((length, width), bf16)]
        + [
            pltpu.VMEM((depth, 2, 2, slim, cols), bf16),
            pltpu.VMEM((width // PAIR, PAIR, PAIR), jnp.float32),
            DMA((4,)), DMA((4,)), DMA((4,)), DMA((8 * depth + 2,)), DMA((8 * depth + 2,)),
        ],
        input_output_aliases={5: 6, 6: 7},
        compiler_params=pltpu.CompilerParams(
            vmem_limit_bytes=63 * 1024 * 1024, collective_id=3, has_side_effects=True
        ),
        cost_estimate=pl.CostEstimate(
            flops=length * width * 1024 * 65, bytes_accessed=length * width * 16,
            transcendentals=length * width * 8,
        ),
        name="project_attend",
    )(
        random, hidden, x_in, q_all, f_deep, n1, n2, segments, live, b_q, b_v, far_q, far_v
    )
    att0, att1, q, k, v, w_qkv, *pieces, lse, key_code, query_code = outs
    w_qkv = w_qkv.reshape(features, cols)
    return att0, att1, q, k, v, lse, w_qkv, [f_deep] + pieces, key_code, query_code


def attend_grad_kernel(
    random, do0, do1, q_in, k_in, v_in, layer, key_code, query_code, lse_ref,
    d_ref, layer_home, sums,
    layer_v, layer_sem, q_v, k_v, v_v, do_v, dk_sum, dv_sum, acc, in_sem,
):
    f32 = jnp.float32
    length, width = q_v.shape
    half_length = length // 2
    loads = start_copies(
        [
            (q_in, q_v), (k_in, k_v), (v_in, v_v),
            (do0, do_v.at[pl.ds(0, half_length)]),
            (do1, do_v.at[pl.ds(half_length, half_length)]),
        ],
        in_sem,
    )
    take = pltpu.make_async_copy(layer, layer_v, layer_sem.at[0])
    put = pltpu.make_async_copy(layer_v, layer_home, layer_sem.at[1])
    take.start()
    wait_copies(loads)
    take.wait()
    put.start()
    parts = [d_ref.at[:, pl.ds(i * width, width)] for i in range(3)]
    blocks = length // BLK
    find, wide = computed(random, blocks // 4, blocks)
    attend_back_blocks(
        find, wide, blocks - 2, q_v, k_v, v_v, do_v, key_code, query_code, lse_ref,
        *parts, dk_sum, dv_sum, acc,
    )
    share = my_spot()[2]
    sums[...] = jnp.zeros_like(sums)
    for s in range(2):

        @pl.when(share == s)
        def _():
            lanes = slice(s * width, (s + 1) * width)
            sums[0:1, lanes] = jnp.sum(d_ref[:, :width].astype(f32), 0, keepdims=True)
            sums[1:2, lanes] = jnp.sum(d_ref[:, 2 * width :].astype(f32), 0, keepdims=True)
    put.wait()


def attend_grad(random, do0, do1, q, k, v, layer, key_code, query_code, lse):
    length, width = q.shape
    f32, bf16, shape = jnp.float32, jnp.bfloat16, jax.ShapeDtypeStruct
    return pl.pallas_call(
        attend_grad_kernel,
        out_shape=(
            shape((length, 3 * width), bf16), shape(layer.shape, bf16), shape((8, 2 * width), f32)
        ),
        in_specs=[SMEM_SPEC] + [ANY_SPEC] * 6 + [VMEM_SPEC] * 3,
        out_specs=(VMEM_SPEC, ANY_SPEC, VMEM_SPEC),
        scratch_shapes=[pltpu.VMEM(layer.shape, bf16), DMA((2,))]
        + [pltpu.VMEM((length, width), bf16)]
        + [pltpu.VMEM((length // BLK, BLK, width), bf16)] * 2
        + [pltpu.VMEM((length, width), bf16)]
        + [pltpu.VMEM((length, width), f32)] * 2
        + [pltpu.VMEM((width // PAIR, PAIR, PAIR), f32), DMA((5,))],
        compiler_params=WIDE_ROOM,
        cost_estimate=pl.CostEstimate(
            flops=length * width * 1024 * 75, bytes_accessed=length * width * 30,
            transcendentals=length * width * 8,
        ),
        name="attend_grad",
    )(random, do0, do1, q, k, v, layer, key_code, query_code, lse)


def load_weights(groups, w_up, w_dn, w_out, up_sem, dn_sem, wo_sem):
    depth, deep, cols = groups[0].shape
    thin = w_up.shape[2]
    slim = deep - 2 * thin
    homes = group_homes()
    out_loads = []
    for g in range(GROUPS):
        half, at = homes[g]
        for d in range(depth):
            spot = pl.ds(pl.multiple_of(d * thin + at * slim, 16), slim)
            out_loads.append(
                pltpu.make_async_copy(
                    groups[g].at[d, pl.ds(2 * thin, slim)], w_out.at[half, spot], wo_sem.at[g, d]
                )
            )
    up_loads = [
        pltpu.make_async_copy(
            groups[g].at[:, pl.ds(0, thin)], w_up.at[g // 2, :, :, lanes_of(g, cols)], up_sem.at[g]
        )
        for g in range(GROUPS)
    ]
    dn_loads = [
        pltpu.make_async_copy(
            groups[g].at[:, pl.ds(thin, thin)],
            w_dn.at[g // 2, :, :, lanes_of(g, cols)],
            dn_sem.at[g],
        )
        for g in range(GROUPS)
    ]
    return out_loads, up_loads, dn_loads


def whole(ref, g):
    depth, thin, cols = ref.shape[1:]
    return ref[g].reshape(depth * thin, cols)


def ffn_front_kernel(att0, att1, hidden, x_in, g_all, *rest):
    groups = rest[:GROUPS]
    (
        key_code, v_out, v_gain1, v_shift1, v_down, v_gain2, v_shift2, b_near, b_far,
        out0_home, out1_home, slope_home, g_second_home, unit_home, norm_t_home, down_home,
        inverse_ref, sums,
        att_v, x_v, g_v, w_up, w_dn, w_out, act, slope, normed_low,
        out_v, g_second_v, unit_v, norm_t, g_ffn_t, stage, b_up, b_all,
        in_sem, up_sem, dn_sem, wo_sem, stage_sem, home_sem, end_sem, g_sem,
    ) = rest[GROUPS:]
    f32, bf16 = jnp.float32, jnp.bfloat16
    rows, width = x_v.shape
    span = hidden.shape[1]
    depth, deep, cols = groups[0].shape
    half, turn, share = my_spot()
    x_chunks = (hidden.at[half * 2 + turn], x_in.at[0])
    g_chunks = (g_all.at[half * 2 + turn],)
    other = (share + 1) % 2
    out_loads, up_loads, dn_loads = load_weights(groups, w_up, w_dn, w_out, up_sem, dn_sem, wo_sem)
    loads = start_copies(
        [(a, att_v.at[:, lanes_of(i, cols)]) for i, a in enumerate((att0, att1))]
        + [(x, x_v.at[pl.ds(i * span, span)]) for i, x in enumerate(x_chunks)]
        + [(g, g_v.at[pl.ds(i * span, span)]) for i, g in enumerate(g_chunks)],
        in_sem,
    )
    for copy in out_loads + up_loads + dn_loads:
        copy.start()
    beside = neighbours()[1]
    signal_all([beside])
    g_next = remote(
        g_all.at[half * 2 + (turn + 1) % 2], g_v.at[pl.ds(span, span)], g_sem.at[0], g_sem.at[1],
        beside,
    )
    g_next.start()
    sums[...] = jnp.zeros_like(sums)
    b_all[0:1, :] = row_of(b_near)
    b_all[1:2, :] = row_of(b_far)
    for g in range(GROUPS):
        at = group_homes()[g][1]
        lanes = pl.ds(pl.multiple_of(at * cols, PAIR), cols)
        value = b_all[g // 2 % 2 : g // 2 % 2 + 1, lanes]
        b_up[g // 2 : g // 2 + 1, (g % 2) * cols : (g % 2 + 1) * cols] = value
    wait_copies(loads + out_loads)
    b_out, gain1, shift1, b_down, gain2, shift2 = (
        row_of(ref) for ref in (v_out, v_gain1, v_shift1, v_down, v_gain2, v_shift2)
    )

    def add_sum(index, value):
        sums[index : index + 1, :] += jnp.sum(value, 0, keepdims=True)

    def homes(tile):
        at = pl.ds(pl.multiple_of(tile * FRONT, FRONT), FRONT)
        return [
            pltpu.make_async_copy(src, dst, home_sem.at[i, tile])
            for i, (src, dst) in enumerate(
                [
                    (slope.at[:, at], slope_home.at[:, at]),
                    (g_second_v.at[at], g_second_home.at[at]),
                    (unit_v.at[at], unit_home.at[at]),
                ]
            )
        ]

    def tile_step(tile, carry):
        at = pl.ds(pl.multiple_of(tile * FRONT, FRONT), FRONT)
        live = (key_code[at, :1] >= 0).astype(f32)
        add_sum(11, jnp.broadcast_to(live, (FRONT, width)))
        attn = b_out + dot_nt(att_v[at, :], jnp.concatenate([w_out[share], w_out[other]], 1))
        x = x_v[at, :].astype(f32)
        first = x + attn
        add_sum(6, live * (x * x))
        add_sum(7, live * (first * first))
        add_sum(9, live * (attn * attn))
        unit1, inverse1 = normalize(first)
        unit_v[at, :] = unit1
        inverse_ref[at, :] = inverse1
        normed = unit1 * gain1 + shift1
        low = normed.astype(bf16)
        normed_low[...] = low
        norm_t[:, at] = low.T

        @pl.when(tile == 0)
        def _():
            wait_copies(up_loads + dn_loads)

        @pl.when(tile == span // FRONT)
        def _():
            g_next.wait_recv()

        def up_step(g, ffn):
            pre = dot_nn(normed_low[...], whole(w_up, g)) + b_up[pl.ds(g, 1), :]
            value, rise = gelu_both(pre)
            value = value.astype(bf16)
            act[g, at, :] = value
            slope[g, at, :] = rise.astype(bf16)
            return ffn + dot_nt(value, whole(w_dn, g))

        ffn = lax.fori_loop(0, DUOS, up_step, jnp.broadcast_to(b_down, (FRONT, width)))
        second = normed + ffn
        add_sum(8, live * (second * second))
        add_sum(10, live * (ffn * ffn))
        unit2, inverse2 = normalize(second)
        out_v[at, :] = (unit2 * gain2 + shift2).astype(bf16)
        g_out = g_v[at, :].astype(f32)
        add_sum(4, g_out * unit2)
        add_sum(5, g_out)
        g_second = normalize_back(g_out * gain2, unit2, inverse2)
        g_second_v[at, :] = g_second
        g_ffn = g_second.astype(bf16)
        add_sum(3, g_ffn.astype(f32))
        g_ffn_t[:, at] = g_ffn.T
        for copy in homes(tile):
            copy.start()
        return carry

    lax.fori_loop(0, rows // FRONT, tile_step, 0)
    last = start_copies(
        [
            (norm_t, norm_t_home),
            (out_v.at[pl.ds(0, span)], out0_home),
            (out_v.at[pl.ds(span, span)], out1_home),
        ],
        end_sem,
    )

    def leave(g):
        return pltpu.make_async_copy(stage.at[g], down_home.at[g], stage_sem.at[g])

    def down_step(duo, carry):
        down = dot_nn(g_ffn_t[...], act[duo]).astype(bf16).reshape(depth, -1, 2 * cols)
        for i in range(2):
            stage[2 * duo + i] = down[:, :, i * cols : (i + 1) * cols]
            leave(2 * duo + i).start()
        return carry

    lax.fori_loop(0, DUOS, down_step, 0)
    for tile in range(rows // FRONT):
        wait_copies(homes(tile))
    wait_copies([leave(g) for g in range(GROUPS)] + last)
    g_next.wait_send()


def ffn_front(att0, att1, hidden, x_in, g_all, groups, key_code, vectors, b_near, b_far):
    rows, part = att0.shape
    width = hidden.shape[2]
    depth, deep, cols = groups[0].shape
    thin = width // depth
    f32, bf16, shape = jnp.float32, jnp.bfloat16, jax.ShapeDtypeStruct
    weights = pltpu.VMEM((DUOS, depth, thin, 2 * cols), bf16)
    flat = pltpu.VMEM((rows, width), bf16)
    tall = pltpu.VMEM((rows, width), f32)
    deep_rows = pltpu.VMEM((DUOS, rows, 2 * cols), bf16)
    turned = pltpu.VMEM((width, rows), bf16)
    return pl.pallas_call(
        ffn_front_kernel,
        out_shape=(
            shape((rows // 2, width), bf16), shape((rows // 2, width), bf16),
            shape((DUOS, rows, 2 * cols), bf16),
            shape((rows, width), f32), shape((rows, width), f32), shape((width, rows), bf16),
            shape((GROUPS, depth, thin, cols), bf16), shape((rows, 1), f32), shape((16, width), f32),
        ),
        in_specs=[ANY_SPEC] * (5 + GROUPS) + [VMEM_SPEC] * 9,
        out_specs=(ANY_SPEC,) * 7 + (VMEM_SPEC,) * 2,
        scratch_shapes=[
            flat, flat, flat, weights, weights, pltpu.VMEM((2, width, part), bf16),
            deep_rows, deep_rows, pltpu.VMEM((FRONT, width), bf16),
            flat, tall, tall, turned, turned, pltpu.VMEM((GROUPS, depth, thin, cols), bf16),
            pltpu.VMEM((DUOS, 2 * cols), f32), pltpu.VMEM((2, 4 * cols), f32),
            DMA((6,)), DMA((GROUPS,)), DMA((GROUPS,)), DMA((GROUPS, depth)), DMA((GROUPS,)),
            DMA((3, rows // FRONT)), DMA((3,)), DMA((2,)),
        ],
        compiler_params=pltpu.CompilerParams(
            vmem_limit_bytes=63 * 1024 * 1024, collective_id=4, has_side_effects=True
        ),
        cost_estimate=pl.CostEstimate(
            flops=38 * 10**9, bytes_accessed=40 * 10**6, transcendentals=rows * GROUPS * cols
        ),
        name="ffn_front",
    )(att0, att1, hidden, x_in, g_all, *groups, key_code, *vectors, b_near, b_far)


def ffn_rear_kernel(
    att0, att1, slope_in, g_second_in, unit_in, norm_t_in, out0, out1, downs, *rest
):
    groups = rest[:GROUPS]
    (
        inverse_ref, v_gain1,
        g_first_home, do_own, do_far, layer_home, *totals
    ) = rest[GROUPS : GROUPS + 5 + DUOS + groups[0].shape[0]]
    corners = totals[DUOS - 1 :]
    (
        sums, up_sums,
        att_v, slope, g_second_v, unit_v, norm_t, w_up, w_dn, w_out, g_pre,
        g_first_v, g_att_v, g_attn_t, out_v, far_v, got_v, got_dn, near_v, stage,
        in_sem, up_sem, dn_sem, wo_sem, stage_sem, home_sem, out_sem,
        l_send, l_recv, a_send, a_recv, u_send, u_recv, corner_sem,
    ) = rest[GROUPS + 5 + DUOS + len(corners) :]
    f32, bf16 = jnp.float32, jnp.bfloat16
    rows, width = unit_v.shape
    span = out0.shape[0]
    depth, deep, cols = groups[0].shape
    thin = w_up.shape[2]
    slim = deep - 2 * thin
    half, turn, share = my_spot()
    other = (share + 1) % 2
    across, beside, partner = neighbours()
    out_loads, up_loads, dn_loads = load_weights(groups, w_up, w_dn, w_out, up_sem, dn_sem, wo_sem)
    wait_order = [
        pltpu.make_async_copy(src, dst, in_sem.at[i])
        for i, (src, dst) in enumerate(
            [
                (g_second_in, g_second_v), (slope_in, slope), (unit_in, unit_v),
                (norm_t_in, norm_t), (att0, att_v.at[:, lanes_of(0, cols)]),
                (att1, att_v.at[:, lanes_of(1, cols)]),
            ]
        )
    ]
    for copy in wait_order[:1] + dn_loads + wait_order[1:2] + up_loads + wait_order[2:3]:
        copy.start()
    for copy in out_loads + wait_order[3:]:
        copy.start()
    late = start_copies([(out0, out_v), (downs.at[pl.ds(0, DUOS)], near_v)], out_sem)
    signal_all([across, beside, partner])
    mine = layer_home.at[half * 2 + turn]
    theirs = layer_home.at[half * 2 + (turn + 1) % 2]
    parts = [pl.ds(i * (span // 2), span // 2) for i in range(2)]
    layer = [
        remote(out1.at[parts[0]], mine.at[parts[0]], l_send.at[0], l_recv.at[0], beside),
        remote(out0, mine, l_send.at[1], l_recv.at[1], across),
        remote(theirs.at[parts[0]], theirs.at[parts[0]], l_send.at[2], l_recv.at[2], across),
        remote(downs.at[pl.ds(DUOS, DUOS)], got_dn, l_send.at[3], l_recv.at[3], partner),
        remote(out1.at[parts[1]], mine.at[parts[1]], l_send.at[4], l_recv.at[4], beside),
        remote(theirs.at[parts[1]], theirs.at[parts[1]], l_send.at[5], l_recv.at[5], across),
    ]
    for i in (0, 4, 1, 3):
        layer[i].start()
    sums[...] = jnp.zeros_like(sums)
    up_sums[...] = jnp.zeros_like(up_sums)
    gain1 = row_of(v_gain1)
    wait_copies(wait_order[:1] + dn_loads + wait_order[1:2])
    out_weight = lambda: jnp.concatenate([w_out[share], w_out[other]], 1)

    def add_sum(index, value):
        sums[index : index + 1, :] += jnp.sum(value, 0, keepdims=True)

    def tile_rows(tile):
        return pl.ds(pl.multiple_of(tile * TILE, TILE), TILE)

    def give(tile):
        at = tile_rows(tile)
        return remote(g_att_v.at[1, at], do_far.at[at], a_send.at[tile], a_recv.at[tile], partner)

    tiles = rows // TILE

    def tile_step(tile, carry):
        at = tile_rows(tile)

        @pl.when(tile == 0)
        def _():
            wait_copies(up_loads + wait_order[2:] + out_loads)

        for late_tile, i in ((tiles - 2, 0), (tiles - 1, 1)):

            @pl.when(tile == late_tile)
            def _():
                layer[(0, 4)[i]].wait_recv()
                layer[(2, 5)[i]].start()

        g_second = g_second_v[at, :]
        g_ffn = g_second.astype(bf16)

        def back_step(g, total):
            grad = (dot_nn(g_ffn, whole(w_dn, g)) * slope[g, at, :].astype(f32)).astype(bf16)
            g_pre[g, at, :] = grad
            up_sums[pl.ds(g, 1), :] += jnp.sum(grad.astype(f32), 0, keepdims=True)
            return total + dot_nt(grad, whole(w_up, g))

        g_normed = lax.fori_loop(0, DUOS, back_step, g_second)
        unit1 = unit_v[at, :]
        add_sum(1, g_normed * unit1)
        add_sum(2, g_normed)
        g_first = normalize_back(g_normed * gain1, unit1, inverse_ref[at, :])
        g_first_v[at, :] = g_first
        g_attn = g_first.astype(bf16)
        add_sum(0, g_attn.astype(f32))
        g_attn_t[:, at] = g_attn.T
        both = dot_nn(g_attn, out_weight()).astype(bf16)
        g_att_v[0, at, :] = both[:, :cols]
        g_att_v[1, at, :] = both[:, cols:]
        give(tile).start()
        return carry

    lax.fori_loop(0, tiles, tile_step, 0)
    homes = start_copies([(g_att_v.at[0], do_own), (g_first_v, g_first_home)], home_sem)
    wait_copies(late)
    own_out = pltpu.make_async_copy(out_v, mine, out_sem.at[0])
    own_out.start()
    both = dot_nn(g_attn_t[...], att_v[...]).astype(bf16)
    w_out[share] = both[:, :cols]
    w_out[other] = both[:, cols:]

    def out_rows(g, d):
        where = (half + g // 2) % 2
        at = ((turn + g) % 2) * 2 + (share + g // 4) % 2
        return w_out[where, pl.ds(pl.multiple_of(d * thin + at * slim, 16), slim), :]

    def up_of(duo):
        up = dot_nn(norm_t[...], g_pre[duo]).astype(bf16).reshape(depth, thin, 2 * cols)
        return [(2 * duo + i, up[:, :, i * cols : (i + 1) * cols]) for i in range(2)]

    def pass_on(i):
        return remote(far_v.at[i], got_v.at[i], u_send.at[i], u_recv.at[i], partner)

    def far_step(duo, carry):
        for g, up in up_of(duo):
            i = g - DUOS
            far_v[i, :, pl.ds(0, thin), :] = up
            for d in range(depth):
                far_v[i, d, pl.ds(thin, slim), :] = out_rows(g, d)
            pass_on(i).start()
        return carry

    lax.fori_loop(DUOS // 2, DUOS, far_step, 0)
    sends = [pass_on(i) for i in range(DUOS)]
    layer[3].wait_recv()
    add = lambda a, b: (a.astype(f32) + b.astype(f32)).astype(bf16)
    stores = [None] * DUOS
    for duo in range(DUOS // 2):
        for g, up in up_of(duo):
            slot = g % 2
            if g >= 2:
                stores[g - 2].wait()
            sends[g].wait_recv()
            stage[slot, :, pl.ds(0, thin), :] = add(up, got_v[g, :, pl.ds(0, thin), :])
            stage[slot, :, pl.ds(thin, thin), :] = add(near_v[g], got_dn[g])
            for d in range(depth):
                stage[slot, d, pl.ds(2 * thin, slim), :] = add(
                    out_rows(g, d), got_v[g, d, pl.ds(thin, slim), :]
                )
            if g == DUOS - 1:
                deep_at = lax.axis_index("dp")
                rounds = start_copies(
                    [
                        (stage.at[slot, (deep_at + j) % depth], home)
                        for j, home in enumerate(corners)
                    ],
                    corner_sem,
                )
                continue
            stores[g] = pltpu.make_async_copy(stage.at[slot], totals[g], stage_sem.at[slot])
            stores[g].start()
    for tile in range(tiles):
        give(tile).wait()
    for i in (1, 2, 5):
        layer[i].wait_recv()
    for copy in layer + sends:
        copy.wait_send()
    wait_copies(stores[-2:-1] + rounds + homes + [own_out])


def ffn_rear(
    att0, att1, slope, g_second, unit, norm_t, out0, out1, downs_in, groups, inverse, gain1
):
    rows, part = att0.shape
    span, width = out0.shape
    depth, deep, cols = groups[0].shape
    thin = width // depth
    f32, bf16, shape, v = jnp.float32, jnp.bfloat16, jax.ShapeDtypeStruct, pltpu.VMEM
    weights = v((DUOS, depth, thin, 2 * cols), bf16)
    flat = v((rows, width), bf16)
    tall = v((rows, width), f32)
    deep_rows = v((DUOS, rows, 2 * cols), bf16)
    turned = v((width, rows), bf16)
    mixed = v((DUOS, depth, deep - thin, cols), bf16)
    downs = v((DUOS, depth, thin, cols), bf16)
    tiles = rows // TILE
    return pl.pallas_call(
        ffn_rear_kernel,
        out_shape=(
            shape((rows, width), f32), shape((rows, part), bf16), shape((rows, part), bf16),
            shape((4, span, width), bf16),
        )
        + (shape((depth, deep, cols), bf16),) * (DUOS - 1)
        + (shape((deep, cols), bf16),) * depth
        + (shape((16, width), f32), shape((DUOS, 2 * cols), f32)),
        in_specs=[ANY_SPEC] * (9 + GROUPS) + [VMEM_SPEC] * 2,
        out_specs=(ANY_SPEC,) * (3 + DUOS + depth) + (VMEM_SPEC,) * 2,
        scratch_shapes=[
            flat, deep_rows, tall, tall, turned, weights, weights,
            v((2, width, part), bf16), deep_rows, tall, v((2, rows, part), bf16), turned,
            v((span, width), bf16), mixed, mixed, downs, downs, v((2, depth, deep, cols), bf16),
            DMA((6,)), DMA((GROUPS,)), DMA((GROUPS,)), DMA((GROUPS, depth)), DMA((2,)), DMA((2,)),
            DMA((2,)), DMA((6,)), DMA((6,)), DMA((tiles,)), DMA((tiles,)), DMA((DUOS,)),
            DMA((DUOS,)), DMA((depth,)),
        ],
        compiler_params=pltpu.CompilerParams(
            vmem_limit_bytes=63 * 1024 * 1024, collective_id=2, has_side_effects=True
        ),
        cost_estimate=pl.CostEstimate(
            flops=45 * 10**9, bytes_accessed=40 * 10**6, transcendentals=0
        ),
        name="ffn_rear",
    )(
        att0, att1, slope, g_second, unit, norm_t, out0, out1, downs_in, *groups, inverse, gain1
    )


MESH = pl.DeviceIdType.MESH
CUTS = 8
THIRDS = 3


def signal_all(devices):
    barrier = pltpu.get_barrier_semaphore()
    for device in devices:
        pl.semaphore_signal(barrier, inc=1, device_id=device, device_id_type=MESH)
    pl.semaphore_wait(barrier, len(devices))


def neighbours():
    half, turn, share = my_spot()
    return (
        {"tensor": (half + 1) % 2},
        {"context": ((turn + 1) % 2) * 2 + share},
        {"context": turn * 2 + (share + 1) % 2},
    )


def remote(src, dst, send_sem, recv_sem, device):
    return pltpu.make_async_remote_copy(
        src_ref=src, dst_ref=dst, send_sem=send_sem, recv_sem=recv_sem,
        device_id=device, device_id_type=MESH,
    )


def fetch_kernel(
    hidden, w_q, w_k, w_v, w_up, w_down, w_out, bias_q, bias_v, bias_u,
    x_out, q_all, f_deep, n1, n2, far_q, far_v, far_u,
    qkv, ffn, cut_sem, own_sem, x_send, x_recv, z_send, z_recv, f_send, f_recv,
    h_send, h_recv, t_send, t_recv, c_send, c_recv, b_sem, n_send, n_recv,
):
    half, turn, share = my_spot()
    deep = lax.axis_index("dp")
    depth = f_deep.shape[0]
    across, beside, partner = neighbours()
    up, down = {"dp": (deep + 1) % depth}, {"dp": (deep + depth - 1) % depth}
    slim, thin, cols = qkv.shape[0], w_q.shape[0], w_q.shape[1]
    place = turn * 2 + share
    my_rows = pl.ds(pl.multiple_of(place * slim, 16), slim)
    my_lanes = pl.ds(pl.multiple_of(place * cols, PAIR), cols)
    cuts = start_copies(
        [(w.at[my_rows], qkv.at[:, pl.ds(i * cols, cols)]) for i, w in enumerate((w_q, w_k, w_v))]
        + [(w.at[:, my_lanes], ffn.at[pl.ds(i * thin, thin)]) for i, w in enumerate((w_up, w_down))]
        + [(w_out.at[my_rows], ffn.at[pl.ds(2 * thin, slim)])],
        cut_sem,
    )
    signal_all([across, beside, partner, up, down])
    wait_copies(cuts)

    slot = lambda h, t, d: q_all.at[h, t, share, d]
    own = start_copies([(qkv, slot(half, turn, deep)), (ffn, f_deep.at[deep])], own_sem)

    def to_up(d):
        return remote(slot(half, turn, d), slot(half, turn, d), z_send.at[0, d], z_recv.at[d], up)

    def to_down(d):
        return remote(slot(half, turn, d), slot(half, turn, d), z_send.at[1, d], z_recv.at[d], down)

    third = f_deep.shape[1] // THIRDS

    def f_copies(d, side, device):
        return [
            remote(
                f_deep.at[d, pl.ds(i * third, third)], f_deep.at[d, pl.ds(i * third, third)],
                f_send.at[side, d, i], f_recv.at[d, i], device,
            )
            for i in range(THIRDS)
        ]

    f_up = lambda d: f_copies(d, 0, up)
    f_down = lambda d: f_copies(d, 1, down)

    def to_across(t, d):
        return remote(slot(half, t, d), slot(half, t, d), h_send.at[t, d], h_recv.at[t, d], across)

    def from_across(t, d):
        other = slot((half + 1) % 2, t, d)
        return remote(other, other, h_send.at[t, d], h_recv.at[t, d], across)

    def to_beside(d):
        return remote(slot(half, turn, d), slot(half, turn, d), t_send.at[d], t_recv.at[d], beside)

    def from_beside(d):
        other = slot(half, (turn + 1) % 2, d)
        return remote(other, other, t_send.at[d], t_recv.at[d], beside)

    def to_partner(t, d):
        piece = slot((share + 1) % 2, t, d)
        return remote(piece, piece, c_send.at[t, d], c_recv.at[t, d], partner)

    def from_partner(t, d):
        piece = q_all.at[share, t, (share + 1) % 2, d]
        return remote(piece, piece, c_send.at[t, d], c_recv.at[t, d], partner)

    cut = x_out.shape[1] // CUTS
    piece_rows = lambda i: pl.ds(i * cut, cut)
    x_next = [
        remote(
            hidden.at[half * 2 + (turn + 1) % 2, piece_rows(i)], x_out.at[0, piece_rows(i)],
            x_send.at[0, i], x_recv.at[0, i], beside,
        )
        for i in range(CUTS)
    ]
    x_mine = remote(
        hidden.at[half * 2 + turn], x_out.at[1], x_send.at[1, 0], x_recv.at[1, 0], partner
    )
    x_relay = [
        remote(
            x_out.at[0, piece_rows(i)], x_out.at[2, piece_rows(i)],
            x_send.at[2, i], x_recv.at[2, i], partner,
        )
        for i in range(CUTS)
    ]
    biases = [
        remote(src, dst, b_sem.at[0, i], b_sem.at[1, i], across)
        for i, (src, dst) in enumerate(((bias_q, far_q), (bias_v, far_v), (bias_u, far_u)))
    ]
    wait_copies(own)
    own_turn = (share + 1) % 2 == half

    def spread_own(d):
        to_across(turn, d).start()
        to_beside(d).start()

        @pl.when(own_turn)
        def _():
            to_partner(turn, d).start()

    def when(condition, *copies):
        @pl.when(condition)
        def _():
            for copy in copies:
                copy.start()

    when(deep < depth - 1, to_up(deep))
    when(deep > 0, to_down(deep))
    when(deep < depth - 1, f_up(deep)[0])
    when(deep > 0, f_down(deep)[0])
    spread_own(deep)
    x_next[0].start()
    for copy in biases:
        copy.start()
    x_mine.start()
    for k in range(1, depth):
        low, high = (deep + depth - k) % depth, (deep + k) % depth

        @pl.when(deep >= k)
        def _():
            to_up(low).wait_recv()
            when(deep < depth - 1, to_up(low))
            spread_own(low)

        @pl.when(deep + k < depth)
        def _():
            to_down(high).wait_recv()
            when(deep > 0, to_down(high))
            spread_own(high)

        if k < THIRDS:
            when(deep < depth - 1, f_up(deep)[k])
            when(deep > 0, f_down(deep)[k])
        x_next[k].start()

    for i in range(depth, THIRDS):
        when(deep < depth - 1, f_up(deep)[i])
        when(deep > 0, f_down(deep)[i])
    for copy in x_next[depth:]:
        copy.start()
    for k in range(depth):
        d = (deep + k) % depth
        from_beside(d).wait_recv()
        to_across((turn + 1) % 2, d).start()

        @pl.when(own_turn)
        def _():
            to_partner((turn + 1) % 2, d).start()

    f_side = [
        remote(
            f_deep.at[deep, pl.ds(i * third, third)], home.at[deep, pl.ds(i * third, third)],
            n_send.at[j, i], n_recv.at[j, i], device,
        )
        for i in range(THIRDS)
        for j, (home, device) in enumerate(((n1, beside), (n2, across)))
    ]
    for copy in f_side:
        copy.start()

    def f_step(k):
        low, high = (deep + depth - k) % depth, (deep + k) % depth

        @pl.when(deep >= k)
        def _():
            for copy in f_up(low):
                copy.wait_recv()
                when(deep < depth - 1, copy)

        @pl.when(deep + k < depth)
        def _():
            for copy in f_down(high):
                copy.wait_recv()
                when(deep > 0, copy)

    def x_step(step):
        for i in range(step * CUTS // (depth + 1), (step + 1) * CUTS // (depth + 1)):
            x_next[i].wait_recv()
            x_relay[i].start()

    f_step(1)
    for step, t in enumerate((turn, (turn + 1) % 2)):
        for k in range(depth):
            d = (deep + k) % depth
            from_across(t, d).wait_recv()

            @pl.when(jnp.logical_not(own_turn))
            def _():
                to_partner(t, d).start()

        x_step(step)
        if step == 0 and depth > 2:
            f_step(2)
    for k in range(3, depth):
        x_step(k - 1)
        f_step(k)
    for step in range(max(2, depth - 1), depth + 1):
        x_step(step)

    for t in range(2):
        for d in range(depth):
            from_partner(t, d).wait_recv()
    x_mine.wait_recv()
    for copy in x_relay + biases + f_side:
        copy.wait_recv()
    for d in range(depth):
        for copy in (to_across(0, d), to_across(1, d), to_beside(d), to_partner(0, d), to_partner(1, d)):
            copy.wait_send()

        @pl.when(jnp.logical_and(deep < depth - 1, deep >= d))
        def _():
            for copy in [to_up(d)] + f_up(d):
                copy.wait_send()

        @pl.when(jnp.logical_and(deep > 0, deep <= d))
        def _():
            for copy in [to_down(d)] + f_down(d):
                copy.wait_send()

    for copy in x_next + x_relay + [x_mine] + biases + f_side:
        copy.wait_send()


def fetch(hidden_in, weights, biases, depth):
    span, width = hidden_in.shape[1:]
    thin, cols = weights[0].shape
    slim = thin // 4
    bf16, shape = jnp.bfloat16, jax.ShapeDtypeStruct
    pair = DMA((2, depth))
    return pl.pallas_call(
        fetch_kernel,
        out_shape=(
            shape((3, span, width), bf16),
            shape((2, 2, 2, depth, slim, 3 * cols), bf16),
            *(shape((depth, 2 * thin + slim, cols), bf16) for _ in range(3)),
            *(shape(b.shape, bf16) for b in biases),
        ),
        in_specs=[ANY_SPEC] * 7 + [VMEM_SPEC] * 3,
        out_specs=(ANY_SPEC, VMEM_SPEC) + (ANY_SPEC,) * 3 + (VMEM_SPEC,) * 3,
        scratch_shapes=[
            pltpu.VMEM((slim, 3 * cols), bf16), pltpu.VMEM((2 * thin + slim, cols), bf16),
            DMA((6,)), DMA((2,)), DMA((3, CUTS)), DMA((3, CUTS)), pair, DMA((depth,)),
            DMA((2, depth, THIRDS)), DMA((depth, THIRDS)),
            pair, pair, DMA((depth,)), DMA((depth,)), pair, pair, DMA((2, 3)),
            DMA((2, THIRDS)), DMA((2, THIRDS)),
        ],
        compiler_params=pltpu.CompilerParams(
            vmem_limit_bytes=63 * 1024 * 1024, collective_id=0, has_side_effects=True
        ),
        cost_estimate=pl.CostEstimate(
            flops=30 * 10**9, bytes_accessed=10 * 10**6, transcendentals=0
        ),
        name="fetch",
    )(hidden_in, *weights, *biases)


SUBS = 4


def settle_kernel(
    parts_depth, hidden, x_in, dqkv, w_qkv, g_first, front_sums, rear_sums, up_sums, head_sums,
    *rest,
):
    f32, bf16 = jnp.float32, jnp.bfloat16
    parts, corners = rest[:3], rest[3 : 3 + parts_depth]
    (
        out, qkv_out, f_out, small_out,
        x_v, d_v, w_v, first_v, part_v, small_v, small_got,
        back_v, got_v, fin_v, land_v, tot_v, zf_v, ff_v,
        corner_v, corner_out, corner_in, grad_v, swap_v, pq_v, yl_v, xs_v, xl_v, rs_v, zq_v, qf_v,
        in_sem, out_sem, send_sem, recv_sem,
    ) = rest[3 + parts_depth :]
    half, turn, share = my_spot()
    deep = lax.axis_index("dp")
    depth = tot_v.shape[0]
    span = hidden.shape[1]
    sub = span // SUBS
    other = (share + 1) % 2
    far_half, far_turn = (half + 1) % 2, (turn + 1) % 2
    across, beside, partner = neighbours()
    deeps = [{"dp": (deep + k) % depth} for k in range(1, depth)]
    ids = iter(range(send_sem.shape[0]))
    started = []

    def link(src, dst, device):
        i = next(ids)
        copy = remote(src, dst, send_sem.at[i], recv_sem.at[i], device)
        started.append(copy)
        return copy

    def go(src, dst, device):
        copy = link(src, dst, device)
        copy.start()
        return copy

    chunk = lambda i: pl.ds(i * span, span)
    chunks = [hidden.at[half * 2 + turn]] + [x_in.at[i] for i in range(3)]
    loads = [
        pltpu.make_async_copy(src, dst, in_sem.at[i])
        for i, (src, dst) in enumerate(
            [(w_qkv, w_v)]
            + [(dqkv.at[chunk(i)], d_v.at[chunk(i)]) for i in (2, 3, 0, 1)]
            + [(p, part_v.at[i]) for i, p in enumerate(parts)]
            + [(g_first, first_v)]
            + [(c, x_v.at[chunk(i)]) for i, c in enumerate(chunks)]
        )
    ]
    corner_loads = start_copies(
        [(c, corner_v.at[i]) for i, c in enumerate(corners)], out_sem
    )
    for copy in loads:
        copy.start()
    diagonal = {"tensor": far_half, "context": far_turn * 2 + share}
    signal_all([across, beside, partner, diagonal] + deeps)
    wait_copies(corner_loads)
    corner_out[...] = sum(
        [corner_v[i].astype(f32) for i in range(1, depth)], corner_v[0].astype(f32)
    ).astype(bf16)
    corner = go(corner_out, corner_in, diagonal)
    small_v[...] = jnp.zeros_like(small_v)
    cols = up_sums.shape[1] // 2
    for g, (where, at) in enumerate(group_homes()):
        row = pl.ds(where * 2 + at // 2, 1)
        lanes = pl.ds(pl.multiple_of((at % 2) * cols, PAIR), cols)
        small_v[row, lanes] = up_sums[g // 2 : g // 2 + 1, (g % 2) * cols : (g % 2 + 1) * cols]
    small_v[4:7, :] = rear_sums[0:3, :]
    small_v[7:10, :] = front_sums[3:6, :]
    lane = lax.broadcasted_iota(jnp.int32, (1, small_v.shape[1]), 1)
    stats = jnp.where(lane == 5, front_sums[11:12, :], 0.0)
    for i in range(5):
        stats = jnp.where(lane == i, jnp.sum(front_sums[6 + i : 7 + i, :], 1, keepdims=True), stats)
    small_v[10:11, :] = stats
    small_v[11:13, :] = head_sums[0:2, :]

    s0 = go(small_v, small_got.at[0], partner)
    wait_copies(loads[:5] + loads[8:9])
    outs = []
    first_id = next(ids)
    next(ids)

    def give(i):
        return remote(
            back_v.at[i], got_v.at[i], send_sem.at[first_id + i], recv_sem.at[first_id + i], partner
        )

    rows = lambda j: pl.ds(j * sub, sub)

    def put(ref, h, t):
        copy = pltpu.make_async_copy(ref, out.at[h * 2 + t], out_sem.at[len(outs)])
        copy.start()
        outs.append(copy)

    own_put = pltpu.make_async_copy(fin_v.at[0], out.at[half * 2 + turn], out_sem.at[0])
    outs.append(own_put)
    x_subs = [link(fin_v.at[0, rows(j)], land_v.at[1, rows(j)], across) for j in range(SUBS)]
    y_subs = [link(fin_v.at[1, rows(j)], land_v.at[0, rows(j)], beside) for j in range(SUBS - 1)]

    def back_step(i, carry):
        at = pl.ds(pl.multiple_of((i + 2) % 4 * span, span), span)
        value = dot_nt(d_v[at, :], w_v[...])

        @pl.when(i < 2)
        def _():
            back_v[i] = value.astype(bf16)
            give(i).start()

        @pl.when(i >= 2)
        def _():
            give(i - 2).wait_recv()
            whole_sum = value + first_v[at, :] + got_v[i - 2].astype(f32)
            fin_v[i - 2] = whole_sum.astype(bf16)

        @pl.when(i == 2)
        def _():
            for copy in x_subs + [own_put]:
                copy.start()

        @pl.when(i == 3)
        def _():
            for copy in y_subs:
                copy.start()

        return carry

    lax.fori_loop(0, 4, back_step, 0)
    started += [give(0), give(1)]
    wait_copies(loads[5:8])
    tot_v[...] = (
        part_v[0].astype(f32) + part_v[1].astype(f32) + part_v[2].astype(f32)
    ).astype(bf16)
    z_f = [
        go(tot_v.at[(deep + k + 1) % depth], zf_v.at[k], device) for k, device in enumerate(deeps)
    ]


    s0.wait_recv()
    s0.wait_send()
    small_v[...] += small_got[0]
    s1 = go(small_v, small_got.at[1], beside)
    wait_copies(loads[9:])
    third = grad_v.shape[0] // 3

    def grad_step(i, carry):
        at = pl.ds(pl.multiple_of(i * third, PAIR), third)
        grad_v[at, :] = dot_tn(x_v[:, at], d_v[...]).astype(bf16)
        return carry

    lax.fori_loop(0, 3, grad_step, 0)
    slim = swap_v.shape[2]

    def grad_rows(d, t, s):
        return grad_v[pl.ds(pl.multiple_of((d * 4 + t * 2 + s) * slim, 16), slim), :]

    for d in range(depth):
        for t in range(2):
            swap_v[d, t] = grad_rows(d, t, other)
    swap = go(swap_v, pq_v.at[share], partner)
    for d in range(depth):
        for t in range(2):
            pq_v[share, d, t] = grad_rows(d, t, share)
    s1.wait_recv()
    s1.wait_send()
    small_v[...] += small_got[1]
    s2 = go(small_v, small_got.at[2], across)
    swap.wait_recv()
    keep_v = lambda h, t: pq_v[h, :, t]
    q1 = go(pq_v.at[far_half, :, far_turn], yl_v.at[0], beside)
    q2 = go(pq_v.at[half, :, far_turn], yl_v.at[1], beside)
    y_subs += [
        go(fin_v.at[1, rows(j)], land_v.at[0, rows(j)], beside) for j in range(SUBS - 1, SUBS)
    ]
    s2.wait_recv()
    s2.wait_send()
    small_v[...] += small_got[2]
    s3 = [go(small_v, small_got.at[3 + k], device) for k, device in enumerate(deeps)]
    relays = []

    def relay(j):
        y_subs[j].wait_recv()
        relays.append(go(land_v.at[0, rows(j)], land_v.at[2, rows(j)], across))

    for j in range(SUBS // 2):
        relay(j)
    q1.wait_recv()
    xs_v[...] = (keep_v(far_half, turn).astype(f32) + yl_v[0].astype(f32)).astype(bf16)
    qx = go(xs_v, xl_v, across)

    for copy in z_f:
        copy.wait_recv()
    ranks = range(depth - 1)
    spread = lambda ref, got: sum([got[k].astype(f32) for k in ranks], ref[deep].astype(f32))
    corner.wait_recv()
    ff_v[turn, share] = (spread(tot_v, zf_v) + corner_in[...].astype(f32)).astype(bf16)

    def gather_first(ref):
        piece = ref.at[turn, share]
        return go(piece, piece, beside), go(piece, piece, partner)

    def gather_next(ref, first):
        first.wait_recv()
        piece = ref.at[far_turn, share]
        return go(piece, piece, partner)

    f_first = gather_first(ff_v)
    q2.wait_recv()
    for j in range(SUBS // 2, SUBS):
        relay(j)
    qx.wait_recv()
    rs_v[...] = (
        keep_v(half, turn).astype(f32) + yl_v[1].astype(f32) + xl_v[...].astype(f32)
    ).astype(bf16)
    z_q = [
        go(rs_v.at[(deep + k + 1) % depth], zq_v.at[k], device) for k, device in enumerate(deeps)
    ]
    for copy in s3:
        copy.wait_recv()
    small_out[...] = small_v[...] + sum([small_got[4 + k] for k in range(depth - 2)], small_got[3])
    f_next = gather_next(ff_v, f_first[0])
    for copy in z_q:
        copy.wait_recv()
    qf_v[turn, share] = spread(rs_v, zq_v).astype(bf16)
    q_first = gather_first(qf_v)
    put(land_v.at[0], half, far_turn)
    for copy in x_subs:
        copy.wait_recv()
    put(land_v.at[1], far_half, turn)
    f_first[1].wait_recv()
    f_next.wait_recv()
    ends = start_copies([(ff_v, f_out)], in_sem)
    q_next = gather_next(qf_v, q_first[0])
    for copy in relays:
        copy.wait_recv()
    put(land_v.at[2], far_half, far_turn)
    q_first[1].wait_recv()
    q_next.wait_recv()
    last = pltpu.make_async_copy(qf_v, qkv_out, in_sem.at[2])
    last.start()
    wait_copies(ends + [last] + outs)
    waited = [s0, s1, s2]
    for copy in started:
        if not any(copy is w for w in waited):
            copy.wait_send()


def settle(hidden_in, x_in, dqkv, w_qkv, g_first, sums, parts, corners):
    rows, width = g_first.shape
    span = hidden_in.shape[1]
    depth, tall, cols = parts[0].shape
    wide = dqkv.shape[1]
    slim = width // depth // 4
    f32, bf16, shape = jnp.float32, jnp.bfloat16, jax.ShapeDtypeStruct
    v = pltpu.VMEM
    count = 80
    return pl.pallas_call(
        functools.partial(settle_kernel, depth),
        out_shape=(
            shape((4, span, width), bf16), shape((2, 2, slim, wide), bf16),
            shape((2, 2, tall, cols), bf16), shape((16, width), f32),
        ),
        in_specs=[ANY_SPEC] * 5 + [VMEM_SPEC] * 4 + [ANY_SPEC] * (3 + depth),
        out_specs=(ANY_SPEC,) * 3 + (VMEM_SPEC,),
        scratch_shapes=[
            v((2 * rows, width), bf16), v((2 * rows, wide), bf16), v((width, wide), bf16),
            v((rows, width), f32), v((3, depth, tall, cols), bf16), v((16, width), f32),
            v((2 + depth, 16, width), f32),
            v((2, span, width), bf16), v((2, span, width), bf16), v((2, span, width), bf16),
            v((3, span, width), bf16),
            v((depth, tall, cols), bf16), v((depth - 1, tall, cols), bf16),
            v((2, 2, tall, cols), bf16),
            v((depth, tall, cols), bf16), v((tall, cols), bf16), v((tall, cols), bf16),
            v((width, wide), bf16), v((depth, 2, slim, wide), bf16),
            v((2, depth, 2, slim, wide), bf16), v((2, depth, slim, wide), bf16),
            v((depth, slim, wide), bf16), v((depth, slim, wide), bf16),
            v((depth, slim, wide), bf16), v((depth - 1, slim, wide), bf16),
            v((2, 2, slim, wide), bf16),
            DMA((20,)), DMA((max(4, depth),)), DMA((count,)), DMA((count,)),
        ],
        compiler_params=pltpu.CompilerParams(
            vmem_limit_bytes=63 * 1024 * 1024, collective_id=1, has_side_effects=True
        ),
        cost_estimate=pl.CostEstimate(
            flops=60 * 10**9, bytes_accessed=30 * 10**6, transcendentals=0
        ),
        name="settle",
    )(hidden_in, x_in, dqkv, w_qkv, g_first, *sums, *parts, *corners)


def finish_kernel(
    grad, qkv, ffn, small,
    grad_home, o_q, o_bq, o_k, o_v, o_bv, o_o, o_bo, o_g1, o_s1, o_up, o_bup, o_down, o_bdown,
    o_g2, o_s2, o_rms,
    grad_in, grad_out, in_sem, out_sem,
):
    f32 = jnp.float32
    seqs, span, width = grad.shape
    half = my_spot()[0]
    thin = o_q.shape[0]
    cols = o_q.shape[1]
    loads = start_copies([(grad.at[i], grad_in.at[i]) for i in range(seqs)], in_sem)
    stores = []
    for i in range(seqs):
        loads[i].wait()
        grad_out[i] = grad_in[i].astype(f32)
        stores.append(pltpu.make_async_copy(grad_out.at[i], grad_home.at[i], out_sem.at[i]))
        stores[i].start()
    for i, ref in enumerate((o_q, o_k, o_v)):
        ref[...] = qkv[:, i * cols : (i + 1) * cols].astype(f32)
    slim = ffn.shape[1] - 2 * thin
    for p in range(4):
        at = slice(p * cols, (p + 1) * cols)
        o_up[:, at] = ffn[p, :thin, :].astype(f32)
        o_down[:, at] = ffn[p, thin : 2 * thin, :].astype(f32)
        o_o[p * slim : (p + 1) * slim, :] = ffn[p, 2 * thin :, :].astype(f32)
    flat = lambda row: row.reshape(row.shape[1])
    up = [small[pl.ds(half * 2 + i, 1), :] for i in range(2)]
    o_bup[...] = flat(jnp.concatenate(up, 1))
    for i, ref in enumerate((o_bo, o_g1, o_s1, o_bdown, o_g2, o_s2)):
        ref[...] = flat(small[4 + i : 5 + i, :])
    own = pl.ds(pl.multiple_of(half * cols, PAIR), cols)
    o_bq[...] = flat(small[11:12, own])
    o_bv[...] = flat(small[12:13, own])
    stats = small[10:11, :]
    o_rms[...] = flat(jnp.sqrt(stats / (jnp.maximum(stats[:, 5:6], 1.0) * width))[:, :5])
    wait_copies(stores)


def finish_all(grad, qkv, ffn, small):
    seqs, span, width = grad.shape
    thin, cols = qkv.shape[0], qkv.shape[1] // 3
    f32 = jnp.float32
    shape = lambda *s: jax.ShapeDtypeStruct(s, f32)
    outs = pl.pallas_call(
        finish_kernel,
        out_shape=(
            shape(seqs, span, width),
            shape(thin, cols), shape(cols), shape(thin, cols),
            shape(thin, cols), shape(cols), shape(thin, cols), shape(width), shape(width),
            shape(width), shape(thin, 4 * cols), shape(4 * cols), shape(thin, 4 * cols),
            shape(width), shape(width), shape(width), shape(5),
        ),
        in_specs=[ANY_SPEC] + [VMEM_SPEC] * 3,
        out_specs=(ANY_SPEC,) + (VMEM_SPEC,) * 16,
        scratch_shapes=[
            pltpu.VMEM((seqs, span, width), grad.dtype), pltpu.VMEM((seqs, span, width), f32),
            DMA((seqs,)), DMA((seqs,)),
        ],
        compiler_params=WIDE_ROOM,
        name="finish_all",
    )(grad, qkv, ffn, small)
    outs = list(outs)
    outs[6], outs[12] = outs[6].T, outs[12].T
    return tuple(outs)


def layer_norm(values, norm_gain, norm_shift):
    row_mean = jnp.mean(values, -1, keepdims=True)
    centered = values - row_mean
    row_var = jnp.mean(centered * centered, -1, keepdims=True)
    return centered * lax.rsqrt(row_var + EPSILON) * norm_gain + norm_shift


def gelu_tanh(values):
    return jax.nn.gelu(values, approximate=True)


def block_tables(random_seq, all_blocks, place):
    block = jnp.arange(2, all_blocks, dtype=jnp.int32)
    last = all_blocks - 1
    zero = jnp.zeros_like(block)
    true_ids = jnp.stack(
        [block, block - 1, block, jnp.minimum(block + 1, last), zero, zero + 1], -1
    )
    true_ids = jnp.concatenate([true_ids, random_seq[2:]], -1)
    flags = jnp.stack([block >= 3, block <= last - 1], -1).astype(jnp.int32)
    return (
        jnp.concatenate([place(true_ids), flags], -1).astype(jnp.int32),
        place(jnp.arange(2, dtype=jnp.int32)),
    )


def local(
    hidden_in, out_grad, segment_ids, token_valid, random_blocks,
    query_weight, query_bias, key_weight, value_weight, value_bias,
    output_weight, output_bias, norm1_gain, norm1_shift,
    up_weight, up_bias, down_weight, down_bias, norm2_gain, norm2_shift,
):
    f32, bf16 = jnp.float32, jnp.bfloat16
    seqs, span, width = hidden_in.shape
    length = segment_ids.shape[1]
    places = length // span
    halves = lax.axis_size("tensor")
    depth = lax.axis_size("dp")
    turns = seqs // halves
    shares = places // turns
    my_half = lax.axis_index("tensor")
    my_place = lax.axis_index("context")
    my_depth = lax.axis_index("dp")
    my_turn, my_share = my_place // shares, my_place % shares
    my_seq = my_half * turns + my_turn
    blocks = length // BLK
    rows = turns * span
    spots = [(h, t) for h in range(halves) for t in range(turns)]

    def send(value, half=0, turn=0, share=0):
        if half % halves == 0 and turn % turns == 0 and share % shares == 0:
            return value
        pairs = []
        for h in range(halves):
            for t in range(turns):
                for s in range(shares):
                    to_place = (t + turn) % turns * shares + (s + share) % shares
                    pairs.append(
                        ((t * shares + s) * halves + h, to_place * halves + (h + half) % halves)
                    )
        return lax.ppermute(value, ("context", "tensor"), pairs)

    def send_deep(value, step):
        return lax.ppermute(value, "dp", [(i, (i + step) % depth) for i in range(depth)])

    def pick(value, index, axis=0):
        return lax.dynamic_index_in_dim(value, index, axis, keepdims=False)

    def own_slice(value, count, which, axis):
        size = value.shape[axis] // count
        return lax.dynamic_slice_in_dim(value, which * size, size, axis)

    def gather_deep(value):
        if depth > 4:
            return lax.all_gather(value, "dp", axis=0)
        got = [value] + [send_deep(value, k) for k in range(1, depth)]
        ring = jnp.stack([got[depth - 1 - i % depth] for i in range(2 * depth - 1)])
        return lax.dynamic_slice_in_dim(ring, depth - 1 - my_depth, depth, 0)

    def reduce_deep(value):
        if depth > 4:
            return lax.psum_scatter(value, "dp", scatter_dimension=0)
        total = pick(value, my_depth).astype(f32)
        for k in range(1, depth):
            total = total + send_deep(pick(value, (my_depth + k) % depth), k).astype(f32)
        return total.astype(bf16)

    def gather_square(value):
        near = {spot: send(value, *spot) for spot in spots}
        near = jnp.stack([near[spot] for spot in spots])
        return [near] + [send(near, 0, 0, s) for s in range(1, shares)]

    def reduce_square(value):
        total = value[0].astype(f32)
        for i, (h, t) in enumerate(spots[1:], 1):
            total = total + send(value[i], -h, -t).astype(f32)
        return total.astype(bf16)

    def gather_places(value):
        near = [send(value, 0, t) for t in range(turns)]
        near = jnp.stack(near)
        far = jnp.stack([near] + [send(near, 0, 0, s) for s in range(1, shares)])
        return jnp.stack(
            [
                pick(pick(far, (my_share - s) % shares), (my_turn - t) % turns)
                for t in range(turns)
                for s in range(shares)
            ]
        )

    def sum_all(value):
        for step in range(halves.bit_length() - 1):
            value = value + send(value, 1 << step)
        size = 1
        while size < places:
            value = value + lax.ppermute(value, "context", [(i, i ^ size) for i in range(places)])
            size *= 2
        size = 1
        while size < depth:
            value = value + lax.ppermute(value, "dp", [(i, i ^ size) for i in range(depth)])
            size *= 2
        return value

    def bring(value):
        return jnp.concatenate(
            [
                send(pick(value, my_half * turns + (my_turn + k) % turns), 0, k)
                for k in range(turns)
            ],
            0,
        )

    def deliver(value):
        value = value.reshape(turns, span, width)
        got = jnp.stack([send(value[t], h, -t) for h, t in spots])
        return jnp.stack(
            [
                pick(got, (my_half - h) % halves * turns + (t - my_turn) % turns)
                for h in range(halves)
                for t in range(turns)
            ]
        )

    def after(value, *earlier):
        return lax.optimization_barrier((value, *earlier))[0]

    per = span // BLK

    def place(block_ids):
        chunk = block_ids // per
        turn, share = chunk // shares, chunk % shares
        spot = ((my_share - share) % shares) * turns + (my_turn - turn) % turns
        return spot * per + block_ids % per

    def in_order(row):
        return jnp.concatenate(
            [
                lax.dynamic_slice_in_dim(
                    row,
                    (((my_turn - k) % turns) * shares + (my_share - s) % shares) * span,
                    span,
                )
                for s in range(shares)
                for k in range(turns)
            ]
        )

    half_width = query_weight.shape[1]
    thin = query_weight.shape[0]
    slim = thin // places
    hidden = up_weight.shape[1] // places
    biases = jnp.concatenate([query_bias, value_bias, up_bias])

    def split_biases(by_half):
        by_half = jnp.stack([pick(by_half, (my_half - h) % halves) for h in range(halves)])
        return (
            by_half[:, at : at + b.shape[0]].reshape(-1)
            for b, at in ((query_bias, 0), (value_bias, half_width), (up_bias, 2 * half_width))
        )

    def spread(value, which, count):
        return lax.dynamic_update_slice_in_dim(
            jnp.zeros((value.shape[0] * count,), value.dtype), value, which * value.shape[0], 0
        )

    def small_rows(up_sums, group_at, norm_sums, stats):
        up_natural = jnp.zeros_like(up_sums)
        for i, at in enumerate(group_at):
            up_natural = lax.dynamic_update_slice_in_dim(
                up_natural, up_sums[i * hidden : (i + 1) * hidden], at * hidden, 0
            )
        stats = jnp.pad(stats, (0, width - stats.shape[0]))
        return jnp.concatenate(
            [up_natural.reshape(-1, width), *(row[None] for row in norm_sums), stats[None]], 0
        )

    def finish(layer_out, input_grad, qkv_shard, up_part, down_part, out_part, small):
        deep = up_weight.shape[1] * halves // width
        s_up, (s_o, s_g1, s_s1, s_down, s_g2, s_s2, stats, s_q, s_v) = (
            small[:deep].reshape(-1), small[deep : deep + 9]
        )
        s_q, s_v, s_up = (own_slice(value, halves, my_half, 0) for value in (s_q, s_v, s_up))
        input_rms = jnp.sqrt(stats[:5] / (jnp.maximum(stats[5], 1.0) * width))
        join = lambda w: jnp.moveaxis(w, 0, 1).reshape(thin, -1).astype(f32)
        shard_o = out_part.reshape(thin, -1)[:, :half_width].astype(f32).T
        shard_q, shard_k, shard_v = (qkv_shard[:, i].astype(f32) for i in range(3))
        return (
            layer_out, input_grad, shard_q, s_q, shard_k, shard_v, s_v, shard_o, s_o,
            s_g1, s_s1, join(up_part), s_up, join(down_part).T, s_down, s_g2, s_s2, input_rms,
        )

    if (turns, shares, halves) == (2, 2, 2) and depth <= 4 and rows % TILE == 0:
        near_b = [query_bias, value_bias, up_bias]
        x_in, q_all, f_deep, n1, n2, *far_b = fetch(
            hidden_in,
            [query_weight, key_weight, value_weight, up_weight, down_weight.T, output_weight.T],
            near_b, depth,
        )
        random = place(pick(random_blocks, my_seq)).reshape(-1)
        (
            att0, att1, q, k, v, lse, w_qkv, groups, key_code, query_code
        ) = project_attend(
            random, hidden_in, x_in, q_all, f_deep, n1, n2, segment_ids, token_valid,
            near_b[0], near_b[1], far_b[0], far_b[1],
        )
        vectors = [output_bias, norm1_gain, norm1_shift, down_bias, norm2_gain, norm2_shift]
        out0, out1, slope, g_second, unit, norm_t, downs, inverse, front_sums = ffn_front(
            att0, att1, hidden_in, x_in, out_grad, groups,
            key_code.reshape(length, PAIR), vectors, near_b[2], far_b[2],
        )
        g_first, do_own, do_far, layer_out, kept, turned, crossed, *corners, rear_sums, up_sums = ffn_rear(
            att0, att1, slope, g_second, unit, norm_t, out0, out1, downs, groups, inverse,
            norm1_gain,
        )
        parts = [kept, send(turned, 0, 1), send(crossed, 1)]
        corners = [send_deep(c, i) if i else c for i, c in enumerate(corners)]
        dqkv, layer_out, head_sums = attend_grad(
            random, do_own, do_far, q, k, v, layer_out, key_code, query_code, lse
        )
        dqkv, head_sums, parts, corners = lax.optimization_barrier(
            (dqkv, head_sums, parts, corners)
        )
        input_grad, qkv_shard, ffn_shard, small = settle(
            hidden_in, x_in, dqkv, w_qkv, g_first, (front_sums, rear_sums, up_sums, head_sums), parts,
            corners,
        )
        return (
            layer_out,
            *finish_all(
                input_grad, qkv_shard.reshape(thin, -1),
                ffn_shard.reshape((places,) + ffn_shard.shape[2:]), small,
            ),
        )

    seg = in_order(pick(segment_ids, my_seq))
    live = in_order(pick(token_valid, my_seq))
    random_seq = pick(random_blocks, my_seq)
    table, wide = block_tables(random_seq, blocks, place)
    key_code = jnp.broadcast_to(jnp.where(live == 1, seg, -1)[:, None], (length, PAIR))
    query_code = jnp.tile(seg.reshape(blocks, BLK), (1, PAIR // BLK))
    part = width // shares
    padded = -(-part // PAIR) * PAIR
    x_own = bring(hidden_in)
    qkv_piece = own_slice(
        jnp.concatenate([query_weight, key_weight, value_weight], 1), places, my_place, 0
    )
    qkv_all = jnp.stack(gather_square(gather_deep(qkv_piece)))
    per_half = shares // halves
    target = my_share // per_half
    qkv_all = jnp.stack(
        [
            pick(
                pick(qkv_all, (my_share - s) % shares),
                (my_half - target) % halves * turns + (my_turn - t) % turns,
            )
            for t in range(turns)
            for s in range(shares)
        ],
        1,
    ).reshape(width, 3, half_width)
    pad_cols = lambda w: jnp.pad(w, [(0, 0)] * (w.ndim - 1) + [(0, padded - part)])
    mine = lambda w: pad_cols(own_slice(w, per_half, my_share % per_half, w.ndim - 1))
    w_qkv = mine(qkv_all).reshape(width, 3 * padded)
    b_q, b_v, b_up = split_biases(jnp.stack([send(biases, h) for h in range(halves)]))
    mine_b = lambda b: pad_cols(own_slice(b, shares, my_share, 0))
    b_qkv = jnp.concatenate([mine_b(b_q), jnp.zeros((padded,), bf16), mine_b(b_v)]).astype(f32)

    ffn_piece = jnp.concatenate(
        [
            own_slice(up_weight, places, my_place, 1),
            own_slice(down_weight, places, my_place, 0).T,
            jnp.pad(
                own_slice(output_weight.T, places, my_place, 0),
                [(0, 0), (0, max(0, hidden - half_width))],
            ).reshape(-1, hidden),
        ],
        0,
    )
    ffn_all = gather_square(gather_deep(ffn_piece))
    groups = [
        (s, i, ffn_all[s][i]) for s in range(shares) for i in range(len(spots))
    ]
    w_up = jnp.concatenate([g[:, :thin].reshape(width, hidden) for _, _, g in groups], 1)
    w_down_t = jnp.concatenate(
        [g[:, thin : 2 * thin].reshape(width, hidden) for _, _, g in groups], 1
    )
    out_all = jnp.stack(
        [jnp.stack([g[:, 2 * thin :] for g in ffn_all[s]]) for s in range(shares)]
    )
    w_out_t = jnp.stack(
        [
            jnp.stack(
                [
                    pick(
                        pick(out_all, (my_share - s) % shares),
                        (my_half - h) % halves * turns + (my_turn - t) % turns,
                    )
                    for t in range(turns)
                    for s in range(shares)
                ],
                1,
            ).reshape(width, half_width)
            for h in range(halves)
        ],
        1,
    ).reshape(width, width)
    w_out_t = jnp.concatenate(
        [own_slice(w_out_t, shares, (my_share + k) % shares, 1) for k in range(shares)], 1
    )
    group_at = [
        ((my_half - spots[i][0]) % halves * places
         + (my_turn - spots[i][1]) % turns * shares + (my_share - s) % shares)
        for s, i, _ in groups
    ]
    b_up = jnp.concatenate(
        [lax.dynamic_slice_in_dim(b_up, at * hidden, hidden) for at in group_at]
    ).astype(f32)

    g_out = bring(out_grad).astype(f32)
    x_seq = jnp.concatenate([send(x_own, 0, 0, k) for k in range(shares)], 0)
    q, k, v = (
        (
            jnp.dot(x_seq, w_qkv[:, i * padded : (i + 1) * padded], preferred_element_type=f32)
            + b_qkv[i * padded : (i + 1) * padded]
        ).astype(bf16)
        for i in range(3)
    )
    att, lse = attend(table, wide, q, k, v, key_code, query_code)
    att = att[:, :part].reshape(shares, rows, part)
    att_own = jnp.concatenate([send(att[s], 0, 0, -s) for s in range(shares)], 1)
    attn_out = lax.dot_general(
        att_own, w_out_t, (((1,), (1,)), ((), ())), preferred_element_type=f32
    ) + output_bias.astype(f32)
    x_full = x_own.astype(f32)
    first_sum = x_full + attn_out
    gain_one, shift_one = norm1_gain.astype(f32), norm1_shift.astype(f32)
    normed = layer_norm(first_sum, gain_one, shift_one)
    normed_low = normed.astype(bf16)
    pre_act = jnp.dot(normed_low, w_up, preferred_element_type=f32) + b_up
    act_low = gelu_tanh(pre_act).astype(bf16)
    ffn_out = lax.dot_general(
        act_low, w_down_t, (((1,), (1,)), ((), ())), preferred_element_type=f32
    ) + down_bias.astype(f32)
    second_sum = normed + ffn_out
    gain_two, shift_two = norm2_gain.astype(f32), norm2_shift.astype(f32)
    layer_out, norm_back = jax.vjp(layer_norm, second_sum, gain_two, shift_two)
    g_second, gain_two_grad, shift_two_grad = norm_back(g_out)
    layer_out = deliver(layer_out.astype(bf16))
    g_ffn = g_second.astype(bf16)
    g_act = jnp.dot(g_ffn, w_down_t, preferred_element_type=f32)
    g_pre = jax.vjp(gelu_tanh, pre_act)[1](g_act)[0].astype(bf16)
    up_part = jnp.dot(normed_low.T, g_pre, preferred_element_type=f32).astype(bf16)
    down_part_t = jnp.dot(g_ffn.T, act_low, preferred_element_type=f32).astype(bf16)
    g_normed = g_second + jnp.dot(g_pre, w_up.T, preferred_element_type=f32)
    g_first, gain_one_grad, shift_one_grad = jax.vjp(layer_norm, first_sum, gain_one, shift_one)[1](
        g_normed
    )
    g_attn = g_first.astype(bf16)
    out_part_t = jnp.dot(g_attn.T, att_own, preferred_element_type=f32).astype(bf16)
    g_att = jnp.dot(g_attn, w_out_t, preferred_element_type=f32).astype(bf16)
    do = jnp.concatenate(
        [send(own_slice(g_att, shares, s, 1), 0, 0, s) for s in range(shares)], 0
    )
    dq, dk, dv = attend_back(table, wide, q, k, v, pad_cols(do), key_code, query_code, lse)

    out_natural = jnp.concatenate(
        [own_slice(out_part_t, shares, (s - my_share) % shares, 1) for s in range(shares)], 1
    ).reshape(depth, turns, shares, slim, halves, half_width)

    def ffn_group(s, i):
        h, t = spots[i]
        at = (s * len(spots) + i) * hidden
        out = pick(out_natural, (my_half - h) % halves, 4)
        out = pick(pick(out, (my_turn - t) % turns, 1), (my_share - s) % shares, 1)
        out = jnp.pad(out, [(0, 0), (0, 0), (0, max(0, hidden - half_width))])
        cut = lambda w: w[:, at : at + hidden].reshape(depth, thin, hidden)
        return jnp.concatenate(
            [cut(up_part), cut(down_part_t), out.reshape(depth, -1, hidden)], 1
        )

    ffn_grads = [
        jnp.stack([ffn_group(s, i) for i in range(len(spots))]) for s in range(shares)
    ]
    total = ffn_grads[0].astype(f32)
    for s in range(1, shares):
        total = total + send(ffn_grads[s], 0, 0, -s).astype(f32)
    ffn_shard = gather_places(reduce_deep(reduce_square(total.astype(bf16))))
    dqkv = jnp.concatenate([dq, dk, dv], 1)
    qkv_part = (
        jnp.dot(x_seq.T, dqkv, preferred_element_type=f32)
        .astype(bf16)
        .reshape(depth, turns, shares, slim, 3, padded)[..., :part]
    )
    got = jnp.stack(
        [send(pick(qkv_part, (my_share + s) % shares, 2), 0, 0, s) for s in range(shares)]
    )
    got = jnp.stack([pick(got, (my_share - s) % shares) for s in range(shares)], 4)
    got = got.reshape(depth, turns, slim, 3, halves, half_width)
    square = jnp.stack(
        [
            pick(pick(got, (my_half - h) % halves, 4), (my_turn - t) % turns, 1)
            for h, t in spots
        ]
    ).reshape(len(spots), depth, slim, 3 * half_width)
    qkv_shard = gather_places(reduce_deep(reduce_square(square))).reshape(thin, 3, half_width)
    back = jnp.dot(dqkv, w_qkv.T, preferred_element_type=f32).reshape(shares, rows, width)
    back_own = back[0]
    for s in range(1, shares):
        back_own = back_own + send(back[s].astype(bf16), 0, 0, -s).astype(f32)
    input_grad = deliver((g_first + back_own).astype(bf16)).astype(f32)

    sums = lambda value: jnp.sum(value.astype(f32), 0)
    valid = live[:rows].astype(f32)
    squares = lambda member: jnp.sum(valid * jnp.sum(member * member, -1))
    stats = jnp.stack(
        [squares(m) for m in (x_full, first_sum, second_sum, attn_out, ffn_out)]
        + [jnp.sum(valid), 0.0, 0.0]
    )
    up_sums = sums(g_pre)
    norm_sums = [
        sums(g_attn), gain_one_grad, shift_one_grad, sums(g_ffn), gain_two_grad, shift_two_grad
    ]
    small = small_rows(up_sums, group_at, norm_sums, stats)
    heads = [spread(sums(d)[:part], my_share, shares)[None] for d in (dq, dv)]
    small = sum_all(jnp.concatenate([small, *heads], 0))
    return finish(
        layer_out, input_grad, qkv_shard, ffn_shard[:, :thin], ffn_shard[:, thin : 2 * thin],
        ffn_shard[:, 2 * thin :], small,
    )


def solution(mesh):
    rows, plain = P("dp", "context", None), P()
    columns, across, halves = P("dp", "tensor"), P("tensor", "dp"), P("tensor")
    return jax.shard_map(
        local,
        mesh=mesh,
        in_specs=(
            rows, rows, P("dp", None), P("dp", None), P("dp", None, None),
            columns, halves, columns, columns, halves, across, plain, plain, plain,
            columns, halves, across, plain, plain, plain,
        ),
        out_specs=(
            rows, rows, columns, halves, columns, columns, halves, across, plain,
            plain, plain, columns, halves, across, plain, plain, plain, plain,
        ),
        check_vma=False,
    )
```
